32 devices in a mesh: dp: 8 (over z, y), tensor: 4 (over x, core).
Axes of the slice: x: 2, y: 2, z: 4, core: 2. Of those that a mesh axis runs over, the one named last changes fastest.
Arguments:
- tokens: bfloat16 [8192, 1536], P('dp', 'tensor'), may hold values from -6 to 6
- segments: int32 [8, 1024], P('dp'), may hold values from 0 to 7, never falling along the last dimension, each value on 1 to 512 neighbouring positions
- attn_gain: bfloat16 [1536], P('tensor'), may hold values from 0.25 to 1.75
- w_qkv: bfloat16 [3, 1536, 1536], P(None, None, 'tensor'), may hold values from -0.15625 to 0.15625
- kq_kernel: float32 [16, 6, 11], P('tensor'), may hold values from -0.8 to 1.8
- head_mix: float32 [16, 2], P('tensor'), may hold values from -0.6 to 1.3
- group_gain: bfloat16 [1536], P('tensor'), may hold values from 0.25 to 1.75
- w_out: bfloat16 [1536, 1536], P('tensor'), may hold values from -0.15625 to 0.15625
- mlp_gain: bfloat16 [1536], P('tensor'), may hold values from 0.25 to 1.75
- w_gate_up: bfloat16 [2, 1536, 4096], P(None, None, 'tensor'), may hold values from -0.15625 to 0.15625
- w_down: bfloat16 [4096, 1536], P('tensor'), may hold values from -0.09375 to 0.09375
- cotangent: bfloat16 [8192, 1536], P('dp', 'tensor'), may hold values from -6 to 6
Outputs:
- layer_out: bfloat16 [8192, 1536], P('dp', 'tensor')
- tokens_grad: float32 [8192, 1536], P('dp', 'tensor')
- attn_gain_grad: float32 [1536], P('tensor')
- w_qkv_grad: float32 [3, 1536, 1536], P(None, None, 'tensor')
- kq_kernel_grad: float32 [16, 6, 11], P('tensor')
- head_mix_grad: float32 [16, 2], P('tensor')
- group_gain_grad: float32 [1536], P('tensor')
- w_out_grad: float32 [1536, 1536], P('tensor')
- mlp_gain_grad: float32 [1536], P('tensor')
- w_gate_up_grad: float32 [2, 1536, 4096], P(None, None, 'tensor')
- w_down_grad: float32 [4096, 1536], P('tensor')
The draws below stay inside these ranges and needn't reach their ends.
Inputs may be any that keep to these rules, and one draw needn't show every extreme that they name: `segments`: within a sequence the numbers never fall; each document holds at most 512 tokens.
All inputs are finite; a program needn't handle non-finite values.
Results may differ from the reference program's by a relative error of at most 0.018.
The reference program's roundings to bfloat16 on the way count: a program that leaves them out, or rounds other values in their place, can miss the bound.
Values may be sent and summed in bfloat16 or wider, within the bound.
A program may use at most 320 MiB of HBM per device.

```python
import math
import jax
import jax.numpy as jnp
import numpy as np
from jax import lax

D = 1536
HEADS = 16
HEAD_DIM = 96
FF = 4096
CQ = 6
CK = 11
LENGTH = 1024
DOCS = 8
DOC_MOST = 512
SEQS = 8
TOKENS = 8192


def draw_kq_kernel(key, part):
    shape = (HEADS, CQ, CK)
    noise = 0.2 * jax.random.truncated_normal(key, -4.0, 4.0, shape, jnp.float32)
    query_place = lax.broadcasted_iota(jnp.int32, shape, 1)
    key_place = lax.broadcasted_iota(jnp.int32, shape, 2)
    centre = jnp.where((query_place == 0) & (key_place == CK // 2), 1.0, 0.0).astype(jnp.float32)
    return noise + centre


def draw_head_mix(key, part):
    own_key, other_key = jax.random.split(jax.random.fold_in(key, 7))
    own = jax.random.uniform(own_key, (HEADS, 2), jnp.float32, 0.7, 1.3)
    other = jax.random.uniform(other_key, (HEADS, 2), jnp.float32, -0.6, 0.6)
    head_place = lax.broadcasted_iota(jnp.int32, (HEADS, 2), 0)
    slot_place = lax.broadcasted_iota(jnp.int32, (HEADS, 2), 1)
    return jnp.where(head_place % 2 == slot_place, own, other)


def level_of(key, dims, shards, least, largest):
    level, own = 1.0, jax.random.fold_in(key, 6)
    for axis_at, parts in shards:
        steps = jnp.exp(jax.random.uniform(jax.random.fold_in(own, axis_at), (parts,), jnp.float32, least / len(shards), largest / len(shards)))
        level = level * jnp.repeat(steps, dims[axis_at] // parts).reshape([-1 if axis == axis_at else 1 for axis in range(len(dims))])
    return level


def length_profile(number_of, total, most, skew):
    portions = [(1 << 20) // math.isqrt(rank ** skew) + 1 for rank in range(2, number_of + 1)]
    rest, given = total - most - (number_of - 1), [1] * (number_of - 1)
    while rest > 0:
        candidates = [i for i in range(number_of - 1) if given[i] < most]
        mass, left = sum([portions[i] for i in candidates]), rest
        for i in candidates:
            extra = min(most - given[i], max(1, left * portions[i] // mass), rest)
            given[i] = given[i] + extra
            rest = rest - extra
    return np.array([most] + given)


def uneven(rng, count, total, most, lean):
    if count == 2:
        one = jax.random.randint(rng, (), max(1, total - most), min(most, total - 1) + 1)
        return jnp.stack([one, total - one])
    lengths = jnp.asarray(length_profile(count, total, most, lean), jnp.int32)
    twos = (count - 1) // 2
    source_of, taker = lengths[1:1 + 2 * twos:2], lengths[2:2 + 2 * twos:2]
    margin = jnp.minimum(source_of - 1, most - taker)
    moved = jax.random.randint(jax.random.fold_in(rng, 1), (twos,), 0, 1 << 20) % (margin + 1)
    lengths = lengths.at[1:1 + 2 * twos:2].set(source_of - moved).at[2:2 + 2 * twos:2].set(taker + moved)
    return lengths[jax.random.permutation(jax.random.fold_in(rng, 2), count)]


def normal_values(key, shape, spread, reach, pieces=(), kind=jnp.bfloat16):
    array = spread * jax.random.normal(key, shape, jnp.float32)
    if pieces:
        array = array * level_of(key, shape, pieces, -0.22, 0.18)
    return jnp.clip(array, -reach, reach).astype(kind)


def setup_inputs(seed: int = 0) -> dict:
    seeds = jax.random.split(jax.random.key(seed), 13)
    return {
        "tokens": normal_values(seeds[0], (TOKENS, D), 1.0, 6.0, ((0, 8), (1, 4))),
        "segments": jax.vmap(lambda own: jnp.searchsorted(jnp.cumsum(uneven(own, DOCS, LENGTH, DOC_MOST, 2)), jnp.arange(LENGTH), side="right"))(jax.random.split(seeds[1], SEQS)).reshape((SEQS, LENGTH)).astype(jnp.int32),
        "attn_gain": jnp.clip(1.0 + 0.15 * jax.random.normal(seeds[2], (D,), jnp.float32), 0.25, 1.75).astype(jnp.bfloat16),
        "w_qkv": normal_values(seeds[3], (3, D, D), D ** -0.5, 0.15625, ((2, 4),)),
        "kq_kernel": draw_kq_kernel(jax.random.fold_in(seeds[12], 71), 0),
        "head_mix": draw_head_mix(jax.random.fold_in(seeds[12], 71), 0),
        "group_gain": jnp.clip(1.0 + 0.15 * jax.random.normal(seeds[6], (D,), jnp.float32), 0.25, 1.75).astype(jnp.bfloat16),
        "w_out": normal_values(seeds[7], (D, D), D ** -0.5, 0.15625, ((0, 4),)),
        "mlp_gain": jnp.clip(1.0 + 0.15 * jax.random.normal(seeds[8], (D,), jnp.float32), 0.25, 1.75).astype(jnp.bfloat16),
        "w_gate_up": normal_values(seeds[9], (2, D, FF), D ** -0.5, 0.15625, ((2, 4),)),
        "w_down": normal_values(seeds[10], (FF, D), FF ** -0.5, 0.09375, ((0, 4),)),
        "cotangent": normal_values(seeds[11], (TOKENS, D), 1.0, 6.0, ((0, 8), (1, 4))),
    }


EPS = 1e-05
NEG = -1e+30
HIGH = lax.Precision.HIGHEST

@jax.custom_vjp
def low(v):
    return lax.optimization_barrier(v.astype(jnp.bfloat16)).astype(jnp.float32)

@jax.custom_vjp
def low_back(v):
    return v

def low_keep(v):
    return (low(v), None)

def low_pass(kept, grad):
    return (grad,)

def back_keep(v):
    return (v, None)

def back_low(kept, grad):
    return (low(grad),)
low.defvjp(low_keep, low_pass)
low_back.defvjp(back_keep, back_low)

def matmul(left, right):
    return jnp.dot(left, right, precision=HIGH)

def rms_norm(values, gain):
    return values * lax.rsqrt(lax.optimization_barrier(jnp.mean(values * values, axis=-1, keepdims=True)) + EPS) * gain

def valid_pairs(seg_row):
    length = seg_row.shape[0]
    place = lax.iota(jnp.int32, length)
    return (place[None, :] <= place[:, None]) & (seg_row[:, None] == seg_row[None, :])

def kq_conv(masked, kernel):
    query_taps = kernel.shape[1]
    key_taps = kernel.shape[2]
    key_half = key_taps // 2
    heads_here = masked.shape[0]
    length = masked.shape[1]
    padded = jnp.pad(masked, ((0, 0), (query_taps - 1, 0), (key_half, key_half)))
    summed = jnp.zeros(masked.shape, jnp.float32)
    for query_shift in range(query_taps):
        for key_shift in range(key_taps):
            row_start = query_taps - 1 - query_shift
            col_start = key_taps - 1 - key_shift
            shifted = lax.slice(padded, (0, row_start, col_start), (heads_here, row_start + length, col_start + length))
            summed = summed + kernel[:, query_shift, key_shift][:, None, None] * shifted
    return summed

def attend(query, keys, values, seg_row, kernel, mix):
    scale = HEAD_DIM ** (-0.5)
    heads_here = query.shape[1]
    length = query.shape[0]
    raw = jnp.einsum('qhd,khd->hqk', query, keys, precision=HIGH)
    valid = valid_pairs(seg_row)[None]
    masked = jnp.where(valid, low_back(raw) * scale, 0.0)
    logits = jnp.where(valid, kq_conv(masked, kernel), NEG)
    probs = jax.nn.softmax(logits, axis=-1)
    paired = probs.reshape(heads_here // 2, 2, length, length)
    weights = mix.reshape(heads_here // 2, 2, 2)
    mixed = jnp.einsum('grs,gsqk->grqk', weights, paired, precision=HIGH).reshape(heads_here, length, length)
    mixed = low(mixed)
    output = jnp.einsum('hqk,khd->qhd', mixed, values, precision=HIGH)
    return low_back(output)

def layer(tokens, attn_gain, w_qkv, kq_kernel, head_mix, group_gain, w_out, mlp_gain, w_gate_up, w_down, segments):
    normed_one = low(rms_norm(tokens, attn_gain))
    query = low(low_back(matmul(normed_one, w_qkv[0])))
    keys = low(low_back(matmul(normed_one, w_qkv[1])))
    values = low(low_back(matmul(normed_one, w_qkv[2])))
    shape = (SEQS, LENGTH, HEADS, HEAD_DIM)

    def one_sequence(items):
        return attend(items[0], items[1], items[2], items[3], kq_kernel, head_mix)
    heads_out = lax.map(jax.checkpoint(one_sequence), (query.reshape(shape), keys.reshape(shape), values.reshape(shape), segments))
    heads_out = heads_out.reshape(TOKENS, HEADS, HEAD_DIM)
    grouped = rms_norm(heads_out, group_gain.reshape(HEADS, HEAD_DIM)).reshape(TOKENS, D)
    attn = low_back(matmul(low(grouped), w_out))
    hidden = tokens + attn
    normed_two = low(rms_norm(hidden, mlp_gain))
    gate = low_back(matmul(normed_two, w_gate_up[0]))
    up = low_back(matmul(normed_two, w_gate_up[1]))
    act = low(jax.nn.silu(gate) * up)
    return hidden + matmul(act, w_down)

def reference(tokens, segments, attn_gain, w_qkv, kq_kernel, head_mix, group_gain, w_out, mlp_gain, w_gate_up, w_down, cotangent):
    floats = (tokens.astype(jnp.float32), attn_gain.astype(jnp.float32), w_qkv.astype(jnp.float32), kq_kernel.astype(jnp.float32), head_mix.astype(jnp.float32), group_gain.astype(jnp.float32), w_out.astype(jnp.float32), mlp_gain.astype(jnp.float32), w_gate_up.astype(jnp.float32), w_down.astype(jnp.float32))

    def forward(x_in, g_one, w_proj, kernel, mix, g_group, w_proj_out, g_two, w_gu, w_dn):
        return layer(x_in, g_one, w_proj, kernel, mix, g_group, w_proj_out, g_two, w_gu, w_dn, segments)
    result, pullback = jax.vjp(forward, *floats)
    grads = pullback(cotangent.astype(jnp.float32))
    return (result.astype(jnp.bfloat16), grads[0], grads[1], grads[2], grads[3], grads[4], grads[5], grads[6], grads[7], grads[8], grads[9])
```

```python
import functools

import jax
import jax.numpy as jnp
from jax import lax
from jax.experimental import pallas as pl
from jax.experimental.pallas import tpu as pltpu
from jax.sharding import PartitionSpec as P

HEAD_DIM = 96
PAD_DIM = 128
DOC_MOST = 512
EPS = 1e-05
NEG = -1e30

ROWS = 128
HALO = 16
WIN = 256
OWN = 16
STEP = WIN - 2 * OWN
TOP = 256
EXT = ROWS + HALO

F32 = jnp.float32
BF16 = jnp.bfloat16


def windows_most(key_half):
    return -(-(DOC_MOST - 1 + ROWS + key_half) // STEP)


def dot_nt(a, b):
    return lax.dot_general(a, b, (((1,), (1,)), ((), ())), preferred_element_type=F32)


def dot_tn(a, b):
    return lax.dot_general(a, b, (((0,), (0,)), ((), ())), preferred_element_type=F32)


def dot_nn(a, b):
    return jnp.dot(a, b, preferred_element_type=F32)


def fill_padded(dst, src, top, length):
    total = dst.shape[0]
    dst[0:top, :] = jnp.zeros((top, dst.shape[1]), dst.dtype)
    dst[top : top + length, :] = src[...]
    if total > top + length:
        dst[top + length : total, :] = jnp.zeros((total - top - length, dst.shape[1]), dst.dtype)


def lanes_between(first, last, width):
    lane = lax.broadcasted_iota(jnp.int32, (first.shape[0], width), 1)
    return (lane >= first) & (lane <= last)


def row_numbers(base, count):
    return base + lax.broadcasted_iota(jnp.int32, (count, 1), 0)


def forward_kernel(
    n_taps, key_half, most, count_ref, mix_ref, q_ref, k_ref, v_ref, start_ref, t_hi_ref, t_lo_ref,
    gain_ref, probs_ref, heads_ref, grouped_ref, qs, ks, vs, logit_ref,
):
    pair = pl.program_id(0)
    block = pl.program_id(1)
    length = q_ref.shape[0]
    scale = HEAD_DIM ** (-0.5)

    @pl.when(block == 0)
    def _():
        fill_padded(qs, q_ref, HALO, length)
        fill_padded(ks, k_ref, TOP, length)
        fill_padded(vs, v_ref, TOP, length)

    row0 = pl.multiple_of(block * ROWS, ROWS)

    def body(n):
        start = start_ref[pl.ds(row0, EXT), :]
        place = row_numbers(row0 - HALO, EXT)
        peaks = [None, None]
        for k in range(n):
            base = row0 + ROWS - STEP * (k + 1) - OWN
            at = pl.multiple_of(TOP + base, 16)
            first = start - base
            last = place - base
            valid = lanes_between(first, last, WIN)
            shown = lanes_between(
                jnp.maximum(first[HALO:], key_half + 1), jnp.minimum(last[HALO:], WIN - 2 - key_half), WIN
            )
            for s in range(2):
                cols = pl.ds(s * PAD_DIM, PAD_DIM)
                raw = dot_nt(qs[pl.ds(row0, EXT), cols], ks[pl.ds(at, WIN), cols])
                masked = jnp.where(valid, raw * scale, 0.0)
                hi = masked.astype(BF16)
                lo = (masked - hi.astype(F32)).astype(BF16)
                total = None
                for a in reversed(range(n_taps)):
                    t_hi = t_hi_ref[s, a]
                    term = dot_nn(hi, t_hi) + dot_nn(lo, t_hi) + dot_nn(hi, t_lo_ref[s, a])
                    total = term if total is None else pltpu.roll(total, 1, 0) + term
                logits = jnp.where(shown, total[HALO:], NEG)
                logit_ref[s, k] = logits
                top = jnp.max(logits, axis=-1, keepdims=True)
                peaks[s] = top if peaks[s] is None else jnp.maximum(peaks[s], top)
        lane = lax.broadcasted_iota(jnp.int32, (ROWS, WIN), 1)
        own = (lane >= OWN) & (lane < WIN - OWN)
        sums = [None, None]
        for k in range(n):
            for s in range(2):
                expo = jnp.exp(logit_ref[s, k] - peaks[s])
                logit_ref[s, k] = expo
                part = jnp.sum(jnp.where(own, expo, 0.0), axis=-1, keepdims=True)
                sums[s] = part if sums[s] is None else sums[s] + part
        inverse = [1.0 / sums[s] for s in range(2)]
        outs = [None, None]
        for k in range(n):
            base = row0 + ROWS - STEP * (k + 1) - OWN
            at = pl.multiple_of(TOP + base, 16)
            probs = []
            for s in range(2):
                prob = logit_ref[s, k] * inverse[s]
                probs_ref[s, 0, k] = prob
                probs.append(jnp.where(own, prob, 0.0))
            for h in range(2):
                mixed = (
                    mix_ref[2 * pair + h, 0] * probs[0] + mix_ref[2 * pair + h, 1] * probs[1]
                ).astype(BF16)
                part = dot_nn(mixed, vs[pl.ds(at, WIN), pl.ds(h * PAD_DIM, PAD_DIM)])
                outs[h] = part if outs[h] is None else outs[h] + part
        for h in range(2):
            cols = slice(h * PAD_DIM, (h + 1) * PAD_DIM)
            out = outs[h]
            heads_ref[:, cols] = out
            factor = lax.rsqrt(jnp.sum(out * out, axis=-1, keepdims=True) * (1.0 / HEAD_DIM) + EPS)
            grouped_ref[:, cols] = (out * factor * gain_ref[:, cols]).astype(BF16)

    for n in range(1, most + 1):
        pl.when(count_ref[block] == n)(functools.partial(body, n))


def attend_forward(proj, start, counts, t_hi, t_lo, mix, gain):
    length = proj.shape[0]
    heads, n_taps = t_hi.shape[:2]
    pairs = heads // 2
    blocks = length // ROWS
    key_half = 5
    most = windows_most(key_half)
    two = 2 * PAD_DIM
    grid_spec = pltpu.PrefetchScalarGridSpec(
        num_scalar_prefetch=2,
        grid=(pairs, blocks),
        in_specs=[
            pl.BlockSpec((length, two), lambda p, b, *_: (0, p)),
            pl.BlockSpec((length, two), lambda p, b, *_: (0, pairs + p)),
            pl.BlockSpec((length, two), lambda p, b, *_: (0, 2 * pairs + p)),
            pl.BlockSpec((HALO + length, 1), lambda p, b, *_: (0, 0)),
            pl.BlockSpec((2, n_taps, WIN, WIN), lambda p, b, *_: (p, 0, 0, 0)),
            pl.BlockSpec((2, n_taps, WIN, WIN), lambda p, b, *_: (p, 0, 0, 0)),
            pl.BlockSpec((1, two), lambda p, b, *_: (0, p)),
        ],
        out_specs=[
            pl.BlockSpec((2, 1, most, ROWS, WIN), lambda p, b, *_: (p, b, 0, 0, 0)),
            pl.BlockSpec((ROWS, two), lambda p, b, *_: (b, p)),
            pl.BlockSpec((ROWS, two), lambda p, b, *_: (b, p)),
        ],
        scratch_shapes=[
            pltpu.VMEM((HALO + length, two), BF16),
            pltpu.VMEM((TOP + length + HALO, two), BF16),
            pltpu.VMEM((TOP + length + HALO, two), BF16),
            pltpu.VMEM((2, most, ROWS, WIN), F32),
        ],
    )
    return pl.pallas_call(
        functools.partial(forward_kernel, n_taps, key_half, most),
        grid_spec=grid_spec,
        out_shape=[
            jax.ShapeDtypeStruct((heads, blocks, most, ROWS, WIN), F32),
            jax.ShapeDtypeStruct((length, heads * PAD_DIM), F32),
            jax.ShapeDtypeStruct((length, heads * PAD_DIM), BF16),
        ],
        compiler_params=pltpu.CompilerParams(vmem_limit_bytes=40 << 20),
        name="attend_forward",
    )(counts, mix, proj, proj, proj, start, t_hi, t_lo, gain)


def backward_kernel(
    n_taps, key_half, most, count_ref, mix_ref, q_ref, k_ref, v_ref, start_ref, t_back_ref, gain_ref,
    probs_ref, heads_ref, grad_ref, dq_ref, dk_ref, dv_ref, gain_grad_ref, tap_ref, mix_grad_ref,
    qs, ks, vs, dq_sum, dk_sum, dv_sum, taps, inputs, tap_sum, mixed_grad,
):
    pair = pl.program_id(0)
    block = pl.program_id(1)
    length = q_ref.shape[0]
    scale = HEAD_DIM ** (-0.5)

    @pl.when(block == 0)
    def _():
        fill_padded(qs, q_ref, HALO, length)
        fill_padded(ks, k_ref, TOP, length)
        fill_padded(vs, v_ref, TOP, length)
        dq_sum[...] = jnp.zeros_like(dq_sum)
        dk_sum[...] = jnp.zeros_like(dk_sum)
        dv_sum[...] = jnp.zeros_like(dv_sum)
        tap_sum[...] = jnp.zeros_like(tap_sum)
        gain_grad_ref[...] = jnp.zeros_like(gain_grad_ref)
        mix_grad_ref[...] = jnp.zeros_like(mix_grad_ref)

    row0 = pl.multiple_of(block * ROWS, ROWS)

    def body(n):
        grads = []
        for h in range(2):
            cols = slice(h * PAD_DIM, (h + 1) * PAD_DIM)
            out = heads_ref[:, cols]
            factor = lax.rsqrt(jnp.sum(out * out, axis=-1, keepdims=True) * (1.0 / HEAD_DIM) + EPS)
            unit = out * factor
            grad = grad_ref[:, cols]
            gain_grad_ref[:, cols] += jnp.sum(grad * unit, axis=0, keepdims=True)
            scaled = grad * gain_ref[:, cols]
            inner = jnp.sum(scaled * unit, axis=-1, keepdims=True) * (1.0 / HEAD_DIM)
            grads.append((factor * (scaled - unit * inner)).astype(BF16))
        lane = lax.broadcasted_iota(jnp.int32, (ROWS, WIN), 1)
        own = (lane >= OWN) & (lane < WIN - OWN)
        inner = [[None, None], [None, None]]
        for k in range(n):
            base = row0 + ROWS - STEP * (k + 1) - OWN
            at = pl.multiple_of(TOP + base, 16)
            probs = [jnp.where(own, probs_ref[s, 0, k], 0.0) for s in range(2)]
            for h in range(2):
                cols = pl.ds(h * PAD_DIM, PAD_DIM)
                grad_mixed = dot_nt(grads[h], vs[pl.ds(at, WIN), cols])
                mixed_grad[h, k] = grad_mixed
                for s in range(2):
                    part = jnp.sum(grad_mixed * probs[s], axis=-1, keepdims=True)
                    inner[h][s] = part if inner[h][s] is None else inner[h][s] + part
                mixed = (
                    mix_ref[2 * pair + h, 0] * probs[0] + mix_ref[2 * pair + h, 1] * probs[1]
                ).astype(BF16)
                dv_sum[pl.ds(at, WIN), cols] += dot_tn(mixed, grads[h])
        for h in range(2):
            for s in range(2):
                row = 2 * h + s
                mix_grad_ref[0, row : row + 1, :] += jnp.broadcast_to(
                    jnp.sum(inner[h][s], axis=0, keepdims=True), (1, PAD_DIM)
                )
        start = start_ref[pl.ds(row0, EXT), :]
        place = row_numbers(row0 - HALO, EXT)
        for s in range(2):
            cols = pl.ds(s * PAD_DIM, PAD_DIM)
            mix0 = mix_ref[2 * pair, s]
            mix1 = mix_ref[2 * pair + 1, s]
            delta = mix0 * inner[0][s] + mix1 * inner[1][s]
            query = qs[pl.ds(row0, EXT), cols]
            for k in range(n):
                base = row0 + ROWS - STEP * (k + 1) - OWN
                at = pl.multiple_of(TOP + base, 16)
                keys = ks[pl.ds(at, WIN), cols]
                mine = lanes_between(
                    jnp.maximum(start - base, OWN), jnp.minimum(place - base, WIN - OWN - 1), WIN
                )
                grad_prob = mix0 * mixed_grad[0, k] + mix1 * mixed_grad[1, k]
                grad_logit = probs_ref[s, 0, k] * (grad_prob - delta)
                grown = jnp.concatenate([jnp.zeros((HALO, WIN), F32), grad_logit], axis=0)
                for a in range(n_taps):
                    moved = grown if a == 0 else pltpu.roll(grown, EXT - a, 0)
                    taps[k * EXT : (k + 1) * EXT, a * WIN : (a + 1) * WIN] = moved.astype(BF16)
                grad_masked = dot_nn(taps[k * EXT : (k + 1) * EXT, :], t_back_ref[s])
                grad_score = jnp.where(mine, grad_masked * scale, 0.0).astype(BF16)
                dq_sum[pl.ds(row0, EXT), cols] += dot_nn(grad_score, keys)
                dk_sum[pl.ds(at, WIN), cols] += dot_tn(grad_score, query)
                raw = dot_nt(query, keys)
                inputs[k * EXT : (k + 1) * EXT, :] = jnp.where(mine, raw * scale, 0.0).astype(BF16)
            tap_sum[s] += dot_tn(inputs[0 : n * EXT, :], taps[0 : n * EXT, :])

    for n in range(1, most + 1):
        pl.when(count_ref[block] == n)(functools.partial(body, n))

    @pl.when(block == pl.num_programs(1) - 1)
    def _():
        dq_ref[...] = dq_sum[HALO : HALO + length, :].astype(BF16)
        dk_ref[...] = dk_sum[TOP : TOP + length, :].astype(BF16)
        dv_ref[...] = dv_sum[TOP : TOP + length, :].astype(BF16)
        row = lax.broadcasted_iota(jnp.int32, (WIN, WIN), 0)
        lane = lax.broadcasted_iota(jnp.int32, (WIN, WIN), 1)
        for s in range(2):
            for a in range(n_taps):
                whole = tap_sum[s, :, a * WIN : (a + 1) * WIN]
                for b in range(2 * key_half + 1):
                    part = jnp.where(lane - row == b - key_half, whole, 0.0)
                    part = jnp.sum(part, axis=0, keepdims=True)
                    part = jnp.sum(part, axis=1, keepdims=True)
                    at = a * (2 * key_half + 1) + b
                    tap_ref[s, at : at + 1, :] = jnp.broadcast_to(part, (1, PAD_DIM))


def attend_backward(proj, start, counts, t_back, mix, gain, probs, heads_out, grad_grouped):
    length = proj.shape[0]
    heads = probs.shape[0]
    n_taps = t_back.shape[1] // WIN
    pairs = heads // 2
    blocks = length // ROWS
    key_half = 5
    most = windows_most(key_half)
    two = 2 * PAD_DIM
    tap_rows = n_taps * (2 * key_half + 1)
    whole = pl.BlockSpec((length, two), lambda p, b, *_: (0, p))
    grid_spec = pltpu.PrefetchScalarGridSpec(
        num_scalar_prefetch=2,
        grid=(pairs, blocks),
        in_specs=[
            pl.BlockSpec((length, two), lambda p, b, *_: (0, p)),
            pl.BlockSpec((length, two), lambda p, b, *_: (0, pairs + p)),
            pl.BlockSpec((length, two), lambda p, b, *_: (0, 2 * pairs + p)),
            pl.BlockSpec((HALO + length, 1), lambda p, b, *_: (0, 0)),
            pl.BlockSpec((2, n_taps * WIN, WIN), lambda p, b, *_: (p, 0, 0)),
            pl.BlockSpec((1, two), lambda p, b, *_: (0, p)),
            pl.BlockSpec((2, 1, most, ROWS, WIN), lambda p, b, *_: (p, b, 0, 0, 0)),
            pl.BlockSpec((ROWS, two), lambda p, b, *_: (b, p)),
            pl.BlockSpec((ROWS, two), lambda p, b, *_: (b, p)),
        ],
        out_specs=[
            whole,
            whole,
            whole,
            pl.BlockSpec((1, two), lambda p, b, *_: (0, p)),
            pl.BlockSpec((2, tap_rows, PAD_DIM), lambda p, b, *_: (p, 0, 0)),
            pl.BlockSpec((1, 4, PAD_DIM), lambda p, b, *_: (p, 0, 0)),
        ],
        scratch_shapes=[
            pltpu.VMEM((HALO + length, two), BF16),
            pltpu.VMEM((TOP + length + HALO, two), BF16),
            pltpu.VMEM((TOP + length + HALO, two), BF16),
            pltpu.VMEM((HALO + length, two), F32),
            pltpu.VMEM((TOP + length + HALO, two), F32),
            pltpu.VMEM((TOP + length + HALO, two), F32),
            pltpu.VMEM((most * EXT, n_taps * WIN), BF16),
            pltpu.VMEM((most * EXT, WIN), BF16),
            pltpu.VMEM((2, WIN, n_taps * WIN), F32),
            pltpu.VMEM((2, most, ROWS, WIN), F32),
        ],
    )
    return pl.pallas_call(
        functools.partial(backward_kernel, n_taps, key_half, most),
        grid_spec=grid_spec,
        out_shape=[
            jax.ShapeDtypeStruct((length, heads * PAD_DIM), BF16),
            jax.ShapeDtypeStruct((length, heads * PAD_DIM), BF16),
            jax.ShapeDtypeStruct((length, heads * PAD_DIM), BF16),
            jax.ShapeDtypeStruct((1, heads * PAD_DIM), F32),
            jax.ShapeDtypeStruct((heads, tap_rows, PAD_DIM), F32),
            jax.ShapeDtypeStruct((pairs, 4, PAD_DIM), F32),
        ],
        compiler_params=pltpu.CompilerParams(vmem_limit_bytes=48 << 20),
        name="attend_backward",
    )(counts, mix, proj, proj, proj, start, t_back, gain, probs, heads_out, grad_grouped)


MESH_ID = pl.DeviceIdType.MESH


def ring_place(member, n):
    z, y = member // 2, member % 2
    return (1 - y) * z + y * (n - 1 - z)


def ring_member(place, n):
    upper = place // (n // 2)
    return (1 - upper) * 2 * place + upper * (2 * (n - 1 - place) + 1)


def ring_kernel(n, count, *refs):
    ins, outs, slots = refs[:count], refs[count : 2 * count], refs[2 * count : 3 * count]
    rs_send, rs_recv, ag_send, ag_recv = refs[3 * count :]
    place = ring_place(lax.axis_index("dp"), n)
    to = (
        ring_member(lax.rem(place + 1, n), n),
        ring_member(lax.rem(place + n - 1, n), n),
    )
    barrier = pltpu.get_barrier_semaphore()
    for peer in to:
        pl.semaphore_signal(barrier, inc=1, device_id={"dp": peer}, device_id_type=MESH_ID)
    pl.semaphore_wait(barrier, 2)

    def chunk(way, back):
        return lax.rem(place - back + 2 * n if way == 0 else place + back, n)

    def sum_copy(way, k, s, src):
        return pltpu.make_async_remote_copy(
            src_ref=src,
            dst_ref=slots[k].at[way, s],
            send_sem=rs_send.at[way, k, s],
            recv_sem=rs_recv.at[way, k, s],
            device_id={"dp": to[way]},
            device_id_type=MESH_ID,
        )

    def share_copy(way, k, s, c):
        return pltpu.make_async_remote_copy(
            src_ref=outs[k].at[c, way],
            dst_ref=outs[k].at[c, way],
            send_sem=ag_send.at[way, k, s],
            recv_sem=ag_recv.at[way, k, s],
            device_id={"dp": to[way]},
            device_id_type=MESH_ID,
        )

    def add(way, k, s, c, dst):
        total = slots[k][way, s].astype(F32) + ins[k][c, way].astype(F32)
        dst[...] = total.astype(dst.dtype)

    both = [(k, way) for k in range(count) for way in range(2)]
    for k, way in both:
        sum_copy(way, k, 0, ins[k].at[chunk(way, 1), way]).start()

    def sum_step(s, carry):
        for k, way in both:
            sum_copy(way, k, s, slots[k].at[way, s]).wait_recv()
            add(way, k, s, chunk(way, 2 + s), slots[k].at[way, s])
            sum_copy(way, k, s + 1, slots[k].at[way, s]).start()
        return carry

    lax.fori_loop(0, n - 2, sum_step, 0)
    for k, way in both:
        sum_copy(way, k, n - 2, slots[k].at[way, n - 2]).wait_recv()
        add(way, k, n - 2, place, outs[k].at[place, way])
        share_copy(way, k, 0, place).start()

    def share_step(s, carry):
        for k, way in both:
            share_copy(way, k, s, chunk(way, s + 1)).wait_recv()
            share_copy(way, k, s + 1, chunk(way, s + 1)).start()
        return carry

    lax.fori_loop(0, n - 2, share_step, 0)
    for k, way in both:
        share_copy(way, k, n - 2, chunk(way, n - 1)).wait_recv()

    def drain(s, carry):
        for k, way in both:
            sum_copy(way, k, s, slots[k].at[way, s]).wait_send()
            share_copy(way, k, s, place).wait_send()
        return carry

    lax.fori_loop(0, n - 1, drain, 0)


def ring_sum(arrays, collective_id):
    n = lax.axis_size("dp")
    split = [a.reshape(n, 2, -1, a.shape[-1]) for a in arrays]
    count = len(arrays)
    vmem = pl.BlockSpec(memory_space=pltpu.VMEM)
    outs = pl.pallas_call(
        functools.partial(ring_kernel, n, count),
        out_shape=[jax.ShapeDtypeStruct(a.shape, a.dtype) for a in split],
        in_specs=[vmem] * count,
        out_specs=[vmem] * count,
        scratch_shapes=[pltpu.VMEM((2, n - 1) + a.shape[2:], a.dtype) for a in split]
        + [pltpu.SemaphoreType.DMA((2, count, n - 1))] * 4,
        compiler_params=pltpu.CompilerParams(
            collective_id=collective_id, has_side_effects=True, vmem_limit_bytes=60 << 20
        ),
        name="ring_sum",
    )(*split)
    return [o.reshape(a.shape) for o, a in zip(outs, arrays)]


def pack_small(arrays, n):
    flat = jnp.concatenate([a.reshape(-1) for a in arrays])
    unit = 2 * n * 8 * 128
    return jnp.pad(flat, (0, -flat.size % unit)).reshape(-1, 128)


def unpack_small(packed, arrays):
    flat, found, at = packed.reshape(-1), [], 0
    for a in arrays:
        found.append(flat[at : at + a.size].reshape(a.shape))
        at += a.size
    return found


def banded(kernel, back):
    half = kernel.shape[2] // 2
    row = lax.broadcasted_iota(jnp.int32, (WIN, WIN), 0)
    lane = lax.broadcasted_iota(jnp.int32, (WIN, WIN), 1)
    apart = (row - lane if back else lane - row) + half
    full = jnp.zeros(kernel.shape[:2] + (WIN, WIN), F32)
    for b in range(kernel.shape[2]):
        full = jnp.where(apart == b, kernel[:, :, b][:, :, None, None], full)
    return full


def pad_heads(array, axis):
    shape = array.shape
    heads = shape[axis] // HEAD_DIM
    split = array.reshape(shape[:axis] + (heads, HEAD_DIM) + shape[axis + 1 :])
    widths = [(0, 0)] * split.ndim
    widths[axis + 1] = (0, PAD_DIM - HEAD_DIM)
    return jnp.pad(split, widths).reshape(shape[:axis] + (heads * PAD_DIM,) + shape[axis + 1 :])


def cut_heads(array, axis):
    shape = array.shape
    heads = shape[axis] // PAD_DIM
    split = array.reshape(shape[:axis] + (heads, PAD_DIM) + shape[axis + 1 :])
    cut = lax.slice_in_dim(split, 0, HEAD_DIM, axis=axis + 1)
    return cut.reshape(shape[:axis] + (heads * HEAD_DIM,) + shape[axis + 1 :])


def windows_needed(start, key_half):
    length = start.shape[0]
    first = start[::ROWS]
    row0 = jnp.arange(0, length, ROWS, dtype=jnp.int32)
    count = jnp.ones_like(first)
    for k in range(1, windows_most(key_half)):
        count = count + (first - key_half < row0 + ROWS - STEP * k).astype(jnp.int32)
    return count


def on_device(
    tokens, segments, attn_gain, w_qkv, kq_kernel, head_mix, group_gain, w_out, mlp_gain, w_gate_up,
    w_down, cotangent,
):
    rows_here, local_width = tokens.shape
    seq_count, length = segments.shape
    heads_here = local_width // HEAD_DIM
    n_taps, key_taps = kq_kernel.shape[1:]
    key_half = key_taps // 2

    t_full = banded(kq_kernel, False)
    t_hi = t_full.astype(BF16)
    t_lo = (t_full - t_hi.astype(F32)).astype(BF16)
    t_back = banded(kq_kernel, True).astype(BF16).reshape(heads_here, n_taps * WIN, WIN)
    w_proj = pad_heads(w_qkv, 2).transpose(1, 0, 2).reshape(w_qkv.shape[1], -1)
    w_out_pad = pad_heads(w_out, 0)
    gain_heads = pad_heads(group_gain.astype(F32), 0)[None]
    starts, counts = [], []
    for n in range(seq_count):
        seg = segments[n]
        start = jnp.sum((seg[None, :] < seg[:, None]).astype(jnp.int32), axis=1)
        counts.append(windows_needed(start, key_half))
        starts.append(jnp.pad(start, (HALO, 0), constant_values=1 << 20)[:, None])

    gathered = lax.all_gather(tokens, "tensor", axis=1, tiled=True)
    gain_one = lax.all_gather(attn_gain, "tensor", axis=0, tiled=True).astype(F32)
    gain_two = lax.all_gather(mlp_gain, "tensor", axis=0, tiled=True).astype(F32)
    full_cot = lax.all_gather(cotangent, "tensor", axis=1, tiled=True)

    resid = gathered.astype(F32)
    full_width = resid.shape[1]
    scale_one = lax.rsqrt(jnp.mean(resid * resid, axis=-1, keepdims=True) + EPS)
    unit_one = resid * scale_one
    normed_one = (unit_one * gain_one).astype(BF16)
    proj = jnp.dot(normed_one, w_proj, preferred_element_type=F32).astype(BF16)

    kept = []
    for n in range(seq_count):
        rows = slice(n * length, (n + 1) * length)
        kept.append(
            attend_forward(proj[rows], starts[n], counts[n], t_hi, t_lo, head_mix, gain_heads)
        )
    grouped = jnp.concatenate([one[2] for one in kept], axis=0)
    attn_part = jnp.dot(grouped, w_out_pad, preferred_element_type=F32).astype(BF16)
    attn_local = lax.psum_scatter(attn_part, "tensor", scatter_dimension=1, tiled=True).astype(F32)
    hidden_local = tokens.astype(F32) + attn_local
    hidden = lax.all_gather(hidden_local.astype(BF16), "tensor", axis=1, tiled=True).astype(F32)
    scale_two = lax.rsqrt(jnp.mean(hidden * hidden, axis=-1, keepdims=True) + EPS)
    unit_two = hidden * scale_two
    normed_two = (unit_two * gain_two).astype(BF16)

    grad_act = dot_nt(full_cot, w_down)
    gate = jnp.dot(normed_two, w_gate_up[0], preferred_element_type=F32)
    up = jnp.dot(normed_two, w_gate_up[1], preferred_element_type=F32)
    sigmoid = jax.nn.sigmoid(gate)
    swish = gate * sigmoid
    act = (swish * up).astype(BF16)
    grad_gate = (grad_act * up * sigmoid * (1.0 + gate * (1.0 - sigmoid))).astype(BF16)
    grad_up = (grad_act * swish).astype(BF16)
    grad_two_part = dot_nt(grad_gate, w_gate_up[0]) + dot_nt(grad_up, w_gate_up[1])
    grad_two_local = lax.psum_scatter(
        grad_two_part.astype(BF16), "tensor", scatter_dimension=1, tiled=True
    ).astype(F32)
    inner_two = lax.psum(
        jnp.sum(grad_two_part * gain_two * unit_two, axis=-1, keepdims=True), "tensor"
    )
    unit_two_local = hidden_local * scale_two
    grad_gain_two = jnp.sum(grad_two_local * unit_two_local, axis=0)
    grad_hidden_local = cotangent.astype(F32) + scale_two * (
        grad_two_local * mlp_gain.astype(F32) - unit_two_local * (inner_two / full_width)
    )
    grad_attn = lax.all_gather(grad_hidden_local.astype(BF16), "tensor", axis=1, tiled=True)

    mlp_part = jnp.dot(act, w_down, preferred_element_type=F32).astype(BF16)
    mlp_local = lax.psum_scatter(mlp_part, "tensor", scatter_dimension=1, tiled=True).astype(F32)
    layer_out = (hidden_local + mlp_local).astype(BF16)
    grad_down = dot_tn(act, full_cot).astype(BF16)
    grad_gate_up = jnp.stack([dot_tn(normed_two, grad_gate), dot_tn(normed_two, grad_up)]).astype(BF16)
    grad_w_out = cut_heads(dot_tn(grouped, grad_attn).astype(BF16), 0)

    grad_grouped = dot_nt(grad_attn, w_out_pad)
    parts = []
    for n in range(seq_count):
        rows = slice(n * length, (n + 1) * length)
        parts.append(
            attend_backward(
                proj[rows], starts[n], counts[n], t_back, head_mix, gain_heads, kept[n][0], kept[n][1],
                grad_grouped[rows],
            )
        )
    grad_proj = jnp.concatenate(
        [jnp.concatenate([cut_heads(one[c], 1) for c in range(3)], axis=1) for one in parts], axis=0
    )
    grad_group_gain = sum(cut_heads(one[3][0], 0) for one in parts)
    grad_kernel = sum(one[4][:, :, 0] for one in parts).reshape(heads_here, n_taps, key_taps)
    grad_mix = sum(one[5][:, :, 0] for one in parts).reshape(heads_here, 2)

    w_flat = w_qkv.transpose(1, 0, 2).reshape(full_width, 3 * local_width)
    grad_qkv = dot_tn(normed_one, grad_proj).astype(BF16)
    grad_qkv = grad_qkv.reshape(full_width, 3, local_width).transpose(1, 0, 2)
    grad_one_part = dot_nt(grad_proj, w_flat)
    grad_one = lax.psum_scatter(
        grad_one_part.astype(BF16), "tensor", scatter_dimension=1, tiled=True
    ).astype(F32)
    inner_one = lax.psum(
        jnp.sum(grad_one_part * gain_one * unit_one, axis=-1, keepdims=True), "tensor"
    )
    unit_local = tokens.astype(F32) * scale_one
    tokens_grad = grad_hidden_local + scale_one * (
        grad_one * attn_gain.astype(F32) - unit_local * (inner_one / full_width)
    )
    grad_gain_one = jnp.sum(grad_one * unit_local, axis=0)
    small = (grad_gain_one, grad_kernel, grad_mix, grad_group_gain, grad_gain_two)
    grad_gate_up, grad_qkv, grad_down, grad_w_out, packed = ring_sum(
        (grad_gate_up, grad_qkv, grad_down, grad_w_out, pack_small(small, lax.axis_size("dp"))), 0
    )
    grad_gain_one, grad_kernel, grad_mix, grad_group_gain, grad_gain_two = unpack_small(packed, small)
    return (
        layer_out,
        tokens_grad,
        grad_gain_one,
        grad_qkv.astype(F32),
        grad_kernel,
        grad_mix,
        grad_group_gain,
        grad_w_out.astype(F32),
        grad_gain_two,
        grad_gate_up.astype(F32),
        grad_down.astype(F32),
    )


def solution(mesh):
    in_specs = (
        P("dp", "tensor"),
        P("dp", None),
        P("tensor"),
        P(None, None, "tensor"),
        P("tensor", None, None),
        P("tensor", None),
        P("tensor"),
        P("tensor", None),
        P("tensor"),
        P(None, None, "tensor"),
        P("tensor", None),
        P("dp", "tensor"),
    )
    out_specs = (
        P("dp", "tensor"),
        P("dp", "tensor"),
        P("tensor"),
        P(None, None, "tensor"),
        P("tensor", None, None),
        P("tensor", None),
        P("tensor"),
        P("tensor", None),
        P("tensor"),
        P(None, None, "tensor"),
        P("tensor", None),
    )
    return jax.shard_map(
        on_device, mesh=mesh, in_specs=in_specs, out_specs=out_specs, check_vma=False
    )
```

```python
import functools

import jax
import jax.numpy as jnp
from jax import lax
from jax.experimental import pallas as pl
from jax.experimental.pallas import tpu as pltpu
from jax.sharding import PartitionSpec as P

HEAD_DIM = 96
PAD_DIM = 128
DOC_MOST = 512
EPS = 1e-05
NEG = -1e30

COST = pl.CostEstimate(flops=1 << 20, bytes_accessed=1 << 10, transcendentals=0)
ROWS = 128
HALO = 16
WIN = 256
OWN = 16
STEP = WIN - 2 * OWN
TOP = 256
EXT = ROWS + HALO

F32 = jnp.float32
BF16 = jnp.bfloat16


def windows_most(key_half):
    return -(-(DOC_MOST - 1 + ROWS + key_half) // STEP)


def dot_nt(a, b):
    return lax.dot_general(a, b, (((1,), (1,)), ((), ())), preferred_element_type=F32)


def dot_tn(a, b):
    return lax.dot_general(a, b, (((0,), (0,)), ((), ())), preferred_element_type=F32)


def dot_nn(a, b):
    return jnp.dot(a, b, preferred_element_type=F32)


def fill_padded(dst, src, top, length):
    total = dst.shape[0]
    dst[0:top, :] = jnp.zeros((top, dst.shape[1]), dst.dtype)
    dst[top : top + length, :] = src[...]
    if total > top + length:
        dst[top + length : total, :] = jnp.zeros((total - top - length, dst.shape[1]), dst.dtype)


def lanes_between(first, last, width):
    lane = lax.broadcasted_iota(jnp.int32, (first.shape[0], width), 1)
    return (lane >= first) & (lane <= last)


def row_numbers(base, count):
    return base + lax.broadcasted_iota(jnp.int32, (count, 1), 0)


def forward_kernel(
    n_taps, key_half, most, count_ref, mix_ref, q_ref, k_ref, v_ref, start_ref, base_ref, gain_ref,
    probs_ref, heads_ref, grouped_ref, qs, ks, vs, logit_ref, t_hi_ref, t_lo_ref,
):
    pair = pl.program_id(0)
    block = pl.program_id(1)
    length = q_ref.shape[0]
    scale = HEAD_DIM ** (-0.5)

    @pl.when(block == 0)
    def _():
        fill_padded(qs, q_ref, HALO, length)
        fill_padded(ks, k_ref, TOP, length)
        fill_padded(vs, v_ref, TOP, length)
        for s in range(2):
            for a in range(n_taps):
                band = banded(base_ref[s, a : a + 1, :])
                high = band.astype(BF16)
                t_hi_ref[s, a] = high
                t_lo_ref[s, a] = (band - high.astype(F32)).astype(BF16)

    row0 = pl.multiple_of(block * ROWS, ROWS)

    def body(n):
        start = start_ref[pl.ds(row0, EXT), :]
        place = row_numbers(row0 - HALO, EXT)
        peaks = [None, None]
        for k in range(n):
            base = row0 + ROWS - STEP * (k + 1) - OWN
            at = pl.multiple_of(TOP + base, 16)
            first = start - base
            last = place - base
            valid = lanes_between(first, last, WIN)
            shown = lanes_between(
                jnp.maximum(first[HALO:], key_half + 1), jnp.minimum(last[HALO:], WIN - 2 - key_half), WIN
            )
            for s in range(2):
                cols = pl.ds(s * PAD_DIM, PAD_DIM)
                raw = dot_nt(qs[pl.ds(row0, EXT), cols], ks[pl.ds(at, WIN), cols])
                masked = jnp.where(valid, raw * scale, 0.0)
                hi = masked.astype(BF16)
                lo = (masked - hi.astype(F32)).astype(BF16)
                total = None
                for a in reversed(range(n_taps)):
                    t_hi = t_hi_ref[s, a]
                    term = dot_nn(hi, t_hi) + dot_nn(lo, t_hi) + dot_nn(hi, t_lo_ref[s, a])
                    total = term if total is None else pltpu.roll(total, 1, 0) + term
                logits = jnp.where(shown, total[HALO:], NEG)
                logit_ref[s, k] = logits
                top = jnp.max(logits, axis=-1, keepdims=True)
                peaks[s] = top if peaks[s] is None else jnp.maximum(peaks[s], top)
        lane = lax.broadcasted_iota(jnp.int32, (ROWS, WIN), 1)
        own = (lane >= OWN) & (lane < WIN - OWN)
        sums = [None, None]
        for k in range(n):
            for s in range(2):
                expo = jnp.exp(logit_ref[s, k] - peaks[s])
                logit_ref[s, k] = expo
                part = jnp.sum(jnp.where(own, expo, 0.0), axis=-1, keepdims=True)
                sums[s] = part if sums[s] is None else sums[s] + part
        inverse = [1.0 / sums[s] for s in range(2)]
        outs = [None, None]
        for k in range(n):
            base = row0 + ROWS - STEP * (k + 1) - OWN
            at = pl.multiple_of(TOP + base, 16)
            probs = []
            for s in range(2):
                prob = logit_ref[s, k] * inverse[s]
                probs_ref[s, 0, k] = prob
                probs.append(jnp.where(own, prob, 0.0))
            for h in range(2):
                mixed = (
                    mix_ref[2 * pair + h, 0] * probs[0] + mix_ref[2 * pair + h, 1] * probs[1]
                ).astype(BF16)
                part = dot_nn(mixed, vs[pl.ds(at, WIN), pl.ds(h * PAD_DIM, PAD_DIM)])
                outs[h] = part if outs[h] is None else outs[h] + part
        for h in range(2):
            cols = slice(h * PAD_DIM, (h + 1) * PAD_DIM)
            out = outs[h]
            heads_ref[:, cols] = out
            factor = lax.rsqrt(jnp.sum(out * out, axis=-1, keepdims=True) * (1.0 / HEAD_DIM) + EPS)
            grouped_ref[:, cols] = (out * factor * gain_ref[:, cols]).astype(BF16)

    for n in range(1, most + 1):
        pl.when(count_ref[block] == n)(functools.partial(body, n))


def attend_forward(proj, start, counts, base, mix, gain):
    length = proj.shape[0]
    heads, n_taps = base.shape[:2]
    pairs = heads // 2
    blocks = length // ROWS
    key_half = 5
    most = windows_most(key_half)
    two = 2 * PAD_DIM
    grid_spec = pltpu.PrefetchScalarGridSpec(
        num_scalar_prefetch=2,
        grid=(pairs, blocks),
        in_specs=[
            pl.BlockSpec((length, two), lambda p, b, *_: (0, p)),
            pl.BlockSpec((length, two), lambda p, b, *_: (0, pairs + p)),
            pl.BlockSpec((length, two), lambda p, b, *_: (0, 2 * pairs + p)),
            pl.BlockSpec((HALO + length, 1), lambda p, b, *_: (0, 0)),
            pl.BlockSpec((2, n_taps, WIN), lambda p, b, *_: (p, 0, 0)),
            pl.BlockSpec((1, two), lambda p, b, *_: (0, p)),
        ],
        out_specs=[
            pl.BlockSpec((2, 1, most, ROWS, WIN), lambda p, b, *_: (p, b, 0, 0, 0)),
            pl.BlockSpec((ROWS, two), lambda p, b, *_: (b, p)),
            pl.BlockSpec((ROWS, two), lambda p, b, *_: (b, p)),
        ],
        scratch_shapes=[
            pltpu.VMEM((HALO + length, two), BF16),
            pltpu.VMEM((TOP + length + HALO, two), BF16),
            pltpu.VMEM((TOP + length + HALO, two), BF16),
            pltpu.VMEM((2, most, ROWS, WIN), F32),
            pltpu.VMEM((2, n_taps, WIN, WIN), BF16),
            pltpu.VMEM((2, n_taps, WIN, WIN), BF16),
        ],
    )
    return pl.pallas_call(
        functools.partial(forward_kernel, n_taps, key_half, most),
        grid_spec=grid_spec,
        out_shape=[
            jax.ShapeDtypeStruct((heads, blocks, most, ROWS, WIN), F32),
            jax.ShapeDtypeStruct((length, heads * PAD_DIM), F32),
            jax.ShapeDtypeStruct((length, heads * PAD_DIM), BF16),
        ],
        compiler_params=pltpu.CompilerParams(vmem_limit_bytes=40 << 20),
        cost_estimate=COST,
        name="attend_forward",
    )(counts, mix, proj, proj, proj, start, base, gain)


def backward_kernel(
    n_taps, key_half, most, count_ref, mix_ref, q_ref, k_ref, v_ref, start_ref, base_ref, gain_ref,
    probs_ref, heads_ref, grad_ref, dqkv_ref, inner_ref, gain_grad_ref, tap_ref, mix_grad_ref,
    qs, ks, vs, dq_sum, dk_sum, dv_sum, taps, inputs, tap_sum, mixed_grad, t_back_ref, kept, inner_sum,
):
    pair = pl.program_id(0)
    block = pl.program_id(1)
    length = q_ref.shape[0]
    scale = HEAD_DIM ** (-0.5)

    @pl.when(block == 0)
    def _():
        fill_padded(qs, q_ref, HALO, length)
        fill_padded(ks, k_ref, TOP, length)
        fill_padded(vs, v_ref, TOP, length)
        dq_sum[...] = jnp.zeros_like(dq_sum)
        dk_sum[...] = jnp.zeros_like(dk_sum)
        dv_sum[...] = jnp.zeros_like(dv_sum)
        tap_sum[...] = jnp.zeros_like(tap_sum)
        gain_grad_ref[...] = jnp.zeros_like(gain_grad_ref)
        mix_grad_ref[...] = jnp.zeros_like(mix_grad_ref)
        for s in range(2):
            for a in range(n_taps):
                t_back_ref[s, a * WIN : (a + 1) * WIN, :] = banded(base_ref[s, a : a + 1, :]).astype(BF16)

    row0 = pl.multiple_of(block * ROWS, ROWS)

    def body(n):
        grads = []
        for h in range(2):
            cols = slice(h * PAD_DIM, (h + 1) * PAD_DIM)
            out = heads_ref[:, cols]
            factor = lax.rsqrt(jnp.sum(out * out, axis=-1, keepdims=True) * (1.0 / HEAD_DIM) + EPS)
            unit = out * factor
            grad = grad_ref[:, cols]
            gain_grad_ref[:, cols] += jnp.sum(grad * unit, axis=0, keepdims=True)
            scaled = grad * gain_ref[:, cols]
            inner = jnp.sum(scaled * unit, axis=-1, keepdims=True) * (1.0 / HEAD_DIM)
            grads.append((factor * (scaled - unit * inner)).astype(BF16))
        lane = lax.broadcasted_iota(jnp.int32, (ROWS, WIN), 1)
        own = (lane >= OWN) & (lane < WIN - OWN)
        inner = [[None, None], [None, None]]
        for k in range(n):
            base = row0 + ROWS - STEP * (k + 1) - OWN
            at = pl.multiple_of(TOP + base, 16)
            probs = [jnp.where(own, probs_ref[s, 0, k], 0.0) for s in range(2)]
            for h in range(2):
                cols = pl.ds(h * PAD_DIM, PAD_DIM)
                grad_mixed = dot_nt(grads[h], vs[pl.ds(at, WIN), cols])
                mixed_grad[h, k] = grad_mixed
                for s in range(2):
                    part = jnp.sum(grad_mixed * probs[s], axis=-1, keepdims=True)
                    inner[h][s] = part if inner[h][s] is None else inner[h][s] + part
                mixed = (
                    mix_ref[2 * pair + h, 0] * probs[0] + mix_ref[2 * pair + h, 1] * probs[1]
                ).astype(BF16)
                dv_sum[pl.ds(at, WIN), cols] += dot_tn(mixed, grads[h])
        for h in range(2):
            for s in range(2):
                row = 2 * h + s
                mix_grad_ref[0, row : row + 1, :] += jnp.broadcast_to(
                    jnp.sum(inner[h][s], axis=0, keepdims=True), (1, PAD_DIM)
                )
        start = start_ref[pl.ds(row0, EXT), :]
        place = row_numbers(row0 - HALO, EXT)
        for s in range(2):
            cols = pl.ds(s * PAD_DIM, PAD_DIM)
            mix0 = mix_ref[2 * pair, s]
            mix1 = mix_ref[2 * pair + 1, s]
            delta = mix0 * inner[0][s] + mix1 * inner[1][s]
            query = qs[pl.ds(row0, EXT), cols]
            for k in range(n):
                base = row0 + ROWS - STEP * (k + 1) - OWN
                at = pl.multiple_of(TOP + base, 16)
                keys = ks[pl.ds(at, WIN), cols]
                mine = lanes_between(
                    jnp.maximum(start - base, OWN), jnp.minimum(place - base, WIN - OWN - 1), WIN
                )
                grad_prob = mix0 * mixed_grad[0, k] + mix1 * mixed_grad[1, k]
                grad_logit = probs_ref[s, 0, k] * (grad_prob - delta)
                grown = jnp.concatenate([jnp.zeros((HALO, WIN), F32), grad_logit], axis=0)
                for a in range(n_taps):
                    moved = grown if a == 0 else pltpu.roll(grown, EXT - a, 0)
                    taps[k * EXT : (k + 1) * EXT, a * WIN : (a + 1) * WIN] = moved.astype(BF16)
                grad_masked = dot_nn(taps[k * EXT : (k + 1) * EXT, :], t_back_ref[s])
                grad_score = jnp.where(mine, grad_masked * scale, 0.0).astype(BF16)
                dq_sum[pl.ds(row0, EXT), cols] += dot_nn(grad_score, keys)
                dk_sum[pl.ds(at, WIN), cols] += dot_tn(grad_score, query)
                raw = dot_nt(query, keys)
                inputs[k * EXT : (k + 1) * EXT, :] = jnp.where(mine, raw * scale, 0.0).astype(BF16)
            tap_sum[s] += dot_tn(inputs[0 : n * EXT, :], taps[0 : n * EXT, :])

    for n in range(1, most + 1):
        pl.when(count_ref[block] == n)(functools.partial(body, n))

    @pl.when(block == pl.num_programs(1) - 1)
    def _():
        inner = None
        sums = ((dq_sum, HALO, q_ref), (dk_sum, TOP, k_ref), (dv_sum, TOP, v_ref))
        for c, (total, top, given) in enumerate(sums):
            grad = total[top : top + length, :].astype(BF16)
            kept[pair, c] = grad
            part = jnp.sum(grad.astype(F32) * given[...].astype(F32), axis=-1, keepdims=True)
            inner = part if inner is None else inner + part

        @pl.when(pair == 0)
        def _():
            inner_sum[...] = inner

        @pl.when(pair > 0)
        def _():
            inner_sum[...] += inner

        row = lax.broadcasted_iota(jnp.int32, (WIN, WIN), 0)
        lane = lax.broadcasted_iota(jnp.int32, (WIN, WIN), 1)
        for s in range(2):
            for a in range(n_taps):
                whole = tap_sum[s, :, a * WIN : (a + 1) * WIN]
                for b in range(2 * key_half + 1):
                    part = jnp.where(lane - row == b - key_half, whole, 0.0)
                    part = jnp.sum(part, axis=0, keepdims=True)
                    part = jnp.sum(part, axis=1, keepdims=True)
                    at = a * (2 * key_half + 1) + b
                    tap_ref[s, at : at + 1, :] = jnp.broadcast_to(part, (1, PAD_DIM))

    pairs = kept.shape[0]

    @pl.when((block == pl.num_programs(1) - 1) & (pair == pairs - 1))
    def _():
        width = 2 * pairs * HEAD_DIM

        def rows_out(n, carry):
            at = pl.ds(pl.multiple_of(n * ROWS, ROWS), ROWS)
            for c in range(3):
                heads = [
                    kept[p, c, at, s * PAD_DIM : s * PAD_DIM + HEAD_DIM]
                    for p in range(pairs)
                    for s in range(2)
                ]
                dqkv_ref[at, c * width : (c + 1) * width] = jnp.concatenate(heads, axis=1)
            column = jnp.broadcast_to(inner_sum[at, :], (ROWS, PAD_DIM))
            inner_ref[pl.ds(n, 1), :] = column.T[0:1, :]
            return carry

        lax.fori_loop(0, length // ROWS, rows_out, 0)


def attend_backward(proj, start, counts, base, mix, gain, probs, heads_out, grad_grouped):
    length = proj.shape[0]
    heads, n_taps = base.shape[:2]
    pairs = heads // 2
    blocks = length // ROWS
    key_half = 5
    most = windows_most(key_half)
    two = 2 * PAD_DIM
    tap_rows = n_taps * (2 * key_half + 1)
    grid_spec = pltpu.PrefetchScalarGridSpec(
        num_scalar_prefetch=2,
        grid=(pairs, blocks),
        in_specs=[
            pl.BlockSpec((length, two), lambda p, b, *_: (0, p)),
            pl.BlockSpec((length, two), lambda p, b, *_: (0, pairs + p)),
            pl.BlockSpec((length, two), lambda p, b, *_: (0, 2 * pairs + p)),
            pl.BlockSpec((HALO + length, 1), lambda p, b, *_: (0, 0)),
            pl.BlockSpec((2, n_taps, WIN), lambda p, b, *_: (p, 0, 0)),
            pl.BlockSpec((1, two), lambda p, b, *_: (0, p)),
            pl.BlockSpec((2, 1, most, ROWS, WIN), lambda p, b, *_: (p, b, 0, 0, 0)),
            pl.BlockSpec((ROWS, two), lambda p, b, *_: (b, p)),
            pl.BlockSpec((ROWS, two), lambda p, b, *_: (b, p)),
        ],
        out_specs=[
            pl.BlockSpec((length, 3 * heads * HEAD_DIM), lambda p, b, *_: (0, 0)),
            pl.BlockSpec((length // ROWS, ROWS), lambda p, b, *_: (0, 0)),
            pl.BlockSpec((1, two), lambda p, b, *_: (0, p)),
            pl.BlockSpec((2, tap_rows, PAD_DIM), lambda p, b, *_: (p, 0, 0)),
            pl.BlockSpec((1, 4, PAD_DIM), lambda p, b, *_: (p, 0, 0)),
        ],
        scratch_shapes=[
            pltpu.VMEM((HALO + length, two), BF16),
            pltpu.VMEM((TOP + length + HALO, two), BF16),
            pltpu.VMEM((TOP + length + HALO, two), BF16),
            pltpu.VMEM((HALO + length, two), F32),
            pltpu.VMEM((TOP + length + HALO, two), F32),
            pltpu.VMEM((TOP + length + HALO, two), F32),
            pltpu.VMEM((most * EXT, n_taps * WIN), BF16),
            pltpu.VMEM((most * EXT, WIN), BF16),
            pltpu.VMEM((2, WIN, n_taps * WIN), F32),
            pltpu.VMEM((2, most, ROWS, WIN), F32),
            pltpu.VMEM((2, n_taps * WIN, WIN), BF16),
            pltpu.VMEM((pairs, 3, length, two), BF16),
            pltpu.VMEM((length, 1), F32),
        ],
    )
    return pl.pallas_call(
        functools.partial(backward_kernel, n_taps, key_half, most),
        grid_spec=grid_spec,
        out_shape=[
            jax.ShapeDtypeStruct((length, 3 * heads * HEAD_DIM), BF16),
            jax.ShapeDtypeStruct((length // ROWS, ROWS), F32),
            jax.ShapeDtypeStruct((1, heads * PAD_DIM), F32),
            jax.ShapeDtypeStruct((heads, tap_rows, PAD_DIM), F32),
            jax.ShapeDtypeStruct((pairs, 4, PAD_DIM), F32),
        ],
        compiler_params=pltpu.CompilerParams(vmem_limit_bytes=48 << 20),
        cost_estimate=COST,
        name="attend_backward",
    )(counts, mix, proj, proj, proj, start, base, gain, probs, heads_out, grad_grouped)


MESH_ID = pl.DeviceIdType.MESH


def ring_place(member, n):
    z, y = member // 2, member % 2
    return (1 - y) * z + y * (n - 1 - z)


def ring_member(place, n):
    upper = place // (n // 2)
    return (1 - upper) * 2 * place + upper * (2 * (n - 1 - place) + 1)


def ring_peers(n):
    place = ring_place(lax.axis_index("dp"), n)
    ahead = ring_member(lax.rem(place + 1, n), n)
    behind = ring_member(lax.rem(place + n - 1, n), n)
    return place, (ahead, behind)


def ring_scratch(arrays, n):
    return [pltpu.VMEM((2, n - 1) + a.shape[2:], a.dtype) for a in arrays] + [
        pltpu.SemaphoreType.DMA((2, len(arrays), n - 1))
    ] * 4


def ring_split(array, n):
    return array.reshape(n, 2, -1, array.shape[-1])


def make_ring(n, ins, outs, scratch):
    count = len(ins)
    slots = scratch[:count]
    rs_send, rs_recv, ag_send, ag_recv = scratch[count:]
    place, to = ring_peers(n)

    def chunk(way, back):
        return lax.rem(place - back + 2 * n if way == 0 else place + back, n)

    def sum_copy(way, k, s, src):
        return pltpu.make_async_remote_copy(
            src_ref=src,
            dst_ref=slots[k].at[way, s],
            send_sem=rs_send.at[way, k, s],
            recv_sem=rs_recv.at[way, k, s],
            device_id={"dp": to[way]},
            device_id_type=MESH_ID,
        )

    def share_copy(way, k, s, c):
        return pltpu.make_async_remote_copy(
            src_ref=outs[k].at[c, way],
            dst_ref=outs[k].at[c, way],
            send_sem=ag_send.at[way, k, s],
            recv_sem=ag_recv.at[way, k, s],
            device_id={"dp": to[way]},
            device_id_type=MESH_ID,
        )

    def add(way, k, s, c, dst):
        total = slots[k][way, s].astype(F32) + ins[k][c, way].astype(F32)
        dst[...] = total.astype(dst.dtype)

    both = [(k, way) for k in range(count) for way in range(2)]

    def start():
        for k, way in both:
            sum_copy(way, k, 0, ins[k].at[chunk(way, 1), way]).start()

    def tick(now):
        @pl.when(now < n - 2)
        def _():
            for k, way in both:
                sum_copy(way, k, now, slots[k].at[way, now]).wait_recv()
                add(way, k, now, chunk(way, 2 + now), slots[k].at[way, now])
                sum_copy(way, k, now + 1, slots[k].at[way, now]).start()

        @pl.when(now == n - 2)
        def _():
            for k, way in both:
                sum_copy(way, k, n - 2, slots[k].at[way, n - 2]).wait_recv()
                add(way, k, n - 2, place, outs[k].at[place, way])
                share_copy(way, k, 0, place).start()

        @pl.when((now > n - 2) & (now < 2 * n - 3))
        def _():
            step = now - (n - 1)
            for k, way in both:
                share_copy(way, k, step, chunk(way, step + 1)).wait_recv()
                share_copy(way, k, step + 1, chunk(way, step + 1)).start()

        @pl.when(now == 2 * n - 3)
        def _():
            for k, way in both:
                share_copy(way, k, n - 2, chunk(way, n - 1)).wait_recv()

    def drain():
        def one(s, carry):
            for k, way in both:
                sum_copy(way, k, s, slots[k].at[way, s]).wait_send()
                share_copy(way, k, s, place).wait_send()
            return carry

        lax.fori_loop(0, n - 1, one, 0)

    return start, tick, drain


def small_rows(size):
    return -(-size // PAD_DIM)


def pack_small(arrays, rows):
    packed = []
    for a in arrays:
        flat = a.reshape(-1)
        packed.append(jnp.pad(flat, (0, -flat.size % PAD_DIM)).reshape(-1, PAD_DIM))
    packed = jnp.concatenate(packed, axis=0)
    return jnp.pad(packed, ((0, rows - packed.shape[0]), (0, 0)))


def unpack_small(packed, arrays):
    found, at = [], 0
    for a in arrays:
        rows = small_rows(a.size)
        found.append(packed[at : at + rows].reshape(-1)[: a.size].reshape(a.shape))
        at += rows
    return found


CHUNK = 128
GROUP = 256


LIVE = 4


def exchange_scratch(steps, width, ranks, share=True):
    half = ranks // 2
    shared = [pltpu.VMEM((steps, ranks, CHUNK, width), BF16)] if share else []
    return [
        pltpu.VMEM((steps, half, CHUNK, width), BF16),
        pltpu.VMEM((steps, half, CHUNK, width), BF16),
        pltpu.VMEM((LIVE, half, CHUNK, width), F32),
        pltpu.VMEM((steps, CHUNK, width), BF16),
        pltpu.VMEM((steps, CHUNK, width), BF16),
        pltpu.SemaphoreType.DMA((5, steps)),
        pltpu.SemaphoreType.DMA((5, steps)),
    ] + shared


def tensor_peers():
    me = lax.axis_index("tensor")
    return me, me + 1 - 2 * lax.rem(me, 2), lax.rem(me + 2, 4)


def meet(signals):
    barrier = pltpu.get_barrier_semaphore()
    for device in signals:
        pl.semaphore_signal(barrier, inc=1, device_id=device, device_id_type=MESH_ID)
    pl.semaphore_wait(barrier, len(signals))


def make_exchange(steps, scratch, partial, local, whole=None, between=None):
    share = whole is not None
    out_a, in_a, kept, out_b, in_b, send, recv = scratch[:7]
    full = scratch[7] if share else None
    many = GROUP // CHUNK
    me, near, far = tensor_peers()

    def copy(kind, step, src, dst, peer):
        return pltpu.make_async_remote_copy(
            src_ref=src,
            dst_ref=dst,
            send_sem=send.at[kind, step],
            recv_sem=recv.at[kind, step],
            device_id={"tensor": peer},
            device_id_type=MESH_ID,
        )

    def cores(step):
        return copy(0, step, out_a.at[step], in_a.at[step], near)

    def chips(step):
        return copy(1, step, out_b.at[step], in_b.at[step], far)

    def back_far(step):
        return copy(2, step, full.at[step, me], full.at[step, me], far)

    def back_near(step):
        return copy(3, step, full.at[step, me], full.at[step, me], near)

    def pass_near(step):
        return copy(4, step, full.at[step, far], full.at[step, far], near)

    def tick(now):
        @pl.when((lax.rem(now, many) == 0) & (now < steps))
        def _():
            for n, owner in ((0, near), (1, lax.rem(near + 2, 4))):

                def put(term, n=n):
                    term = term.astype(BF16)
                    for m in range(many):
                        out_a[now + m, n] = term[m * CHUNK : (m + 1) * CHUNK]

                partial(now, owner, put)
            for m in range(many):
                cores(now + m).start()
            for n, owner in ((1, far), (0, me)):

                def put(term, n=n):
                    for m in range(many):
                        kept[lax.rem(now + m, LIVE), n] = term[m * CHUNK : (m + 1) * CHUNK]

                partial(now, owner, put)

        if between is not None:
            between(now)

        @pl.when((now >= 1) & (now < steps + 1))
        def _():
            step = now - 1
            cores(step).wait_recv()
            out_b[step] = (kept[lax.rem(step, LIVE), 1] + in_a[step, 1].astype(F32)).astype(BF16)
            chips(step).start()

        @pl.when((now >= 2) & (now < steps + 2))
        def _():
            step = now - 2
            chips(step).wait_recv()
            total = kept[lax.rem(step, LIVE), 0] + in_a[step, 0].astype(F32) + in_b[step].astype(F32)
            shared = local(step, total)
            if share:
                full[step, me] = shared.astype(BF16)
                back_far(step).start()
                back_near(step).start()

        if share:

            @pl.when((now >= 3) & (now < steps + 3))
            def _():
                step = now - 3
                back_far(step).wait_recv()
                pass_near(step).start()

            @pl.when((now >= 4) & (now < steps + 4))
            def _():
                step = now - 4
                back_near(step).wait_recv()
                pass_near(step).wait_recv()
                whole(step, full)

    def drain():
        def one(step, carry):
            cores(step).wait_send()
            chips(step).wait_send()
            if share:
                back_far(step).wait_send()
                back_near(step).wait_send()
                pass_near(step).wait_send()
            return carry

        lax.fori_loop(0, steps, one, 0)

    return tick, steps + (4 if share else 2), drain


def run_ticks(count, *ticks):
    def one(now, carry):
        for tick in ticks:
            tick(now)
        return carry

    lax.fori_loop(0, count, one, 0)


def group_rows(step):
    return pl.ds(pl.multiple_of(step * CHUNK, CHUNK), GROUP)


def owner_cols(owner, width):
    return pl.ds(pl.multiple_of(owner * width, PAD_DIM), width)


def step_rows(step):
    return pl.ds(pl.multiple_of(step * CHUNK, CHUNK), CHUNK)


def attn_exit_kernel(
    grouped_ref, w_ref, tokens_ref, gain_ref, hidden_local_ref, hidden_ref, normed_ref, *scratch
):
    rows, width = tokens_ref.shape
    ranks = hidden_ref.shape[1] // width

    def partial(step, owner, put):
        put(dot_nn(grouped_ref[group_rows(step), :], w_ref[:, owner_cols(owner, width)]))

    def local(step, total):
        hidden = tokens_ref[step_rows(step), :].astype(F32) + total
        hidden_local_ref[step_rows(step), :] = hidden
        return hidden

    def whole(step, full):
        squares = None
        for n in range(ranks):
            block = full[step, n]
            hidden_ref[step_rows(step), n * width : (n + 1) * width] = block
            block = block.astype(F32)
            part = jnp.sum(block * block, axis=-1, keepdims=True)
            squares = part if squares is None else squares + part
        factor = lax.rsqrt(squares * (1.0 / (ranks * width)) + EPS)
        for n in range(ranks):
            cols = slice(n * width, (n + 1) * width)
            unit = full[step, n].astype(F32) * factor
            normed_ref[step_rows(step), cols] = (unit * gain_ref[:, cols]).astype(BF16)

    me, near, far = tensor_peers()
    meet([{"tensor": near}, {"tensor": far}])
    tick, ticks, drain = make_exchange(rows // CHUNK, scratch, partial, local, whole)
    run_ticks(ticks, tick)
    drain()


def attn_exit(grouped, w_out_pad, tokens, gain):
    rows, width = tokens.shape
    full_width = w_out_pad.shape[1]
    vmem = pl.BlockSpec(memory_space=pltpu.VMEM)
    return pl.pallas_call(
        attn_exit_kernel,
        out_shape=[
            jax.ShapeDtypeStruct((rows, width), F32),
            jax.ShapeDtypeStruct((rows, full_width), BF16),
            jax.ShapeDtypeStruct((rows, full_width), BF16),
        ],
        in_specs=[vmem] * 4,
        out_specs=[vmem] * 3,
        scratch_shapes=exchange_scratch(rows // CHUNK, width, full_width // width),
        compiler_params=pltpu.CompilerParams(
            collective_id=1, has_side_effects=True, vmem_limit_bytes=48 << 20
        ),
        cost_estimate=COST,
        name="attn_exit",
    )(grouped, w_out_pad, tokens, gain)


def mlp_exit_kernel(
    gate_ref, up_ref, w_ref, hidden_ref, cot_ref, hidden_local_ref, cot_local_ref, gain_ref, gain_local_ref,
    grad_attn_ref, grad_hidden_ref, gain_grad_ref, grad_local, *scratch
):
    rows, width = cot_local_ref.shape
    full_width = hidden_ref.shape[1]
    ranks = full_width // width
    gain_grad_ref[...] = jnp.zeros_like(gain_grad_ref)

    def partial(step, owner, put):
        cols = owner_cols(owner, width)
        at = group_rows(step)
        put(dot_nt(gate_ref[at, :], w_ref[0, cols, :]) + dot_nt(up_ref[at, :], w_ref[1, cols, :]))

    def local(step, total):
        grad_local[step_rows(step), :] = total
        return total

    def whole(step, full):
        at = step_rows(step)
        squares, inner = None, None
        for n in range(ranks):
            cols = slice(n * width, (n + 1) * width)
            hidden = hidden_ref[at, cols].astype(F32)
            part = jnp.sum(hidden * hidden, axis=-1, keepdims=True)
            squares = part if squares is None else squares + part
            part = jnp.sum(full[step, n].astype(F32) * gain_ref[:, cols] * hidden, axis=-1, keepdims=True)
            inner = part if inner is None else inner + part
        factor = lax.rsqrt(squares * (1.0 / full_width) + EPS)
        inner = inner * factor * (1.0 / full_width)
        for n in range(ranks):
            cols = slice(n * width, (n + 1) * width)
            unit = hidden_ref[at, cols].astype(F32) * factor
            grad = full[step, n].astype(F32) * gain_ref[:, cols] - unit * inner
            grad_attn_ref[at, cols] = (cot_ref[at, cols].astype(F32) + factor * grad).astype(BF16)
        total = grad_local[at, :]
        unit = hidden_local_ref[at, :] * factor
        gain_grad_ref[...] += jnp.sum(total * unit, axis=0, keepdims=True)
        grad_hidden_ref[at, :] = cot_local_ref[at, :].astype(F32) + factor * (
            total * gain_local_ref[...] - unit * inner
        )

    me, near, far = tensor_peers()
    meet([{"tensor": near}, {"tensor": far}])
    tick, ticks, drain = make_exchange(rows // CHUNK, scratch, partial, local, whole)
    run_ticks(ticks, tick)
    drain()


def mlp_exit(grad_gate, grad_up, w_gate_up, hidden, full_cot, hidden_local, cotangent, gain, gain_local):
    rows, width = hidden_local.shape
    full_width = hidden.shape[1]
    vmem = pl.BlockSpec(memory_space=pltpu.VMEM)
    return pl.pallas_call(
        mlp_exit_kernel,
        out_shape=[
            jax.ShapeDtypeStruct((rows, full_width), BF16),
            jax.ShapeDtypeStruct((rows, width), F32),
            jax.ShapeDtypeStruct((1, width), F32),
        ],
        in_specs=[vmem] * 9,
        out_specs=[vmem] * 3,
        scratch_shapes=[pltpu.VMEM((rows, width), F32)]
        + exchange_scratch(rows // CHUNK, width, full_width // width),
        compiler_params=pltpu.CompilerParams(
            collective_id=2, has_side_effects=True, vmem_limit_bytes=56 << 20
        ),
        cost_estimate=COST,
        name="mlp_exit",
    )(grad_gate, grad_up, w_gate_up, hidden, full_cot, hidden_local, cotangent, gain, gain_local)


def last_exit_kernel(
    n_ring, count, grad_ref, w_ref, tokens_ref, grad_hidden_ref, factor_ref, inner_ref, gain_ref, act_ref,
    w_down_ref, hidden_ref, small_ref, *refs,
):
    ins, refs = refs[:count], refs[count:]
    tokens_grad_ref, out_ref, small_sum_ref = refs[:3]
    outs, refs = refs[3 : 3 + count], refs[3 + count :]
    gain_grad, mine, all_small, small_send, small_recv = refs[:5]
    inner_in, inner_sum, inner_col, inner_send, inner_recv = refs[5:10]
    ring_refs, scratch = refs[10 : 14 + count], refs[14 + count :]
    rows, width = tokens_ref.shape
    full_width = w_ref.shape[1]
    half = rows // CHUNK
    me, near, far = tensor_peers()
    here = lax.axis_index("dp")
    gain_grad[...] = jnp.zeros_like(gain_grad)

    def partial(step, owner, put):
        cols = owner_cols(owner, width)

        @pl.when(step < half)
        def _():
            total = None
            for c in range(3):
                term = dot_nt(grad_ref[group_rows(step), c * width : (c + 1) * width], w_ref[c, cols, :])
                total = term if total is None else total + term
            put(total)

        @pl.when(step >= half)
        def _():
            put(dot_nn(act_ref[group_rows(step - half), :], w_down_ref[:, cols]))

    def between(now):
        def copy(n, src, peer):
            return pltpu.make_async_remote_copy(
                src_ref=src,
                dst_ref=inner_in.at[n],
                send_sem=inner_send.at[n],
                recv_sem=inner_recv.at[n],
                device_id={"tensor": peer},
                device_id_type=MESH_ID,
            )

        @pl.when(now == 0)
        def _():
            copy(0, inner_ref, near).start()

        @pl.when(now == 1)
        def _():
            copy(0, inner_ref, near).wait()
            inner_sum[...] = inner_ref[...] + inner_in[0]
            copy(1, inner_sum, far).start()

        @pl.when(now == 2)
        def _():
            copy(1, inner_sum, far).wait()
            total = (inner_sum[...] + inner_in[1]) * (1.0 / full_width)
            for n in range(rows // ROWS):
                line = jnp.broadcast_to(total[n : n + 1, :], (ROWS, ROWS))
                inner_col[n * ROWS : (n + 1) * ROWS, :] = line.T[:, 0:1]

    def local(step, total):
        @pl.when(step < half)
        def _():
            at = step_rows(step)
            factor = factor_ref[at, :]
            unit = tokens_ref[at, :].astype(F32) * factor
            gain_grad[...] += jnp.sum(total * unit, axis=0, keepdims=True)
            tokens_grad_ref[at, :] = grad_hidden_ref[at, :] + factor * (
                total * gain_ref[...] - unit * inner_col[at, :]
            )

        @pl.when(step >= half)
        def _():
            at = step_rows(step - half)
            out_ref[at, :] = (hidden_ref[at, :] + total).astype(BF16)

    def small_copy(peer, sender):
        return pltpu.make_async_remote_copy(
            src_ref=mine,
            dst_ref=all_small.at[sender],
            send_sem=small_send.at[peer],
            recv_sem=small_recv.at[sender],
            device_id={"dp": peer},
            device_id_type=MESH_ID,
        )

    def small_start(now):
        @pl.when(now == half + 2)
        def _():
            mine[...] = small_ref[...]
            for n in range(width // PAD_DIM):
                mine[n : n + 1, :] = gain_grad[:, n * PAD_DIM : (n + 1) * PAD_DIM]
            all_small[here] = mine[...]

            def one(away, carry):
                small_copy(lax.rem(here + away, n_ring), here).start()
                return carry

            lax.fori_loop(1, n_ring, one, 0)

    barrier = pltpu.get_barrier_semaphore()
    for peer in (near, far):
        pl.semaphore_signal(barrier, inc=1, device_id={"tensor": peer}, device_id_type=MESH_ID)

    def greet(away, carry):
        peer = lax.rem(here + away, n_ring)
        pl.semaphore_signal(barrier, inc=1, device_id={"dp": peer}, device_id_type=MESH_ID)
        return carry

    lax.fori_loop(1, n_ring, greet, 0)
    pl.semaphore_wait(barrier, 2 + n_ring - 1)

    ring_start, ring_tick, ring_drain = make_ring(n_ring, ins, outs, ring_refs)
    tick, ticks, drain = make_exchange(2 * half, scratch, partial, local, between=between)
    ring_start()

    def two(now):
        for m in range(2):
            tick(2 * now + m)
            small_start(2 * now + m)

    run_ticks(max(-(-ticks // 2), 2 * (n_ring - 1)), two, ring_tick)

    def one(away, carry):
        peer = lax.rem(here + away, n_ring)
        small_copy(peer, peer).wait()
        return carry

    lax.fori_loop(1, n_ring, one, 0)

    def add(n, total):
        return total + all_small[n]

    small_sum_ref[...] = lax.fori_loop(1, n_ring, add, all_small[0])
    drain()
    ring_drain()


def last_exit(
    grad_proj, w_qkv, tokens, grad_hidden, factor, inner, gain, act, w_down, hidden_local, small, sums
):
    rows, width = tokens.shape
    n_ring = lax.axis_size("dp")
    count = len(sums)
    split = [ring_split(a, n_ring) for a in sums]
    gain_rows = width // PAD_DIM
    need = gain_rows + sum(small_rows(a.size) for a in small)
    packed = jnp.pad(pack_small(small, need - gain_rows), ((gain_rows, -need % 8), (0, 0)))
    vmem = pl.BlockSpec(memory_space=pltpu.VMEM)
    steps = 2 * rows // CHUNK
    tokens_grad, out, packed, *totals = pl.pallas_call(
        functools.partial(last_exit_kernel, n_ring, count),
        out_shape=[
            jax.ShapeDtypeStruct((rows, width), F32),
            jax.ShapeDtypeStruct((rows, width), BF16),
            jax.ShapeDtypeStruct(packed.shape, F32),
        ]
        + [jax.ShapeDtypeStruct(a.shape, a.dtype) for a in split],
        in_specs=[vmem] * (11 + count),
        out_specs=[vmem] * (3 + count),
        scratch_shapes=[
            pltpu.VMEM((1, width), F32),
            pltpu.VMEM(packed.shape, F32),
            pltpu.VMEM((n_ring,) + packed.shape, F32),
            pltpu.SemaphoreType.DMA((n_ring,)),
            pltpu.SemaphoreType.DMA((n_ring,)),
            pltpu.VMEM((2,) + inner.shape, F32),
            pltpu.VMEM(inner.shape, F32),
            pltpu.VMEM((rows, 1), F32),
            pltpu.SemaphoreType.DMA((2,)),
            pltpu.SemaphoreType.DMA((2,)),
        ]
        + ring_scratch(split, n_ring)
        + exchange_scratch(steps, width, w_qkv.shape[1] // width, share=False),
        compiler_params=pltpu.CompilerParams(
            collective_id=3, has_side_effects=True, vmem_limit_bytes=62 << 20
        ),
        cost_estimate=COST,
        name="last_exit",
    )(grad_proj, w_qkv, tokens, grad_hidden, factor, inner, gain, act, w_down, hidden_local, packed, *split)
    gain_grad = packed[:gain_rows].reshape(width)
    totals = [t.reshape(a.shape) for t, a in zip(totals, sums)]
    return tokens_grad, gain_grad, out, unpack_small(packed[gain_rows:], small), totals


def banded(line):
    return pltpu.roll(jnp.broadcast_to(line, (WIN, WIN)), 0, 1, stride=1, stride_axis=0)


def band_lines(kernel):
    taps = kernel.shape[2]
    wide = jnp.pad(kernel, ((0, 0), (0, 0), (0, WIN - taps)))
    back = jnp.pad(kernel[:, :, ::-1], ((0, 0), (0, 0), (0, WIN - taps)))
    return jnp.roll(wide, -(taps // 2), axis=2), jnp.roll(back, -(taps // 2), axis=2)


def pad_heads(array, axis):
    shape = array.shape
    heads = shape[axis] // HEAD_DIM
    split = array.reshape(shape[:axis] + (heads, HEAD_DIM) + shape[axis + 1 :])
    widths = [(0, 0)] * split.ndim
    widths[axis + 1] = (0, PAD_DIM - HEAD_DIM)
    return jnp.pad(split, widths).reshape(shape[:axis] + (heads * PAD_DIM,) + shape[axis + 1 :])


def cut_heads(array, axis):
    shape = array.shape
    heads = shape[axis] // PAD_DIM
    split = array.reshape(shape[:axis] + (heads, PAD_DIM) + shape[axis + 1 :])
    cut = lax.slice_in_dim(split, 0, HEAD_DIM, axis=axis + 1)
    return cut.reshape(shape[:axis] + (heads * HEAD_DIM,) + shape[axis + 1 :])


def windows_needed(start, key_half):
    length = start.shape[0]
    first = start[::ROWS]
    row0 = jnp.arange(0, length, ROWS, dtype=jnp.int32)
    count = jnp.ones_like(first)
    for k in range(1, windows_most(key_half)):
        count = count + (first - key_half < row0 + ROWS - STEP * k).astype(jnp.int32)
    return count


def on_device(
    tokens, segments, attn_gain, w_qkv, kq_kernel, head_mix, group_gain, w_out, mlp_gain, w_gate_up,
    w_down, cotangent,
):
    rows_here, local_width = tokens.shape
    seq_count, length = segments.shape
    heads_here = local_width // HEAD_DIM
    n_taps, key_taps = kq_kernel.shape[1:]
    key_half = key_taps // 2

    lines, lines_back = band_lines(kq_kernel)
    w_proj = pad_heads(w_qkv, 2).transpose(1, 0, 2).reshape(w_qkv.shape[1], -1)
    w_out_pad = pad_heads(w_out, 0)
    gain_heads = pad_heads(group_gain.astype(F32), 0)[None]
    starts, counts = [], []
    for n in range(seq_count):
        seg = segments[n]
        start = jnp.sum((seg[None, :] < seg[:, None]).astype(jnp.int32), axis=1)
        counts.append(windows_needed(start, key_half))
        starts.append(jnp.pad(start, (HALO, 0), constant_values=1 << 20)[:, None])

    gathered = lax.all_gather(tokens, "tensor", axis=1, tiled=True)
    gains = lax.all_gather(jnp.stack([attn_gain, mlp_gain]), "tensor", axis=1, tiled=True).astype(F32)
    gain_one, gain_two = gains[0], gains[1]
    full_cot = lax.all_gather(cotangent, "tensor", axis=1, tiled=True)

    resid = gathered.astype(F32)
    full_width = resid.shape[1]
    scale_one = lax.rsqrt(jnp.mean(resid * resid, axis=-1, keepdims=True) + EPS)
    unit_one = resid * scale_one
    normed_one = (unit_one * gain_one).astype(BF16)
    proj = jnp.dot(normed_one, w_proj, preferred_element_type=F32).astype(BF16)

    kept = []
    for n in range(seq_count):
        rows = slice(n * length, (n + 1) * length)
        kept.append(
            attend_forward(proj[rows], starts[n], counts[n], lines, head_mix, gain_heads)
        )
    grouped = jnp.concatenate([one[2] for one in kept], axis=0)
    grouped, full_cot = lax.optimization_barrier((grouped, full_cot))
    hidden_local, hidden, normed_two = attn_exit(grouped, w_out_pad, tokens, gain_two[None])

    grad_act = dot_nt(full_cot, w_down)
    gate = jnp.dot(normed_two, w_gate_up[0], preferred_element_type=F32)
    up = jnp.dot(normed_two, w_gate_up[1], preferred_element_type=F32)
    sigmoid = jax.nn.sigmoid(gate)
    swish = gate * sigmoid
    act = (swish * up).astype(BF16)
    grad_gate = (grad_act * up * sigmoid * (1.0 + gate * (1.0 - sigmoid))).astype(BF16)
    grad_up = (grad_act * swish).astype(BF16)
    grad_down = dot_tn(act, full_cot).astype(BF16)
    grad_up_w = dot_tn(normed_two, grad_up).astype(BF16)
    grad_gate, grad_up_w, grad_down = lax.optimization_barrier((grad_gate, grad_up_w, grad_down))
    grad_up_w, grad_down = lax.psum((grad_up_w, grad_down), "dp")
    grad_attn, grad_hidden_local, grad_gain_two = mlp_exit(
        grad_gate, grad_up, w_gate_up, hidden, full_cot, hidden_local, cotangent, gain_two[None],
        mlp_gain.astype(F32)[None],
    )
    grad_gate_w = dot_tn(normed_two, grad_gate).astype(BF16)
    grad_w_out = cut_heads(dot_tn(grouped, grad_attn).astype(BF16), 0)

    grad_grouped = dot_nt(grad_attn, w_out_pad)
    parts = []
    for n in range(seq_count):
        rows = slice(n * length, (n + 1) * length)
        parts.append(
            attend_backward(
                proj[rows], starts[n], counts[n], lines_back, head_mix, gain_heads, kept[n][0], kept[n][1],
                grad_grouped[rows],
            )
        )
    grad_proj = jnp.concatenate([one[0] for one in parts], axis=0)
    inner_part = jnp.concatenate([one[1] for one in parts], axis=0)
    grad_group_gain = sum(cut_heads(one[2][0], 0) for one in parts)
    grad_kernel = sum(one[3][:, :, 0] for one in parts).reshape(heads_here, n_taps, key_taps)
    grad_mix = sum(one[4][:, :, 0] for one in parts).reshape(heads_here, 2)

    grad_qkv = [
        dot_tn(normed_one, grad_proj[:, c * local_width : (c + 1) * local_width]).astype(BF16)
        for c in range(3)
    ]
    tokens_grad, grad_gain_one, layer_out, small, sums = last_exit(
        grad_proj, w_qkv, tokens, grad_hidden_local, scale_one, inner_part, attn_gain.astype(F32)[None],
        act, w_down, hidden_local, (grad_kernel, grad_mix, grad_group_gain, grad_gain_two[0]),
        (grad_gate_w, grad_w_out, *grad_qkv),
    )
    grad_kernel, grad_mix, grad_group_gain, grad_gain_two = small
    grad_gate_w, grad_w_out, *grad_qkv = sums
    grad_gate_up = jnp.stack([grad_gate_w, grad_up_w])
    grad_qkv = jnp.stack(grad_qkv)
    return (
        layer_out,
        tokens_grad,
        grad_gain_one,
        grad_qkv.astype(F32),
        grad_kernel,
        grad_mix,
        grad_group_gain,
        grad_w_out.astype(F32),
        grad_gain_two,
        grad_gate_up.astype(F32),
        grad_down.astype(F32),
    )


def solution(mesh):
    in_specs = (
        P("dp", "tensor"),
        P("dp", None),
        P("tensor"),
        P(None, None, "tensor"),
        P("tensor", None, None),
        P("tensor", None),
        P("tensor"),
        P("tensor", None),
        P("tensor"),
        P(None, None, "tensor"),
        P("tensor", None),
        P("dp", "tensor"),
    )
    out_specs = (
        P("dp", "tensor"),
        P("dp", "tensor"),
        P("tensor"),
        P(None, None, "tensor"),
        P("tensor", None, None),
        P("tensor", None),
        P("tensor"),
        P("tensor", None),
        P("tensor"),
        P(None, None, "tensor"),
        P("tensor", None),
    )
    return jax.shard_map(
        on_device, mesh=mesh, in_specs=in_specs, out_specs=out_specs, check_vma=False
    )
```

```python
import functools

import jax
import jax.numpy as jnp
from jax import lax
from jax.experimental import pallas as pl
from jax.experimental.pallas import tpu as pltpu
from jax.sharding import PartitionSpec as P

HEAD_DIM = 96
PAD_DIM = 128
DOC_MOST = 512
EPS = 1e-05
NEG = -1e30

COST = pl.CostEstimate(flops=1 << 20, bytes_accessed=1 << 10, transcendentals=0)
EARLY_SHARE = 0.75
ROWS = 128
HALO = 16
WIN = 256
OWN = 16
STEP = WIN - 2 * OWN
TOP = 256
EXT = ROWS + HALO

F32 = jnp.float32
BF16 = jnp.bfloat16


def windows_most(key_half):
    return -(-(DOC_MOST - 1 + ROWS + key_half) // STEP)


def dot_nt(a, b):
    return lax.dot_general(a, b, (((1,), (1,)), ((), ())), preferred_element_type=F32)


def dot_tn(a, b):
    return lax.dot_general(a, b, (((0,), (0,)), ((), ())), preferred_element_type=F32)


def dot_nn(a, b):
    return jnp.dot(a, b, preferred_element_type=F32)


def fill_padded(dst, src, top, length):
    total = dst.shape[0]
    dst[0:top, :] = jnp.zeros((top, dst.shape[1]), dst.dtype)
    dst[top : top + length, :] = src[...]
    if total > top + length:
        dst[top + length : total, :] = jnp.zeros((total - top - length, dst.shape[1]), dst.dtype)


def lanes_between(first, last, width):
    lane = lax.broadcasted_iota(jnp.int32, (first.shape[0], width), 1)
    return (lane >= first) & (lane <= last)


def row_numbers(base, count):
    return base + lax.broadcasted_iota(jnp.int32, (count, 1), 0)


def forward_kernel(
    n_taps, key_half, most, count_ref, mix_ref, q_ref, k_ref, v_ref, start_ref, base_ref, gain_ref,
    probs_ref, heads_ref, grouped_ref, qs, ks, vs, logit_ref, t_hi_ref, t_lo_ref,
):
    pair = pl.program_id(0)
    block = pl.program_id(1)
    length = q_ref.shape[0]
    scale = HEAD_DIM ** (-0.5)

    @pl.when(block == 0)
    def _():
        fill_padded(qs, q_ref, HALO, length)
        fill_padded(ks, k_ref, TOP, length)
        fill_padded(vs, v_ref, TOP, length)
        for s in range(2):
            for a in range(n_taps):
                band = banded(base_ref[s, a : a + 1, :])
                high = band.astype(BF16)
                t_hi_ref[s, a] = high
                t_lo_ref[s, a] = (band - high.astype(F32)).astype(BF16)

    row0 = pl.multiple_of(block * ROWS, ROWS)

    def body(n):
        start = start_ref[pl.ds(row0, EXT), :]
        place = row_numbers(row0 - HALO, EXT)
        peaks = [None, None]
        for k in range(n):
            base = row0 + ROWS - STEP * (k + 1) - OWN
            at = pl.multiple_of(TOP + base, 16)
            first = start - base
            last = place - base
            valid = lanes_between(first, last, WIN)
            shown = lanes_between(
                jnp.maximum(first[HALO:], key_half + 1), jnp.minimum(last[HALO:], WIN - 2 - key_half), WIN
            )
            for s in range(2):
                cols = pl.ds(s * PAD_DIM, PAD_DIM)
                raw = dot_nt(qs[pl.ds(row0, EXT), cols], ks[pl.ds(at, WIN), cols])
                masked = jnp.where(valid, raw * scale, 0.0)
                hi = masked.astype(BF16)
                lo = (masked - hi.astype(F32)).astype(BF16)
                total = None
                for a in reversed(range(n_taps)):
                    t_hi = t_hi_ref[s, a]
                    term = dot_nn(hi, t_hi) + dot_nn(lo, t_hi) + dot_nn(hi, t_lo_ref[s, a])
                    total = term if total is None else pltpu.roll(total, 1, 0) + term
                logits = jnp.where(shown, total[HALO:], NEG)
                logit_ref[s, k] = logits
                top = jnp.max(logits, axis=-1, keepdims=True)
                peaks[s] = top if peaks[s] is None else jnp.maximum(peaks[s], top)
        lane = lax.broadcasted_iota(jnp.int32, (ROWS, WIN), 1)
        own = (lane >= OWN) & (lane < WIN - OWN)
        sums = [None, None]
        for k in range(n):
            for s in range(2):
                expo = jnp.exp(logit_ref[s, k] - peaks[s])
                logit_ref[s, k] = expo
                part = jnp.sum(jnp.where(own, expo, 0.0), axis=-1, keepdims=True)
                sums[s] = part if sums[s] is None else sums[s] + part
        inverse = [1.0 / sums[s] for s in range(2)]
        outs = [None, None]
        for k in range(n):
            base = row0 + ROWS - STEP * (k + 1) - OWN
            at = pl.multiple_of(TOP + base, 16)
            probs = []
            for s in range(2):
                prob = logit_ref[s, k] * inverse[s]
                probs_ref[s, 0, k] = prob
                probs.append(jnp.where(own, prob, 0.0))
            for h in range(2):
                mixed = (
                    mix_ref[2 * pair + h, 0] * probs[0] + mix_ref[2 * pair + h, 1] * probs[1]
                ).astype(BF16)
                part = dot_nn(mixed, vs[pl.ds(at, WIN), pl.ds(h * PAD_DIM, PAD_DIM)])
                outs[h] = part if outs[h] is None else outs[h] + part
        for h in range(2):
            cols = slice(h * PAD_DIM, (h + 1) * PAD_DIM)
            out = outs[h]
            heads_ref[:, cols] = out
            factor = lax.rsqrt(jnp.sum(out * out, axis=-1, keepdims=True) * (1.0 / HEAD_DIM) + EPS)
            grouped_ref[:, cols] = (out * factor * gain_ref[:, cols]).astype(BF16)

    for n in range(1, most + 1):
        pl.when(count_ref[block] == n)(functools.partial(body, n))


def attend_forward(proj, start, counts, base, mix, gain):
    length = proj.shape[0]
    heads, n_taps = base.shape[:2]
    pairs = heads // 2
    blocks = length // ROWS
    key_half = 5
    most = windows_most(key_half)
    two = 2 * PAD_DIM
    grid_spec = pltpu.PrefetchScalarGridSpec(
        num_scalar_prefetch=2,
        grid=(pairs, blocks),
        in_specs=[
            pl.BlockSpec((length, two), lambda p, b, *_: (0, p)),
            pl.BlockSpec((length, two), lambda p, b, *_: (0, pairs + p)),
            pl.BlockSpec((length, two), lambda p, b, *_: (0, 2 * pairs + p)),
            pl.BlockSpec((HALO + length, 1), lambda p, b, *_: (0, 0)),
            pl.BlockSpec((2, n_taps, WIN), lambda p, b, *_: (p, 0, 0)),
            pl.BlockSpec((1, two), lambda p, b, *_: (0, p)),
        ],
        out_specs=[
            pl.BlockSpec((2, 1, most, ROWS, WIN), lambda p, b, *_: (p, b, 0, 0, 0)),
            pl.BlockSpec((ROWS, two), lambda p, b, *_: (b, p)),
            pl.BlockSpec((ROWS, two), lambda p, b, *_: (b, p)),
        ],
        scratch_shapes=[
            pltpu.VMEM((HALO + length, two), BF16),
            pltpu.VMEM((TOP + length + HALO, two), BF16),
            pltpu.VMEM((TOP + length + HALO, two), BF16),
            pltpu.VMEM((2, most, ROWS, WIN), F32),
            pltpu.VMEM((2, n_taps, WIN, WIN), BF16),
            pltpu.VMEM((2, n_taps, WIN, WIN), BF16),
        ],
    )
    return pl.pallas_call(
        functools.partial(forward_kernel, n_taps, key_half, most),
        grid_spec=grid_spec,
        out_shape=[
            jax.ShapeDtypeStruct((heads, blocks, most, ROWS, WIN), F32),
            jax.ShapeDtypeStruct((length, heads * PAD_DIM), F32),
            jax.ShapeDtypeStruct((length, heads * PAD_DIM), BF16),
        ],
        compiler_params=pltpu.CompilerParams(vmem_limit_bytes=56 << 20),
        cost_estimate=COST,
        name="attend_forward",
    )(counts, mix, proj, proj, proj, start, base, gain)


def backward_kernel(
    n_taps, key_half, most, count_ref, mix_ref, q_ref, k_ref, v_ref, start_ref, base_ref, gain_ref,
    probs_ref, heads_ref, grad_ref, dqkv_ref, inner_ref, gain_grad_ref, tap_ref, mix_grad_ref,
    qs, ks, vs, dq_sum, dk_sum, dv_sum, taps, inputs, tap_sum, mixed_grad, t_back_ref, kept, inner_sum,
):
    pair = pl.program_id(0)
    block = pl.program_id(1)
    length = q_ref.shape[0]
    scale = HEAD_DIM ** (-0.5)

    @pl.when(block == 0)
    def _():
        fill_padded(qs, q_ref, HALO, length)
        fill_padded(ks, k_ref, TOP, length)
        fill_padded(vs, v_ref, TOP, length)
        dq_sum[...] = jnp.zeros_like(dq_sum)
        dk_sum[...] = jnp.zeros_like(dk_sum)
        dv_sum[...] = jnp.zeros_like(dv_sum)
        tap_sum[...] = jnp.zeros_like(tap_sum)
        gain_grad_ref[...] = jnp.zeros_like(gain_grad_ref)
        mix_grad_ref[...] = jnp.zeros_like(mix_grad_ref)
        for s in range(2):
            for a in range(n_taps):
                t_back_ref[s, a * WIN : (a + 1) * WIN, :] = banded(base_ref[s, a : a + 1, :]).astype(BF16)

    row0 = pl.multiple_of(block * ROWS, ROWS)

    def body(n):
        grads = []
        for h in range(2):
            cols = slice(h * PAD_DIM, (h + 1) * PAD_DIM)
            out = heads_ref[:, cols]
            factor = lax.rsqrt(jnp.sum(out * out, axis=-1, keepdims=True) * (1.0 / HEAD_DIM) + EPS)
            unit = out * factor
            grad = grad_ref[:, cols]
            gain_grad_ref[:, cols] += jnp.sum(grad * unit, axis=0, keepdims=True)
            scaled = grad * gain_ref[:, cols]
            inner = jnp.sum(scaled * unit, axis=-1, keepdims=True) * (1.0 / HEAD_DIM)
            grads.append((factor * (scaled - unit * inner)).astype(BF16))
        lane = lax.broadcasted_iota(jnp.int32, (ROWS, WIN), 1)
        own = (lane >= OWN) & (lane < WIN - OWN)
        inner = [[None, None], [None, None]]
        for k in range(n):
            base = row0 + ROWS - STEP * (k + 1) - OWN
            at = pl.multiple_of(TOP + base, 16)
            probs = [jnp.where(own, probs_ref[s, 0, k], 0.0) for s in range(2)]
            for h in range(2):
                cols = pl.ds(h * PAD_DIM, PAD_DIM)
                grad_mixed = dot_nt(grads[h], vs[pl.ds(at, WIN), cols])
                mixed_grad[h, k] = grad_mixed
                for s in range(2):
                    part = jnp.sum(grad_mixed * probs[s], axis=-1, keepdims=True)
                    inner[h][s] = part if inner[h][s] is None else inner[h][s] + part
                mixed = (
                    mix_ref[2 * pair + h, 0] * probs[0] + mix_ref[2 * pair + h, 1] * probs[1]
                ).astype(BF16)
                dv_sum[pl.ds(at, WIN), cols] += dot_tn(mixed, grads[h])
        for h in range(2):
            for s in range(2):
                row = 2 * h + s
                mix_grad_ref[0, row : row + 1, :] += jnp.broadcast_to(
                    jnp.sum(inner[h][s], axis=0, keepdims=True), (1, PAD_DIM)
                )
        start = start_ref[pl.ds(row0, EXT), :]
        place = row_numbers(row0 - HALO, EXT)
        for s in range(2):
            cols = pl.ds(s * PAD_DIM, PAD_DIM)
            mix0 = mix_ref[2 * pair, s]
            mix1 = mix_ref[2 * pair + 1, s]
            delta = mix0 * inner[0][s] + mix1 * inner[1][s]
            query = qs[pl.ds(row0, EXT), cols]
            for k in range(n):
                base = row0 + ROWS - STEP * (k + 1) - OWN
                at = pl.multiple_of(TOP + base, 16)
                keys = ks[pl.ds(at, WIN), cols]
                mine = lanes_between(
                    jnp.maximum(start - base, OWN), jnp.minimum(place - base, WIN - OWN - 1), WIN
                )
                grad_prob = mix0 * mixed_grad[0, k] + mix1 * mixed_grad[1, k]
                grad_logit = probs_ref[s, 0, k] * (grad_prob - delta)
                grown = jnp.concatenate([jnp.zeros((HALO, WIN), F32), grad_logit], axis=0)
                for a in range(n_taps):
                    moved = grown if a == 0 else pltpu.roll(grown, EXT - a, 0)
                    taps[k * EXT : (k + 1) * EXT, a * WIN : (a + 1) * WIN] = moved.astype(BF16)
                grad_masked = dot_nn(taps[k * EXT : (k + 1) * EXT, :], t_back_ref[s])
                grad_score = jnp.where(mine, grad_masked * scale, 0.0).astype(BF16)
                dq_sum[pl.ds(row0, EXT), cols] += dot_nn(grad_score, keys)
                dk_sum[pl.ds(at, WIN), cols] += dot_tn(grad_score, query)
                raw = dot_nt(query, keys)
                inputs[k * EXT : (k + 1) * EXT, :] = jnp.where(mine, raw * scale, 0.0).astype(BF16)
            tap_sum[s] += dot_tn(inputs[0 : n * EXT, :], taps[0 : n * EXT, :])

    for n in range(1, most + 1):
        pl.when(count_ref[block] == n)(functools.partial(body, n))

    @pl.when(block == pl.num_programs(1) - 1)
    def _():
        inner = None
        sums = ((dq_sum, HALO, q_ref), (dk_sum, TOP, k_ref), (dv_sum, TOP, v_ref))
        for c, (total, top, given) in enumerate(sums):
            grad = total[top : top + length, :].astype(BF16)
            kept[pair, c] = grad
            part = jnp.sum(grad.astype(F32) * given[...].astype(F32), axis=-1, keepdims=True)
            inner = part if inner is None else inner + part

        @pl.when(pair == 0)
        def _():
            inner_sum[...] = inner

        @pl.when(pair > 0)
        def _():
            inner_sum[...] += inner

        row = lax.broadcasted_iota(jnp.int32, (WIN, WIN), 0)
        lane = lax.broadcasted_iota(jnp.int32, (WIN, WIN), 1)
        for s in range(2):
            for a in range(n_taps):
                whole = tap_sum[s, :, a * WIN : (a + 1) * WIN]
                for b in range(2 * key_half + 1):
                    part = jnp.where(lane - row == b - key_half, whole, 0.0)
                    part = jnp.sum(part, axis=0, keepdims=True)
                    part = jnp.sum(part, axis=1, keepdims=True)
                    at = a * (2 * key_half + 1) + b
                    tap_ref[s, at : at + 1, :] = jnp.broadcast_to(part, (1, PAD_DIM))

    pairs = kept.shape[0]

    @pl.when((block == pl.num_programs(1) - 1) & (pair == pairs - 1))
    def _():
        width = 2 * pairs * HEAD_DIM

        def rows_out(n, carry):
            at = pl.ds(pl.multiple_of(n * ROWS, ROWS), ROWS)
            for c in range(3):
                heads = [
                    kept[p, c, at, s * PAD_DIM : s * PAD_DIM + HEAD_DIM]
                    for p in range(pairs)
                    for s in range(2)
                ]
                dqkv_ref[at, c * width : (c + 1) * width] = jnp.concatenate(heads, axis=1)
            column = jnp.broadcast_to(inner_sum[at, :], (ROWS, PAD_DIM))
            inner_ref[pl.ds(n, 1), :] = column.T[0:1, :]
            return carry

        lax.fori_loop(0, length // ROWS, rows_out, 0)


def attend_backward(proj, start, counts, base, mix, gain, probs, heads_out, grad_grouped):
    length = proj.shape[0]
    heads, n_taps = base.shape[:2]
    pairs = heads // 2
    blocks = length // ROWS
    key_half = 5
    most = windows_most(key_half)
    two = 2 * PAD_DIM
    tap_rows = n_taps * (2 * key_half + 1)
    grid_spec = pltpu.PrefetchScalarGridSpec(
        num_scalar_prefetch=2,
        grid=(pairs, blocks),
        in_specs=[
            pl.BlockSpec((length, two), lambda p, b, *_: (0, p)),
            pl.BlockSpec((length, two), lambda p, b, *_: (0, pairs + p)),
            pl.BlockSpec((length, two), lambda p, b, *_: (0, 2 * pairs + p)),
            pl.BlockSpec((HALO + length, 1), lambda p, b, *_: (0, 0)),
            pl.BlockSpec((2, n_taps, WIN), lambda p, b, *_: (p, 0, 0)),
            pl.BlockSpec((1, two), lambda p, b, *_: (0, p)),
            pl.BlockSpec((2, 1, most, ROWS, WIN), lambda p, b, *_: (p, b, 0, 0, 0)),
            pl.BlockSpec((ROWS, two), lambda p, b, *_: (b, p)),
            pl.BlockSpec((ROWS, two), lambda p, b, *_: (b, p)),
        ],
        out_specs=[
            pl.BlockSpec((length, 3 * heads * HEAD_DIM), lambda p, b, *_: (0, 0)),
            pl.BlockSpec((length // ROWS, ROWS), lambda p, b, *_: (0, 0)),
            pl.BlockSpec((1, two), lambda p, b, *_: (0, p)),
            pl.BlockSpec((2, tap_rows, PAD_DIM), lambda p, b, *_: (p, 0, 0)),
            pl.BlockSpec((1, 4, PAD_DIM), lambda p, b, *_: (p, 0, 0)),
        ],
        scratch_shapes=[
            pltpu.VMEM((HALO + length, two), BF16),
            pltpu.VMEM((TOP + length + HALO, two), BF16),
            pltpu.VMEM((TOP + length + HALO, two), BF16),
            pltpu.VMEM((HALO + length, two), F32),
            pltpu.VMEM((TOP + length + HALO, two), F32),
            pltpu.VMEM((TOP + length + HALO, two), F32),
            pltpu.VMEM((most * EXT, n_taps * WIN), BF16),
            pltpu.VMEM((most * EXT, WIN), BF16),
            pltpu.VMEM((2, WIN, n_taps * WIN), F32),
            pltpu.VMEM((2, most, ROWS, WIN), F32),
            pltpu.VMEM((2, n_taps * WIN, WIN), BF16),
            pltpu.VMEM((pairs, 3, length, two), BF16),
            pltpu.VMEM((length, 1), F32),
        ],
    )
    return pl.pallas_call(
        functools.partial(backward_kernel, n_taps, key_half, most),
        grid_spec=grid_spec,
        out_shape=[
            jax.ShapeDtypeStruct((length, 3 * heads * HEAD_DIM), BF16),
            jax.ShapeDtypeStruct((length // ROWS, ROWS), F32),
            jax.ShapeDtypeStruct((1, heads * PAD_DIM), F32),
            jax.ShapeDtypeStruct((heads, tap_rows, PAD_DIM), F32),
            jax.ShapeDtypeStruct((pairs, 4, PAD_DIM), F32),
        ],
        compiler_params=pltpu.CompilerParams(vmem_limit_bytes=56 << 20),
        cost_estimate=COST,
        name="attend_backward",
    )(counts, mix, proj, proj, proj, start, base, gain, probs, heads_out, grad_grouped)


MESH_ID = pl.DeviceIdType.MESH


def ring_place(member, n):
    z, y = member // 2, member % 2
    return (1 - y) * z + y * (n - 1 - z)


def ring_member(place, n):
    upper = place // (n // 2)
    return (1 - upper) * 2 * place + upper * (2 * (n - 1 - place) + 1)


def ring_peers(n):
    place = ring_place(lax.axis_index("dp"), n)
    ahead = ring_member(lax.rem(place + 1, n), n)
    behind = ring_member(lax.rem(place + n - 1, n), n)
    return place, (ahead, behind)


def ring_scratch(arrays, n):
    return [pltpu.VMEM((2, n - 1) + a.shape[2:], a.dtype) for a in arrays] + [
        pltpu.SemaphoreType.DMA((2, len(arrays), n - 1))
    ] * 4


def ring_split(array, n):
    return array.reshape(n, 2, -1, array.shape[-1])


def make_ring(n, ins, outs, scratch):
    count = len(ins)
    slots = scratch[:count]
    rs_send, rs_recv, ag_send, ag_recv = scratch[count:]
    place, to = ring_peers(n)

    def chunk(way, back):
        return lax.rem(place - back + 2 * n if way == 0 else place + back, n)

    def sum_copy(way, k, s, src):
        return pltpu.make_async_remote_copy(
            src_ref=src,
            dst_ref=slots[k].at[way, s],
            send_sem=rs_send.at[way, k, s],
            recv_sem=rs_recv.at[way, k, s],
            device_id={"dp": to[way]},
            device_id_type=MESH_ID,
        )

    def share_copy(way, k, s, c):
        return pltpu.make_async_remote_copy(
            src_ref=outs[k].at[c, way],
            dst_ref=outs[k].at[c, way],
            send_sem=ag_send.at[way, k, s],
            recv_sem=ag_recv.at[way, k, s],
            device_id={"dp": to[way]},
            device_id_type=MESH_ID,
        )

    def add(way, k, s, c, dst):
        total = slots[k][way, s].astype(F32) + ins[k][c, way].astype(F32)
        dst[...] = total.astype(dst.dtype)

    both = [(k, way) for k in range(count) for way in range(2)]

    def start():
        for k, way in both:
            sum_copy(way, k, 0, ins[k].at[chunk(way, 1), way]).start()

    def tick(now):
        @pl.when(now < n - 2)
        def _():
            for k, way in both:
                sum_copy(way, k, now, slots[k].at[way, now]).wait_recv()
                add(way, k, now, chunk(way, 2 + now), slots[k].at[way, now])
                sum_copy(way, k, now + 1, slots[k].at[way, now]).start()

        @pl.when(now == n - 2)
        def _():
            for k, way in both:
                sum_copy(way, k, n - 2, slots[k].at[way, n - 2]).wait_recv()
                add(way, k, n - 2, place, outs[k].at[place, way])
                share_copy(way, k, 0, place).start()

        @pl.when((now > n - 2) & (now < 2 * n - 3))
        def _():
            step = now - (n - 1)
            for k, way in both:
                share_copy(way, k, step, chunk(way, step + 1)).wait_recv()
                share_copy(way, k, step + 1, chunk(way, step + 1)).start()

        @pl.when(now == 2 * n - 3)
        def _():
            for k, way in both:
                share_copy(way, k, n - 2, chunk(way, n - 1)).wait_recv()

    def drain():
        def one(s, carry):
            for k, way in both:
                sum_copy(way, k, s, slots[k].at[way, s]).wait_send()
                share_copy(way, k, s, place).wait_send()
            return carry

        lax.fori_loop(0, n - 1, one, 0)

    return start, tick, drain


def small_rows(size):
    return -(-size // PAD_DIM)


def pack_small(arrays, rows):
    packed = []
    for a in arrays:
        flat = a.reshape(-1)
        packed.append(jnp.pad(flat, (0, -flat.size % PAD_DIM)).reshape(-1, PAD_DIM))
    packed = jnp.concatenate(packed, axis=0)
    return jnp.pad(packed, ((0, rows - packed.shape[0]), (0, 0)))


def unpack_small(packed, arrays):
    found, at = [], 0
    for a in arrays:
        rows = small_rows(a.size)
        found.append(packed[at : at + rows].reshape(-1)[: a.size].reshape(a.shape))
        at += rows
    return found


CHUNK = 128
GROUP = 256


LIVE = 4


def exchange_scratch(steps, width, ranks, share=True, chunk=CHUNK):
    half = ranks // 2
    live = steps if share else LIVE
    shared = [pltpu.VMEM((steps, ranks, chunk, width), BF16)] if share else []
    return [
        pltpu.VMEM((steps, half, chunk, width), BF16),
        pltpu.VMEM((steps, half, chunk, width), BF16),
        pltpu.VMEM((live, half, chunk, width), F32),
        pltpu.VMEM((steps, chunk, width), BF16),
        pltpu.VMEM((steps, chunk, width), BF16),
        pltpu.SemaphoreType.DMA((5, steps)),
        pltpu.SemaphoreType.DMA((5, steps)),
    ] + shared


def tensor_peers():
    me = lax.axis_index("tensor")
    return me, me + 1 - 2 * lax.rem(me, 2), lax.rem(me + 2, 4)


def meet(signals):
    barrier = pltpu.get_barrier_semaphore()
    for device in signals:
        pl.semaphore_signal(barrier, inc=1, device_id=device, device_id_type=MESH_ID)
    pl.semaphore_wait(barrier, len(signals))


def exchange_copies(scratch):
    out_a, in_a, _, out_b, in_b, send, recv, *full = scratch
    me, near, far = tensor_peers()

    def copy(kind, step, src, dst, peer):
        return pltpu.make_async_remote_copy(
            src_ref=src,
            dst_ref=dst,
            send_sem=send.at[kind, step],
            recv_sem=recv.at[kind, step],
            device_id={"tensor": peer},
            device_id_type=MESH_ID,
        )

    def cores(step):
        return copy(0, step, out_a.at[step], in_a.at[step], near)

    def chips(step):
        return copy(1, step, out_b.at[step], in_b.at[step], far)

    def back_far(step):
        return copy(2, step, full[0].at[step, me], full[0].at[step, me], far)

    def back_near(step):
        return copy(3, step, full[0].at[step, me], full[0].at[step, me], near)

    def pass_near(step):
        return copy(4, step, full[0].at[step, far], full[0].at[step, far], near)

    return cores, chips, back_far, back_near, pass_near


def exchange_stages(scratch, partial, live, chunk):
    out_a, in_a, kept, out_b, in_b = scratch[:5]
    cores, chips = exchange_copies(scratch)[:2]
    many = GROUP // chunk
    me, near, far = tensor_peers()

    def begin(step):
        for n, owner in ((0, near), (1, lax.rem(near + 2, 4))):

            def put(term, n=n):
                term = term.astype(BF16)
                for m in range(many):
                    out_a[step + m, n] = term[m * chunk : (m + 1) * chunk]

            partial(step, owner, put)
        for m in range(many):
            cores(step + m).start()
        for n, owner in ((1, far), (0, me)):

            def put(term, n=n):
                for m in range(many):
                    kept[lax.rem(step + m, live), n] = term[m * chunk : (m + 1) * chunk]

            partial(step, owner, put)

    def over(step):
        cores(step).wait_recv()
        out_b[step] = (kept[lax.rem(step, live), 1] + in_a[step, 1].astype(F32)).astype(BF16)
        chips(step).start()

    def total(step):
        chips(step).wait_recv()
        return kept[lax.rem(step, live), 0] + in_a[step, 0].astype(F32) + in_b[step].astype(F32)

    return begin, over, total


def make_exchange(steps, scratch, partial, local, between, chunk):
    cores, chips = exchange_copies(scratch)[:2]
    begin, over, total = exchange_stages(scratch, partial, LIVE, chunk)
    many = GROUP // chunk

    def tick(now):
        @pl.when((lax.rem(now, many) == 0) & (now < steps))
        def _():
            begin(now)

        between(now)

        @pl.when((now >= 1) & (now < steps + 1))
        def _():
            over(now - 1)

        @pl.when((now >= 2) & (now < steps + 2))
        def _():
            local(now - 2, total(now - 2))

    def drain():
        def one(step, carry):
            cores(step).wait_send()
            chips(step).wait_send()
            return carry

        lax.fori_loop(0, steps, one, 0)

    return tick, steps + 2, drain


def run_exchange(steps, scratch, partial, local, whole, beside=None, ahead=None):
    cores, chips, back_far, back_near, pass_near = exchange_copies(scratch)
    begin, over, total = exchange_stages(scratch, partial, steps, CHUNK)
    full = scratch[7]
    many = GROUP // CHUNK
    me = tensor_peers()[0]

    def send_group(group, carry):
        @pl.when(group < steps // many)
        def _():
            begin(group * many)

        @pl.when(group >= 1)
        def _():
            for m in range(many):
                over((group - 1) * many + m)

        return carry

    lax.fori_loop(0, steps // many + 1, send_group, 0)

    def sum_group(group, carry):
        if beside is not None:
            beside(group)
        for m in range(many):
            step = group * many + m
            full[step, me] = local(step, total(step)).astype(BF16)
            back_far(step).start()
            back_near(step).start()
        return carry

    lax.fori_loop(0, steps // many, sum_group, 0)
    if ahead is not None:
        ahead()

    def share_step(now, carry):
        @pl.when(now < steps)
        def _():
            back_far(now).wait_recv()
            pass_near(now).start()

        @pl.when(now >= 1)
        def _():
            back_near(now - 1).wait_recv()
            pass_near(now - 1).wait_recv()
            whole(now - 1, full)

        return carry

    lax.fori_loop(0, steps + 1, share_step, 0)

    def drain(step, carry):
        for copy in (cores, chips, back_far, back_near, pass_near):
            copy(step).wait_send()
        return carry

    lax.fori_loop(0, steps, drain, 0)


def run_ticks(count, *ticks):
    def one(now, carry):
        for tick in ticks:
            tick(now)
        return carry

    lax.fori_loop(0, count, one, 0)


def group_rows(step, chunk=CHUNK):
    return pl.ds(pl.multiple_of(step * chunk, chunk), GROUP)


def owner_cols(owner, width):
    return pl.ds(pl.multiple_of(owner * width, PAD_DIM), width)


def step_rows(step, chunk=CHUNK):
    return pl.ds(pl.multiple_of(step * chunk, chunk), chunk)


def first_entry_kernel(
    tokens_ref, w_ref, gains_ref, proj_ref, normed_ref, factor_ref, gains_all_ref, full, gains_in,
    send, recv, gains_send, gains_recv,
):
    rows, width = tokens_ref.shape
    ranks = normed_ref.shape[1] // width
    heads = width // HEAD_DIM
    steps, many = rows // CHUNK, GROUP // CHUNK
    me, near, far = tensor_peers()
    across = lax.rem(near + 2, 4)
    meet([{"tensor": near}, {"tensor": far}, {"tensor": across}])

    def copy(kind, step, src, dst, peer):
        return pltpu.make_async_remote_copy(
            src_ref=src,
            dst_ref=dst,
            send_sem=send.at[kind, step],
            recv_sem=recv.at[kind, step],
            device_id={"tensor": peer},
            device_id_type=MESH_ID,
        )

    def to_far(step):
        return copy(0, step, tokens_ref.at[step_rows(step)], full.at[step, me], far)

    def to_near(step):
        return copy(1, step, tokens_ref.at[step_rows(step)], full.at[step, me], near)

    def pass_near(step):
        return copy(2, step, full.at[step, far], full.at[step, far], near)

    def gains_copy(kind, peer, sender):
        return pltpu.make_async_remote_copy(
            src_ref=gains_ref,
            dst_ref=gains_in.at[sender],
            send_sem=gains_send.at[kind],
            recv_sem=gains_recv.at[sender],
            device_id={"tensor": peer},
            device_id_type=MESH_ID,
        )

    peers = (near, far, across)
    for kind, peer in enumerate(peers):
        gains_copy(kind, peer, me).start()

    def send_all(step, carry):
        to_far(step).start()
        to_near(step).start()
        full[step, me] = tokens_ref[step_rows(step), :]
        return carry

    lax.fori_loop(0, steps, send_all, 0)
    gains_in[me] = gains_ref[...]
    for kind, peer in enumerate(peers):
        gains_copy(kind, peer, peer).wait()
    for n in range(ranks):
        gains_all_ref[:, n * width : (n + 1) * width] = gains_in[n]

    def tick(now):
        @pl.when(now < steps)
        def _():
            to_far(now).wait_recv()
            pass_near(now).start()

        @pl.when(now >= 1)
        def _():
            to_near(now - 1).wait_recv()
            pass_near(now - 1).wait_recv()

        @pl.when((now >= many) & (lax.rem(now, many) == 0))
        def _():
            first = now - many
            at = group_rows(first)
            blocks = [
                jnp.concatenate([full[first + m, n] for m in range(many)], axis=0).astype(F32)
                for n in range(ranks)
            ]
            squares = sum(jnp.sum(block * block, axis=-1, keepdims=True) for block in blocks)
            factor = lax.rsqrt(squares * (1.0 / (ranks * width)) + EPS)
            factor_ref[at, :] = factor
            for n, block in enumerate(blocks):
                cols = slice(n * width, (n + 1) * width)
                normed_ref[at, cols] = (block * factor * gains_all_ref[0:1, cols]).astype(BF16)
            for c in range(3):
                out = dot_nn(normed_ref[at, :], w_ref[c])
                empty = jnp.zeros((GROUP, PAD_DIM - HEAD_DIM), F32)
                for h in range(heads):
                    head = jnp.concatenate([out[:, h * HEAD_DIM : (h + 1) * HEAD_DIM], empty], axis=1)
                    lane = (c * heads + h) * PAD_DIM
                    proj_ref[at, lane : lane + PAD_DIM] = head.astype(BF16)

    run_ticks(steps + 1, tick)

    def drain(step, carry):
        to_far(step).wait_send()
        to_near(step).wait_send()
        pass_near(step).wait_send()
        return carry

    lax.fori_loop(0, steps, drain, 0)


def first_entry(tokens, w_qkv, gains):
    rows, width = tokens.shape
    full_width = w_qkv.shape[1]
    ranks = full_width // width
    steps = rows // CHUNK
    vmem = pl.BlockSpec(memory_space=pltpu.VMEM)
    return pl.pallas_call(
        first_entry_kernel,
        out_shape=[
            jax.ShapeDtypeStruct((rows, 3 * width // HEAD_DIM * PAD_DIM), BF16),
            jax.ShapeDtypeStruct((rows, full_width), BF16),
            jax.ShapeDtypeStruct((rows, 1), F32),
            jax.ShapeDtypeStruct((8, full_width), F32),
        ],
        in_specs=[vmem] * 3,
        out_specs=[vmem] * 4,
        scratch_shapes=[
            pltpu.VMEM((steps, ranks, CHUNK, width), BF16),
            pltpu.VMEM((ranks, 8, width), F32),
            pltpu.SemaphoreType.DMA((3, steps)),
            pltpu.SemaphoreType.DMA((3, steps)),
            pltpu.SemaphoreType.DMA((3,)),
            pltpu.SemaphoreType.DMA((ranks,)),
        ],
        compiler_params=pltpu.CompilerParams(
            collective_id=4, has_side_effects=True, vmem_limit_bytes=40 << 20
        ),
        cost_estimate=COST,
        name="first_entry",
    )(tokens, w_qkv, gains)


def attn_exit_kernel(
    grouped_ref, w_out_ref, tokens_ref, gain_ref, cot_in, w_gate_up_in, w_down_in, hidden_local_ref,
    hidden_ref, normed_ref, w_ref, act_ref, grad_gate_ref, grad_up_ref, grad_act, cot_ref, w_gate_up_ref,
    w_down_ref, load, *scratch
):
    loads = [
        pltpu.make_async_copy(src, dst, load.at[n])
        for n, (src, dst) in enumerate(
            ((cot_in, cot_ref), (w_down_in, w_down_ref), (w_gate_up_in, w_gate_up_ref))
        )
    ]
    for one in loads:
        one.start()
    rows, width = tokens_ref.shape
    ranks = hidden_ref.shape[1] // width
    many = GROUP // CHUNK
    for h in range(width // HEAD_DIM):
        lead = h * PAD_DIM
        w_ref[lead : lead + HEAD_DIM, :] = w_out_ref[h * HEAD_DIM : (h + 1) * HEAD_DIM, :]
        w_ref[lead + HEAD_DIM : lead + PAD_DIM, :] = jnp.zeros((PAD_DIM - HEAD_DIM, w_ref.shape[1]), BF16)

    def partial(step, owner, put):
        put(dot_nn(grouped_ref[group_rows(step), :], w_ref[:, owner_cols(owner, width)]))

    def local(step, total):
        hidden = tokens_ref[step_rows(step), :].astype(F32) + total
        hidden_local_ref[step_rows(step), :] = hidden
        return hidden

    def whole(step, full):
        squares = None
        for n in range(ranks):
            block = full[step, n]
            hidden_ref[step_rows(step), n * width : (n + 1) * width] = block
            block = block.astype(F32)
            part = jnp.sum(block * block, axis=-1, keepdims=True)
            squares = part if squares is None else squares + part
        factor = lax.rsqrt(squares * (1.0 / (ranks * width)) + EPS)
        for n in range(ranks):
            cols = slice(n * width, (n + 1) * width)
            unit = full[step, n].astype(F32) * factor
            normed_ref[step_rows(step), cols] = (unit * gain_ref[:, cols]).astype(BF16)

        @pl.when(lax.rem(step, many) == many - 1)
        def _():
            at = group_rows(step - (many - 1))
            gate = dot_nn(normed_ref[at, :], w_gate_up_ref[0])
            up = dot_nn(normed_ref[at, :], w_gate_up_ref[1])
            sigmoid = jax.nn.sigmoid(gate)
            swish = gate * sigmoid
            grad = grad_act[at, :]
            act_ref[at, :] = (swish * up).astype(BF16)
            grad_gate_ref[at, :] = (grad * up * sigmoid * (1.0 + gate * (1.0 - sigmoid))).astype(BF16)
            grad_up_ref[at, :] = (grad * swish).astype(BF16)

    def beside(group):
        @pl.when(group == 0)
        def _():
            loads[0].wait()
            loads[1].wait()

        at = group_rows(group * many)
        grad_act[at, :] = dot_nt(cot_ref[at, :], w_down_ref[...])

    me, near, far = tensor_peers()
    meet([{"tensor": near}, {"tensor": far}])
    run_exchange(rows // CHUNK, scratch, partial, local, whole, beside, loads[2].wait)


def attn_exit(grouped, w_out, tokens, gain, full_cot, w_gate_up, w_down):
    rows, width = tokens.shape
    full_width = w_out.shape[1]
    units = w_down.shape[0]
    vmem = pl.BlockSpec(memory_space=pltpu.VMEM)
    return pl.pallas_call(
        attn_exit_kernel,
        out_shape=[
            jax.ShapeDtypeStruct((rows, width), F32),
            jax.ShapeDtypeStruct((rows, full_width), BF16),
            jax.ShapeDtypeStruct((rows, full_width), BF16),
            jax.ShapeDtypeStruct((grouped.shape[1], full_width), BF16),
        ]
        + [jax.ShapeDtypeStruct((rows, units), BF16)] * 3,
        in_specs=[vmem] * 4 + [pl.BlockSpec(memory_space=pl.ANY)] * 3,
        out_specs=[vmem] * 7,
        scratch_shapes=[
            pltpu.VMEM((rows, units), F32),
            pltpu.VMEM(full_cot.shape, BF16),
            pltpu.VMEM(w_gate_up.shape, BF16),
            pltpu.VMEM(w_down.shape, BF16),
            pltpu.SemaphoreType.DMA((3,)),
        ]
        + exchange_scratch(rows // CHUNK, width, full_width // width),
        compiler_params=pltpu.CompilerParams(
            collective_id=1, has_side_effects=True, vmem_limit_bytes=56 << 20
        ),
        cost_estimate=COST,
        name="attn_exit",
    )(grouped, w_out, tokens, gain, full_cot, w_gate_up, w_down)


def mlp_exit_kernel(
    gate_ref, up_ref, w_ref, hidden_in, cot_in, hidden_local_ref, cot_local_ref, gain_ref, gain_local_ref,
    grad_attn_ref, grad_hidden_ref, gain_grad_ref, grad_local, hidden_ref, cot_ref, load, *scratch
):
    loads = [
        pltpu.make_async_copy(hidden_in, hidden_ref, load.at[0]),
        pltpu.make_async_copy(cot_in, cot_ref, load.at[1]),
    ]
    for one in loads:
        one.start()
    rows, width = cot_local_ref.shape
    full_width = hidden_ref.shape[1]
    ranks = full_width // width
    gain_grad_ref[...] = jnp.zeros_like(gain_grad_ref)

    def partial(step, owner, put):
        cols = owner_cols(owner, width)
        at = group_rows(step)
        put(dot_nt(gate_ref[at, :], w_ref[0, cols, :]) + dot_nt(up_ref[at, :], w_ref[1, cols, :]))

    def local(step, total):
        grad_local[step_rows(step), :] = total
        return total

    def whole(step, full):
        at = step_rows(step)
        squares, inner = None, None
        for n in range(ranks):
            cols = slice(n * width, (n + 1) * width)
            hidden = hidden_ref[at, cols].astype(F32)
            part = jnp.sum(hidden * hidden, axis=-1, keepdims=True)
            squares = part if squares is None else squares + part
            part = jnp.sum(full[step, n].astype(F32) * gain_ref[:, cols] * hidden, axis=-1, keepdims=True)
            inner = part if inner is None else inner + part
        factor = lax.rsqrt(squares * (1.0 / full_width) + EPS)
        inner = inner * factor * (1.0 / full_width)
        for n in range(ranks):
            cols = slice(n * width, (n + 1) * width)
            unit = hidden_ref[at, cols].astype(F32) * factor
            grad = full[step, n].astype(F32) * gain_ref[:, cols] - unit * inner
            grad_attn_ref[at, cols] = (cot_ref[at, cols].astype(F32) + factor * grad).astype(BF16)
        total = grad_local[at, :]
        unit = hidden_local_ref[at, :] * factor
        gain_grad_ref[...] += jnp.sum(total * unit, axis=0, keepdims=True)
        grad_hidden_ref[at, :] = cot_local_ref[at, :].astype(F32) + factor * (
            total * gain_local_ref[...] - unit * inner
        )

    me, near, far = tensor_peers()
    meet([{"tensor": near}, {"tensor": far}])

    def ahead():
        for one in loads:
            one.wait()

    run_exchange(rows // CHUNK, scratch, partial, local, whole, ahead=ahead)


def mlp_exit(grad_gate, grad_up, w_gate_up, hidden, full_cot, hidden_local, cotangent, gain, gain_local):
    rows, width = hidden_local.shape
    full_width = hidden.shape[1]
    vmem = pl.BlockSpec(memory_space=pltpu.VMEM)
    return pl.pallas_call(
        mlp_exit_kernel,
        out_shape=[
            jax.ShapeDtypeStruct((rows, full_width), BF16),
            jax.ShapeDtypeStruct((rows, width), F32),
            jax.ShapeDtypeStruct((1, width), F32),
        ],
        in_specs=[vmem] * 3 + [pl.BlockSpec(memory_space=pl.ANY)] * 2 + [vmem] * 4,
        out_specs=[vmem] * 3,
        scratch_shapes=[
            pltpu.VMEM((rows, width), F32),
            pltpu.VMEM(hidden.shape, BF16),
            pltpu.VMEM(full_cot.shape, BF16),
            pltpu.SemaphoreType.DMA((2,)),
        ]
        + exchange_scratch(rows // CHUNK, width, full_width // width),
        compiler_params=pltpu.CompilerParams(
            collective_id=2, has_side_effects=True, vmem_limit_bytes=56 << 20
        ),
        cost_estimate=COST,
        name="mlp_exit",
    )(grad_gate, grad_up, w_gate_up, hidden, full_cot, hidden_local, cotangent, gain, gain_local)


def last_exit_kernel(
    n_ring, count, grad_ref, w_ref, tokens_ref, grad_hidden_ref, factor_ref, inner_ref, gain_ref, act_ref,
    w_down_ref, hidden_ref, small_ref, *refs,
):
    ins, refs = refs[:count], refs[count:]
    tokens_grad_ref, out_ref, small_sum_ref = refs[:3]
    outs, refs = refs[3 : 3 + count], refs[3 + count :]
    gain_grad, mine, all_small, small_send, small_recv = refs[:5]
    inner_in, inner_sum, inner_col, inner_send, inner_recv = refs[5:10]
    ring_refs, scratch = refs[10 : 14 + count], refs[14 + count :]
    rows, width = tokens_ref.shape
    full_width = w_ref.shape[1]
    half = rows // GROUP
    me, near, far = tensor_peers()
    here = lax.axis_index("dp")
    gain_grad[...] = jnp.zeros_like(gain_grad)

    def partial(step, owner, put):
        cols = owner_cols(owner, width)

        @pl.when(step < half)
        def _():
            total = None
            for c in range(3):
                term = dot_nt(grad_ref[group_rows(step, GROUP), c * width : (c + 1) * width], w_ref[c, cols, :])
                total = term if total is None else total + term
            put(total)

        @pl.when(step >= half)
        def _():
            put(dot_nn(act_ref[group_rows(step - half, GROUP), :], w_down_ref[:, cols]))

    def between(now):
        def copy(n, src, peer):
            return pltpu.make_async_remote_copy(
                src_ref=src,
                dst_ref=inner_in.at[n],
                send_sem=inner_send.at[n],
                recv_sem=inner_recv.at[n],
                device_id={"tensor": peer},
                device_id_type=MESH_ID,
            )

        @pl.when(now == 0)
        def _():
            copy(0, inner_ref, near).start()

        @pl.when(now == 1)
        def _():
            copy(0, inner_ref, near).wait()
            inner_sum[...] = inner_ref[...] + inner_in[0]
            copy(1, inner_sum, far).start()

        @pl.when(now == 2)
        def _():
            copy(1, inner_sum, far).wait()
            total = (inner_sum[...] + inner_in[1]) * (1.0 / full_width)
            for n in range(rows // ROWS):
                line = jnp.broadcast_to(total[n : n + 1, :], (ROWS, ROWS))
                inner_col[n * ROWS : (n + 1) * ROWS, :] = line.T[:, 0:1]

    def local(step, total):
        @pl.when(step < half)
        def _():
            at = step_rows(step, GROUP)
            factor = factor_ref[at, :]
            unit = tokens_ref[at, :].astype(F32) * factor
            gain_grad[...] += jnp.sum(total * unit, axis=0, keepdims=True)
            tokens_grad_ref[at, :] = grad_hidden_ref[at, :] + factor * (
                total * gain_ref[...] - unit * inner_col[at, :]
            )

        @pl.when(step >= half)
        def _():
            at = step_rows(step - half, GROUP)
            out_ref[at, :] = (hidden_ref[at, :] + total).astype(BF16)

    def small_copy(peer, sender):
        return pltpu.make_async_remote_copy(
            src_ref=mine,
            dst_ref=all_small.at[sender],
            send_sem=small_send.at[peer],
            recv_sem=small_recv.at[sender],
            device_id={"dp": peer},
            device_id_type=MESH_ID,
        )

    def small_start(now):
        @pl.when(now == half + 2)
        def _():
            mine[...] = small_ref[...]
            for n in range(width // PAD_DIM):
                mine[n : n + 1, :] = gain_grad[:, n * PAD_DIM : (n + 1) * PAD_DIM]
            all_small[here] = mine[...]

            def one(away, carry):
                small_copy(lax.rem(here + away, n_ring), here).start()
                return carry

            lax.fori_loop(1, n_ring, one, 0)

    barrier = pltpu.get_barrier_semaphore()
    for peer in (near, far):
        pl.semaphore_signal(barrier, inc=1, device_id={"tensor": peer}, device_id_type=MESH_ID)

    def greet(away, carry):
        peer = lax.rem(here + away, n_ring)
        pl.semaphore_signal(barrier, inc=1, device_id={"dp": peer}, device_id_type=MESH_ID)
        return carry

    lax.fori_loop(1, n_ring, greet, 0)
    pl.semaphore_wait(barrier, 2 + n_ring - 1)

    ring_start, ring_tick, ring_drain = make_ring(n_ring, ins, outs, ring_refs)
    tick, ticks, drain = make_exchange(2 * half, scratch, partial, local, between, GROUP)
    ring_start()

    run_ticks(max(ticks, 2 * (n_ring - 1)), ring_tick, tick, small_start)

    def one(away, carry):
        peer = lax.rem(here + away, n_ring)
        small_copy(peer, peer).wait()
        return carry

    lax.fori_loop(1, n_ring, one, 0)

    def add(n, total):
        return total + all_small[n]

    small_sum_ref[...] = lax.fori_loop(1, n_ring, add, all_small[0])
    drain()
    ring_drain()


def last_exit(
    grad_proj, w_qkv, tokens, grad_hidden, factor, inner, gain, act, w_down, hidden_local, small, sums
):
    rows, width = tokens.shape
    n_ring = lax.axis_size("dp")
    count = len(sums)
    split = [ring_split(a, n_ring) for a in sums]
    gain_rows = width // PAD_DIM
    need = gain_rows + sum(small_rows(a.size) for a in small)
    packed = jnp.pad(pack_small(small, need - gain_rows), ((gain_rows, -need % 8), (0, 0)))
    vmem = pl.BlockSpec(memory_space=pltpu.VMEM)
    steps = 2 * rows // GROUP
    tokens_grad, out, packed, *totals = pl.pallas_call(
        functools.partial(last_exit_kernel, n_ring, count),
        out_shape=[
            jax.ShapeDtypeStruct((rows, width), F32),
            jax.ShapeDtypeStruct((rows, width), BF16),
            jax.ShapeDtypeStruct(packed.shape, F32),
        ]
        + [jax.ShapeDtypeStruct(a.shape, a.dtype) for a in split],
        in_specs=[vmem] * (11 + count),
        out_specs=[vmem] * (3 + count),
        scratch_shapes=[
            pltpu.VMEM((1, width), F32),
            pltpu.VMEM(packed.shape, F32),
            pltpu.VMEM((n_ring,) + packed.shape, F32),
            pltpu.SemaphoreType.DMA((n_ring,)),
            pltpu.SemaphoreType.DMA((n_ring,)),
            pltpu.VMEM((2,) + inner.shape, F32),
            pltpu.VMEM(inner.shape, F32),
            pltpu.VMEM((rows, 1), F32),
            pltpu.SemaphoreType.DMA((2,)),
            pltpu.SemaphoreType.DMA((2,)),
        ]
        + ring_scratch(split, n_ring)
        + exchange_scratch(steps, width, w_qkv.shape[1] // width, False, GROUP),
        compiler_params=pltpu.CompilerParams(
            collective_id=3, has_side_effects=True, vmem_limit_bytes=62 << 20
        ),
        cost_estimate=COST,
        name="last_exit",
    )(grad_proj, w_qkv, tokens, grad_hidden, factor, inner, gain, act, w_down, hidden_local, packed, *split)
    gain_grad = packed[:gain_rows].reshape(width)
    totals = [t.reshape(a.shape) for t, a in zip(totals, sums)]
    return tokens_grad, gain_grad, out, unpack_small(packed[gain_rows:], small), totals


def banded(line):
    return pltpu.roll(jnp.broadcast_to(line, (WIN, WIN)), 0, 1, stride=1, stride_axis=0)


def band_lines(kernel):
    taps = kernel.shape[2]
    wide = jnp.pad(kernel, ((0, 0), (0, 0), (0, WIN - taps)))
    back = jnp.pad(kernel[:, :, ::-1], ((0, 0), (0, 0), (0, WIN - taps)))
    return jnp.roll(wide, -(taps // 2), axis=2), jnp.roll(back, -(taps // 2), axis=2)


def pad_heads(array, axis):
    shape = array.shape
    heads = shape[axis] // HEAD_DIM
    split = array.reshape(shape[:axis] + (heads, HEAD_DIM) + shape[axis + 1 :])
    widths = [(0, 0)] * split.ndim
    widths[axis + 1] = (0, PAD_DIM - HEAD_DIM)
    return jnp.pad(split, widths).reshape(shape[:axis] + (heads * PAD_DIM,) + shape[axis + 1 :])


def cut_heads(array, axis):
    shape = array.shape
    heads = shape[axis] // PAD_DIM
    split = array.reshape(shape[:axis] + (heads, PAD_DIM) + shape[axis + 1 :])
    cut = lax.slice_in_dim(split, 0, HEAD_DIM, axis=axis + 1)
    return cut.reshape(shape[:axis] + (heads * HEAD_DIM,) + shape[axis + 1 :])


def windows_needed(start, key_half):
    length = start.shape[0]
    first = start[::ROWS]
    row0 = jnp.arange(0, length, ROWS, dtype=jnp.int32)
    count = jnp.ones_like(first)
    for k in range(1, windows_most(key_half)):
        count = count + (first - key_half < row0 + ROWS - STEP * k).astype(jnp.int32)
    return count


def on_device(
    tokens, segments, attn_gain, w_qkv, kq_kernel, head_mix, group_gain, w_out, mlp_gain, w_gate_up,
    w_down, cotangent,
):
    rows_here, local_width = tokens.shape
    seq_count, length = segments.shape
    heads_here = local_width // HEAD_DIM
    n_taps, key_taps = kq_kernel.shape[1:]
    key_half = key_taps // 2

    lines, lines_back = band_lines(kq_kernel)
    gain_heads = pad_heads(group_gain.astype(F32), 0)[None]
    starts, counts = [], []
    for n in range(seq_count):
        seg = segments[n]
        start = jnp.sum((seg[None, :] < seg[:, None]).astype(jnp.int32), axis=1)
        counts.append(windows_needed(start, key_half))
        starts.append(jnp.pad(start, (HALO, 0), constant_values=1 << 20)[:, None])

    full_width = w_qkv.shape[1]
    own_gains = jnp.pad(jnp.stack([attn_gain, mlp_gain]).astype(F32), ((0, 6), (0, 0)))
    proj, normed_one, scale_one, gains = first_entry(tokens, w_qkv, own_gains)
    gain_two = gains[1:2]
    cot_here, proj = lax.optimization_barrier((cotangent, proj))
    full_cot = lax.all_gather(cot_here, "tensor", axis=1, tiled=True)

    kept = []
    for n in range(seq_count):
        rows = slice(n * length, (n + 1) * length)
        kept.append(
            attend_forward(proj[rows], starts[n], counts[n], lines, head_mix, gain_heads)
        )
    grouped = jnp.concatenate([one[2] for one in kept], axis=0)
    grouped, full_cot = lax.optimization_barrier((grouped, full_cot))
    hidden_local, hidden, normed_two, w_out_pad, act, grad_gate, grad_up = attn_exit(
        grouped, w_out, tokens, gain_two, full_cot, w_gate_up, w_down
    )

    grad_down = dot_tn(act, full_cot).astype(BF16)
    early_rows = int(full_width * EARLY_SHARE)
    early_up = dot_tn(normed_two[:, :early_rows], grad_up).astype(BF16)
    grad_gate, early_up, grad_down = lax.optimization_barrier((grad_gate, early_up, grad_down))
    early_up, grad_down = lax.psum((early_up, grad_down), "dp")
    grad_attn, grad_hidden_local, grad_gain_two = mlp_exit(
        grad_gate, grad_up, w_gate_up, hidden, full_cot, hidden_local, cotangent, gain_two,
        mlp_gain.astype(F32)[None],
    )
    grad_gate_w = dot_tn(normed_two, grad_gate).astype(BF16)
    late_up = dot_tn(normed_two[:, early_rows:], grad_up).astype(BF16)
    grad_w_out = cut_heads(dot_tn(grouped, grad_attn).astype(BF16), 0)

    grad_grouped = dot_nt(grad_attn, w_out_pad)
    parts = []
    for n in range(seq_count):
        rows = slice(n * length, (n + 1) * length)
        parts.append(
            attend_backward(
                proj[rows], starts[n], counts[n], lines_back, head_mix, gain_heads, kept[n][0], kept[n][1],
                grad_grouped[rows],
            )
        )
    grad_proj = jnp.concatenate([one[0] for one in parts], axis=0)
    inner_part = jnp.concatenate([one[1] for one in parts], axis=0)
    grad_group_gain = sum(cut_heads(one[2][0], 0) for one in parts)
    grad_kernel = sum(one[3][:, :, 0] for one in parts).reshape(heads_here, n_taps, key_taps)
    grad_mix = sum(one[4][:, :, 0] for one in parts).reshape(heads_here, 2)

    grad_qkv = [
        dot_tn(normed_one, grad_proj[:, c * local_width : (c + 1) * local_width]).astype(BF16)
        for c in range(3)
    ]
    tokens_grad, grad_gain_one, layer_out, small, sums = last_exit(
        grad_proj, w_qkv, tokens, grad_hidden_local, scale_one, inner_part, attn_gain.astype(F32)[None],
        act, w_down, hidden_local, (grad_kernel, grad_mix, grad_group_gain, grad_gain_two[0]),
        (grad_gate_w, late_up, grad_w_out, *grad_qkv),
    )
    grad_kernel, grad_mix, grad_group_gain, grad_gain_two = small
    grad_gate_w, late_up, grad_w_out, *grad_qkv = sums
    grad_gate_up = jnp.stack([grad_gate_w, jnp.concatenate([early_up, late_up], axis=0)])
    grad_qkv = jnp.stack(grad_qkv)
    return (
        layer_out,
        tokens_grad,
        grad_gain_one,
        grad_qkv.astype(F32),
        grad_kernel,
        grad_mix,
        grad_group_gain,
        grad_w_out.astype(F32),
        grad_gain_two,
        grad_gate_up.astype(F32),
        grad_down.astype(F32),
    )


def solution(mesh):
    in_specs = (
        P("dp", "tensor"),
        P("dp", None),
        P("tensor"),
        P(None, None, "tensor"),
        P("tensor", None, None),
        P("tensor", None),
        P("tensor"),
        P("tensor", None),
        P("tensor"),
        P(None, None, "tensor"),
        P("tensor", None),
        P("dp", "tensor"),
    )
    out_specs = (
        P("dp", "tensor"),
        P("dp", "tensor"),
        P("tensor"),
        P(None, None, "tensor"),
        P("tensor", None, None),
        P("tensor", None),
        P("tensor"),
        P("tensor", None),
        P("tensor"),
        P(None, None, "tensor"),
        P("tensor", None),
    )
    return jax.shard_map(
        on_device, mesh=mesh, in_specs=in_specs, out_specs=out_specs, check_vma=False
    )
```

```python
import functools

import jax
import jax.numpy as jnp
from jax import lax
from jax.experimental import pallas as pl
from jax.experimental.pallas import tpu as pltpu
from jax.sharding import PartitionSpec as P

HEAD_DIM = 96
PAD_DIM = 128
DOC_MOST = 512
EPS = 1e-05
NEG = -1e30

COST = pl.CostEstimate(flops=1 << 20, bytes_accessed=1 << 10, transcendentals=0)
EARLY_SHARE = 0.75
ROWS = 128
HALO = 16
WIN = 256
OWN = 16
STEP = WIN - 2 * OWN
TOP = 256
EXT = ROWS + HALO

F32 = jnp.float32
BF16 = jnp.bfloat16


def windows_most(key_half):
    return -(-(DOC_MOST - 1 + ROWS + key_half) // STEP)


def dot_nt(a, b):
    return lax.dot_general(a, b, (((1,), (1,)), ((), ())), preferred_element_type=F32)


def dot_tn(a, b):
    return lax.dot_general(a, b, (((0,), (0,)), ((), ())), preferred_element_type=F32)


def dot_nn(a, b):
    return jnp.dot(a, b, preferred_element_type=F32)


def fill_padded(dst, src, top, length):
    total = dst.shape[0]
    dst[0:top, :] = jnp.zeros((top, dst.shape[1]), dst.dtype)
    dst[top : top + length, :] = src[...]
    if total > top + length:
        dst[top + length : total, :] = jnp.zeros((total - top - length, dst.shape[1]), dst.dtype)


def lanes_between(first, last, width):
    lane = lax.broadcasted_iota(jnp.int32, (first.shape[0], width), 1)
    return (lane >= first) & (lane <= last)


def row_numbers(base, count):
    return base + lax.broadcasted_iota(jnp.int32, (count, 1), 0)


def forward_kernel(
    n_taps, key_half, most, count_ref, mix_ref, q_ref, k_ref, v_ref, start_ref, base_ref, gain_ref,
    probs_ref, heads_ref, grouped_ref, qs, ks, vs, logit_ref, band_ref, inputs,
):
    pair = pl.program_id(0)
    block = pl.program_id(1)
    length = q_ref.shape[0]
    scale = HEAD_DIM ** (-0.5)

    @pl.when(block == 0)
    def _():
        fill_padded(qs, q_ref, HALO, length)
        fill_padded(ks, k_ref, TOP, length)
        fill_padded(vs, v_ref, TOP, length)
        for s in range(2):
            for a in range(n_taps):
                band = banded(base_ref[s, a : a + 1, :])
                high = band.astype(BF16)
                band_ref[s, a, 0:WIN] = high
                band_ref[s, a, WIN : 2 * WIN] = high
                band_ref[s, a, 2 * WIN : 3 * WIN] = (band - high.astype(F32)).astype(BF16)

    row0 = pl.multiple_of(block * ROWS, ROWS)

    def body(n):
        start = start_ref[pl.ds(row0, EXT), :]
        place = row_numbers(row0 - HALO, EXT)
        firsts, lasts = [], []
        for k in range(n):
            base = row0 + ROWS - STEP * (k + 1) - OWN
            at = pl.multiple_of(TOP + base, 16)
            firsts.append(start - base)
            lasts.append(place - base)
            valid = lanes_between(firsts[k], lasts[k], WIN)
            rows = slice(k * EXT, (k + 1) * EXT)
            for s in range(2):
                cols = pl.ds(s * PAD_DIM, PAD_DIM)
                raw = dot_nt(qs[pl.ds(row0, EXT), cols], ks[pl.ds(at, WIN), cols])
                masked = jnp.where(valid, raw * scale, 0.0)
                high = masked.astype(BF16)
                inputs[s, rows, 0:WIN] = high
                inputs[s, rows, WIN : 2 * WIN] = (masked - high.astype(F32)).astype(BF16)
                inputs[s, rows, 2 * WIN : 3 * WIN] = high
        peaks = [None, None]
        for s in range(2):
            total = None
            for a in reversed(range(n_taps)):
                term = dot_nn(inputs[s, 0 : n * EXT, :], band_ref[s, a])
                total = term if total is None else pltpu.roll(total, 1, 0) + term
            for k in range(n):
                shown = lanes_between(
                    jnp.maximum(firsts[k][HALO:], key_half + 1),
                    jnp.minimum(lasts[k][HALO:], WIN - 2 - key_half),
                    WIN,
                )
                logits = jnp.where(shown, total[k * EXT + HALO : (k + 1) * EXT], NEG)
                logit_ref[s, k] = logits
                top = jnp.max(logits, axis=-1, keepdims=True)
                peaks[s] = top if peaks[s] is None else jnp.maximum(peaks[s], top)
        lane = lax.broadcasted_iota(jnp.int32, (ROWS, WIN), 1)
        own = (lane >= OWN) & (lane < WIN - OWN)
        sums = [None, None]
        for k in range(n):
            for s in range(2):
                expo = jnp.exp(logit_ref[s, k] - peaks[s])
                logit_ref[s, k] = expo
                part = jnp.sum(jnp.where(own, expo, 0.0), axis=-1, keepdims=True)
                sums[s] = part if sums[s] is None else sums[s] + part
        inverse = [1.0 / sums[s] for s in range(2)]
        outs = [None, None]
        for k in range(n):
            base = row0 + ROWS - STEP * (k + 1) - OWN
            at = pl.multiple_of(TOP + base, 16)
            probs = []
            for s in range(2):
                prob = logit_ref[s, k] * inverse[s]
                probs_ref[s, 0, k] = prob
                probs.append(jnp.where(own, prob, 0.0))
            for h in range(2):
                mixed = (
                    mix_ref[2 * pair + h, 0] * probs[0] + mix_ref[2 * pair + h, 1] * probs[1]
                ).astype(BF16)
                part = dot_nn(mixed, vs[pl.ds(at, WIN), pl.ds(h * PAD_DIM, PAD_DIM)])
                outs[h] = part if outs[h] is None else outs[h] + part
        for h in range(2):
            cols = slice(h * PAD_DIM, (h + 1) * PAD_DIM)
            out = outs[h]
            heads_ref[:, cols] = out
            factor = lax.rsqrt(jnp.sum(out * out, axis=-1, keepdims=True) * (1.0 / HEAD_DIM) + EPS)
            grouped_ref[:, cols] = (out * factor * gain_ref[:, cols]).astype(BF16)

    for n in range(1, most + 1):
        pl.when(count_ref[block] == n)(functools.partial(body, n))


def attend_forward(proj, start, counts, base, mix, gain):
    length = proj.shape[0]
    heads, n_taps = base.shape[:2]
    pairs = heads // 2
    blocks = length // ROWS
    key_half = 5
    most = windows_most(key_half)
    two = 2 * PAD_DIM
    grid_spec = pltpu.PrefetchScalarGridSpec(
        num_scalar_prefetch=2,
        grid=(pairs, blocks),
        in_specs=[
            pl.BlockSpec((length, two), lambda p, b, *_: (0, p)),
            pl.BlockSpec((length, two), lambda p, b, *_: (0, pairs + p)),
            pl.BlockSpec((length, two), lambda p, b, *_: (0, 2 * pairs + p)),
            pl.BlockSpec((HALO + length, 1), lambda p, b, *_: (0, 0)),
            pl.BlockSpec((2, n_taps, WIN), lambda p, b, *_: (p, 0, 0)),
            pl.BlockSpec((1, two), lambda p, b, *_: (0, p)),
        ],
        out_specs=[
            pl.BlockSpec((2, 1, most, ROWS, WIN), lambda p, b, *_: (p, b, 0, 0, 0)),
            pl.BlockSpec((ROWS, two), lambda p, b, *_: (b, p)),
            pl.BlockSpec((ROWS, two), lambda p, b, *_: (b, p)),
        ],
        scratch_shapes=[
            pltpu.VMEM((HALO + length, two), BF16),
            pltpu.VMEM((TOP + length + HALO, two), BF16),
            pltpu.VMEM((TOP + length + HALO, two), BF16),
            pltpu.VMEM((2, most, ROWS, WIN), F32),
            pltpu.VMEM((2, n_taps, 3 * WIN, WIN), BF16),
            pltpu.VMEM((2, most * EXT, 3 * WIN), BF16),
        ],
    )
    return pl.pallas_call(
        functools.partial(forward_kernel, n_taps, key_half, most),
        grid_spec=grid_spec,
        out_shape=[
            jax.ShapeDtypeStruct((heads, blocks, most, ROWS, WIN), F32),
            jax.ShapeDtypeStruct((length, heads * PAD_DIM), F32),
            jax.ShapeDtypeStruct((length, heads * PAD_DIM), BF16),
        ],
        compiler_params=pltpu.CompilerParams(vmem_limit_bytes=56 << 20),
        cost_estimate=COST,
        name="attend_forward",
    )(counts, mix, proj, proj, proj, start, base, gain)


def backward_kernel(
    n_taps, key_half, most, count_ref, mix_ref, q_ref, k_ref, v_ref, start_ref, base_ref, gain_ref,
    probs_ref, heads_ref, grad_ref, dqkv_ref, inner_ref, gain_grad_ref, tap_ref, mix_grad_ref,
    qs, ks, vs, dq_sum, dk_sum, dv_sum, taps, inputs, tap_sum, mixed_grad, t_back_ref, kept, inner_sum,
):
    pair = pl.program_id(0)
    block = pl.program_id(1)
    length = q_ref.shape[0]
    scale = HEAD_DIM ** (-0.5)

    @pl.when(block == 0)
    def _():
        fill_padded(qs, q_ref, HALO, length)
        fill_padded(ks, k_ref, TOP, length)
        fill_padded(vs, v_ref, TOP, length)
        dq_sum[...] = jnp.zeros_like(dq_sum)
        dk_sum[...] = jnp.zeros_like(dk_sum)
        dv_sum[...] = jnp.zeros_like(dv_sum)
        tap_sum[...] = jnp.zeros_like(tap_sum)
        gain_grad_ref[...] = jnp.zeros_like(gain_grad_ref)
        mix_grad_ref[...] = jnp.zeros_like(mix_grad_ref)
        for s in range(2):
            for a in range(n_taps):
                t_back_ref[s, a * WIN : (a + 1) * WIN, :] = banded(base_ref[s, a : a + 1, :]).astype(BF16)

    row0 = pl.multiple_of(block * ROWS, ROWS)

    def body(n):
        grads = []
        for h in range(2):
            cols = slice(h * PAD_DIM, (h + 1) * PAD_DIM)
            out = heads_ref[:, cols]
            factor = lax.rsqrt(jnp.sum(out * out, axis=-1, keepdims=True) * (1.0 / HEAD_DIM) + EPS)
            unit = out * factor
            grad = grad_ref[:, cols]
            gain_grad_ref[:, cols] += jnp.sum(grad * unit, axis=0, keepdims=True)
            scaled = grad * gain_ref[:, cols]
            inner = jnp.sum(scaled * unit, axis=-1, keepdims=True) * (1.0 / HEAD_DIM)
            grads.append((factor * (scaled - unit * inner)).astype(BF16))
        lane = lax.broadcasted_iota(jnp.int32, (ROWS, WIN), 1)
        own = (lane >= OWN) & (lane < WIN - OWN)
        inner = [[None, None], [None, None]]
        for k in range(n):
            base = row0 + ROWS - STEP * (k + 1) - OWN
            at = pl.multiple_of(TOP + base, 16)
            probs = [jnp.where(own, probs_ref[s, 0, k], 0.0) for s in range(2)]
            for h in range(2):
                cols = pl.ds(h * PAD_DIM, PAD_DIM)
                grad_mixed = dot_nt(grads[h], vs[pl.ds(at, WIN), cols])
                mixed_grad[h, k] = grad_mixed
                for s in range(2):
                    part = jnp.sum(grad_mixed * probs[s], axis=-1, keepdims=True)
                    inner[h][s] = part if inner[h][s] is None else inner[h][s] + part
                mixed = (
                    mix_ref[2 * pair + h, 0] * probs[0] + mix_ref[2 * pair + h, 1] * probs[1]
                ).astype(BF16)
                dv_sum[pl.ds(at, WIN), cols] += dot_tn(mixed, grads[h])
        for h in range(2):
            for s in range(2):
                row = 2 * h + s
                mix_grad_ref[0, row : row + 1, :] += jnp.broadcast_to(
                    jnp.sum(inner[h][s], axis=0, keepdims=True), (1, PAD_DIM)
                )
        start = start_ref[pl.ds(row0, EXT), :]
        place = row_numbers(row0 - HALO, EXT)
        for s in range(2):
            cols = pl.ds(s * PAD_DIM, PAD_DIM)
            mix0 = mix_ref[2 * pair, s]
            mix1 = mix_ref[2 * pair + 1, s]
            delta = mix0 * inner[0][s] + mix1 * inner[1][s]
            query = qs[pl.ds(row0, EXT), cols]
            for k in range(n):
                grad_prob = mix0 * mixed_grad[0, k] + mix1 * mixed_grad[1, k]
                grad_logit = probs_ref[s, 0, k] * (grad_prob - delta)
                grown = jnp.concatenate([jnp.zeros((HALO, WIN), F32), grad_logit], axis=0)
                for a in range(n_taps):
                    moved = grown if a == 0 else pltpu.roll(grown, EXT - a, 0)
                    taps[k * EXT : (k + 1) * EXT, a * WIN : (a + 1) * WIN] = moved.astype(BF16)
            grad_inputs = dot_nn(taps[0 : n * EXT, :], t_back_ref[s])
            for k in range(n):
                base = row0 + ROWS - STEP * (k + 1) - OWN
                at = pl.multiple_of(TOP + base, 16)
                keys = ks[pl.ds(at, WIN), cols]
                mine = lanes_between(
                    jnp.maximum(start - base, OWN), jnp.minimum(place - base, WIN - OWN - 1), WIN
                )
                grad_masked = grad_inputs[k * EXT : (k + 1) * EXT]
                grad_score = jnp.where(mine, grad_masked * scale, 0.0).astype(BF16)
                dq_sum[pl.ds(row0, EXT), cols] += dot_nn(grad_score, keys)
                dk_sum[pl.ds(at, WIN), cols] += dot_tn(grad_score, query)
                raw = dot_nt(query, keys)
                inputs[k * EXT : (k + 1) * EXT, :] = jnp.where(mine, raw * scale, 0.0).astype(BF16)
            tap_sum[s] += dot_tn(inputs[0 : n * EXT, :], taps[0 : n * EXT, :])

    for n in range(1, most + 1):
        pl.when(count_ref[block] == n)(functools.partial(body, n))

    @pl.when(block == pl.num_programs(1) - 1)
    def _():
        inner = None
        sums = ((dq_sum, HALO, q_ref), (dk_sum, TOP, k_ref), (dv_sum, TOP, v_ref))
        for c, (total, top, given) in enumerate(sums):
            grad = total[top : top + length, :].astype(BF16)
            kept[pair, c] = grad
            part = jnp.sum(grad.astype(F32) * given[...].astype(F32), axis=-1, keepdims=True)
            inner = part if inner is None else inner + part

        @pl.when(pair == 0)
        def _():
            inner_sum[...] = inner

        @pl.when(pair > 0)
        def _():
            inner_sum[...] += inner

        row = lax.broadcasted_iota(jnp.int32, (WIN, WIN), 0)
        lane = lax.broadcasted_iota(jnp.int32, (WIN, WIN), 1)
        for s in range(2):
            for a in range(n_taps):
                whole = tap_sum[s, :, a * WIN : (a + 1) * WIN]
                for b in range(2 * key_half + 1):
                    part = jnp.where(lane - row == b - key_half, whole, 0.0)
                    part = jnp.sum(part, axis=0, keepdims=True)
                    part = jnp.sum(part, axis=1, keepdims=True)
                    at = a * (2 * key_half + 1) + b
                    tap_ref[s, at : at + 1, :] = jnp.broadcast_to(part, (1, PAD_DIM))

    pairs = kept.shape[0]

    @pl.when((block == pl.num_programs(1) - 1) & (pair == pairs - 1))
    def _():
        width = 2 * pairs * HEAD_DIM

        def rows_out(n, carry):
            at = pl.ds(pl.multiple_of(n * ROWS, ROWS), ROWS)
            for c in range(3):
                heads = [
                    kept[p, c, at, s * PAD_DIM : s * PAD_DIM + HEAD_DIM]
                    for p in range(pairs)
                    for s in range(2)
                ]
                dqkv_ref[at, c * width : (c + 1) * width] = jnp.concatenate(heads, axis=1)
            column = jnp.broadcast_to(inner_sum[at, :], (ROWS, PAD_DIM))
            inner_ref[pl.ds(n, 1), :] = column.T[0:1, :]
            return carry

        lax.fori_loop(0, length // ROWS, rows_out, 0)


def attend_backward(proj, start, counts, base, mix, gain, probs, heads_out, grad_grouped):
    length = proj.shape[0]
    heads, n_taps = base.shape[:2]
    pairs = heads // 2
    blocks = length // ROWS
    key_half = 5
    most = windows_most(key_half)
    two = 2 * PAD_DIM
    tap_rows = n_taps * (2 * key_half + 1)
    grid_spec = pltpu.PrefetchScalarGridSpec(
        num_scalar_prefetch=2,
        grid=(pairs, blocks),
        in_specs=[
            pl.BlockSpec((length, two), lambda p, b, *_: (0, p)),
            pl.BlockSpec((length, two), lambda p, b, *_: (0, pairs + p)),
            pl.BlockSpec((length, two), lambda p, b, *_: (0, 2 * pairs + p)),
            pl.BlockSpec((HALO + length, 1), lambda p, b, *_: (0, 0)),
            pl.BlockSpec((2, n_taps, WIN), lambda p, b, *_: (p, 0, 0)),
            pl.BlockSpec((1, two), lambda p, b, *_: (0, p)),
            pl.BlockSpec((2, 1, most, ROWS, WIN), lambda p, b, *_: (p, b, 0, 0, 0)),
            pl.BlockSpec((ROWS, two), lambda p, b, *_: (b, p)),
            pl.BlockSpec((ROWS, two), lambda p, b, *_: (b, p)),
        ],
        out_specs=[
            pl.BlockSpec((length, 3 * heads * HEAD_DIM), lambda p, b, *_: (0, 0)),
            pl.BlockSpec((length // ROWS, ROWS), lambda p, b, *_: (0, 0)),
            pl.BlockSpec((1, two), lambda p, b, *_: (0, p)),
            pl.BlockSpec((2, tap_rows, PAD_DIM), lambda p, b, *_: (p, 0, 0)),
            pl.BlockSpec((1, 4, PAD_DIM), lambda p, b, *_: (p, 0, 0)),
        ],
        scratch_shapes=[
            pltpu.VMEM((HALO + length, two), BF16),
            pltpu.VMEM((TOP + length + HALO, two), BF16),
            pltpu.VMEM((TOP + length + HALO, two), BF16),
            pltpu.VMEM((HALO + length, two), F32),
            pltpu.VMEM((TOP + length + HALO, two), F32),
            pltpu.VMEM((TOP + length + HALO, two), F32),
            pltpu.VMEM((most * EXT, n_taps * WIN), BF16),
            pltpu.VMEM((most * EXT, WIN), BF16),
            pltpu.VMEM((2, WIN, n_taps * WIN), F32),
            pltpu.VMEM((2, most, ROWS, WIN), F32),
            pltpu.VMEM((2, n_taps * WIN, WIN), BF16),
            pltpu.VMEM((pairs, 3, length, two), BF16),
            pltpu.VMEM((length, 1), F32),
        ],
    )
    return pl.pallas_call(
        functools.partial(backward_kernel, n_taps, key_half, most),
        grid_spec=grid_spec,
        out_shape=[
            jax.ShapeDtypeStruct((length, 3 * heads * HEAD_DIM), BF16),
            jax.ShapeDtypeStruct((length // ROWS, ROWS), F32),
            jax.ShapeDtypeStruct((1, heads * PAD_DIM), F32),
            jax.ShapeDtypeStruct((heads, tap_rows, PAD_DIM), F32),
            jax.ShapeDtypeStruct((pairs, 4, PAD_DIM), F32),
        ],
        compiler_params=pltpu.CompilerParams(vmem_limit_bytes=56 << 20),
        cost_estimate=COST,
        name="attend_backward",
    )(counts, mix, proj, proj, proj, start, base, gain, probs, heads_out, grad_grouped)


MESH_ID = pl.DeviceIdType.MESH


def ring_place(member, n):
    z, y = member // 2, member % 2
    return (1 - y) * z + y * (n - 1 - z)


def ring_member(place, n):
    upper = place // (n // 2)
    return (1 - upper) * 2 * place + upper * (2 * (n - 1 - place) + 1)


def ring_peers(n):
    place = ring_place(lax.axis_index("dp"), n)
    ahead = ring_member(lax.rem(place + 1, n), n)
    behind = ring_member(lax.rem(place + n - 1, n), n)
    return place, (ahead, behind)


def ring_scratch(arrays, n):
    return [pltpu.VMEM((2, n - 1) + a.shape[2:], a.dtype) for a in arrays] + [
        pltpu.SemaphoreType.DMA((2, len(arrays), n - 1))
    ] * 4


def ring_split(array, n):
    return array.reshape(n, 2, -1, array.shape[-1])


def make_ring(n, sources, ins, outs, scratch):
    count = len(ins)
    slots = scratch[:count]
    rs_send, rs_recv, ag_send, ag_recv = scratch[count:]
    place, to = ring_peers(n)

    def chunk(way, back):
        return lax.rem(place - back + 2 * n if way == 0 else place + back, n)

    def sum_copy(way, k, s, src):
        return pltpu.make_async_remote_copy(
            src_ref=src,
            dst_ref=slots[k].at[way, s],
            send_sem=rs_send.at[way, k, s],
            recv_sem=rs_recv.at[way, k, s],
            device_id={"dp": to[way]},
            device_id_type=MESH_ID,
        )

    def share_copy(way, k, s, c):
        return pltpu.make_async_remote_copy(
            src_ref=outs[k].at[c, way],
            dst_ref=outs[k].at[c, way],
            send_sem=ag_send.at[way, k, s],
            recv_sem=ag_recv.at[way, k, s],
            device_id={"dp": to[way]},
            device_id_type=MESH_ID,
        )

    def add(way, k, s, c, dst):
        total = slots[k][way, s].astype(F32) + ins[k][c, way].astype(F32)
        dst[...] = total.astype(dst.dtype)

    both = [(k, way) for k in range(count) for way in range(2)]

    def start():
        for k, way in both:
            sum_copy(way, k, 0, sources[k].at[chunk(way, 1), way]).start()

    def tick(now):
        @pl.when(now < n - 2)
        def _():
            for k, way in both:
                sum_copy(way, k, now, slots[k].at[way, now]).wait_recv()
                add(way, k, now, chunk(way, 2 + now), slots[k].at[way, now])
                sum_copy(way, k, now + 1, slots[k].at[way, now]).start()

        @pl.when(now == n - 2)
        def _():
            for k, way in both:
                sum_copy(way, k, n - 2, slots[k].at[way, n - 2]).wait_recv()
                add(way, k, n - 2, place, outs[k].at[place, way])
                share_copy(way, k, 0, place).start()

        @pl.when((now > n - 2) & (now < 2 * n - 3))
        def _():
            step = now - (n - 1)
            for k, way in both:
                share_copy(way, k, step, chunk(way, step + 1)).wait_recv()
                share_copy(way, k, step + 1, chunk(way, step + 1)).start()

        @pl.when(now == 2 * n - 3)
        def _():
            for k, way in both:
                share_copy(way, k, n - 2, chunk(way, n - 1)).wait_recv()

    def drain():
        def one(s, carry):
            for k, way in both:
                sum_copy(way, k, s, slots[k].at[way, s]).wait_send()
                share_copy(way, k, s, place).wait_send()
            return carry

        lax.fori_loop(0, n - 1, one, 0)

    return start, tick, drain


def small_rows(size):
    return -(-size // PAD_DIM)


def pack_small(arrays, rows):
    packed = []
    for a in arrays:
        flat = a.reshape(-1)
        packed.append(jnp.pad(flat, (0, -flat.size % PAD_DIM)).reshape(-1, PAD_DIM))
    packed = jnp.concatenate(packed, axis=0)
    return jnp.pad(packed, ((0, rows - packed.shape[0]), (0, 0)))


def unpack_small(packed, arrays):
    found, at = [], 0
    for a in arrays:
        rows = small_rows(a.size)
        found.append(packed[at : at + rows].reshape(-1)[: a.size].reshape(a.shape))
        at += rows
    return found


CHUNK = 128
GROUP = 256


LIVE = 4


def exchange_scratch(steps, width, ranks, share=True, chunk=CHUNK):
    half = ranks // 2
    live = steps if share else LIVE
    shared = [pltpu.VMEM((steps, ranks, chunk, width), BF16)] if share else []
    return [
        pltpu.VMEM((steps, half, chunk, width), BF16),
        pltpu.VMEM((steps, half, chunk, width), BF16),
        pltpu.VMEM((live, half, chunk, width), F32),
        pltpu.VMEM((steps, chunk, width), BF16),
        pltpu.VMEM((steps, chunk, width), BF16),
        pltpu.SemaphoreType.DMA((5, steps)),
        pltpu.SemaphoreType.DMA((5, steps)),
    ] + shared


def tensor_peers():
    me = lax.axis_index("tensor")
    return me, me + 1 - 2 * lax.rem(me, 2), lax.rem(me + 2, 4)


def meet(signals):
    barrier = pltpu.get_barrier_semaphore()
    for device in signals:
        pl.semaphore_signal(barrier, inc=1, device_id=device, device_id_type=MESH_ID)
    pl.semaphore_wait(barrier, len(signals))


def exchange_copies(scratch):
    out_a, in_a, _, out_b, in_b, send, recv, *full = scratch
    me, near, far = tensor_peers()

    def copy(kind, step, src, dst, peer):
        return pltpu.make_async_remote_copy(
            src_ref=src,
            dst_ref=dst,
            send_sem=send.at[kind, step],
            recv_sem=recv.at[kind, step],
            device_id={"tensor": peer},
            device_id_type=MESH_ID,
        )

    def cores(step):
        return copy(0, step, out_a.at[step], in_a.at[step], near)

    def chips(step):
        return copy(1, step, out_b.at[step], in_b.at[step], far)

    def back_far(step):
        return copy(2, step, full[0].at[step, me], full[0].at[step, me], far)

    def back_near(step):
        return copy(3, step, full[0].at[step, me], full[0].at[step, me], near)

    def pass_near(step):
        return copy(4, step, full[0].at[step, far], full[0].at[step, far], near)

    return cores, chips, back_far, back_near, pass_near


def exchange_stages(scratch, partial, live, chunk):
    out_a, in_a, kept, out_b, in_b = scratch[:5]
    cores, chips = exchange_copies(scratch)[:2]
    many = GROUP // chunk
    me, near, far = tensor_peers()

    def begin(step):
        for n, owner in ((0, near), (1, lax.rem(near + 2, 4))):

            def put(term, n=n):
                term = term.astype(BF16)
                for m in range(many):
                    out_a[step + m, n] = term[m * chunk : (m + 1) * chunk]

            partial(step, owner, put)
        for m in range(many):
            cores(step + m).start()
        for n, owner in ((1, far), (0, me)):

            def put(term, n=n):
                for m in range(many):
                    kept[lax.rem(step + m, live), n] = term[m * chunk : (m + 1) * chunk]

            partial(step, owner, put)

    def over(step):
        cores(step).wait_recv()
        out_b[step] = (kept[lax.rem(step, live), 1] + in_a[step, 1].astype(F32)).astype(BF16)
        chips(step).start()

    def total(step):
        chips(step).wait_recv()
        return kept[lax.rem(step, live), 0] + in_a[step, 0].astype(F32) + in_b[step].astype(F32)

    return begin, over, total


def make_exchange(steps, scratch, partial, local, between, chunk):
    cores, chips = exchange_copies(scratch)[:2]
    begin, over, total = exchange_stages(scratch, partial, LIVE, chunk)
    many = GROUP // chunk

    def tick(now):
        @pl.when((lax.rem(now, many) == 0) & (now < steps))
        def _():
            begin(now)

        between(now)

        @pl.when((now >= 1) & (now < steps + 1))
        def _():
            over(now - 1)

        @pl.when((now >= 2) & (now < steps + 2))
        def _():
            local(now - 2, total(now - 2))

    def drain():
        def one(step, carry):
            cores(step).wait_send()
            chips(step).wait_send()
            return carry

        lax.fori_loop(0, steps, one, 0)

    return tick, steps + 2, drain


def run_exchange(steps, scratch, partial, local, whole, beside=None, ahead=None):
    cores, chips, back_far, back_near, pass_near = exchange_copies(scratch)
    begin, over, total = exchange_stages(scratch, partial, steps, CHUNK)
    full = scratch[7]
    many = GROUP // CHUNK
    me = tensor_peers()[0]

    def send_group(group, carry):
        @pl.when(group < steps // many)
        def _():
            begin(group * many)

        @pl.when(group >= 1)
        def _():
            for m in range(many):
                over((group - 1) * many + m)

        return carry

    lax.fori_loop(0, steps // many + 1, send_group, 0)

    def sum_group(group, carry):
        if beside is not None:
            beside(group)
        for m in range(many):
            step = group * many + m
            full[step, me] = local(step, total(step)).astype(BF16)
            back_far(step).start()
            back_near(step).start()
        return carry

    lax.fori_loop(0, steps // many, sum_group, 0)
    if ahead is not None:
        ahead()

    def share_step(now, carry):
        @pl.when(now < steps)
        def _():
            back_far(now).wait_recv()
            pass_near(now).start()

        @pl.when(now >= 1)
        def _():
            back_near(now - 1).wait_recv()
            pass_near(now - 1).wait_recv()
            whole(now - 1, full)

        return carry

    lax.fori_loop(0, steps + 1, share_step, 0)

    def drain(step, carry):
        for copy in (cores, chips, back_far, back_near, pass_near):
            copy(step).wait_send()
        return carry

    lax.fori_loop(0, steps, drain, 0)


def run_ticks(count, *ticks):
    def one(now, carry):
        for tick in ticks:
            tick(now)
        return carry

    lax.fori_loop(0, count, one, 0)


def group_rows(step, chunk=CHUNK):
    return pl.ds(pl.multiple_of(step * chunk, chunk), GROUP)


def owner_cols(owner, width):
    return pl.ds(pl.multiple_of(owner * width, PAD_DIM), width)


def step_rows(step, chunk=CHUNK):
    return pl.ds(pl.multiple_of(step * chunk, chunk), chunk)


def first_entry_kernel(
    tokens_ref, w_ref, gains_ref, proj_ref, normed_ref, factor_ref, gains_all_ref, full, gains_in,
    send, recv, gains_send, gains_recv,
):
    rows, width = tokens_ref.shape
    ranks = normed_ref.shape[1] // width
    heads = width // HEAD_DIM
    steps, many = rows // CHUNK, GROUP // CHUNK
    me, near, far = tensor_peers()
    across = lax.rem(near + 2, 4)
    meet([{"tensor": near}, {"tensor": far}, {"tensor": across}])

    def copy(kind, step, src, dst, peer):
        return pltpu.make_async_remote_copy(
            src_ref=src,
            dst_ref=dst,
            send_sem=send.at[kind, step],
            recv_sem=recv.at[kind, step],
            device_id={"tensor": peer},
            device_id_type=MESH_ID,
        )

    def to_far(step):
        return copy(0, step, tokens_ref.at[step_rows(step)], full.at[step, me], far)

    def to_near(step):
        return copy(1, step, tokens_ref.at[step_rows(step)], full.at[step, me], near)

    def pass_near(step):
        return copy(2, step, full.at[step, far], full.at[step, far], near)

    def gains_copy(kind, peer, sender):
        return pltpu.make_async_remote_copy(
            src_ref=gains_ref,
            dst_ref=gains_in.at[sender],
            send_sem=gains_send.at[kind],
            recv_sem=gains_recv.at[sender],
            device_id={"tensor": peer},
            device_id_type=MESH_ID,
        )

    peers = (near, far, across)
    for kind, peer in enumerate(peers):
        gains_copy(kind, peer, me).start()

    def send_all(step, carry):
        to_far(step).start()
        to_near(step).start()
        full[step, me] = tokens_ref[step_rows(step), :]
        return carry

    lax.fori_loop(0, steps, send_all, 0)
    gains_in[me] = gains_ref[...]
    for kind, peer in enumerate(peers):
        gains_copy(kind, peer, peer).wait()
    for n in range(ranks):
        gains_all_ref[:, n * width : (n + 1) * width] = gains_in[n]

    def tick(now):
        @pl.when(now < steps)
        def _():
            to_far(now).wait_recv()
            pass_near(now).start()

        @pl.when(now >= 1)
        def _():
            to_near(now - 1).wait_recv()
            pass_near(now - 1).wait_recv()

        @pl.when((now >= many) & (lax.rem(now, many) == 0))
        def _():
            first = now - many
            at = group_rows(first)
            blocks = [
                jnp.concatenate([full[first + m, n] for m in range(many)], axis=0).astype(F32)
                for n in range(ranks)
            ]
            squares = sum(jnp.sum(block * block, axis=-1, keepdims=True) for block in blocks)
            factor = lax.rsqrt(squares * (1.0 / (ranks * width)) + EPS)
            factor_ref[at, :] = factor
            for n, block in enumerate(blocks):
                cols = slice(n * width, (n + 1) * width)
                normed_ref[at, cols] = (block * factor * gains_all_ref[0:1, cols]).astype(BF16)
            for c in range(3):
                out = dot_nn(normed_ref[at, :], w_ref[c])
                empty = jnp.zeros((GROUP, PAD_DIM - HEAD_DIM), F32)
                for h in range(heads):
                    head = jnp.concatenate([out[:, h * HEAD_DIM : (h + 1) * HEAD_DIM], empty], axis=1)
                    lane = (c * heads + h) * PAD_DIM
                    proj_ref[at, lane : lane + PAD_DIM] = head.astype(BF16)

    run_ticks(steps + 1, tick)

    def drain(step, carry):
        to_far(step).wait_send()
        to_near(step).wait_send()
        pass_near(step).wait_send()
        return carry

    lax.fori_loop(0, steps, drain, 0)


def first_entry(tokens, w_qkv, gains):
    rows, width = tokens.shape
    full_width = w_qkv.shape[1]
    ranks = full_width // width
    steps = rows // CHUNK
    vmem = pl.BlockSpec(memory_space=pltpu.VMEM)
    return pl.pallas_call(
        first_entry_kernel,
        out_shape=[
            jax.ShapeDtypeStruct((rows, 3 * width // HEAD_DIM * PAD_DIM), BF16),
            jax.ShapeDtypeStruct((rows, full_width), BF16),
            jax.ShapeDtypeStruct((rows, 1), F32),
            jax.ShapeDtypeStruct((8, full_width), F32),
        ],
        in_specs=[vmem] * 3,
        out_specs=[vmem] * 4,
        scratch_shapes=[
            pltpu.VMEM((steps, ranks, CHUNK, width), BF16),
            pltpu.VMEM((ranks, 8, width), F32),
            pltpu.SemaphoreType.DMA((3, steps)),
            pltpu.SemaphoreType.DMA((3, steps)),
            pltpu.SemaphoreType.DMA((3,)),
            pltpu.SemaphoreType.DMA((ranks,)),
        ],
        compiler_params=pltpu.CompilerParams(
            collective_id=4, has_side_effects=True, vmem_limit_bytes=40 << 20
        ),
        cost_estimate=COST,
        name="first_entry",
    )(tokens, w_qkv, gains)


def attn_exit_kernel(
    grouped_ref, w_out_ref, tokens_ref, gain_ref, cot_in, w_gate_up_in, w_down_in, hidden_local_ref,
    hidden_out, normed_out, w_ref, act_out, grad_gate_out, grad_up_out, hidden_ref, normed_ref, act_ref,
    grad_gate_ref, grad_up_ref, grad_act, cot_ref, w_gate_up_ref, w_down_ref, load, store, *scratch
):
    loads = [
        pltpu.make_async_copy(src, dst, load.at[n])
        for n, (src, dst) in enumerate(
            ((cot_in, cot_ref), (w_down_in, w_down_ref), (w_gate_up_in, w_gate_up_ref))
        )
    ]
    for one in loads:
        one.start()
    rows, width = tokens_ref.shape
    ranks = hidden_ref.shape[1] // width
    many = GROUP // CHUNK
    for h in range(width // HEAD_DIM):
        lead = h * PAD_DIM
        w_ref[lead : lead + HEAD_DIM, :] = w_out_ref[h * HEAD_DIM : (h + 1) * HEAD_DIM, :]
        w_ref[lead + HEAD_DIM : lead + PAD_DIM, :] = jnp.zeros((PAD_DIM - HEAD_DIM, w_ref.shape[1]), BF16)

    def partial(step, owner, put):
        put(dot_nn(grouped_ref[group_rows(step), :], w_ref[:, owner_cols(owner, width)]))

    def local(step, total):
        hidden = tokens_ref[step_rows(step), :].astype(F32) + total
        hidden_local_ref[step_rows(step), :] = hidden
        return hidden

    def whole(step, full):
        squares = None
        for n in range(ranks):
            block = full[step, n]
            hidden_ref[step_rows(step), n * width : (n + 1) * width] = block
            block = block.astype(F32)
            part = jnp.sum(block * block, axis=-1, keepdims=True)
            squares = part if squares is None else squares + part
        factor = lax.rsqrt(squares * (1.0 / (ranks * width)) + EPS)
        for n in range(ranks):
            cols = slice(n * width, (n + 1) * width)
            unit = full[step, n].astype(F32) * factor
            normed_ref[step_rows(step), cols] = (unit * gain_ref[:, cols]).astype(BF16)

        @pl.when(lax.rem(step, many) == many - 1)
        def _():
            at = group_rows(step - (many - 1))
            gate = dot_nn(normed_ref[at, :], w_gate_up_ref[0])
            up = dot_nn(normed_ref[at, :], w_gate_up_ref[1])
            sigmoid = jax.nn.sigmoid(gate)
            swish = gate * sigmoid
            grad = grad_act[at, :]
            act_ref[at, :] = (swish * up).astype(BF16)
            grad_gate_ref[at, :] = (grad * up * sigmoid * (1.0 + gate * (1.0 - sigmoid))).astype(BF16)
            grad_up_ref[at, :] = (grad * swish).astype(BF16)
            for one in stores(step // many):
                one.start()

    def stores(group):
        at = group_rows(group * many)
        pairs = (
            (hidden_ref, hidden_out),
            (normed_ref, normed_out),
            (act_ref, act_out),
            (grad_gate_ref, grad_gate_out),
            (grad_up_ref, grad_up_out),
        )
        return [
            pltpu.make_async_copy(src.at[at], dst.at[at], store.at[n, group])
            for n, (src, dst) in enumerate(pairs)
        ]

    def beside(group):
        @pl.when(group == 0)
        def _():
            loads[0].wait()
            loads[1].wait()

        at = group_rows(group * many)
        grad_act[at, :] = dot_nt(cot_ref[at, :], w_down_ref[...])

    me, near, far = tensor_peers()
    meet([{"tensor": near}, {"tensor": far}])
    run_exchange(rows // CHUNK, scratch, partial, local, whole, beside, loads[2].wait)

    def stored(group, carry):
        for one in stores(group):
            one.wait()
        return carry

    lax.fori_loop(0, rows // GROUP, stored, 0)


def attn_exit(grouped, w_out, tokens, gain, full_cot, w_gate_up, w_down):
    rows, width = tokens.shape
    full_width = w_out.shape[1]
    units = w_down.shape[0]
    vmem = pl.BlockSpec(memory_space=pltpu.VMEM)
    anywhere = pl.BlockSpec(memory_space=pl.ANY)
    return pl.pallas_call(
        attn_exit_kernel,
        out_shape=[
            jax.ShapeDtypeStruct((rows, width), F32),
            jax.ShapeDtypeStruct((rows, full_width), BF16),
            jax.ShapeDtypeStruct((rows, full_width), BF16),
            jax.ShapeDtypeStruct((grouped.shape[1], full_width), BF16),
        ]
        + [jax.ShapeDtypeStruct((rows, units), BF16)] * 3,
        in_specs=[vmem] * 4 + [anywhere] * 3,
        out_specs=[vmem, anywhere, anywhere, vmem] + [anywhere] * 3,
        scratch_shapes=[pltpu.VMEM((rows, full_width), BF16)] * 2
        + [pltpu.VMEM((rows, units), BF16)] * 3
        + [
            pltpu.VMEM((rows, units), F32),
            pltpu.VMEM(full_cot.shape, BF16),
            pltpu.VMEM(w_gate_up.shape, BF16),
            pltpu.VMEM(w_down.shape, BF16),
            pltpu.SemaphoreType.DMA((3,)),
            pltpu.SemaphoreType.DMA((5, rows // GROUP)),
        ]
        + exchange_scratch(rows // CHUNK, width, full_width // width),
        compiler_params=pltpu.CompilerParams(
            collective_id=1, has_side_effects=True, vmem_limit_bytes=56 << 20
        ),
        cost_estimate=COST,
        name="attn_exit",
    )(grouped, w_out, tokens, gain, full_cot, w_gate_up, w_down)


def mlp_exit_kernel(
    gate_ref, up_ref, w_ref, hidden_in, cot_in, hidden_local_ref, cot_local_ref, gain_ref, gain_local_ref,
    grad_attn_ref, grad_hidden_ref, gain_grad_ref, grad_local, hidden_ref, cot_ref, load, *scratch
):
    loads = [
        pltpu.make_async_copy(hidden_in, hidden_ref, load.at[0]),
        pltpu.make_async_copy(cot_in, cot_ref, load.at[1]),
    ]
    for one in loads:
        one.start()
    rows, width = cot_local_ref.shape
    full_width = hidden_ref.shape[1]
    ranks = full_width // width
    gain_grad_ref[...] = jnp.zeros_like(gain_grad_ref)

    def partial(step, owner, put):
        cols = owner_cols(owner, width)
        at = group_rows(step)
        put(dot_nt(gate_ref[at, :], w_ref[0, cols, :]) + dot_nt(up_ref[at, :], w_ref[1, cols, :]))

    def local(step, total):
        grad_local[step_rows(step), :] = total
        return total

    def whole(step, full):
        at = step_rows(step)
        squares, inner = None, None
        for n in range(ranks):
            cols = slice(n * width, (n + 1) * width)
            hidden = hidden_ref[at, cols].astype(F32)
            part = jnp.sum(hidden * hidden, axis=-1, keepdims=True)
            squares = part if squares is None else squares + part
            part = jnp.sum(full[step, n].astype(F32) * gain_ref[:, cols] * hidden, axis=-1, keepdims=True)
            inner = part if inner is None else inner + part
        factor = lax.rsqrt(squares * (1.0 / full_width) + EPS)
        inner = inner * factor * (1.0 / full_width)
        for n in range(ranks):
            cols = slice(n * width, (n + 1) * width)
            unit = hidden_ref[at, cols].astype(F32) * factor
            grad = full[step, n].astype(F32) * gain_ref[:, cols] - unit * inner
            grad_attn_ref[at, cols] = (cot_ref[at, cols].astype(F32) + factor * grad).astype(BF16)
        total = grad_local[at, :]
        unit = hidden_local_ref[at, :] * factor
        gain_grad_ref[...] += jnp.sum(total * unit, axis=0, keepdims=True)
        grad_hidden_ref[at, :] = cot_local_ref[at, :].astype(F32) + factor * (
            total * gain_local_ref[...] - unit * inner
        )

    me, near, far = tensor_peers()
    meet([{"tensor": near}, {"tensor": far}])

    def ahead():
        for one in loads:
            one.wait()

    run_exchange(rows // CHUNK, scratch, partial, local, whole, ahead=ahead)


def mlp_exit(grad_gate, grad_up, w_gate_up, hidden, full_cot, hidden_local, cotangent, gain, gain_local):
    rows, width = hidden_local.shape
    full_width = hidden.shape[1]
    vmem = pl.BlockSpec(memory_space=pltpu.VMEM)
    return pl.pallas_call(
        mlp_exit_kernel,
        out_shape=[
            jax.ShapeDtypeStruct((rows, full_width), BF16),
            jax.ShapeDtypeStruct((rows, width), F32),
            jax.ShapeDtypeStruct((1, width), F32),
        ],
        in_specs=[vmem] * 3 + [pl.BlockSpec(memory_space=pl.ANY)] * 2 + [vmem] * 4,
        out_specs=[vmem] * 3,
        scratch_shapes=[
            pltpu.VMEM((rows, width), F32),
            pltpu.VMEM(hidden.shape, BF16),
            pltpu.VMEM(full_cot.shape, BF16),
            pltpu.SemaphoreType.DMA((2,)),
        ]
        + exchange_scratch(rows // CHUNK, width, full_width // width),
        compiler_params=pltpu.CompilerParams(
            collective_id=2, has_side_effects=True, vmem_limit_bytes=56 << 20
        ),
        cost_estimate=COST,
        name="mlp_exit",
    )(grad_gate, grad_up, w_gate_up, hidden, full_cot, hidden_local, cotangent, gain, gain_local)


def last_exit_kernel(
    n_ring, count, factor_ref, inner_ref, gain_ref, small_ref, *refs,
):
    given, sources, refs = refs[:7], refs[7 : 7 + count], refs[7 + count :]
    tokens_grad_ref, out_ref, small_sum_ref = refs[:3]
    outs, refs = refs[3 : 3 + count], refs[3 + count :]
    here_too, ins, load, refs = refs[:7], refs[7 : 7 + count], refs[7 + count], refs[8 + count :]
    grad_ref, w_ref, tokens_ref, grad_hidden_ref, act_ref, w_down_ref, hidden_ref = here_too
    loads = [
        pltpu.make_async_copy(src, dst, load.at[n])
        for n, (src, dst) in enumerate(zip((*sources, *given), (*ins, *here_too)))
    ]
    for one in loads:
        one.start()
    gain_grad, mine, all_small, small_send, small_recv = refs[:5]
    inner_in, inner_sum, inner_col, inner_send, inner_recv = refs[5:10]
    ring_refs, scratch = refs[10 : 14 + count], refs[14 + count :]
    rows, width = tokens_ref.shape
    full_width = w_ref.shape[1]
    half = rows // GROUP
    me, near, far = tensor_peers()
    here = lax.axis_index("dp")
    gain_grad[...] = jnp.zeros_like(gain_grad)

    def partial(step, owner, put):
        cols = owner_cols(owner, width)

        @pl.when(step < half)
        def _():
            total = None
            for c in range(3):
                term = dot_nt(grad_ref[group_rows(step, GROUP), c * width : (c + 1) * width], w_ref[c, cols, :])
                total = term if total is None else total + term
            put(total)

        @pl.when(step >= half)
        def _():
            put(dot_nn(act_ref[group_rows(step - half, GROUP), :], w_down_ref[:, cols]))

    def between(now):
        def copy(n, src, peer):
            return pltpu.make_async_remote_copy(
                src_ref=src,
                dst_ref=inner_in.at[n],
                send_sem=inner_send.at[n],
                recv_sem=inner_recv.at[n],
                device_id={"tensor": peer},
                device_id_type=MESH_ID,
            )

        @pl.when(now == 0)
        def _():
            copy(0, inner_ref, near).start()

        @pl.when(now == 1)
        def _():
            copy(0, inner_ref, near).wait()
            inner_sum[...] = inner_ref[...] + inner_in[0]
            copy(1, inner_sum, far).start()

        @pl.when(now == 2)
        def _():
            copy(1, inner_sum, far).wait()
            total = (inner_sum[...] + inner_in[1]) * (1.0 / full_width)
            for n in range(rows // ROWS):
                line = jnp.broadcast_to(total[n : n + 1, :], (ROWS, ROWS))
                inner_col[n * ROWS : (n + 1) * ROWS, :] = line.T[:, 0:1]

    def local(step, total):
        @pl.when(step < half)
        def _():
            at = step_rows(step, GROUP)
            factor = factor_ref[at, :]
            unit = tokens_ref[at, :].astype(F32) * factor
            gain_grad[...] += jnp.sum(total * unit, axis=0, keepdims=True)
            tokens_grad_ref[at, :] = grad_hidden_ref[at, :] + factor * (
                total * gain_ref[...] - unit * inner_col[at, :]
            )

        @pl.when(step >= half)
        def _():
            at = step_rows(step - half, GROUP)
            out_ref[at, :] = (hidden_ref[at, :] + total).astype(BF16)

    def small_copy(peer, sender):
        return pltpu.make_async_remote_copy(
            src_ref=mine,
            dst_ref=all_small.at[sender],
            send_sem=small_send.at[peer],
            recv_sem=small_recv.at[sender],
            device_id={"dp": peer},
            device_id_type=MESH_ID,
        )

    def small_start(now):
        @pl.when(now == half + 2)
        def _():
            mine[...] = small_ref[...]
            for n in range(width // PAD_DIM):
                mine[n : n + 1, :] = gain_grad[:, n * PAD_DIM : (n + 1) * PAD_DIM]
            all_small[here] = mine[...]

            def one(away, carry):
                small_copy(lax.rem(here + away, n_ring), here).start()
                return carry

            lax.fori_loop(1, n_ring, one, 0)

    barrier = pltpu.get_barrier_semaphore()
    for peer in (near, far):
        pl.semaphore_signal(barrier, inc=1, device_id={"tensor": peer}, device_id_type=MESH_ID)

    def greet(away, carry):
        peer = lax.rem(here + away, n_ring)
        pl.semaphore_signal(barrier, inc=1, device_id={"dp": peer}, device_id_type=MESH_ID)
        return carry

    lax.fori_loop(1, n_ring, greet, 0)
    pl.semaphore_wait(barrier, 2 + n_ring - 1)

    ring_start, ring_tick, ring_drain = make_ring(n_ring, sources, ins, outs, ring_refs)
    tick, ticks, drain = make_exchange(2 * half, scratch, partial, local, between, GROUP)
    ring_start()
    for one in loads:
        one.wait()
    run_ticks(max(ticks, 2 * (n_ring - 1)), ring_tick, tick, small_start)

    def one(away, carry):
        peer = lax.rem(here + away, n_ring)
        small_copy(peer, peer).wait()
        return carry

    lax.fori_loop(1, n_ring, one, 0)

    def add(n, total):
        return total + all_small[n]

    small_sum_ref[...] = lax.fori_loop(1, n_ring, add, all_small[0])
    drain()
    ring_drain()


def last_exit(
    grad_proj, w_qkv, tokens, grad_hidden, factor, inner, gain, act, w_down, hidden_local, small, sums
):
    rows, width = tokens.shape
    n_ring = lax.axis_size("dp")
    count = len(sums)
    split = [ring_split(a, n_ring) for a in sums]
    gain_rows = width // PAD_DIM
    need = gain_rows + sum(small_rows(a.size) for a in small)
    packed = jnp.pad(pack_small(small, need - gain_rows), ((gain_rows, -need % 8), (0, 0)))
    vmem = pl.BlockSpec(memory_space=pltpu.VMEM)
    steps = 2 * rows // GROUP
    given = (grad_proj, w_qkv, tokens, grad_hidden, act, w_down, hidden_local)
    tokens_grad, out, packed, *totals = pl.pallas_call(
        functools.partial(last_exit_kernel, n_ring, count),
        out_shape=[
            jax.ShapeDtypeStruct((rows, width), F32),
            jax.ShapeDtypeStruct((rows, width), BF16),
            jax.ShapeDtypeStruct(packed.shape, F32),
        ]
        + [jax.ShapeDtypeStruct(a.shape, a.dtype) for a in split],
        in_specs=[vmem] * 4 + [pl.BlockSpec(memory_space=pl.ANY)] * (7 + count),
        out_specs=[vmem] * (3 + count),
        scratch_shapes=[pltpu.VMEM(a.shape, a.dtype) for a in (*given, *split)]
        + [
            pltpu.SemaphoreType.DMA((7 + count,)),
            pltpu.VMEM((1, width), F32),
            pltpu.VMEM(packed.shape, F32),
            pltpu.VMEM((n_ring,) + packed.shape, F32),
            pltpu.SemaphoreType.DMA((n_ring,)),
            pltpu.SemaphoreType.DMA((n_ring,)),
            pltpu.VMEM((2,) + inner.shape, F32),
            pltpu.VMEM(inner.shape, F32),
            pltpu.VMEM((rows, 1), F32),
            pltpu.SemaphoreType.DMA((2,)),
            pltpu.SemaphoreType.DMA((2,)),
        ]
        + ring_scratch(split, n_ring)
        + exchange_scratch(steps, width, w_qkv.shape[1] // width, False, GROUP),
        compiler_params=pltpu.CompilerParams(
            collective_id=3, has_side_effects=True, vmem_limit_bytes=62 << 20
        ),
        cost_estimate=COST,
        name="last_exit",
    )(factor, inner, gain, packed, *given, *split)
    gain_grad = packed[:gain_rows].reshape(width)
    totals = [t.reshape(a.shape) for t, a in zip(totals, sums)]
    return tokens_grad, gain_grad, out, unpack_small(packed[gain_rows:], small), totals


def banded(line):
    return pltpu.roll(jnp.broadcast_to(line, (WIN, WIN)), 0, 1, stride=1, stride_axis=0)


def band_lines(kernel):
    taps = kernel.shape[2]
    wide = jnp.pad(kernel, ((0, 0), (0, 0), (0, WIN - taps)))
    back = jnp.pad(kernel[:, :, ::-1], ((0, 0), (0, 0), (0, WIN - taps)))
    return jnp.roll(wide, -(taps // 2), axis=2), jnp.roll(back, -(taps // 2), axis=2)


def pad_heads(array, axis):
    shape = array.shape
    heads = shape[axis] // HEAD_DIM
    split = array.reshape(shape[:axis] + (heads, HEAD_DIM) + shape[axis + 1 :])
    widths = [(0, 0)] * split.ndim
    widths[axis + 1] = (0, PAD_DIM - HEAD_DIM)
    return jnp.pad(split, widths).reshape(shape[:axis] + (heads * PAD_DIM,) + shape[axis + 1 :])


def cut_heads(array, axis):
    shape = array.shape
    heads = shape[axis] // PAD_DIM
    split = array.reshape(shape[:axis] + (heads, PAD_DIM) + shape[axis + 1 :])
    cut = lax.slice_in_dim(split, 0, HEAD_DIM, axis=axis + 1)
    return cut.reshape(shape[:axis] + (heads * HEAD_DIM,) + shape[axis + 1 :])


def windows_needed(start, key_half):
    length = start.shape[0]
    first = start[::ROWS]
    row0 = jnp.arange(0, length, ROWS, dtype=jnp.int32)
    count = jnp.ones_like(first)
    for k in range(1, windows_most(key_half)):
        count = count + (first - key_half < row0 + ROWS - STEP * k).astype(jnp.int32)
    return count


def on_device(
    tokens, segments, attn_gain, w_qkv, kq_kernel, head_mix, group_gain, w_out, mlp_gain, w_gate_up,
    w_down, cotangent,
):
    rows_here, local_width = tokens.shape
    seq_count, length = segments.shape
    heads_here = local_width // HEAD_DIM
    n_taps, key_taps = kq_kernel.shape[1:]
    key_half = key_taps // 2

    lines, lines_back = band_lines(kq_kernel)
    gain_heads = pad_heads(group_gain.astype(F32), 0)[None]
    starts, counts = [], []
    for n in range(seq_count):
        seg = segments[n]
        start = jnp.sum((seg[None, :] < seg[:, None]).astype(jnp.int32), axis=1)
        counts.append(windows_needed(start, key_half))
        starts.append(jnp.pad(start, (HALO, 0), constant_values=1 << 20)[:, None])

    full_width = w_qkv.shape[1]
    own_gains = jnp.pad(jnp.stack([attn_gain, mlp_gain]).astype(F32), ((0, 6), (0, 0)))
    proj, normed_one, scale_one, gains = first_entry(tokens, w_qkv, own_gains)
    gain_two = gains[1:2]
    cot_here, proj = lax.optimization_barrier((cotangent, proj))
    full_cot = lax.all_gather(cot_here, "tensor", axis=1, tiled=True)

    kept = []
    for n in range(seq_count):
        rows = slice(n * length, (n + 1) * length)
        kept.append(
            attend_forward(proj[rows], starts[n], counts[n], lines, head_mix, gain_heads)
        )
    grouped = jnp.concatenate([one[2] for one in kept], axis=0)
    grouped, full_cot = lax.optimization_barrier((grouped, full_cot))
    hidden_local, hidden, normed_two, w_out_pad, act, grad_gate, grad_up = attn_exit(
        grouped, w_out, tokens, gain_two, full_cot, w_gate_up, w_down
    )

    grad_down = dot_tn(act, full_cot).astype(BF16)
    early_rows = int(full_width * EARLY_SHARE)
    early_up = dot_tn(normed_two[:, :early_rows], grad_up).astype(BF16)
    grad_gate, early_up, grad_down = lax.optimization_barrier((grad_gate, early_up, grad_down))
    early_up, grad_down = lax.psum((early_up, grad_down), "dp")
    grad_attn, grad_hidden_local, grad_gain_two = mlp_exit(
        grad_gate, grad_up, w_gate_up, hidden, full_cot, hidden_local, cotangent, gain_two,
        mlp_gain.astype(F32)[None],
    )
    grad_gate_w = dot_tn(normed_two, grad_gate).astype(BF16)
    late_up = dot_tn(normed_two[:, early_rows:], grad_up).astype(BF16)
    grad_w_out = cut_heads(dot_tn(grouped, grad_attn).astype(BF16), 0)

    grad_grouped = dot_nt(grad_attn, w_out_pad)
    parts = []
    for n in range(seq_count):
        rows = slice(n * length, (n + 1) * length)
        parts.append(
            attend_backward(
                proj[rows], starts[n], counts[n], lines_back, head_mix, gain_heads, kept[n][0], kept[n][1],
                grad_grouped[rows],
            )
        )
    grad_proj = jnp.concatenate([one[0] for one in parts], axis=0)
    inner_part = jnp.concatenate([one[1] for one in parts], axis=0)
    grad_group_gain = sum(cut_heads(one[2][0], 0) for one in parts)
    grad_kernel = sum(one[3][:, :, 0] for one in parts).reshape(heads_here, n_taps, key_taps)
    grad_mix = sum(one[4][:, :, 0] for one in parts).reshape(heads_here, 2)

    grad_qkv = [
        dot_tn(normed_one, grad_proj[:, c * local_width : (c + 1) * local_width]).astype(BF16)
        for c in range(3)
    ]
    tokens_grad, grad_gain_one, layer_out, small, sums = last_exit(
        grad_proj, w_qkv, tokens, grad_hidden_local, scale_one, inner_part, attn_gain.astype(F32)[None],
        act, w_down, hidden_local, (grad_kernel, grad_mix, grad_group_gain, grad_gain_two[0]),
        (grad_gate_w, late_up, grad_w_out, *grad_qkv),
    )
    grad_kernel, grad_mix, grad_group_gain, grad_gain_two = small
    grad_gate_w, late_up, grad_w_out, *grad_qkv = sums
    grad_gate_up = jnp.stack([grad_gate_w, jnp.concatenate([early_up, late_up], axis=0)])
    grad_qkv = jnp.stack(grad_qkv)
    return (
        layer_out,
        tokens_grad,
        grad_gain_one,
        grad_qkv.astype(F32),
        grad_kernel,
        grad_mix,
        grad_group_gain,
        grad_w_out.astype(F32),
        grad_gain_two,
        grad_gate_up.astype(F32),
        grad_down.astype(F32),
    )


def solution(mesh):
    in_specs = (
        P("dp", "tensor"),
        P("dp", None),
        P("tensor"),
        P(None, None, "tensor"),
        P("tensor", None, None),
        P("tensor", None),
        P("tensor"),
        P("tensor", None),
        P("tensor"),
        P(None, None, "tensor"),
        P("tensor", None),
        P("dp", "tensor"),
    )
    out_specs = (
        P("dp", "tensor"),
        P("dp", "tensor"),
        P("tensor"),
        P(None, None, "tensor"),
        P("tensor", None, None),
        P("tensor", None),
        P("tensor"),
        P("tensor", None),
        P("tensor"),
        P(None, None, "tensor"),
        P("tensor", None),
    )
    return jax.shard_map(
        on_device, mesh=mesh, in_specs=in_specs, out_specs=out_specs, check_vma=False
    )
```

```python
import functools

import jax
import jax.numpy as jnp
from jax import lax
from jax.experimental import pallas as pl
from jax.experimental.pallas import tpu as pltpu
from jax.sharding import PartitionSpec as P

HEAD_DIM = 96
PAD_DIM = 128
DOC_MOST = 512
EPS = 1e-05
NEG = -1e30

COST = pl.CostEstimate(flops=1 << 20, bytes_accessed=1 << 10, transcendentals=0)
EARLY_SHARE = 0.75
ROWS = 128
HALO = 16
WIN = 256
OWN = 16
STEP = WIN - 2 * OWN
TOP = 256
EXT = ROWS + HALO

F32 = jnp.float32
BF16 = jnp.bfloat16


def windows_most(key_half):
    return -(-(DOC_MOST - 1 + ROWS + key_half) // STEP)


def dot_nt(a, b):
    return lax.dot_general(a, b, (((1,), (1,)), ((), ())), preferred_element_type=F32)


def dot_tn(a, b):
    return lax.dot_general(a, b, (((0,), (0,)), ((), ())), preferred_element_type=F32)


def dot_nn(a, b):
    return jnp.dot(a, b, preferred_element_type=F32)


def fill_padded(dst, src, top, length):
    total = dst.shape[0]
    dst[0:top, :] = jnp.zeros((top, dst.shape[1]), dst.dtype)
    dst[top : top + length, :] = src[...]
    if total > top + length:
        dst[top + length : total, :] = jnp.zeros((total - top - length, dst.shape[1]), dst.dtype)


def lanes_between(first, last, width):
    lane = lax.broadcasted_iota(jnp.int32, (first.shape[0], width), 1)
    return (lane >= first) & (lane <= last)


def row_numbers(base, count):
    return base + lax.broadcasted_iota(jnp.int32, (count, 1), 0)


def forward_kernel(
    n_taps, key_half, most, count_ref, mix_ref, q_ref, k_ref, v_ref, start_ref, base_ref, gain_ref,
    probs_ref, heads_ref, grouped_ref, qs, ks, vs, logit_ref, band_ref, inputs,
):
    pair = pl.program_id(0)
    block = pl.program_id(1)
    length = q_ref.shape[0]
    scale = HEAD_DIM ** (-0.5)

    @pl.when(block == 0)
    def _():
        fill_padded(qs, q_ref, HALO, length)
        fill_padded(ks, k_ref, TOP, length)
        fill_padded(vs, v_ref, TOP, length)
        for s in range(2):
            for a in range(n_taps):
                band = banded(band_line(base_ref[s, a : a + 1, :], key_half, 1))
                high = band.astype(BF16)
                band_ref[s, a, 0:WIN] = high
                band_ref[s, a, WIN : 2 * WIN] = high
                band_ref[s, a, 2 * WIN : 3 * WIN] = (band - high.astype(F32)).astype(BF16)

    row0 = pl.multiple_of(block * ROWS, ROWS)

    def body(n):
        start = start_ref[pl.ds(row0, EXT), :]
        place = row_numbers(row0 - HALO, EXT)
        firsts, lasts = [], []
        for k in range(n):
            base = row0 + ROWS - STEP * (k + 1) - OWN
            at = pl.multiple_of(TOP + base, 16)
            firsts.append(start - base)
            lasts.append(place - base)
            valid = lanes_between(firsts[k], lasts[k], WIN)
            rows = slice(k * EXT, (k + 1) * EXT)
            for s in range(2):
                cols = pl.ds(s * PAD_DIM, PAD_DIM)
                raw = dot_nt(qs[pl.ds(row0, EXT), cols], ks[pl.ds(at, WIN), cols])
                masked = jnp.where(valid, raw * scale, 0.0)
                high = masked.astype(BF16)
                inputs[s, rows, 0:WIN] = high
                inputs[s, rows, WIN : 2 * WIN] = (masked - high.astype(F32)).astype(BF16)
                inputs[s, rows, 2 * WIN : 3 * WIN] = high
        peaks = [None, None]
        for s in range(2):
            total = None
            for a in reversed(range(n_taps)):
                term = dot_nn(inputs[s, 0 : n * EXT, :], band_ref[s, a])
                total = term if total is None else pltpu.roll(total, 1, 0) + term
            for k in range(n):
                shown = lanes_between(
                    jnp.maximum(firsts[k][HALO:], key_half + 1),
                    jnp.minimum(lasts[k][HALO:], WIN - 2 - key_half),
                    WIN,
                )
                logits = jnp.where(shown, total[k * EXT + HALO : (k + 1) * EXT], NEG)
                logit_ref[s, k] = logits
                top = jnp.max(logits, axis=-1, keepdims=True)
                peaks[s] = top if peaks[s] is None else jnp.maximum(peaks[s], top)
        lane = lax.broadcasted_iota(jnp.int32, (ROWS, WIN), 1)
        own = (lane >= OWN) & (lane < WIN - OWN)
        sums = [None, None]
        for k in range(n):
            for s in range(2):
                expo = jnp.exp(logit_ref[s, k] - peaks[s])
                logit_ref[s, k] = expo
                part = jnp.sum(jnp.where(own, expo, 0.0), axis=-1, keepdims=True)
                sums[s] = part if sums[s] is None else sums[s] + part
        inverse = [1.0 / sums[s] for s in range(2)]
        outs = [None, None]
        for k in range(n):
            base = row0 + ROWS - STEP * (k + 1) - OWN
            at = pl.multiple_of(TOP + base, 16)
            probs = []
            for s in range(2):
                prob = logit_ref[s, k] * inverse[s]
                probs_ref[s, 0, k] = prob
                probs.append(jnp.where(own, prob, 0.0))
            for h in range(2):
                mixed = (
                    mix_ref[2 * pair + h, 0] * probs[0] + mix_ref[2 * pair + h, 1] * probs[1]
                ).astype(BF16)
                part = dot_nn(mixed, vs[pl.ds(at, WIN), pl.ds(h * PAD_DIM, PAD_DIM)])
                outs[h] = part if outs[h] is None else outs[h] + part
        for h in range(2):
            cols = slice(h * PAD_DIM, (h + 1) * PAD_DIM)
            out = outs[h]
            heads_ref[:, cols] = out
            factor = lax.rsqrt(jnp.sum(out * out, axis=-1, keepdims=True) * (1.0 / HEAD_DIM) + EPS)
            grouped_ref[:, cols] = (out * factor * gain_ref[:, cols]).astype(BF16)

    for n in range(1, most + 1):
        pl.when(count_ref[0, block] == n)(functools.partial(body, n))


def attend_forward(proj, start, counts, base, mix, gain):
    length = proj.shape[0]
    heads, n_taps = base.shape[:2]
    pairs = heads // 2
    blocks = length // ROWS
    key_half = 5
    most = windows_most(key_half)
    two = 2 * PAD_DIM
    grid_spec = pltpu.PrefetchScalarGridSpec(
        num_scalar_prefetch=2,
        grid=(pairs, blocks),
        in_specs=[
            pl.BlockSpec((length, two), lambda p, b, *_: (0, p)),
            pl.BlockSpec((length, two), lambda p, b, *_: (0, pairs + p)),
            pl.BlockSpec((length, two), lambda p, b, *_: (0, 2 * pairs + p)),
            pl.BlockSpec((HALO + length, 1), lambda p, b, *_: (0, 0)),
            pl.BlockSpec((2,) + base.shape[1:], lambda p, b, *_: (p, 0, 0)),
            pl.BlockSpec((1, two), lambda p, b, *_: (0, p)),
        ],
        out_specs=[
            pl.BlockSpec((2, 1, most, ROWS, WIN), lambda p, b, *_: (p, b, 0, 0, 0)),
            pl.BlockSpec((ROWS, two), lambda p, b, *_: (b, p)),
            pl.BlockSpec((ROWS, two), lambda p, b, *_: (b, p)),
        ],
        scratch_shapes=[
            pltpu.VMEM((HALO + length, two), BF16),
            pltpu.VMEM((TOP + length + HALO, two), BF16),
            pltpu.VMEM((TOP + length + HALO, two), BF16),
            pltpu.VMEM((2, most, ROWS, WIN), F32),
            pltpu.VMEM((2, n_taps, 3 * WIN, WIN), BF16),
            pltpu.VMEM((2, most * EXT, 3 * WIN), BF16),
        ],
    )
    return pl.pallas_call(
        functools.partial(forward_kernel, n_taps, key_half, most),
        grid_spec=grid_spec,
        out_shape=[
            jax.ShapeDtypeStruct((heads, blocks, most, ROWS, WIN), F32),
            jax.ShapeDtypeStruct((length, heads * PAD_DIM), F32),
            jax.ShapeDtypeStruct((length, heads * PAD_DIM), BF16),
        ],
        compiler_params=pltpu.CompilerParams(vmem_limit_bytes=56 << 20),
        cost_estimate=COST,
        name="attend_forward",
    )(counts, mix, proj, proj, proj, start, base, gain)


def backward_kernel(
    n_taps, key_half, most, count_ref, mix_ref, q_ref, k_ref, v_ref, start_ref, base_ref, gain_ref,
    probs_ref, heads_ref, grad_ref, dqkv_ref, inner_ref, gain_grad_ref, tap_ref, mix_grad_ref,
    qs, ks, vs, dq_sum, dk_sum, dv_sum, taps, inputs, tap_sum, mixed_grad, t_back_ref, kept, inner_sum,
):
    pair = pl.program_id(0)
    block = pl.program_id(1)
    length = q_ref.shape[0]
    scale = HEAD_DIM ** (-0.5)

    @pl.when(block == 0)
    def _():
        fill_padded(qs, q_ref, HALO, length)
        fill_padded(ks, k_ref, TOP, length)
        fill_padded(vs, v_ref, TOP, length)
        dq_sum[...] = jnp.zeros_like(dq_sum)
        dk_sum[...] = jnp.zeros_like(dk_sum)
        dv_sum[...] = jnp.zeros_like(dv_sum)
        tap_sum[...] = jnp.zeros_like(tap_sum)
        gain_grad_ref[...] = jnp.zeros_like(gain_grad_ref)
        mix_grad_ref[...] = jnp.zeros_like(mix_grad_ref)
        for s in range(2):
            for a in range(n_taps):
                t_back_ref[s, a * WIN : (a + 1) * WIN, :] = banded(
                    band_line(base_ref[s, a : a + 1, :], key_half, -1)
                ).astype(BF16)

    row0 = pl.multiple_of(block * ROWS, ROWS)

    def body(n):
        grads = []
        for h in range(2):
            cols = slice(h * PAD_DIM, (h + 1) * PAD_DIM)
            out = heads_ref[:, cols]
            factor = lax.rsqrt(jnp.sum(out * out, axis=-1, keepdims=True) * (1.0 / HEAD_DIM) + EPS)
            unit = out * factor
            grad = grad_ref[:, cols]
            gain_grad_ref[:, cols] += jnp.sum(grad * unit, axis=0, keepdims=True)
            scaled = grad * gain_ref[:, cols]
            inner = jnp.sum(scaled * unit, axis=-1, keepdims=True) * (1.0 / HEAD_DIM)
            grads.append((factor * (scaled - unit * inner)).astype(BF16))
        lane = lax.broadcasted_iota(jnp.int32, (ROWS, WIN), 1)
        own = (lane >= OWN) & (lane < WIN - OWN)
        inner = [[None, None], [None, None]]
        for k in range(n):
            base = row0 + ROWS - STEP * (k + 1) - OWN
            at = pl.multiple_of(TOP + base, 16)
            probs = [jnp.where(own, probs_ref[s, 0, k], 0.0) for s in range(2)]
            for h in range(2):
                cols = pl.ds(h * PAD_DIM, PAD_DIM)
                grad_mixed = dot_nt(grads[h], vs[pl.ds(at, WIN), cols])
                mixed_grad[h, k] = grad_mixed
                for s in range(2):
                    part = jnp.sum(grad_mixed * probs[s], axis=-1, keepdims=True)
                    inner[h][s] = part if inner[h][s] is None else inner[h][s] + part
                mixed = (
                    mix_ref[2 * pair + h, 0] * probs[0] + mix_ref[2 * pair + h, 1] * probs[1]
                ).astype(BF16)
                dv_sum[pl.ds(at, WIN), cols] += dot_tn(mixed, grads[h])
        for h in range(2):
            for s in range(2):
                row = 2 * h + s
                mix_grad_ref[0, row : row + 1, :] += jnp.broadcast_to(
                    jnp.sum(inner[h][s], axis=0, keepdims=True), (1, PAD_DIM)
                )
        start = start_ref[pl.ds(row0, EXT), :]
        place = row_numbers(row0 - HALO, EXT)
        for s in range(2):
            cols = pl.ds(s * PAD_DIM, PAD_DIM)
            mix0 = mix_ref[2 * pair, s]
            mix1 = mix_ref[2 * pair + 1, s]
            delta = mix0 * inner[0][s] + mix1 * inner[1][s]
            query = qs[pl.ds(row0, EXT), cols]
            for k in range(n):
                grad_prob = mix0 * mixed_grad[0, k] + mix1 * mixed_grad[1, k]
                grad_logit = probs_ref[s, 0, k] * (grad_prob - delta)
                grown = jnp.concatenate([jnp.zeros((HALO, WIN), F32), grad_logit], axis=0)
                for a in range(n_taps):
                    moved = grown if a == 0 else pltpu.roll(grown, EXT - a, 0)
                    taps[k * EXT : (k + 1) * EXT, a * WIN : (a + 1) * WIN] = moved.astype(BF16)
            grad_inputs = dot_nn(taps[0 : n * EXT, :], t_back_ref[s])
            for k in range(n):
                base = row0 + ROWS - STEP * (k + 1) - OWN
                at = pl.multiple_of(TOP + base, 16)
                keys = ks[pl.ds(at, WIN), cols]
                mine = lanes_between(
                    jnp.maximum(start - base, OWN), jnp.minimum(place - base, WIN - OWN - 1), WIN
                )
                grad_masked = grad_inputs[k * EXT : (k + 1) * EXT]
                grad_score = jnp.where(mine, grad_masked * scale, 0.0).astype(BF16)
                dq_sum[pl.ds(row0, EXT), cols] += dot_nn(grad_score, keys)
                dk_sum[pl.ds(at, WIN), cols] += dot_tn(grad_score, query)
                raw = dot_nt(query, keys)
                inputs[k * EXT : (k + 1) * EXT, :] = jnp.where(mine, raw * scale, 0.0).astype(BF16)
            tap_sum[s] += dot_tn(inputs[0 : n * EXT, :], taps[0 : n * EXT, :])

    for n in range(1, most + 1):
        pl.when(count_ref[0, block] == n)(functools.partial(body, n))

    @pl.when(block == pl.num_programs(1) - 1)
    def _():
        inner = None
        sums = ((dq_sum, HALO, q_ref), (dk_sum, TOP, k_ref), (dv_sum, TOP, v_ref))
        for c, (total, top, given) in enumerate(sums):
            grad = total[top : top + length, :].astype(BF16)
            kept[pair, c] = grad
            part = jnp.sum(grad.astype(F32) * given[...].astype(F32), axis=-1, keepdims=True)
            inner = part if inner is None else inner + part

        @pl.when(pair == 0)
        def _():
            inner_sum[...] = inner

        @pl.when(pair > 0)
        def _():
            inner_sum[...] += inner

        row = lax.broadcasted_iota(jnp.int32, (WIN, WIN), 0)
        lane = lax.broadcasted_iota(jnp.int32, (WIN, WIN), 1)
        for s in range(2):
            for a in range(n_taps):
                whole = tap_sum[s, :, a * WIN : (a + 1) * WIN]
                for b in range(2 * key_half + 1):
                    part = jnp.where(lane - row == b - key_half, whole, 0.0)
                    part = jnp.sum(part, axis=0, keepdims=True)
                    part = jnp.sum(part, axis=1, keepdims=True)
                    at = a * (2 * key_half + 1) + b
                    tap_ref[s, at : at + 1, :] = jnp.broadcast_to(part, (1, PAD_DIM))

    pairs = kept.shape[0]

    @pl.when((block == pl.num_programs(1) - 1) & (pair == pairs - 1))
    def _():
        width = 2 * pairs * HEAD_DIM

        def rows_out(n, carry):
            at = pl.ds(pl.multiple_of(n * ROWS, ROWS), ROWS)
            for c in range(3):
                heads = [
                    kept[p, c, at, s * PAD_DIM : s * PAD_DIM + HEAD_DIM]
                    for p in range(pairs)
                    for s in range(2)
                ]
                dqkv_ref[at, c * width : (c + 1) * width] = jnp.concatenate(heads, axis=1)
            column = jnp.broadcast_to(inner_sum[at, :], (ROWS, PAD_DIM))
            inner_ref[pl.ds(n, 1), :] = column.T[0:1, :]
            return carry

        lax.fori_loop(0, length // ROWS, rows_out, 0)


def attend_backward(proj, start, counts, base, mix, gain, probs, heads_out, grad_grouped):
    length = proj.shape[0]
    heads, n_taps = base.shape[:2]
    pairs = heads // 2
    blocks = length // ROWS
    key_half = 5
    most = windows_most(key_half)
    two = 2 * PAD_DIM
    tap_rows = n_taps * (2 * key_half + 1)
    grid_spec = pltpu.PrefetchScalarGridSpec(
        num_scalar_prefetch=2,
        grid=(pairs, blocks),
        in_specs=[
            pl.BlockSpec((length, two), lambda p, b, *_: (0, p)),
            pl.BlockSpec((length, two), lambda p, b, *_: (0, pairs + p)),
            pl.BlockSpec((length, two), lambda p, b, *_: (0, 2 * pairs + p)),
            pl.BlockSpec((HALO + length, 1), lambda p, b, *_: (0, 0)),
            pl.BlockSpec((2,) + base.shape[1:], lambda p, b, *_: (p, 0, 0)),
            pl.BlockSpec((1, two), lambda p, b, *_: (0, p)),
            pl.BlockSpec((2, 1, most, ROWS, WIN), lambda p, b, *_: (p, b, 0, 0, 0)),
            pl.BlockSpec((ROWS, two), lambda p, b, *_: (b, p)),
            pl.BlockSpec((ROWS, two), lambda p, b, *_: (b, p)),
        ],
        out_specs=[
            pl.BlockSpec((length, 3 * heads * HEAD_DIM), lambda p, b, *_: (0, 0)),
            pl.BlockSpec((length // ROWS, ROWS), lambda p, b, *_: (0, 0)),
            pl.BlockSpec((1, two), lambda p, b, *_: (0, p)),
            pl.BlockSpec((2, tap_rows, PAD_DIM), lambda p, b, *_: (p, 0, 0)),
            pl.BlockSpec((1, 4, PAD_DIM), lambda p, b, *_: (p, 0, 0)),
        ],
        scratch_shapes=[
            pltpu.VMEM((HALO + length, two), BF16),
            pltpu.VMEM((TOP + length + HALO, two), BF16),
            pltpu.VMEM((TOP + length + HALO, two), BF16),
            pltpu.VMEM((HALO + length, two), F32),
            pltpu.VMEM((TOP + length + HALO, two), F32),
            pltpu.VMEM((TOP + length + HALO, two), F32),
            pltpu.VMEM((most * EXT, n_taps * WIN), BF16),
            pltpu.VMEM((most * EXT, WIN), BF16),
            pltpu.VMEM((2, WIN, n_taps * WIN), F32),
            pltpu.VMEM((2, most, ROWS, WIN), F32),
            pltpu.VMEM((2, n_taps * WIN, WIN), BF16),
            pltpu.VMEM((pairs, 3, length, two), BF16),
            pltpu.VMEM((length, 1), F32),
        ],
    )
    return pl.pallas_call(
        functools.partial(backward_kernel, n_taps, key_half, most),
        grid_spec=grid_spec,
        out_shape=[
            jax.ShapeDtypeStruct((length, 3 * heads * HEAD_DIM), BF16),
            jax.ShapeDtypeStruct((length // ROWS, ROWS), F32),
            jax.ShapeDtypeStruct((1, heads * PAD_DIM), F32),
            jax.ShapeDtypeStruct((heads, tap_rows, PAD_DIM), F32),
            jax.ShapeDtypeStruct((pairs, 4, PAD_DIM), F32),
        ],
        compiler_params=pltpu.CompilerParams(vmem_limit_bytes=56 << 20),
        cost_estimate=COST,
        name="attend_backward",
    )(counts, mix, proj, proj, proj, start, base, gain, probs, heads_out, grad_grouped)


MESH_ID = pl.DeviceIdType.MESH


def ring_place(member, n):
    z, y = member // 2, member % 2
    return (1 - y) * z + y * (n - 1 - z)


def ring_member(place, n):
    upper = place // (n // 2)
    return (1 - upper) * 2 * place + upper * (2 * (n - 1 - place) + 1)


def ring_peers(n):
    place = ring_place(lax.axis_index("dp"), n)
    ahead = ring_member(lax.rem(place + 1, n), n)
    behind = ring_member(lax.rem(place + n - 1, n), n)
    return place, (ahead, behind)


def ring_scratch(arrays, n):
    return [pltpu.VMEM((2, n - 1) + a.shape[2:], a.dtype) for a in arrays] + [
        pltpu.SemaphoreType.DMA((2, len(arrays), n - 1))
    ] * 4


def ring_split(array, n):
    return array.reshape(n, 2, -1, array.shape[-1])


def make_ring(n, sources, ins, outs, scratch):
    count = len(ins)
    slots = scratch[:count]
    rs_send, rs_recv, ag_send, ag_recv = scratch[count:]
    place, to = ring_peers(n)

    def chunk(way, back):
        return lax.rem(place - back + 2 * n if way == 0 else place + back, n)

    def sum_copy(way, k, s, src):
        return pltpu.make_async_remote_copy(
            src_ref=src,
            dst_ref=slots[k].at[way, s],
            send_sem=rs_send.at[way, k, s],
            recv_sem=rs_recv.at[way, k, s],
            device_id={"dp": to[way]},
            device_id_type=MESH_ID,
        )

    def share_copy(way, k, s, c):
        return pltpu.make_async_remote_copy(
            src_ref=outs[k].at[c, way],
            dst_ref=outs[k].at[c, way],
            send_sem=ag_send.at[way, k, s],
            recv_sem=ag_recv.at[way, k, s],
            device_id={"dp": to[way]},
            device_id_type=MESH_ID,
        )

    def add(way, k, s, c, dst):
        total = slots[k][way, s].astype(F32) + ins[k][c, way].astype(F32)
        dst[...] = total.astype(dst.dtype)

    both = [(k, way) for k in range(count) for way in range(2)]

    def start():
        for k, way in both:
            sum_copy(way, k, 0, sources[k].at[chunk(way, 1), way]).start()

    def tick(now):
        @pl.when(now < n - 2)
        def _():
            for k, way in both:
                sum_copy(way, k, now, slots[k].at[way, now]).wait_recv()
                add(way, k, now, chunk(way, 2 + now), slots[k].at[way, now])
                sum_copy(way, k, now + 1, slots[k].at[way, now]).start()

        @pl.when(now == n - 2)
        def _():
            for k, way in both:
                sum_copy(way, k, n - 2, slots[k].at[way, n - 2]).wait_recv()
                add(way, k, n - 2, place, outs[k].at[place, way])
                share_copy(way, k, 0, place).start()

        @pl.when((now > n - 2) & (now < 2 * n - 3))
        def _():
            step = now - (n - 1)
            for k, way in both:
                share_copy(way, k, step, chunk(way, step + 1)).wait_recv()
                share_copy(way, k, step + 1, chunk(way, step + 1)).start()

        @pl.when(now == 2 * n - 3)
        def _():
            for k, way in both:
                share_copy(way, k, n - 2, chunk(way, n - 1)).wait_recv()

    def drain():
        def one(s, carry):
            for k, way in both:
                sum_copy(way, k, s, slots[k].at[way, s]).wait_send()
                share_copy(way, k, s, place).wait_send()
            return carry

        lax.fori_loop(0, n - 1, one, 0)

    return start, tick, drain


def small_rows(size):
    return -(-size // PAD_DIM)


def pack_small(arrays, rows):
    packed = []
    for a in arrays:
        flat = a.reshape(-1)
        packed.append(jnp.pad(flat, (0, -flat.size % PAD_DIM)).reshape(-1, PAD_DIM))
    packed = jnp.concatenate(packed, axis=0)
    return jnp.pad(packed, ((0, rows - packed.shape[0]), (0, 0)))


def unpack_small(packed, arrays):
    found, at = [], 0
    for a in arrays:
        rows = small_rows(a.size)
        found.append(packed[at : at + rows].reshape(-1)[: a.size].reshape(a.shape))
        at += rows
    return found


CHUNK = 128
GROUP = 256


LIVE = 4


def exchange_scratch(steps, width, ranks, share=True, chunk=CHUNK):
    half = ranks // 2
    live = steps if share else LIVE
    shared = [pltpu.VMEM((steps, ranks, chunk, width), BF16)] if share else []
    return [
        pltpu.VMEM((steps, half, chunk, width), BF16),
        pltpu.VMEM((steps, half, chunk, width), BF16),
        pltpu.VMEM((live, half, chunk, width), F32),
        pltpu.VMEM((steps, chunk, width), BF16),
        pltpu.VMEM((steps, chunk, width), BF16),
        pltpu.SemaphoreType.DMA((5, steps)),
        pltpu.SemaphoreType.DMA((5, steps)),
    ] + shared


def tensor_peers():
    me = lax.axis_index("tensor")
    return me, me + 1 - 2 * lax.rem(me, 2), lax.rem(me + 2, 4)


def meet(signals):
    barrier = pltpu.get_barrier_semaphore()
    for device in signals:
        pl.semaphore_signal(barrier, inc=1, device_id=device, device_id_type=MESH_ID)
    pl.semaphore_wait(barrier, len(signals))


def exchange_copies(scratch):
    out_a, in_a, _, out_b, in_b, send, recv, *full = scratch
    me, near, far = tensor_peers()

    def copy(kind, step, src, dst, peer):
        return pltpu.make_async_remote_copy(
            src_ref=src,
            dst_ref=dst,
            send_sem=send.at[kind, step],
            recv_sem=recv.at[kind, step],
            device_id={"tensor": peer},
            device_id_type=MESH_ID,
        )

    def cores(step):
        return copy(0, step, out_a.at[step], in_a.at[step], near)

    def chips(step):
        return copy(1, step, out_b.at[step], in_b.at[step], far)

    def back_far(step):
        return copy(2, step, full[0].at[step, me], full[0].at[step, me], far)

    def back_near(step):
        return copy(3, step, full[0].at[step, me], full[0].at[step, me], near)

    def pass_near(step):
        return copy(4, step, full[0].at[step, far], full[0].at[step, far], near)

    return cores, chips, back_far, back_near, pass_near


def exchange_stages(scratch, partial, live, chunk):
    out_a, in_a, kept, out_b, in_b = scratch[:5]
    cores, chips = exchange_copies(scratch)[:2]
    many = GROUP // chunk
    me, near, far = tensor_peers()

    def begin(step):
        for n, owner in ((0, near), (1, lax.rem(near + 2, 4))):

            def put(term, n=n):
                term = term.astype(BF16)
                for m in range(many):
                    out_a[step + m, n] = term[m * chunk : (m + 1) * chunk]

            partial(step, owner, put)
        for m in range(many):
            cores(step + m).start()
        for n, owner in ((1, far), (0, me)):

            def put(term, n=n):
                for m in range(many):
                    kept[lax.rem(step + m, live), n] = term[m * chunk : (m + 1) * chunk]

            partial(step, owner, put)

    def over(step):
        cores(step).wait_recv()
        out_b[step] = (kept[lax.rem(step, live), 1] + in_a[step, 1].astype(F32)).astype(BF16)
        chips(step).start()

    def total(step):
        chips(step).wait_recv()
        return kept[lax.rem(step, live), 0] + in_a[step, 0].astype(F32) + in_b[step].astype(F32)

    return begin, over, total


def make_exchange(steps, scratch, partial, local, between, chunk):
    cores, chips = exchange_copies(scratch)[:2]
    begin, over, total = exchange_stages(scratch, partial, LIVE, chunk)
    many = GROUP // chunk

    def tick(now):
        @pl.when((lax.rem(now, many) == 0) & (now < steps))
        def _():
            begin(now)

        between(now)

        @pl.when((now >= 1) & (now < steps + 1))
        def _():
            over(now - 1)

        @pl.when((now >= 2) & (now < steps + 2))
        def _():
            local(now - 2, total(now - 2))

    def drain():
        def one(step, carry):
            cores(step).wait_send()
            chips(step).wait_send()
            return carry

        lax.fori_loop(0, steps, one, 0)

    return tick, steps + 2, drain


def run_exchange(steps, scratch, partial, local, whole, beside=None, ahead=None):
    cores, chips, back_far, back_near, pass_near = exchange_copies(scratch)
    begin, over, total = exchange_stages(scratch, partial, steps, CHUNK)
    full = scratch[7]
    many = GROUP // CHUNK
    me = tensor_peers()[0]

    def send_group(group, carry):
        @pl.when(group < steps // many)
        def _():
            begin(group * many)

        @pl.when(group >= 1)
        def _():
            for m in range(many):
                over((group - 1) * many + m)

        return carry

    lax.fori_loop(0, steps // many + 1, send_group, 0)

    def sum_group(group, carry):
        if beside is not None:
            beside(group)
        for m in range(many):
            step = group * many + m
            full[step, me] = local(step, total(step)).astype(BF16)
            back_far(step).start()
            back_near(step).start()
        return carry

    lax.fori_loop(0, steps // many, sum_group, 0)
    if ahead is not None:
        ahead()

    def share_step(now, carry):
        @pl.when(now < steps)
        def _():
            back_far(now).wait_recv()
            pass_near(now).start()

        @pl.when(now >= 1)
        def _():
            back_near(now - 1).wait_recv()
            pass_near(now - 1).wait_recv()
            whole(now - 1, full)

        return carry

    lax.fori_loop(0, steps + 1, share_step, 0)

    def drain(step, carry):
        for copy in (cores, chips, back_far, back_near, pass_near):
            copy(step).wait_send()
        return carry

    lax.fori_loop(0, steps, drain, 0)


def run_ticks(count, *ticks):
    def one(now, carry):
        for tick in ticks:
            tick(now)
        return carry

    lax.fori_loop(0, count, one, 0)


def group_rows(step, chunk=CHUNK):
    return pl.ds(pl.multiple_of(step * chunk, chunk), GROUP)


def owner_cols(owner, width):
    return pl.ds(pl.multiple_of(owner * width, PAD_DIM), width)


def step_rows(step, chunk=CHUNK):
    return pl.ds(pl.multiple_of(step * chunk, chunk), chunk)


def first_entry_kernel(
    key_half, tokens_ref, w_in, gains_ref, segments_ref, proj_out, normed_out, factor_ref, gains_all_ref, gain_heads_ref,
    start_ref, count_ref, w_ref, proj_ref, normed_ref, load, store, full, gains_in, send, recv, gains_send, gains_recv,
):
    weights = pltpu.make_async_copy(w_in, w_ref, load.at[0])
    weights.start()
    rows, width = tokens_ref.shape
    ranks = normed_ref.shape[1] // width
    heads = width // HEAD_DIM
    steps, many = rows // CHUNK, GROUP // CHUNK
    me, near, far = tensor_peers()
    across = lax.rem(near + 2, 4)
    meet([{"tensor": near}, {"tensor": far}, {"tensor": across}])

    def copy(kind, step, src, dst, peer):
        return pltpu.make_async_remote_copy(
            src_ref=src,
            dst_ref=dst,
            send_sem=send.at[kind, step],
            recv_sem=recv.at[kind, step],
            device_id={"tensor": peer},
            device_id_type=MESH_ID,
        )

    def to_far(step):
        return copy(0, step, tokens_ref.at[step_rows(step)], full.at[step, me], far)

    def to_near(step):
        return copy(1, step, tokens_ref.at[step_rows(step)], full.at[step, me], near)

    def pass_near(step):
        return copy(2, step, full.at[step, far], full.at[step, far], near)

    def gains_copy(kind, peer, sender):
        return pltpu.make_async_remote_copy(
            src_ref=gains_ref,
            dst_ref=gains_in.at[sender],
            send_sem=gains_send.at[kind],
            recv_sem=gains_recv.at[sender],
            device_id={"tensor": peer},
            device_id_type=MESH_ID,
        )

    peers = (near, far, across)
    for kind, peer in enumerate(peers):
        gains_copy(kind, peer, me).start()

    def send_all(step, carry):
        to_far(step).start()
        to_near(step).start()
        full[step, me] = tokens_ref[step_rows(step), :]
        return carry

    lax.fori_loop(0, steps, send_all, 0)
    gains_in[me] = gains_ref[...]
    for kind, peer in enumerate(peers):
        gains_copy(kind, peer, peer).wait()
    for n in range(ranks):
        gains_all_ref[:, n * width : (n + 1) * width] = gains_in[n]

    def stores(group):
        at = group_rows(group * many)
        return [
            pltpu.make_async_copy(src.at[at], dst.at[at], store.at[n, group])
            for n, (src, dst) in enumerate(((proj_ref, proj_out), (normed_ref, normed_out)))
        ]

    weights.wait()
    for h in range(heads):
        own = gains_ref[2:3, h * HEAD_DIM : (h + 1) * HEAD_DIM]
        gain_heads_ref[:, h * PAD_DIM : (h + 1) * PAD_DIM] = jnp.concatenate(
            [own, jnp.zeros((1, PAD_DIM - HEAD_DIM), F32)], axis=1
        )
    seqs, length = segments_ref.shape
    for n in range(seqs):
        lead = n * (HALO + length)
        start_ref[lead : lead + HALO, :] = jnp.full((HALO, 1), 1 << 20, jnp.int32)
        line = segments_ref[n : n + 1, :].astype(F32)
        for b in range(length // ROWS):
            column = jnp.broadcast_to(line[:, b * ROWS : (b + 1) * ROWS], (ROWS, ROWS)).T[:, 0:1]
            before = jnp.sum(jnp.where(line < column, 1.0, 0.0), axis=1, keepdims=True)
            at = lead + HALO + b * ROWS
            before = before.astype(jnp.int32)
            start_ref[at : at + ROWS, :] = before
            count = jnp.ones((1, 1), jnp.int32)
            for k in range(1, windows_most(key_half)):
                reach = b * ROWS + ROWS - STEP * k + key_half
                count = count + jnp.where(before[0:1] < reach, 1, 0)
            count_ref[n : n + 1, b : b + 1] = count

    def tick(now):
        @pl.when(now < steps)
        def _():
            to_far(now).wait_recv()
            pass_near(now).start()

        @pl.when(now >= 1)
        def _():
            to_near(now - 1).wait_recv()
            pass_near(now - 1).wait_recv()

        @pl.when((now >= many) & (lax.rem(now, many) == 0))
        def _():
            first = now - many
            at = group_rows(first)
            blocks = [
                jnp.concatenate([full[first + m, n] for m in range(many)], axis=0).astype(F32)
                for n in range(ranks)
            ]
            squares = sum(jnp.sum(block * block, axis=-1, keepdims=True) for block in blocks)
            factor = lax.rsqrt(squares * (1.0 / (ranks * width)) + EPS)
            factor_ref[at, :] = factor
            for n, block in enumerate(blocks):
                cols = slice(n * width, (n + 1) * width)
                normed_ref[at, cols] = (block * factor * gains_all_ref[0:1, cols]).astype(BF16)
            for c in range(3):
                out = dot_nn(normed_ref[at, :], w_ref[c])
                empty = jnp.zeros((GROUP, PAD_DIM - HEAD_DIM), F32)
                for h in range(heads):
                    head = jnp.concatenate([out[:, h * HEAD_DIM : (h + 1) * HEAD_DIM], empty], axis=1)
                    lane = (c * heads + h) * PAD_DIM
                    proj_ref[at, lane : lane + PAD_DIM] = head.astype(BF16)
            for one in stores(first // many):
                one.start()

    run_ticks(steps + 1, tick)

    def stored(group, carry):
        for one in stores(group):
            one.wait()
        return carry

    lax.fori_loop(0, steps // many, stored, 0)

    def drain(step, carry):
        to_far(step).wait_send()
        to_near(step).wait_send()
        pass_near(step).wait_send()
        return carry

    lax.fori_loop(0, steps, drain, 0)


def first_entry(tokens, w_qkv, gains, segments, key_half):
    rows, width = tokens.shape
    full_width = w_qkv.shape[1]
    ranks = full_width // width
    steps = rows // CHUNK
    padded = 3 * width // HEAD_DIM * PAD_DIM
    vmem = pl.BlockSpec(memory_space=pltpu.VMEM)
    anywhere = pl.BlockSpec(memory_space=pl.ANY)
    return pl.pallas_call(
        functools.partial(first_entry_kernel, key_half),
        out_shape=[
            jax.ShapeDtypeStruct((rows, padded), BF16),
            jax.ShapeDtypeStruct((rows, full_width), BF16),
            jax.ShapeDtypeStruct((rows, 1), F32),
            jax.ShapeDtypeStruct((8, full_width), F32),
            jax.ShapeDtypeStruct((1, width // HEAD_DIM * PAD_DIM), F32),
            jax.ShapeDtypeStruct((segments.shape[0] * (HALO + segments.shape[1]), 1), jnp.int32),
            jax.ShapeDtypeStruct((segments.shape[0], segments.shape[1] // ROWS), jnp.int32),
        ],
        in_specs=[vmem, anywhere, vmem, vmem],
        out_specs=[anywhere, anywhere] + [vmem] * 5,
        scratch_shapes=[
            pltpu.VMEM(w_qkv.shape, BF16),
            pltpu.VMEM((rows, padded), BF16),
            pltpu.VMEM((rows, full_width), BF16),
            pltpu.SemaphoreType.DMA((1,)),
            pltpu.SemaphoreType.DMA((2, rows // GROUP)),
            pltpu.VMEM((steps, ranks, CHUNK, width), BF16),
            pltpu.VMEM((ranks, 8, width), F32),
            pltpu.SemaphoreType.DMA((3, steps)),
            pltpu.SemaphoreType.DMA((3, steps)),
            pltpu.SemaphoreType.DMA((3,)),
            pltpu.SemaphoreType.DMA((ranks,)),
        ],
        compiler_params=pltpu.CompilerParams(
            collective_id=4, has_side_effects=True, vmem_limit_bytes=60 << 20
        ),
        cost_estimate=COST,
        name="first_entry",
    )(tokens, w_qkv, gains, segments)


def attn_exit_kernel(
    grouped_ref, w_out_ref, tokens_ref, gain_ref, cot_in, w_gate_up_in, w_down_in, hidden_local_ref,
    hidden_out, normed_out, w_ref, act_out, grad_gate_out, grad_up_out, hidden_ref, normed_ref, act_ref,
    grad_gate_ref, grad_up_ref, grad_act, cot_ref, w_gate_up_ref, w_down_ref, load, store, *scratch
):
    loads = [
        pltpu.make_async_copy(src, dst, load.at[n])
        for n, (src, dst) in enumerate(
            ((cot_in, cot_ref), (w_down_in, w_down_ref), (w_gate_up_in, w_gate_up_ref))
        )
    ]
    for one in loads:
        one.start()
    rows, width = tokens_ref.shape
    ranks = hidden_ref.shape[1] // width
    many = GROUP // CHUNK
    for h in range(width // HEAD_DIM):
        lead = h * PAD_DIM
        w_ref[lead : lead + HEAD_DIM, :] = w_out_ref[h * HEAD_DIM : (h + 1) * HEAD_DIM, :]
        w_ref[lead + HEAD_DIM : lead + PAD_DIM, :] = jnp.zeros((PAD_DIM - HEAD_DIM, w_ref.shape[1]), BF16)

    def partial(step, owner, put):
        put(dot_nn(grouped_ref[group_rows(step), :], w_ref[:, owner_cols(owner, width)]))

    def local(step, total):
        hidden = tokens_ref[step_rows(step), :].astype(F32) + total
        hidden_local_ref[step_rows(step), :] = hidden
        return hidden

    def whole(step, full):
        squares = None
        for n in range(ranks):
            block = full[step, n]
            hidden_ref[step_rows(step), n * width : (n + 1) * width] = block
            block = block.astype(F32)
            part = jnp.sum(block * block, axis=-1, keepdims=True)
            squares = part if squares is None else squares + part
        factor = lax.rsqrt(squares * (1.0 / (ranks * width)) + EPS)
        for n in range(ranks):
            cols = slice(n * width, (n + 1) * width)
            unit = full[step, n].astype(F32) * factor
            normed_ref[step_rows(step), cols] = (unit * gain_ref[1:2, cols]).astype(BF16)

        @pl.when(lax.rem(step, many) == many - 1)
        def _():
            at = group_rows(step - (many - 1))
            gate = dot_nn(normed_ref[at, :], w_gate_up_ref[0])
            up = dot_nn(normed_ref[at, :], w_gate_up_ref[1])
            sigmoid = jax.nn.sigmoid(gate)
            swish = gate * sigmoid
            grad = grad_act[at, :]
            act_ref[at, :] = (swish * up).astype(BF16)
            grad_gate_ref[at, :] = (grad * up * sigmoid * (1.0 + gate * (1.0 - sigmoid))).astype(BF16)
            grad_up_ref[at, :] = (grad * swish).astype(BF16)
            for one in stores(step // many):
                one.start()

    def stores(group):
        at = group_rows(group * many)
        pairs = (
            (hidden_ref, hidden_out),
            (normed_ref, normed_out),
            (act_ref, act_out),
            (grad_gate_ref, grad_gate_out),
            (grad_up_ref, grad_up_out),
        )
        return [
            pltpu.make_async_copy(src.at[at], dst.at[at], store.at[n, group])
            for n, (src, dst) in enumerate(pairs)
        ]

    def beside(group):
        @pl.when(group == 0)
        def _():
            loads[0].wait()
            loads[1].wait()

        at = group_rows(group * many)
        grad_act[at, :] = dot_nt(cot_ref[at, :], w_down_ref[...])

    me, near, far = tensor_peers()
    meet([{"tensor": near}, {"tensor": far}])
    run_exchange(rows // CHUNK, scratch, partial, local, whole, beside, loads[2].wait)

    def stored(group, carry):
        for one in stores(group):
            one.wait()
        return carry

    lax.fori_loop(0, rows // GROUP, stored, 0)


def attn_exit(grouped, w_out, tokens, gain, full_cot, w_gate_up, w_down):
    rows, width = tokens.shape
    full_width = w_out.shape[1]
    units = w_down.shape[0]
    vmem = pl.BlockSpec(memory_space=pltpu.VMEM)
    anywhere = pl.BlockSpec(memory_space=pl.ANY)
    return pl.pallas_call(
        attn_exit_kernel,
        out_shape=[
            jax.ShapeDtypeStruct((rows, width), F32),
            jax.ShapeDtypeStruct((rows, full_width), BF16),
            jax.ShapeDtypeStruct((rows, full_width), BF16),
            jax.ShapeDtypeStruct((grouped.shape[1], full_width), BF16),
        ]
        + [jax.ShapeDtypeStruct((rows, units), BF16)] * 3,
        in_specs=[vmem] * 4 + [anywhere] * 3,
        out_specs=[vmem, anywhere, anywhere, vmem] + [anywhere] * 3,
        scratch_shapes=[pltpu.VMEM((rows, full_width), BF16)] * 2
        + [pltpu.VMEM((rows, units), BF16)] * 3
        + [
            pltpu.VMEM((rows, units), F32),
            pltpu.VMEM(full_cot.shape, BF16),
            pltpu.VMEM(w_gate_up.shape, BF16),
            pltpu.VMEM(w_down.shape, BF16),
            pltpu.SemaphoreType.DMA((3,)),
            pltpu.SemaphoreType.DMA((5, rows // GROUP)),
        ]
        + exchange_scratch(rows // CHUNK, width, full_width // width),
        compiler_params=pltpu.CompilerParams(
            collective_id=1, has_side_effects=True, vmem_limit_bytes=56 << 20
        ),
        cost_estimate=COST,
        name="attn_exit",
    )(grouped, w_out, tokens, gain, full_cot, w_gate_up, w_down)


def mlp_exit_kernel(
    gate_ref, up_ref, w_ref, hidden_in, cot_in, hidden_local_ref, cot_local_ref, gain_ref, gain_local_ref,
    grad_attn_ref, grad_hidden_ref, gain_grad_ref, grad_local, hidden_ref, cot_ref, load, *scratch
):
    loads = [
        pltpu.make_async_copy(hidden_in, hidden_ref, load.at[0]),
        pltpu.make_async_copy(cot_in, cot_ref, load.at[1]),
    ]
    for one in loads:
        one.start()
    rows, width = cot_local_ref.shape
    full_width = hidden_ref.shape[1]
    ranks = full_width // width
    gain_grad_ref[...] = jnp.zeros_like(gain_grad_ref)

    def partial(step, owner, put):
        cols = owner_cols(owner, width)
        at = group_rows(step)
        put(dot_nt(gate_ref[at, :], w_ref[0, cols, :]) + dot_nt(up_ref[at, :], w_ref[1, cols, :]))

    def local(step, total):
        grad_local[step_rows(step), :] = total
        return total

    def whole(step, full):
        at = step_rows(step)
        squares, inner = None, None
        for n in range(ranks):
            cols = slice(n * width, (n + 1) * width)
            hidden = hidden_ref[at, cols].astype(F32)
            part = jnp.sum(hidden * hidden, axis=-1, keepdims=True)
            squares = part if squares is None else squares + part
            part = jnp.sum(full[step, n].astype(F32) * gain_ref[1:2, cols] * hidden, axis=-1, keepdims=True)
            inner = part if inner is None else inner + part
        factor = lax.rsqrt(squares * (1.0 / full_width) + EPS)
        inner = inner * factor * (1.0 / full_width)
        for n in range(ranks):
            cols = slice(n * width, (n + 1) * width)
            unit = hidden_ref[at, cols].astype(F32) * factor
            grad = full[step, n].astype(F32) * gain_ref[1:2, cols] - unit * inner
            grad_attn_ref[at, cols] = (cot_ref[at, cols].astype(F32) + factor * grad).astype(BF16)
        total = grad_local[at, :]
        unit = hidden_local_ref[at, :] * factor
        gain_grad_ref[...] += jnp.sum(total * unit, axis=0, keepdims=True)
        grad_hidden_ref[at, :] = cot_local_ref[at, :].astype(F32) + factor * (
            total * gain_local_ref[...] - unit * inner
        )

    me, near, far = tensor_peers()
    meet([{"tensor": near}, {"tensor": far}])

    def ahead():
        for one in loads:
            one.wait()

    run_exchange(rows // CHUNK, scratch, partial, local, whole, ahead=ahead)


def mlp_exit(grad_gate, grad_up, w_gate_up, hidden, full_cot, hidden_local, cotangent, gain, gain_local):
    rows, width = hidden_local.shape
    full_width = hidden.shape[1]
    vmem = pl.BlockSpec(memory_space=pltpu.VMEM)
    return pl.pallas_call(
        mlp_exit_kernel,
        out_shape=[
            jax.ShapeDtypeStruct((rows, full_width), BF16),
            jax.ShapeDtypeStruct((rows, width), F32),
            jax.ShapeDtypeStruct((1, width), F32),
        ],
        in_specs=[vmem] * 3 + [pl.BlockSpec(memory_space=pl.ANY)] * 2 + [vmem] * 4,
        out_specs=[vmem] * 3,
        scratch_shapes=[
            pltpu.VMEM((rows, width), F32),
            pltpu.VMEM(hidden.shape, BF16),
            pltpu.VMEM(full_cot.shape, BF16),
            pltpu.SemaphoreType.DMA((2,)),
        ]
        + exchange_scratch(rows // CHUNK, width, full_width // width),
        compiler_params=pltpu.CompilerParams(
            collective_id=2, has_side_effects=True, vmem_limit_bytes=56 << 20
        ),
        cost_estimate=COST,
        name="mlp_exit",
    )(grad_gate, grad_up, w_gate_up, hidden, full_cot, hidden_local, cotangent, gain, gain_local)


def last_exit_kernel(
    n_ring, count, factor_ref, inner_ref, gain_ref, small_ref, *refs,
):
    given, sources, refs = refs[:7], refs[7 : 7 + count], refs[7 + count :]
    tokens_grad_ref, out_ref, small_sum_ref = refs[:3]
    outs, refs = refs[3 : 3 + count], refs[3 + count :]
    here_too, ins, load, refs = refs[:7], refs[7 : 7 + count], refs[7 + count], refs[8 + count :]
    grad_ref, w_ref, tokens_ref, grad_hidden_ref, act_ref, w_down_ref, hidden_ref = here_too
    loads = [
        pltpu.make_async_copy(src, dst, load.at[n])
        for n, (src, dst) in enumerate(zip((*sources, *given), (*ins, *here_too)))
    ]
    for one in loads:
        one.start()
    gain_grad, mine, all_small, small_send, small_recv = refs[:5]
    inner_in, inner_sum, inner_col, inner_send, inner_recv = refs[5:10]
    ring_refs, scratch = refs[10 : 14 + count], refs[14 + count :]
    rows, width = tokens_ref.shape
    full_width = w_ref.shape[1]
    half = rows // GROUP
    me, near, far = tensor_peers()
    here = lax.axis_index("dp")
    gain_grad[...] = jnp.zeros_like(gain_grad)

    def partial(step, owner, put):
        cols = owner_cols(owner, width)

        @pl.when(step < half)
        def _():
            total = None
            for c in range(3):
                term = dot_nt(grad_ref[group_rows(step, GROUP), c * width : (c + 1) * width], w_ref[c, cols, :])
                total = term if total is None else total + term
            put(total)

        @pl.when(step >= half)
        def _():
            put(dot_nn(act_ref[group_rows(step - half, GROUP), :], w_down_ref[:, cols]))

    def between(now):
        def copy(n, src, peer):
            return pltpu.make_async_remote_copy(
                src_ref=src,
                dst_ref=inner_in.at[n],
                send_sem=inner_send.at[n],
                recv_sem=inner_recv.at[n],
                device_id={"tensor": peer},
                device_id_type=MESH_ID,
            )

        @pl.when(now == 0)
        def _():
            copy(0, inner_ref, near).start()

        @pl.when(now == 1)
        def _():
            copy(0, inner_ref, near).wait()
            inner_sum[...] = inner_ref[...] + inner_in[0]
            copy(1, inner_sum, far).start()

        @pl.when(now == 2)
        def _():
            copy(1, inner_sum, far).wait()
            total = (inner_sum[...] + inner_in[1]) * (1.0 / full_width)
            for n in range(rows // ROWS):
                line = jnp.broadcast_to(total[n : n + 1, :], (ROWS, ROWS))
                inner_col[n * ROWS : (n + 1) * ROWS, :] = line.T[:, 0:1]

    def local(step, total):
        @pl.when(step < half)
        def _():
            at = step_rows(step, GROUP)
            factor = factor_ref[at, :]
            unit = tokens_ref[at, :].astype(F32) * factor
            gain_grad[...] += jnp.sum(total * unit, axis=0, keepdims=True)
            tokens_grad_ref[at, :] = grad_hidden_ref[at, :] + factor * (
                total * gain_ref[...] - unit * inner_col[at, :]
            )

        @pl.when(step >= half)
        def _():
            at = step_rows(step - half, GROUP)
            out_ref[at, :] = (hidden_ref[at, :] + total).astype(BF16)

    def small_copy(peer, sender):
        return pltpu.make_async_remote_copy(
            src_ref=mine,
            dst_ref=all_small.at[sender],
            send_sem=small_send.at[peer],
            recv_sem=small_recv.at[sender],
            device_id={"dp": peer},
            device_id_type=MESH_ID,
        )

    def small_start(now):
        @pl.when(now == half + 2)
        def _():
            mine[...] = small_ref[...]
            for n in range(width // PAD_DIM):
                mine[n : n + 1, :] = gain_grad[:, n * PAD_DIM : (n + 1) * PAD_DIM]
            all_small[here] = mine[...]

            def one(away, carry):
                small_copy(lax.rem(here + away, n_ring), here).start()
                return carry

            lax.fori_loop(1, n_ring, one, 0)

    barrier = pltpu.get_barrier_semaphore()
    for peer in (near, far):
        pl.semaphore_signal(barrier, inc=1, device_id={"tensor": peer}, device_id_type=MESH_ID)

    def greet(away, carry):
        peer = lax.rem(here + away, n_ring)
        pl.semaphore_signal(barrier, inc=1, device_id={"dp": peer}, device_id_type=MESH_ID)
        return carry

    lax.fori_loop(1, n_ring, greet, 0)
    pl.semaphore_wait(barrier, 2 + n_ring - 1)

    ring_start, ring_tick, ring_drain = make_ring(n_ring, sources, ins, outs, ring_refs)
    tick, ticks, drain = make_exchange(2 * half, scratch, partial, local, between, GROUP)
    ring_start()
    for one in loads:
        one.wait()
    run_ticks(max(ticks, 2 * (n_ring - 1)), ring_tick, tick, small_start)

    def one(away, carry):
        peer = lax.rem(here + away, n_ring)
        small_copy(peer, peer).wait()
        return carry

    lax.fori_loop(1, n_ring, one, 0)

    def add(n, total):
        return total + all_small[n]

    small_sum_ref[...] = lax.fori_loop(1, n_ring, add, all_small[0])
    drain()
    ring_drain()


def last_exit(
    grad_proj, w_qkv, tokens, grad_hidden, factor, inner, gain, act, w_down, hidden_local, small, sums
):
    rows, width = tokens.shape
    n_ring = lax.axis_size("dp")
    count = len(sums)
    split = [ring_split(a, n_ring) for a in sums]
    gain_rows = width // PAD_DIM
    need = gain_rows + sum(small_rows(a.size) for a in small)
    packed = jnp.pad(pack_small(small, need - gain_rows), ((gain_rows, -need % 8), (0, 0)))
    vmem = pl.BlockSpec(memory_space=pltpu.VMEM)
    steps = 2 * rows // GROUP
    given = (grad_proj, w_qkv, tokens, grad_hidden, act, w_down, hidden_local)
    tokens_grad, out, packed, *totals = pl.pallas_call(
        functools.partial(last_exit_kernel, n_ring, count),
        out_shape=[
            jax.ShapeDtypeStruct((rows, width), F32),
            jax.ShapeDtypeStruct((rows, width), BF16),
            jax.ShapeDtypeStruct(packed.shape, F32),
        ]
        + [jax.ShapeDtypeStruct(a.shape, a.dtype) for a in split],
        in_specs=[vmem] * 4 + [pl.BlockSpec(memory_space=pl.ANY)] * (7 + count),
        out_specs=[vmem] * (3 + count),
        scratch_shapes=[pltpu.VMEM(a.shape, a.dtype) for a in (*given, *split)]
        + [
            pltpu.SemaphoreType.DMA((7 + count,)),
            pltpu.VMEM((1, width), F32),
            pltpu.VMEM(packed.shape, F32),
            pltpu.VMEM((n_ring,) + packed.shape, F32),
            pltpu.SemaphoreType.DMA((n_ring,)),
            pltpu.SemaphoreType.DMA((n_ring,)),
            pltpu.VMEM((2,) + inner.shape, F32),
            pltpu.VMEM(inner.shape, F32),
            pltpu.VMEM((rows, 1), F32),
            pltpu.SemaphoreType.DMA((2,)),
            pltpu.SemaphoreType.DMA((2,)),
        ]
        + ring_scratch(split, n_ring)
        + exchange_scratch(steps, width, w_qkv.shape[1] // width, False, GROUP),
        compiler_params=pltpu.CompilerParams(
            collective_id=3, has_side_effects=True, vmem_limit_bytes=62 << 20
        ),
        cost_estimate=COST,
        name="last_exit",
    )(factor, inner, gain, packed, *given, *split)
    gain_grad = packed[:gain_rows].reshape(width)
    totals = [t.reshape(a.shape) for t, a in zip(totals, sums)]
    return tokens_grad, gain_grad, out, unpack_small(packed[gain_rows:], small), totals


def widen_kernel(
    early_steps, gate_ref, early_ref, late_ref, down_ref, out_ref, query_ref, key_ref, value_ref,
    tokens_ref, layer_ref, gate_up_to, down_to, out_to, qkv_to, tokens_to, layer_to,
):
    step = pl.program_id(0)
    tokens_to[...] = tokens_ref[...]
    layer_to[...] = layer_ref[...]
    gate_up_to[0] = gate_ref[...].astype(F32)

    @pl.when(step < early_steps)
    def _():
        gate_up_to[1] = early_ref[...].astype(F32)

    @pl.when(step >= early_steps)
    def _():
        gate_up_to[1] = late_ref[...].astype(F32)

    down_to[...] = down_ref[...].astype(F32)
    out_to[...] = out_ref[...].astype(F32)
    for c, ref in enumerate((query_ref, key_ref, value_ref)):
        qkv_to[c] = ref[...].astype(F32)


def widen(gate, early_up, late_up, down, out, query, key, value, tokens_grad, layer_out):
    steps = 8
    full_width, units = gate.shape
    rows = full_width // steps
    early_steps = early_up.shape[0] // rows
    width = query.shape[1]

    def block(array):
        return pl.BlockSpec((array.shape[0] // steps, array.shape[1]), lambda i: (i, 0))

    return pl.pallas_call(
        functools.partial(widen_kernel, early_steps),
        grid=(steps,),
        out_shape=[
            jax.ShapeDtypeStruct((2, full_width, units), F32),
            jax.ShapeDtypeStruct(down.shape, F32),
            jax.ShapeDtypeStruct(out.shape, F32),
            jax.ShapeDtypeStruct((3, full_width, width), F32),
            jax.ShapeDtypeStruct(tokens_grad.shape, tokens_grad.dtype),
            jax.ShapeDtypeStruct(layer_out.shape, layer_out.dtype),
        ],
        in_specs=[
            block(gate),
            pl.BlockSpec((rows, units), lambda i: (jnp.minimum(i, early_steps - 1), 0)),
            pl.BlockSpec((rows, units), lambda i: (jnp.maximum(i - early_steps, 0), 0)),
            block(down),
            block(out),
            block(query),
            block(key),
            block(value),
            block(tokens_grad),
            block(layer_out),
        ],
        out_specs=[
            pl.BlockSpec((2, rows, units), lambda i: (0, i, 0)),
            block(down),
            block(out),
            pl.BlockSpec((3, rows, width), lambda i: (0, i, 0)),
            block(tokens_grad),
            block(layer_out),
        ],
        compiler_params=pltpu.CompilerParams(vmem_limit_bytes=60 << 20),
        name="widen",
    )(gate, early_up, late_up, down, out, query, key, value, tokens_grad, layer_out)


def banded(line):
    return pltpu.roll(jnp.broadcast_to(line, (WIN, WIN)), 0, 1, stride=1, stride_axis=0)


def band_line(taps, half, sign):
    lane = lax.broadcasted_iota(jnp.int32, (1, WIN), 1)
    line = jnp.zeros((1, WIN), F32)
    for b in range(taps.shape[1]):
        line = jnp.where(lane == (sign * (b - half)) % WIN, taps[:, b : b + 1], line)
    return line


def cut_heads(array, axis):
    shape = array.shape
    heads = shape[axis] // PAD_DIM
    split = array.reshape(shape[:axis] + (heads, PAD_DIM) + shape[axis + 1 :])
    cut = lax.slice_in_dim(split, 0, HEAD_DIM, axis=axis + 1)
    return cut.reshape(shape[:axis] + (heads * HEAD_DIM,) + shape[axis + 1 :])


def on_device(
    tokens, segments, attn_gain, w_qkv, kq_kernel, head_mix, group_gain, w_out, mlp_gain, w_gate_up,
    w_down, cotangent,
):
    rows_here, local_width = tokens.shape
    seq_count, length = segments.shape
    heads_here = local_width // HEAD_DIM
    n_taps, key_taps = kq_kernel.shape[1:]
    key_half = key_taps // 2

    full_width = w_qkv.shape[1]
    own_gains = jnp.pad(jnp.stack([attn_gain, mlp_gain, group_gain]).astype(F32), ((0, 5), (0, 0)))
    proj, normed_one, scale_one, gains, gain_heads, start, counts = first_entry(
        tokens, w_qkv, own_gains, segments, key_half
    )
    starts = [start[n * (HALO + length) : (n + 1) * (HALO + length)] for n in range(seq_count)]
    counts = [counts[n : n + 1] for n in range(seq_count)]
    cot_here, proj = lax.optimization_barrier((cotangent, proj))
    full_cot = lax.all_gather(cot_here, "tensor", axis=1, tiled=True)

    kept = []
    for n in range(seq_count):
        rows = slice(n * length, (n + 1) * length)
        kept.append(
            attend_forward(proj[rows], starts[n], counts[n], kq_kernel, head_mix, gain_heads)
        )
    grouped = jnp.concatenate([one[2] for one in kept], axis=0)
    grouped, full_cot = lax.optimization_barrier((grouped, full_cot))
    hidden_local, hidden, normed_two, w_out_pad, act, grad_gate, grad_up = attn_exit(
        grouped, w_out, tokens, gains, full_cot, w_gate_up, w_down
    )

    grad_down = dot_tn(act, full_cot).astype(BF16)
    early_rows = int(full_width * EARLY_SHARE)
    early_up = dot_tn(normed_two[:, :early_rows], grad_up).astype(BF16)
    grad_gate, early_up, grad_down = lax.optimization_barrier((grad_gate, early_up, grad_down))
    early_up, grad_down = lax.psum((early_up, grad_down), "dp")
    grad_attn, grad_hidden_local, grad_gain_two = mlp_exit(
        grad_gate, grad_up, w_gate_up, hidden, full_cot, hidden_local, cotangent, gains,
        mlp_gain.astype(F32)[None],
    )
    grad_gate_w = dot_tn(normed_two, grad_gate).astype(BF16)
    late_up = dot_tn(normed_two[:, early_rows:], grad_up).astype(BF16)
    grad_w_out = cut_heads(dot_tn(grouped, grad_attn).astype(BF16), 0)

    grad_grouped = dot_nt(grad_attn, w_out_pad)
    parts = []
    for n in range(seq_count):
        rows = slice(n * length, (n + 1) * length)
        parts.append(
            attend_backward(
                proj[rows], starts[n], counts[n], kq_kernel, head_mix, gain_heads, kept[n][0], kept[n][1],
                grad_grouped[rows],
            )
        )
    grad_proj = jnp.concatenate([one[0] for one in parts], axis=0)
    inner_part = jnp.concatenate([one[1] for one in parts], axis=0)
    grad_group_gain = sum(cut_heads(one[2][0], 0) for one in parts)
    grad_kernel = sum(one[3][:, :, 0] for one in parts).reshape(heads_here, n_taps, key_taps)
    grad_mix = sum(one[4][:, :, 0] for one in parts).reshape(heads_here, 2)

    grad_qkv = [
        dot_tn(normed_one, grad_proj[:, c * local_width : (c + 1) * local_width]).astype(BF16)
        for c in range(3)
    ]
    tokens_grad, grad_gain_one, layer_out, small, sums = last_exit(
        grad_proj, w_qkv, tokens, grad_hidden_local, scale_one, inner_part, attn_gain.astype(F32)[None],
        act, w_down, hidden_local, (grad_kernel, grad_mix, grad_group_gain, grad_gain_two[0]),
        (grad_gate_w, late_up, grad_w_out, *grad_qkv),
    )
    grad_kernel, grad_mix, grad_group_gain, grad_gain_two = small
    grad_gate_w, late_up, grad_w_out, *grad_qkv = sums
    grad_gate_up, grad_down, grad_w_out, grad_qkv, tokens_grad, layer_out = widen(
        grad_gate_w, early_up, late_up, grad_down, grad_w_out, *grad_qkv, tokens_grad, layer_out
    )
    return (
        layer_out,
        tokens_grad,
        grad_gain_one,
        grad_qkv,
        grad_kernel,
        grad_mix,
        grad_group_gain,
        grad_w_out,
        grad_gain_two,
        grad_gate_up,
        grad_down,
    )


def solution(mesh):
    in_specs = (
        P("dp", "tensor"),
        P("dp", None),
        P("tensor"),
        P(None, None, "tensor"),
        P("tensor", None, None),
        P("tensor", None),
        P("tensor"),
        P("tensor", None),
        P("tensor"),
        P(None, None, "tensor"),
        P("tensor", None),
        P("dp", "tensor"),
    )
    out_specs = (
        P("dp", "tensor"),
        P("dp", "tensor"),
        P("tensor"),
        P(None, None, "tensor"),
        P("tensor", None, None),
        P("tensor", None),
        P("tensor"),
        P("tensor", None),
        P("tensor"),
        P(None, None, "tensor"),
        P("tensor", None),
    )
    return jax.shard_map(
        on_device, mesh=mesh, in_specs=in_specs, out_specs=out_specs, check_vma=False
    )
```

```python
import functools

import jax
import jax.numpy as jnp
from jax import lax
from jax.experimental import pallas as pl
from jax.experimental.pallas import tpu as pltpu
from jax.sharding import PartitionSpec as P

HEAD_DIM = 96
PAD_DIM = 128
DOC_MOST = 512
EPS = 1e-05
NEG = -1e30

COST = pl.CostEstimate(flops=1 << 20, bytes_accessed=1 << 10, transcendentals=0)
EARLY_SHARE = 0.75
ROWS = 128
HALO = 16
WIN = 256
OWN = 16
STEP = WIN - 2 * OWN
TOP = 256
EXT = ROWS + HALO

F32 = jnp.float32
BF16 = jnp.bfloat16


def windows_most(key_half):
    return -(-(DOC_MOST - 1 + ROWS + key_half) // STEP)


def dot_nt(a, b):
    return lax.dot_general(a, b, (((1,), (1,)), ((), ())), preferred_element_type=F32)


def dot_tn(a, b):
    return lax.dot_general(a, b, (((0,), (0,)), ((), ())), preferred_element_type=F32)


def dot_nn(a, b):
    return jnp.dot(a, b, preferred_element_type=F32)


def fill_padded(dst, src, top, length):
    total = dst.shape[0]
    dst[0:top, :] = jnp.zeros((top, dst.shape[1]), dst.dtype)
    dst[top : top + length, :] = src[...]
    if total > top + length:
        dst[top + length : total, :] = jnp.zeros((total - top - length, dst.shape[1]), dst.dtype)


def lanes_between(first, last, width):
    lane = lax.broadcasted_iota(jnp.int32, (first.shape[0], width), 1)
    return (lane >= first) & (lane <= last)


def row_numbers(base, count):
    return base + lax.broadcasted_iota(jnp.int32, (count, 1), 0)


def forward_kernel(
    n_taps, key_half, most, count_ref, mix_ref, q_ref, k_ref, v_ref, start_ref, base_ref, gain_ref,
    probs_ref, heads_ref, grouped_ref, qs, ks, vs, logit_ref, band_ref, inputs,
):
    pair = pl.program_id(0)
    block = pl.program_id(1)
    length = q_ref.shape[0]
    scale = HEAD_DIM ** (-0.5)

    @pl.when(block == 0)
    def _():
        fill_padded(qs, q_ref, HALO, length)
        fill_padded(ks, k_ref, TOP, length)
        fill_padded(vs, v_ref, TOP, length)
        for s in range(2):
            for a in range(n_taps):
                band = banded(band_line(base_ref[a, pl.ds(2 * pair + s, 1), :], key_half, 1))
                high = band.astype(BF16)
                band_ref[s, a, 0:WIN] = high
                band_ref[s, a, WIN : 2 * WIN] = high
                band_ref[s, a, 2 * WIN : 3 * WIN] = (band - high.astype(F32)).astype(BF16)

    row0 = pl.multiple_of(block * ROWS, ROWS)

    def body(n):
        start = start_ref[pl.ds(row0, EXT), :]
        place = row_numbers(row0 - HALO, EXT)
        firsts, lasts = [], []
        for k in range(n):
            base = row0 + ROWS - STEP * (k + 1) - OWN
            at = pl.multiple_of(TOP + base, 16)
            firsts.append(start - base)
            lasts.append(place - base)
            valid = lanes_between(firsts[k], lasts[k], WIN)
            rows = slice(k * EXT, (k + 1) * EXT)
            for s in range(2):
                cols = pl.ds(s * PAD_DIM, PAD_DIM)
                raw = dot_nt(qs[pl.ds(row0, EXT), cols], ks[pl.ds(at, WIN), cols])
                masked = jnp.where(valid, raw * scale, 0.0)
                high = masked.astype(BF16)
                inputs[s, rows, 0:WIN] = high
                inputs[s, rows, WIN : 2 * WIN] = (masked - high.astype(F32)).astype(BF16)
                inputs[s, rows, 2 * WIN : 3 * WIN] = high
        peaks = [None, None]
        for s in range(2):
            total = None
            for a in reversed(range(n_taps)):
                term = dot_nn(inputs[s, 0 : n * EXT, :], band_ref[s, a])
                total = term if total is None else pltpu.roll(total, 1, 0) + term
            for k in range(n):
                shown = lanes_between(
                    jnp.maximum(firsts[k][HALO:], key_half + 1),
                    jnp.minimum(lasts[k][HALO:], WIN - 2 - key_half),
                    WIN,
                )
                logits = jnp.where(shown, total[k * EXT + HALO : (k + 1) * EXT], NEG)
                logit_ref[s, k] = logits
                top = jnp.max(logits, axis=-1, keepdims=True)
                peaks[s] = top if peaks[s] is None else jnp.maximum(peaks[s], top)
        lane = lax.broadcasted_iota(jnp.int32, (ROWS, WIN), 1)
        own = (lane >= OWN) & (lane < WIN - OWN)
        sums = [None, None]
        for k in range(n):
            for s in range(2):
                expo = jnp.exp(logit_ref[s, k] - peaks[s])
                logit_ref[s, k] = expo
                part = jnp.sum(jnp.where(own, expo, 0.0), axis=-1, keepdims=True)
                sums[s] = part if sums[s] is None else sums[s] + part
        inverse = [1.0 / sums[s] for s in range(2)]
        outs = [None, None]
        for k in range(n):
            base = row0 + ROWS - STEP * (k + 1) - OWN
            at = pl.multiple_of(TOP + base, 16)
            probs = []
            for s in range(2):
                prob = logit_ref[s, k] * inverse[s]
                probs_ref[s, 0, k] = prob
                probs.append(jnp.where(own, prob, 0.0))
            for h in range(2):
                mixed = (
                    mix_ref[0, 2 * pair + h] * probs[0] + mix_ref[1, 2 * pair + h] * probs[1]
                ).astype(BF16)
                part = dot_nn(mixed, vs[pl.ds(at, WIN), pl.ds(h * PAD_DIM, PAD_DIM)])
                outs[h] = part if outs[h] is None else outs[h] + part
        for h in range(2):
            cols = slice(h * PAD_DIM, (h + 1) * PAD_DIM)
            out = outs[h]
            heads_ref[:, cols] = out
            factor = lax.rsqrt(jnp.sum(out * out, axis=-1, keepdims=True) * (1.0 / HEAD_DIM) + EPS)
            grouped_ref[:, cols] = (out * factor * gain_ref[:, cols]).astype(BF16)

    for n in range(1, most + 1):
        pl.when(count_ref[0, block] == n)(functools.partial(body, n))


def attend_forward(proj, start, counts, base, mix, gain):
    length = proj.shape[0]
    n_taps, heads = base.shape[:2]
    pairs = heads // 2
    blocks = length // ROWS
    key_half = 5
    most = windows_most(key_half)
    two = 2 * PAD_DIM
    grid_spec = pltpu.PrefetchScalarGridSpec(
        num_scalar_prefetch=2,
        grid=(pairs, blocks),
        in_specs=[
            pl.BlockSpec((length, two), lambda p, b, *_: (0, p)),
            pl.BlockSpec((length, two), lambda p, b, *_: (0, pairs + p)),
            pl.BlockSpec((length, two), lambda p, b, *_: (0, 2 * pairs + p)),
            pl.BlockSpec((HALO + length, 1), lambda p, b, *_: (0, 0)),
            pl.BlockSpec(base.shape, lambda p, b, *_: (0, 0, 0)),
            pl.BlockSpec((1, two), lambda p, b, *_: (0, p)),
        ],
        out_specs=[
            pl.BlockSpec((2, 1, most, ROWS, WIN), lambda p, b, *_: (p, b, 0, 0, 0)),
            pl.BlockSpec((ROWS, two), lambda p, b, *_: (b, p)),
            pl.BlockSpec((ROWS, two), lambda p, b, *_: (b, p)),
        ],
        scratch_shapes=[
            pltpu.VMEM((HALO + length, two), BF16),
            pltpu.VMEM((TOP + length + HALO, two), BF16),
            pltpu.VMEM((TOP + length + HALO, two), BF16),
            pltpu.VMEM((2, most, ROWS, WIN), F32),
            pltpu.VMEM((2, n_taps, 3 * WIN, WIN), BF16),
            pltpu.VMEM((2, most * EXT, 3 * WIN), BF16),
        ],
    )
    return pl.pallas_call(
        functools.partial(forward_kernel, n_taps, key_half, most),
        grid_spec=grid_spec,
        out_shape=[
            jax.ShapeDtypeStruct((heads, blocks, most, ROWS, WIN), F32),
            jax.ShapeDtypeStruct((length, heads * PAD_DIM), F32),
            jax.ShapeDtypeStruct((length, heads * PAD_DIM), BF16),
        ],
        compiler_params=pltpu.CompilerParams(vmem_limit_bytes=56 << 20),
        cost_estimate=COST,
        name="attend_forward",
    )(counts, mix, proj, proj, proj, start, base, gain)


def backward_kernel(
    n_taps, key_half, most, count_ref, mix_ref, q_ref, k_ref, v_ref, start_ref, base_ref, gain_ref,
    probs_ref, heads_ref, grad_ref, dqkv_ref, inner_ref, gain_grad_ref, tap_ref, mix_grad_ref,
    qs, ks, vs, dq_sum, dk_sum, dv_sum, taps, inputs, tap_sum, mixed_grad, t_back_ref, kept, inner_sum,
):
    pair = pl.program_id(0)
    block = pl.program_id(1)
    length = q_ref.shape[0]
    scale = HEAD_DIM ** (-0.5)

    @pl.when(block == 0)
    def _():
        fill_padded(qs, q_ref, HALO, length)
        fill_padded(ks, k_ref, TOP, length)
        fill_padded(vs, v_ref, TOP, length)
        dq_sum[...] = jnp.zeros_like(dq_sum)
        dk_sum[...] = jnp.zeros_like(dk_sum)
        dv_sum[...] = jnp.zeros_like(dv_sum)
        tap_sum[...] = jnp.zeros_like(tap_sum)
        gain_grad_ref[...] = jnp.zeros_like(gain_grad_ref)
        mix_grad_ref[...] = jnp.zeros_like(mix_grad_ref)
        for s in range(2):
            for a in range(n_taps):
                t_back_ref[s, a * WIN : (a + 1) * WIN, :] = banded(
                    band_line(base_ref[a, pl.ds(2 * pair + s, 1), :], key_half, -1)
                ).astype(BF16)

    row0 = pl.multiple_of(block * ROWS, ROWS)

    def body(n):
        grads = []
        for h in range(2):
            cols = slice(h * PAD_DIM, (h + 1) * PAD_DIM)
            out = heads_ref[:, cols]
            factor = lax.rsqrt(jnp.sum(out * out, axis=-1, keepdims=True) * (1.0 / HEAD_DIM) + EPS)
            unit = out * factor
            grad = grad_ref[:, cols]
            gain_grad_ref[:, cols] += jnp.sum(grad * unit, axis=0, keepdims=True)
            scaled = grad * gain_ref[:, cols]
            inner = jnp.sum(scaled * unit, axis=-1, keepdims=True) * (1.0 / HEAD_DIM)
            grads.append((factor * (scaled - unit * inner)).astype(BF16))
        lane = lax.broadcasted_iota(jnp.int32, (ROWS, WIN), 1)
        own = (lane >= OWN) & (lane < WIN - OWN)
        inner = [[None, None], [None, None]]
        for k in range(n):
            base = row0 + ROWS - STEP * (k + 1) - OWN
            at = pl.multiple_of(TOP + base, 16)
            probs = [jnp.where(own, probs_ref[s, 0, k], 0.0) for s in range(2)]
            for h in range(2):
                cols = pl.ds(h * PAD_DIM, PAD_DIM)
                grad_mixed = dot_nt(grads[h], vs[pl.ds(at, WIN), cols])
                mixed_grad[h, k] = grad_mixed
                for s in range(2):
                    part = jnp.sum(grad_mixed * probs[s], axis=-1, keepdims=True)
                    inner[h][s] = part if inner[h][s] is None else inner[h][s] + part
                mixed = (
                    mix_ref[0, 2 * pair + h] * probs[0] + mix_ref[1, 2 * pair + h] * probs[1]
                ).astype(BF16)
                dv_sum[pl.ds(at, WIN), cols] += dot_tn(mixed, grads[h])
        for h in range(2):
            for s in range(2):
                row = 2 * h + s
                mix_grad_ref[0, row : row + 1, :] += jnp.broadcast_to(
                    jnp.sum(inner[h][s], axis=0, keepdims=True), (1, PAD_DIM)
                )
        start = start_ref[pl.ds(row0, EXT), :]
        place = row_numbers(row0 - HALO, EXT)
        for s in range(2):
            cols = pl.ds(s * PAD_DIM, PAD_DIM)
            mix0 = mix_ref[s, 2 * pair]
            mix1 = mix_ref[s, 2 * pair + 1]
            delta = mix0 * inner[0][s] + mix1 * inner[1][s]
            query = qs[pl.ds(row0, EXT), cols]
            for k in range(n):
                grad_prob = mix0 * mixed_grad[0, k] + mix1 * mixed_grad[1, k]
                grad_logit = probs_ref[s, 0, k] * (grad_prob - delta)
                grown = jnp.concatenate([jnp.zeros((HALO, WIN), F32), grad_logit], axis=0)
                for a in range(n_taps):
                    moved = grown if a == 0 else pltpu.roll(grown, EXT - a, 0)
                    taps[k * EXT : (k + 1) * EXT, a * WIN : (a + 1) * WIN] = moved.astype(BF16)
            grad_inputs = dot_nn(taps[0 : n * EXT, :], t_back_ref[s])
            for k in range(n):
                base = row0 + ROWS - STEP * (k + 1) - OWN
                at = pl.multiple_of(TOP + base, 16)
                keys = ks[pl.ds(at, WIN), cols]
                mine = lanes_between(
                    jnp.maximum(start - base, OWN), jnp.minimum(place - base, WIN - OWN - 1), WIN
                )
                grad_masked = grad_inputs[k * EXT : (k + 1) * EXT]
                grad_score = jnp.where(mine, grad_masked * scale, 0.0).astype(BF16)
                dq_sum[pl.ds(row0, EXT), cols] += dot_nn(grad_score, keys)
                dk_sum[pl.ds(at, WIN), cols] += dot_tn(grad_score, query)
                raw = dot_nt(query, keys)
                inputs[k * EXT : (k + 1) * EXT, :] = jnp.where(mine, raw * scale, 0.0).astype(BF16)
            tap_sum[s] += dot_tn(inputs[0 : n * EXT, :], taps[0 : n * EXT, :])

    for n in range(1, most + 1):
        pl.when(count_ref[0, block] == n)(functools.partial(body, n))

    @pl.when(block == pl.num_programs(1) - 1)
    def _():
        inner = None
        sums = ((dq_sum, HALO, q_ref), (dk_sum, TOP, k_ref), (dv_sum, TOP, v_ref))
        for c, (total, top, given) in enumerate(sums):
            grad = total[top : top + length, :].astype(BF16)
            kept[pair, c] = grad
            part = jnp.sum(grad.astype(F32) * given[...].astype(F32), axis=-1, keepdims=True)
            inner = part if inner is None else inner + part

        @pl.when(pair == 0)
        def _():
            inner_sum[...] = inner

        @pl.when(pair > 0)
        def _():
            inner_sum[...] += inner

        row = lax.broadcasted_iota(jnp.int32, (WIN, WIN), 0)
        lane = lax.broadcasted_iota(jnp.int32, (WIN, WIN), 1)
        for s in range(2):
            for a in range(n_taps):
                whole = tap_sum[s, :, a * WIN : (a + 1) * WIN]
                for b in range(2 * key_half + 1):
                    part = jnp.where(lane - row == b - key_half, whole, 0.0)
                    part = jnp.sum(part, axis=0, keepdims=True)
                    part = jnp.sum(part, axis=1, keepdims=True)
                    at = a * (2 * key_half + 1) + b
                    tap_ref[s, at : at + 1, :] = jnp.broadcast_to(part, (1, PAD_DIM))

    pairs = kept.shape[0]

    @pl.when((block == pl.num_programs(1) - 1) & (pair == pairs - 1))
    def _():
        width = 2 * pairs * HEAD_DIM

        def rows_out(n, carry):
            at = pl.ds(pl.multiple_of(n * ROWS, ROWS), ROWS)
            for c in range(3):
                heads = [
                    kept[p, c, at, s * PAD_DIM : s * PAD_DIM + HEAD_DIM]
                    for p in range(pairs)
                    for s in range(2)
                ]
                dqkv_ref[at, c * width : (c + 1) * width] = jnp.concatenate(heads, axis=1)
            column = jnp.broadcast_to(inner_sum[at, :], (ROWS, PAD_DIM))
            inner_ref[pl.ds(n, 1), :] = column.T[0:1, :]
            return carry

        lax.fori_loop(0, length // ROWS, rows_out, 0)


def attend_backward(proj, start, counts, base, mix, gain, probs, heads_out, grad_grouped):
    length = proj.shape[0]
    n_taps, heads = base.shape[:2]
    pairs = heads // 2
    blocks = length // ROWS
    key_half = 5
    most = windows_most(key_half)
    two = 2 * PAD_DIM
    tap_rows = n_taps * (2 * key_half + 1)
    grid_spec = pltpu.PrefetchScalarGridSpec(
        num_scalar_prefetch=2,
        grid=(pairs, blocks),
        in_specs=[
            pl.BlockSpec((length, two), lambda p, b, *_: (0, p)),
            pl.BlockSpec((length, two), lambda p, b, *_: (0, pairs + p)),
            pl.BlockSpec((length, two), lambda p, b, *_: (0, 2 * pairs + p)),
            pl.BlockSpec((HALO + length, 1), lambda p, b, *_: (0, 0)),
            pl.BlockSpec(base.shape, lambda p, b, *_: (0, 0, 0)),
            pl.BlockSpec((1, two), lambda p, b, *_: (0, p)),
            pl.BlockSpec((2, 1, most, ROWS, WIN), lambda p, b, *_: (p, b, 0, 0, 0)),
            pl.BlockSpec((ROWS, two), lambda p, b, *_: (b, p)),
            pl.BlockSpec((ROWS, two), lambda p, b, *_: (b, p)),
        ],
        out_specs=[
            pl.BlockSpec((length, 3 * heads * HEAD_DIM), lambda p, b, *_: (0, 0)),
            pl.BlockSpec((length // ROWS, ROWS), lambda p, b, *_: (0, 0)),
            pl.BlockSpec((1, two), lambda p, b, *_: (0, p)),
            pl.BlockSpec((2, tap_rows, PAD_DIM), lambda p, b, *_: (p, 0, 0)),
            pl.BlockSpec((1, 4, PAD_DIM), lambda p, b, *_: (p, 0, 0)),
        ],
        scratch_shapes=[
            pltpu.VMEM((HALO + length, two), BF16),
            pltpu.VMEM((TOP + length + HALO, two), BF16),
            pltpu.VMEM((TOP + length + HALO, two), BF16),
            pltpu.VMEM((HALO + length, two), F32),
            pltpu.VMEM((TOP + length + HALO, two), F32),
            pltpu.VMEM((TOP + length + HALO, two), F32),
            pltpu.VMEM((most * EXT, n_taps * WIN), BF16),
            pltpu.VMEM((most * EXT, WIN), BF16),
            pltpu.VMEM((2, WIN, n_taps * WIN), F32),
            pltpu.VMEM((2, most, ROWS, WIN), F32),
            pltpu.VMEM((2, n_taps * WIN, WIN), BF16),
            pltpu.VMEM((pairs, 3, length, two), BF16),
            pltpu.VMEM((length, 1), F32),
        ],
    )
    return pl.pallas_call(
        functools.partial(backward_kernel, n_taps, key_half, most),
        grid_spec=grid_spec,
        out_shape=[
            jax.ShapeDtypeStruct((length, 3 * heads * HEAD_DIM), BF16),
            jax.ShapeDtypeStruct((length // ROWS, ROWS), F32),
            jax.ShapeDtypeStruct((1, heads * PAD_DIM), F32),
            jax.ShapeDtypeStruct((heads, tap_rows, PAD_DIM), F32),
            jax.ShapeDtypeStruct((pairs, 4, PAD_DIM), F32),
        ],
        compiler_params=pltpu.CompilerParams(vmem_limit_bytes=56 << 20),
        cost_estimate=COST,
        name="attend_backward",
    )(counts, mix, proj, proj, proj, start, base, gain, probs, heads_out, grad_grouped)


MESH_ID = pl.DeviceIdType.MESH


def ring_place(member, n):
    z, y = member // 2, member % 2
    return (1 - y) * z + y * (n - 1 - z)


def ring_member(place, n):
    upper = place // (n // 2)
    return (1 - upper) * 2 * place + upper * (2 * (n - 1 - place) + 1)


def ring_peers(n):
    place = ring_place(lax.axis_index("dp"), n)
    ahead = ring_member(lax.rem(place + 1, n), n)
    behind = ring_member(lax.rem(place + n - 1, n), n)
    return place, (ahead, behind)


def ring_scratch(arrays, n):
    return [pltpu.VMEM((2, n - 1) + a.shape[2:], a.dtype) for a in arrays] + [
        pltpu.SemaphoreType.DMA((2, len(arrays), n - 1))
    ] * 4


def ring_split(array, n):
    return array.reshape(n, 2, -1, array.shape[-1])


def make_ring(n, sources, ins, outs, scratch):
    count = len(ins)
    slots = scratch[:count]
    rs_send, rs_recv, ag_send, ag_recv = scratch[count:]
    place, to = ring_peers(n)

    def chunk(way, back):
        return lax.rem(place - back + 2 * n if way == 0 else place + back, n)

    def sum_copy(way, k, s, src):
        return pltpu.make_async_remote_copy(
            src_ref=src,
            dst_ref=slots[k].at[way, s],
            send_sem=rs_send.at[way, k, s],
            recv_sem=rs_recv.at[way, k, s],
            device_id={"dp": to[way]},
            device_id_type=MESH_ID,
        )

    def share_copy(way, k, s, c):
        return pltpu.make_async_remote_copy(
            src_ref=outs[k].at[c, way],
            dst_ref=outs[k].at[c, way],
            send_sem=ag_send.at[way, k, s],
            recv_sem=ag_recv.at[way, k, s],
            device_id={"dp": to[way]},
            device_id_type=MESH_ID,
        )

    def add(way, k, s, c, dst):
        total = slots[k][way, s].astype(F32) + ins[k][c, way].astype(F32)
        dst[...] = total.astype(dst.dtype)

    both = [(k, way) for k in range(count) for way in range(2)]

    def start():
        for k, way in both:
            sum_copy(way, k, 0, sources[k].at[chunk(way, 1), way]).start()

    def tick(now):
        @pl.when(now < n - 2)
        def _():
            for k, way in both:
                sum_copy(way, k, now, slots[k].at[way, now]).wait_recv()
                add(way, k, now, chunk(way, 2 + now), slots[k].at[way, now])
                sum_copy(way, k, now + 1, slots[k].at[way, now]).start()

        @pl.when(now == n - 2)
        def _():
            for k, way in both:
                sum_copy(way, k, n - 2, slots[k].at[way, n - 2]).wait_recv()
                add(way, k, n - 2, place, outs[k].at[place, way])
                share_copy(way, k, 0, place).start()

        @pl.when((now > n - 2) & (now < 2 * n - 3))
        def _():
            step = now - (n - 1)
            for k, way in both:
                share_copy(way, k, step, chunk(way, step + 1)).wait_recv()
                share_copy(way, k, step + 1, chunk(way, step + 1)).start()

        @pl.when(now == 2 * n - 3)
        def _():
            for k, way in both:
                share_copy(way, k, n - 2, chunk(way, n - 1)).wait_recv()

    def drain():
        def one(s, carry):
            for k, way in both:
                sum_copy(way, k, s, slots[k].at[way, s]).wait_send()
                share_copy(way, k, s, place).wait_send()
            return carry

        lax.fori_loop(0, n - 1, one, 0)

    return start, tick, drain


def small_rows(size):
    return -(-size // PAD_DIM)


def pack_small(arrays, rows):
    packed = []
    for a in arrays:
        flat = a.reshape(-1)
        packed.append(jnp.pad(flat, (0, -flat.size % PAD_DIM)).reshape(-1, PAD_DIM))
    packed = jnp.concatenate(packed, axis=0)
    return jnp.pad(packed, ((0, rows - packed.shape[0]), (0, 0)))


def unpack_small(packed, arrays):
    found, at = [], 0
    for a in arrays:
        rows = small_rows(a.size)
        found.append(packed[at : at + rows].reshape(-1)[: a.size].reshape(a.shape))
        at += rows
    return found


CHUNK = 128
GROUP = 256


LIVE = 4


def exchange_scratch(steps, width, ranks, share=True, chunk=CHUNK):
    half = ranks // 2
    live = steps if share else LIVE
    shared = [pltpu.VMEM((steps, ranks, chunk, width), BF16)] if share else []
    return [
        pltpu.VMEM((steps, half, chunk, width), BF16),
        pltpu.VMEM((steps, half, chunk, width), BF16),
        pltpu.VMEM((live, half, chunk, width), F32),
        pltpu.VMEM((steps, chunk, width), BF16),
        pltpu.VMEM((steps, chunk, width), BF16),
        pltpu.SemaphoreType.DMA((5, steps)),
        pltpu.SemaphoreType.DMA((5, steps)),
    ] + shared


def tensor_peers():
    me = lax.axis_index("tensor")
    return me, me + 1 - 2 * lax.rem(me, 2), lax.rem(me + 2, 4)


def meet(signals):
    barrier = pltpu.get_barrier_semaphore()
    for device in signals:
        pl.semaphore_signal(barrier, inc=1, device_id=device, device_id_type=MESH_ID)
    pl.semaphore_wait(barrier, len(signals))


def exchange_copies(scratch):
    out_a, in_a, _, out_b, in_b, send, recv, *full = scratch
    me, near, far = tensor_peers()

    def copy(kind, step, src, dst, peer):
        return pltpu.make_async_remote_copy(
            src_ref=src,
            dst_ref=dst,
            send_sem=send.at[kind, step],
            recv_sem=recv.at[kind, step],
            device_id={"tensor": peer},
            device_id_type=MESH_ID,
        )

    def cores(step):
        return copy(0, step, out_a.at[step], in_a.at[step], near)

    def chips(step):
        return copy(1, step, out_b.at[step], in_b.at[step], far)

    def back_far(step):
        return copy(2, step, full[0].at[step, me], full[0].at[step, me], far)

    def back_near(step):
        return copy(3, step, full[0].at[step, me], full[0].at[step, me], near)

    def pass_near(step):
        return copy(4, step, full[0].at[step, far], full[0].at[step, far], near)

    return cores, chips, back_far, back_near, pass_near


def exchange_stages(scratch, partial, live, chunk):
    out_a, in_a, kept, out_b, in_b = scratch[:5]
    cores, chips = exchange_copies(scratch)[:2]
    many = GROUP // chunk
    me, near, far = tensor_peers()

    def begin(step):
        for n, owner in ((0, near), (1, lax.rem(near + 2, 4))):

            def put(term, n=n):
                term = term.astype(BF16)
                for m in range(many):
                    out_a[step + m, n] = term[m * chunk : (m + 1) * chunk]

            partial(step, owner, put)
        for m in range(many):
            cores(step + m).start()
        for n, owner in ((1, far), (0, me)):

            def put(term, n=n):
                for m in range(many):
                    kept[lax.rem(step + m, live), n] = term[m * chunk : (m + 1) * chunk]

            partial(step, owner, put)

    def over(step):
        cores(step).wait_recv()
        out_b[step] = (kept[lax.rem(step, live), 1] + in_a[step, 1].astype(F32)).astype(BF16)
        chips(step).start()

    def total(step):
        chips(step).wait_recv()
        return kept[lax.rem(step, live), 0] + in_a[step, 0].astype(F32) + in_b[step].astype(F32)

    return begin, over, total


def make_exchange(steps, scratch, partial, local, between, chunk):
    cores, chips = exchange_copies(scratch)[:2]
    begin, over, total = exchange_stages(scratch, partial, LIVE, chunk)
    many = GROUP // chunk

    def tick(now):
        @pl.when((lax.rem(now, many) == 0) & (now < steps))
        def _():
            begin(now)

        between(now)

        @pl.when((now >= 1) & (now < steps + 1))
        def _():
            over(now - 1)

        @pl.when((now >= 2) & (now < steps + 2))
        def _():
            local(now - 2, total(now - 2))

    def drain():
        def one(step, carry):
            cores(step).wait_send()
            chips(step).wait_send()
            return carry

        lax.fori_loop(0, steps, one, 0)

    return tick, steps + 2, drain


def run_exchange(steps, scratch, partial, local, whole, beside=None, ahead=None):
    cores, chips, back_far, back_near, pass_near = exchange_copies(scratch)
    begin, over, total = exchange_stages(scratch, partial, steps, CHUNK)
    full = scratch[7]
    many = GROUP // CHUNK
    me = tensor_peers()[0]

    def send_group(group, carry):
        @pl.when(group < steps // many)
        def _():
            begin(group * many)

        @pl.when(group >= 1)
        def _():
            for m in range(many):
                over((group - 1) * many + m)

        return carry

    lax.fori_loop(0, steps // many + 1, send_group, 0)

    def sum_group(group, carry):
        if beside is not None:
            beside(group)
        for m in range(many):
            step = group * many + m
            full[step, me] = local(step, total(step)).astype(BF16)
            back_far(step).start()
            back_near(step).start()
        return carry

    lax.fori_loop(0, steps // many, sum_group, 0)
    if ahead is not None:
        ahead()

    def share_step(now, carry):
        @pl.when(now < steps)
        def _():
            back_far(now).wait_recv()
            pass_near(now).start()

        @pl.when(now >= 1)
        def _():
            back_near(now - 1).wait_recv()
            pass_near(now - 1).wait_recv()
            whole(now - 1, full)

        return carry

    lax.fori_loop(0, steps + 1, share_step, 0)

    def drain(step, carry):
        for copy in (cores, chips, back_far, back_near, pass_near):
            copy(step).wait_send()
        return carry

    lax.fori_loop(0, steps, drain, 0)


def run_ticks(count, *ticks):
    def one(now, carry):
        for tick in ticks:
            tick(now)
        return carry

    lax.fori_loop(0, count, one, 0)


def group_rows(step, chunk=CHUNK):
    return pl.ds(pl.multiple_of(step * chunk, chunk), GROUP)


def owner_cols(owner, width):
    return pl.ds(pl.multiple_of(owner * width, PAD_DIM), width)


def step_rows(step, chunk=CHUNK):
    return pl.ds(pl.multiple_of(step * chunk, chunk), chunk)


def first_entry_kernel(
    key_half, tokens_ref, w_in, gains_line_ref, segments_ref, proj_out, normed_out, factor_ref, gains_all_ref, gain_heads_ref,
    start_ref, count_ref, w_ref, proj_ref, normed_ref, load, store, full, gains_ref, gains_in, send, recv, gains_send, gains_recv,
):
    weights = pltpu.make_async_copy(w_in, w_ref, load.at[0])
    weights.start()
    rows, width = tokens_ref.shape
    ranks = normed_ref.shape[1] // width
    heads = width // HEAD_DIM
    steps, many = rows // CHUNK, GROUP // CHUNK
    me, near, far = tensor_peers()
    across = lax.rem(near + 2, 4)
    meet([{"tensor": near}, {"tensor": far}, {"tensor": across}])

    def copy(kind, step, src, dst, peer):
        return pltpu.make_async_remote_copy(
            src_ref=src,
            dst_ref=dst,
            send_sem=send.at[kind, step],
            recv_sem=recv.at[kind, step],
            device_id={"tensor": peer},
            device_id_type=MESH_ID,
        )

    def to_far(step):
        return copy(0, step, tokens_ref.at[step_rows(step)], full.at[step, me], far)

    def to_near(step):
        return copy(1, step, tokens_ref.at[step_rows(step)], full.at[step, me], near)

    def pass_near(step):
        return copy(2, step, full.at[step, far], full.at[step, far], near)

    def gains_copy(kind, peer, sender):
        return pltpu.make_async_remote_copy(
            src_ref=gains_ref,
            dst_ref=gains_in.at[sender],
            send_sem=gains_send.at[kind],
            recv_sem=gains_recv.at[sender],
            device_id={"tensor": peer},
            device_id_type=MESH_ID,
        )

    gains_ref[...] = jnp.zeros_like(gains_ref)
    for n in range(3):
        gains_ref[n : n + 1, :] = gains_line_ref[:, n * width : (n + 1) * width].astype(F32)
    peers = (near, far, across)
    for kind, peer in enumerate(peers):
        gains_copy(kind, peer, me).start()

    def send_all(step, carry):
        to_far(step).start()
        to_near(step).start()
        full[step, me] = tokens_ref[step_rows(step), :]
        return carry

    lax.fori_loop(0, steps, send_all, 0)
    gains_in[me] = gains_ref[...]
    for kind, peer in enumerate(peers):
        gains_copy(kind, peer, peer).wait()
    for n in range(ranks):
        gains_all_ref[:, n * width : (n + 1) * width] = gains_in[n]

    def stores(group):
        at = group_rows(group * many)
        return [
            pltpu.make_async_copy(src.at[at], dst.at[at], store.at[n, group])
            for n, (src, dst) in enumerate(((proj_ref, proj_out), (normed_ref, normed_out)))
        ]

    weights.wait()
    for h in range(heads):
        own = gains_ref[2:3, h * HEAD_DIM : (h + 1) * HEAD_DIM]
        gain_heads_ref[:, h * PAD_DIM : (h + 1) * PAD_DIM] = jnp.concatenate(
            [own, jnp.zeros((1, PAD_DIM - HEAD_DIM), F32)], axis=1
        )
    seqs, length = segments_ref.shape
    for n in range(seqs):
        lead = n * (HALO + length)
        start_ref[lead : lead + HALO, :] = jnp.full((HALO, 1), 1 << 20, jnp.int32)
        line = segments_ref[n : n + 1, :].astype(F32)
        for b in range(length // ROWS):
            column = jnp.broadcast_to(line[:, b * ROWS : (b + 1) * ROWS], (ROWS, ROWS)).T[:, 0:1]
            before = jnp.sum(jnp.where(line < column, 1.0, 0.0), axis=1, keepdims=True)
            at = lead + HALO + b * ROWS
            before = before.astype(jnp.int32)
            start_ref[at : at + ROWS, :] = before
            count = jnp.ones((1, 1), jnp.int32)
            for k in range(1, windows_most(key_half)):
                reach = b * ROWS + ROWS - STEP * k + key_half
                count = count + jnp.where(before[0:1] < reach, 1, 0)
            count_ref[n : n + 1, b : b + 1] = count

    def tick(now):
        @pl.when(now < steps)
        def _():
            to_far(now).wait_recv()
            pass_near(now).start()

        @pl.when(now >= 1)
        def _():
            to_near(now - 1).wait_recv()
            pass_near(now - 1).wait_recv()

        @pl.when((now >= many) & (lax.rem(now, many) == 0))
        def _():
            first = now - many
            at = group_rows(first)
            blocks = [
                jnp.concatenate([full[first + m, n] for m in range(many)], axis=0).astype(F32)
                for n in range(ranks)
            ]
            squares = sum(jnp.sum(block * block, axis=-1, keepdims=True) for block in blocks)
            factor = lax.rsqrt(squares * (1.0 / (ranks * width)) + EPS)
            factor_ref[at, :] = factor
            for n, block in enumerate(blocks):
                cols = slice(n * width, (n + 1) * width)
                normed_ref[at, cols] = (block * factor * gains_all_ref[0:1, cols]).astype(BF16)
            for c in range(3):
                out = dot_nn(normed_ref[at, :], w_ref[c])
                empty = jnp.zeros((GROUP, PAD_DIM - HEAD_DIM), F32)
                for h in range(heads):
                    head = jnp.concatenate([out[:, h * HEAD_DIM : (h + 1) * HEAD_DIM], empty], axis=1)
                    lane = (c * heads + h) * PAD_DIM
                    proj_ref[at, lane : lane + PAD_DIM] = head.astype(BF16)
            for one in stores(first // many):
                one.start()

    run_ticks(steps + 1, tick)

    def stored(group, carry):
        for one in stores(group):
            one.wait()
        return carry

    lax.fori_loop(0, steps // many, stored, 0)

    def drain(step, carry):
        to_far(step).wait_send()
        to_near(step).wait_send()
        pass_near(step).wait_send()
        return carry

    lax.fori_loop(0, steps, drain, 0)


def first_entry(tokens, w_qkv, gains, segments, key_half):
    rows, width = tokens.shape
    full_width = w_qkv.shape[1]
    ranks = full_width // width
    steps = rows // CHUNK
    padded = 3 * width // HEAD_DIM * PAD_DIM
    vmem = pl.BlockSpec(memory_space=pltpu.VMEM)
    anywhere = pl.BlockSpec(memory_space=pl.ANY)
    return pl.pallas_call(
        functools.partial(first_entry_kernel, key_half),
        out_shape=[
            jax.ShapeDtypeStruct((rows, padded), BF16),
            jax.ShapeDtypeStruct((rows, full_width), BF16),
            jax.ShapeDtypeStruct((rows, 1), F32),
            jax.ShapeDtypeStruct((8, full_width), F32),
            jax.ShapeDtypeStruct((1, width // HEAD_DIM * PAD_DIM), F32),
            jax.ShapeDtypeStruct((segments.shape[0] * (HALO + segments.shape[1]), 1), jnp.int32),
            jax.ShapeDtypeStruct((segments.shape[0], segments.shape[1] // ROWS), jnp.int32),
        ],
        in_specs=[vmem, anywhere, vmem, vmem],
        out_specs=[anywhere, anywhere] + [vmem] * 5,
        scratch_shapes=[
            pltpu.VMEM(w_qkv.shape, BF16),
            pltpu.VMEM((rows, padded), BF16),
            pltpu.VMEM((rows, full_width), BF16),
            pltpu.SemaphoreType.DMA((1,)),
            pltpu.SemaphoreType.DMA((2, rows // GROUP)),
            pltpu.VMEM((steps, ranks, CHUNK, width), BF16),
            pltpu.VMEM((8, width), F32),
            pltpu.VMEM((ranks, 8, width), F32),
            pltpu.SemaphoreType.DMA((3, steps)),
            pltpu.SemaphoreType.DMA((3, steps)),
            pltpu.SemaphoreType.DMA((3,)),
            pltpu.SemaphoreType.DMA((ranks,)),
        ],
        compiler_params=pltpu.CompilerParams(
            collective_id=4, has_side_effects=True, vmem_limit_bytes=60 << 20
        ),
        cost_estimate=COST,
        name="first_entry",
    )(tokens, w_qkv, gains, segments)


def attn_exit_kernel(
    grouped_ref, w_out_ref, tokens_ref, gain_ref, cot_in, w_gate_up_in, w_down_in, hidden_local_ref,
    hidden_out, normed_out, w_ref, act_out, grad_gate_out, grad_up_out, hidden_ref, normed_ref, act_ref,
    grad_gate_ref, grad_up_ref, grad_act, cot_ref, w_gate_up_ref, w_down_ref, load, store, *scratch
):
    loads = [
        pltpu.make_async_copy(src, dst, load.at[n])
        for n, (src, dst) in enumerate(
            ((cot_in, cot_ref), (w_down_in, w_down_ref), (w_gate_up_in, w_gate_up_ref))
        )
    ]
    for one in loads:
        one.start()
    rows, width = tokens_ref.shape
    ranks = hidden_ref.shape[1] // width
    many = GROUP // CHUNK
    for h in range(width // HEAD_DIM):
        lead = h * PAD_DIM
        w_ref[lead : lead + HEAD_DIM, :] = w_out_ref[h * HEAD_DIM : (h + 1) * HEAD_DIM, :]
        w_ref[lead + HEAD_DIM : lead + PAD_DIM, :] = jnp.zeros((PAD_DIM - HEAD_DIM, w_ref.shape[1]), BF16)

    def partial(step, owner, put):
        put(dot_nn(grouped_ref[group_rows(step), :], w_ref[:, owner_cols(owner, width)]))

    def local(step, total):
        hidden = tokens_ref[step_rows(step), :].astype(F32) + total
        hidden_local_ref[step_rows(step), :] = hidden
        return hidden

    def whole(step, full):
        squares = None
        for n in range(ranks):
            block = full[step, n]
            hidden_ref[step_rows(step), n * width : (n + 1) * width] = block
            block = block.astype(F32)
            part = jnp.sum(block * block, axis=-1, keepdims=True)
            squares = part if squares is None else squares + part
        factor = lax.rsqrt(squares * (1.0 / (ranks * width)) + EPS)
        for n in range(ranks):
            cols = slice(n * width, (n + 1) * width)
            unit = full[step, n].astype(F32) * factor
            normed_ref[step_rows(step), cols] = (unit * gain_ref[1:2, cols]).astype(BF16)

        @pl.when(lax.rem(step, many) == many - 1)
        def _():
            at = group_rows(step - (many - 1))
            gate = dot_nn(normed_ref[at, :], w_gate_up_ref[0])
            up = dot_nn(normed_ref[at, :], w_gate_up_ref[1])
            sigmoid = jax.nn.sigmoid(gate)
            swish = gate * sigmoid
            grad = grad_act[at, :]
            act_ref[at, :] = (swish * up).astype(BF16)
            grad_gate_ref[at, :] = (grad * up * sigmoid * (1.0 + gate * (1.0 - sigmoid))).astype(BF16)
            grad_up_ref[at, :] = (grad * swish).astype(BF16)
            for one in stores(step // many):
                one.start()

    def stores(group):
        at = group_rows(group * many)
        pairs = (
            (hidden_ref, hidden_out),
            (normed_ref, normed_out),
            (act_ref, act_out),
            (grad_gate_ref, grad_gate_out),
            (grad_up_ref, grad_up_out),
        )
        return [
            pltpu.make_async_copy(src.at[at], dst.at[at], store.at[n, group])
            for n, (src, dst) in enumerate(pairs)
        ]

    def beside(group):
        @pl.when(group == 0)
        def _():
            loads[0].wait()
            loads[1].wait()

        at = group_rows(group * many)
        grad_act[at, :] = dot_nt(cot_ref[at, :], w_down_ref[...])

    me, near, far = tensor_peers()
    meet([{"tensor": near}, {"tensor": far}])
    run_exchange(rows // CHUNK, scratch, partial, local, whole, beside, loads[2].wait)

    def stored(group, carry):
        for one in stores(group):
            one.wait()
        return carry

    lax.fori_loop(0, rows // GROUP, stored, 0)


def attn_exit(grouped, w_out, tokens, gain, full_cot, w_gate_up, w_down):
    rows, width = tokens.shape
    full_width = w_out.shape[1]
    units = w_down.shape[0]
    vmem = pl.BlockSpec(memory_space=pltpu.VMEM)
    anywhere = pl.BlockSpec(memory_space=pl.ANY)
    return pl.pallas_call(
        attn_exit_kernel,
        out_shape=[
            jax.ShapeDtypeStruct((rows, width), F32),
            jax.ShapeDtypeStruct((rows, full_width), BF16),
            jax.ShapeDtypeStruct((rows, full_width), BF16),
            jax.ShapeDtypeStruct((grouped.shape[1], full_width), BF16),
        ]
        + [jax.ShapeDtypeStruct((rows, units), BF16)] * 3,
        in_specs=[vmem] * 4 + [anywhere] * 3,
        out_specs=[vmem, anywhere, anywhere, vmem] + [anywhere] * 3,
        scratch_shapes=[pltpu.VMEM((rows, full_width), BF16)] * 2
        + [pltpu.VMEM((rows, units), BF16)] * 3
        + [
            pltpu.VMEM((rows, units), F32),
            pltpu.VMEM(full_cot.shape, BF16),
            pltpu.VMEM(w_gate_up.shape, BF16),
            pltpu.VMEM(w_down.shape, BF16),
            pltpu.SemaphoreType.DMA((3,)),
            pltpu.SemaphoreType.DMA((5, rows // GROUP)),
        ]
        + exchange_scratch(rows // CHUNK, width, full_width // width),
        compiler_params=pltpu.CompilerParams(
            collective_id=1, has_side_effects=True, vmem_limit_bytes=56 << 20
        ),
        cost_estimate=COST,
        name="attn_exit",
    )(grouped, w_out, tokens, gain, full_cot, w_gate_up, w_down)


def mlp_exit_kernel(
    gate_ref, up_ref, w_ref, hidden_in, cot_in, hidden_local_ref, cot_local_ref, gain_ref, gain_local_ref,
    grad_attn_ref, grad_hidden_ref, gain_grad_ref, grad_local, hidden_ref, cot_ref, load, *scratch
):
    loads = [
        pltpu.make_async_copy(hidden_in, hidden_ref, load.at[0]),
        pltpu.make_async_copy(cot_in, cot_ref, load.at[1]),
    ]
    for one in loads:
        one.start()
    rows, width = cot_local_ref.shape
    full_width = hidden_ref.shape[1]
    ranks = full_width // width
    gain_grad_ref[...] = jnp.zeros_like(gain_grad_ref)

    def partial(step, owner, put):
        cols = owner_cols(owner, width)
        at = group_rows(step)
        put(dot_nt(gate_ref[at, :], w_ref[0, cols, :]) + dot_nt(up_ref[at, :], w_ref[1, cols, :]))

    def local(step, total):
        grad_local[step_rows(step), :] = total
        return total

    def whole(step, full):
        at = step_rows(step)
        squares, inner = None, None
        for n in range(ranks):
            cols = slice(n * width, (n + 1) * width)
            hidden = hidden_ref[at, cols].astype(F32)
            part = jnp.sum(hidden * hidden, axis=-1, keepdims=True)
            squares = part if squares is None else squares + part
            part = jnp.sum(full[step, n].astype(F32) * gain_ref[1:2, cols] * hidden, axis=-1, keepdims=True)
            inner = part if inner is None else inner + part
        factor = lax.rsqrt(squares * (1.0 / full_width) + EPS)
        inner = inner * factor * (1.0 / full_width)
        for n in range(ranks):
            cols = slice(n * width, (n + 1) * width)
            unit = hidden_ref[at, cols].astype(F32) * factor
            grad = full[step, n].astype(F32) * gain_ref[1:2, cols] - unit * inner
            grad_attn_ref[at, cols] = (cot_ref[at, cols].astype(F32) + factor * grad).astype(BF16)
        total = grad_local[at, :]
        unit = hidden_local_ref[at, :] * factor
        gain_grad_ref[...] += jnp.sum(total * unit, axis=0, keepdims=True)
        grad_hidden_ref[at, :] = cot_local_ref[at, :].astype(F32) + factor * (
            total * gain_local_ref[...] - unit * inner
        )

    me, near, far = tensor_peers()
    meet([{"tensor": near}, {"tensor": far}])

    def ahead():
        for one in loads:
            one.wait()

    run_exchange(rows // CHUNK, scratch, partial, local, whole, ahead=ahead)


def mlp_exit(grad_gate, grad_up, w_gate_up, hidden, full_cot, hidden_local, cotangent, gain, gain_local):
    rows, width = hidden_local.shape
    full_width = hidden.shape[1]
    vmem = pl.BlockSpec(memory_space=pltpu.VMEM)
    return pl.pallas_call(
        mlp_exit_kernel,
        out_shape=[
            jax.ShapeDtypeStruct((rows, full_width), BF16),
            jax.ShapeDtypeStruct((rows, width), F32),
            jax.ShapeDtypeStruct((1, width), F32),
        ],
        in_specs=[vmem] * 3 + [pl.BlockSpec(memory_space=pl.ANY)] * 2 + [vmem] * 4,
        out_specs=[vmem] * 3,
        scratch_shapes=[
            pltpu.VMEM((rows, width), F32),
            pltpu.VMEM(hidden.shape, BF16),
            pltpu.VMEM(full_cot.shape, BF16),
            pltpu.SemaphoreType.DMA((2,)),
        ]
        + exchange_scratch(rows // CHUNK, width, full_width // width),
        compiler_params=pltpu.CompilerParams(
            collective_id=2, has_side_effects=True, vmem_limit_bytes=56 << 20
        ),
        cost_estimate=COST,
        name="mlp_exit",
    )(grad_gate, grad_up, w_gate_up, hidden, full_cot, hidden_local, cotangent, gain, gain_local)


def last_exit_kernel(
    n_ring, count, factor_ref, inner_ref, gain_ref, small_ref, *refs,
):
    given, sources, refs = refs[:7], refs[7 : 7 + count], refs[7 + count :]
    tokens_grad_ref, out_ref, small_sum_ref = refs[:3]
    outs, refs = refs[3 : 3 + count], refs[3 + count :]
    here_too, ins, load, refs = refs[:7], refs[7 : 7 + count], refs[7 + count], refs[8 + count :]
    grad_ref, w_ref, tokens_ref, grad_hidden_ref, act_ref, w_down_ref, hidden_ref = here_too
    loads = [
        pltpu.make_async_copy(src, dst, load.at[n])
        for n, (src, dst) in enumerate(zip((*sources, *given), (*ins, *here_too)))
    ]
    for one in loads:
        one.start()
    gain_grad, mine, all_small, small_send, small_recv = refs[:5]
    inner_in, inner_sum, inner_col, inner_send, inner_recv = refs[5:10]
    ring_refs, scratch = refs[10 : 14 + count], refs[14 + count :]
    rows, width = tokens_ref.shape
    full_width = w_ref.shape[1]
    half = rows // GROUP
    me, near, far = tensor_peers()
    here = lax.axis_index("dp")
    gain_grad[...] = jnp.zeros_like(gain_grad)

    def partial(step, owner, put):
        cols = owner_cols(owner, width)

        @pl.when(step < half)
        def _():
            total = None
            for c in range(3):
                term = dot_nt(grad_ref[group_rows(step, GROUP), c * width : (c + 1) * width], w_ref[c, cols, :])
                total = term if total is None else total + term
            put(total)

        @pl.when(step >= half)
        def _():
            put(dot_nn(act_ref[group_rows(step - half, GROUP), :], w_down_ref[:, cols]))

    def between(now):
        def copy(n, src, peer):
            return pltpu.make_async_remote_copy(
                src_ref=src,
                dst_ref=inner_in.at[n],
                send_sem=inner_send.at[n],
                recv_sem=inner_recv.at[n],
                device_id={"tensor": peer},
                device_id_type=MESH_ID,
            )

        @pl.when(now == 0)
        def _():
            copy(0, inner_ref, near).start()

        @pl.when(now == 1)
        def _():
            copy(0, inner_ref, near).wait()
            inner_sum[...] = inner_ref[...] + inner_in[0]
            copy(1, inner_sum, far).start()

        @pl.when(now == 2)
        def _():
            copy(1, inner_sum, far).wait()
            total = (inner_sum[...] + inner_in[1]) * (1.0 / full_width)
            for n in range(rows // ROWS):
                line = jnp.broadcast_to(total[n : n + 1, :], (ROWS, ROWS))
                inner_col[n * ROWS : (n + 1) * ROWS, :] = line.T[:, 0:1]

    def local(step, total):
        @pl.when(step < half)
        def _():
            at = step_rows(step, GROUP)
            factor = factor_ref[at, :]
            unit = tokens_ref[at, :].astype(F32) * factor
            gain_grad[...] += jnp.sum(total * unit, axis=0, keepdims=True)
            tokens_grad_ref[at, :] = grad_hidden_ref[at, :] + factor * (
                total * gain_ref[...] - unit * inner_col[at, :]
            )

        @pl.when(step >= half)
        def _():
            at = step_rows(step - half, GROUP)
            out_ref[at, :] = (hidden_ref[at, :] + total).astype(BF16)

    def small_copy(peer, sender):
        return pltpu.make_async_remote_copy(
            src_ref=mine,
            dst_ref=all_small.at[sender],
            send_sem=small_send.at[peer],
            recv_sem=small_recv.at[sender],
            device_id={"dp": peer},
            device_id_type=MESH_ID,
        )

    def small_start(now):
        @pl.when(now == half + 2)
        def _():
            mine[...] = small_ref[...]
            for n in range(width // PAD_DIM):
                mine[n : n + 1, :] = gain_grad[:, n * PAD_DIM : (n + 1) * PAD_DIM]
            all_small[here] = mine[...]

            def one(away, carry):
                small_copy(lax.rem(here + away, n_ring), here).start()
                return carry

            lax.fori_loop(1, n_ring, one, 0)

    barrier = pltpu.get_barrier_semaphore()
    for peer in (near, far):
        pl.semaphore_signal(barrier, inc=1, device_id={"tensor": peer}, device_id_type=MESH_ID)

    def greet(away, carry):
        peer = lax.rem(here + away, n_ring)
        pl.semaphore_signal(barrier, inc=1, device_id={"dp": peer}, device_id_type=MESH_ID)
        return carry

    lax.fori_loop(1, n_ring, greet, 0)
    pl.semaphore_wait(barrier, 2 + n_ring - 1)

    ring_start, ring_tick, ring_drain = make_ring(n_ring, sources, ins, outs, ring_refs)
    tick, ticks, drain = make_exchange(2 * half, scratch, partial, local, between, GROUP)
    ring_start()
    for one in loads:
        one.wait()
    run_ticks(max(ticks, 2 * (n_ring - 1)), ring_tick, tick, small_start)

    def one(away, carry):
        peer = lax.rem(here + away, n_ring)
        small_copy(peer, peer).wait()
        return carry

    lax.fori_loop(1, n_ring, one, 0)

    def add(n, total):
        return total + all_small[n]

    small_sum_ref[...] = lax.fori_loop(1, n_ring, add, all_small[0])
    drain()
    ring_drain()


def last_exit(
    grad_proj, w_qkv, tokens, grad_hidden, factor, inner, gain, act, w_down, hidden_local, small, sums
):
    rows, width = tokens.shape
    n_ring = lax.axis_size("dp")
    count = len(sums)
    split = [ring_split(a, n_ring) for a in sums]
    gain_rows = width // PAD_DIM
    need = gain_rows + sum(small_rows(a.size) for a in small)
    packed = jnp.pad(pack_small(small, need - gain_rows), ((gain_rows, -need % 8), (0, 0)))
    vmem = pl.BlockSpec(memory_space=pltpu.VMEM)
    steps = 2 * rows // GROUP
    given = (grad_proj, w_qkv, tokens, grad_hidden, act, w_down, hidden_local)
    tokens_grad, out, packed, *totals = pl.pallas_call(
        functools.partial(last_exit_kernel, n_ring, count),
        out_shape=[
            jax.ShapeDtypeStruct((rows, width), F32),
            jax.ShapeDtypeStruct((rows, width), BF16),
            jax.ShapeDtypeStruct(packed.shape, F32),
        ]
        + [jax.ShapeDtypeStruct(a.shape, a.dtype) for a in split],
        in_specs=[vmem] * 4 + [pl.BlockSpec(memory_space=pl.ANY)] * (7 + count),
        out_specs=[vmem] * (3 + count),
        scratch_shapes=[pltpu.VMEM(a.shape, a.dtype) for a in (*given, *split)]
        + [
            pltpu.SemaphoreType.DMA((7 + count,)),
            pltpu.VMEM((1, width), F32),
            pltpu.VMEM(packed.shape, F32),
            pltpu.VMEM((n_ring,) + packed.shape, F32),
            pltpu.SemaphoreType.DMA((n_ring,)),
            pltpu.SemaphoreType.DMA((n_ring,)),
            pltpu.VMEM((2,) + inner.shape, F32),
            pltpu.VMEM(inner.shape, F32),
            pltpu.VMEM((rows, 1), F32),
            pltpu.SemaphoreType.DMA((2,)),
            pltpu.SemaphoreType.DMA((2,)),
        ]
        + ring_scratch(split, n_ring)
        + exchange_scratch(steps, width, w_qkv.shape[1] // width, False, GROUP),
        compiler_params=pltpu.CompilerParams(
            collective_id=3, has_side_effects=True, vmem_limit_bytes=62 << 20
        ),
        cost_estimate=COST,
        name="last_exit",
    )(factor, inner, gain, packed, *given, *split)
    gain_grad = packed[:gain_rows].reshape(width)
    totals = [t.reshape(a.shape) for t, a in zip(totals, sums)]
    return tokens_grad, gain_grad, out, unpack_small(packed[gain_rows:], small), totals


def widen_kernel(
    early_steps, gate_ref, early_ref, late_ref, down_ref, out_ref, query_ref, key_ref, value_ref,
    tokens_ref, layer_ref, gate_up_to, down_to, out_to, qkv_to, tokens_to, layer_to,
):
    step = pl.program_id(0)
    tokens_to[...] = tokens_ref[...]
    layer_to[...] = layer_ref[...]
    gate_up_to[0] = gate_ref[...].astype(F32)

    @pl.when(step < early_steps)
    def _():
        gate_up_to[1] = early_ref[...].astype(F32)

    @pl.when(step >= early_steps)
    def _():
        gate_up_to[1] = late_ref[...].astype(F32)

    down_to[...] = down_ref[...].astype(F32)
    out_to[...] = out_ref[...].astype(F32)
    for c, ref in enumerate((query_ref, key_ref, value_ref)):
        qkv_to[c] = ref[...].astype(F32)


def widen(gate, early_up, late_up, down, out, query, key, value, tokens_grad, layer_out):
    steps = 8
    full_width, units = gate.shape
    rows = full_width // steps
    early_steps = early_up.shape[0] // rows
    width = query.shape[1]

    def block(array):
        return pl.BlockSpec((array.shape[0] // steps, array.shape[1]), lambda i: (i, 0))

    return pl.pallas_call(
        functools.partial(widen_kernel, early_steps),
        grid=(steps,),
        out_shape=[
            jax.ShapeDtypeStruct((2, full_width, units), F32),
            jax.ShapeDtypeStruct(down.shape, F32),
            jax.ShapeDtypeStruct(out.shape, F32),
            jax.ShapeDtypeStruct((3, full_width, width), F32),
            jax.ShapeDtypeStruct(tokens_grad.shape, tokens_grad.dtype),
            jax.ShapeDtypeStruct(layer_out.shape, layer_out.dtype),
        ],
        in_specs=[
            block(gate),
            pl.BlockSpec((rows, units), lambda i: (jnp.minimum(i, early_steps - 1), 0)),
            pl.BlockSpec((rows, units), lambda i: (jnp.maximum(i - early_steps, 0), 0)),
            block(down),
            block(out),
            block(query),
            block(key),
            block(value),
            block(tokens_grad),
            block(layer_out),
        ],
        out_specs=[
            pl.BlockSpec((2, rows, units), lambda i: (0, i, 0)),
            block(down),
            block(out),
            pl.BlockSpec((3, rows, width), lambda i: (0, i, 0)),
            block(tokens_grad),
            block(layer_out),
        ],
        compiler_params=pltpu.CompilerParams(vmem_limit_bytes=60 << 20),
        name="widen",
    )(gate, early_up, late_up, down, out, query, key, value, tokens_grad, layer_out)


def banded(line):
    return pltpu.roll(jnp.broadcast_to(line, (WIN, WIN)), 0, 1, stride=1, stride_axis=0)


def band_line(taps, half, sign):
    lane = lax.broadcasted_iota(jnp.int32, (1, WIN), 1)
    line = jnp.zeros((1, WIN), F32)
    for b in range(taps.shape[1]):
        line = jnp.where(lane == (sign * (b - half)) % WIN, taps[:, b : b + 1], line)
    return line


def cut_heads(array, axis):
    shape = array.shape
    heads = shape[axis] // PAD_DIM
    split = array.reshape(shape[:axis] + (heads, PAD_DIM) + shape[axis + 1 :])
    cut = lax.slice_in_dim(split, 0, HEAD_DIM, axis=axis + 1)
    return cut.reshape(shape[:axis] + (heads * HEAD_DIM,) + shape[axis + 1 :])


def on_device(
    tokens, segments, attn_gain, w_qkv, kq_kernel, head_mix, group_gain, w_out, mlp_gain, w_gate_up,
    w_down, cotangent,
):
    rows_here, local_width = tokens.shape
    seq_count, length = segments.shape
    heads_here = local_width // HEAD_DIM
    n_taps, key_taps = kq_kernel.shape[1:]
    key_half = key_taps // 2

    full_width = w_qkv.shape[1]
    own_gains = jnp.concatenate([attn_gain, mlp_gain, group_gain])[None]
    taps, mixes = kq_kernel.transpose(1, 0, 2), head_mix.T
    proj, normed_one, scale_one, gains, gain_heads, start, counts = first_entry(
        tokens, w_qkv, own_gains, segments, key_half
    )
    starts = [start[n * (HALO + length) : (n + 1) * (HALO + length)] for n in range(seq_count)]
    counts = [counts[n : n + 1] for n in range(seq_count)]
    cot_here, proj = lax.optimization_barrier((cotangent, proj))
    full_cot = lax.all_gather(cot_here, "tensor", axis=1, tiled=True)

    kept = []
    for n in range(seq_count):
        rows = slice(n * length, (n + 1) * length)
        kept.append(
            attend_forward(proj[rows], starts[n], counts[n], taps, mixes, gain_heads)
        )
    grouped = jnp.concatenate([one[2] for one in kept], axis=0)
    grouped, full_cot = lax.optimization_barrier((grouped, full_cot))
    hidden_local, hidden, normed_two, w_out_pad, act, grad_gate, grad_up = attn_exit(
        grouped, w_out, tokens, gains, full_cot, w_gate_up, w_down
    )

    grad_down = dot_tn(act, full_cot).astype(BF16)
    early_rows = int(full_width * EARLY_SHARE)
    early_up = dot_tn(normed_two[:, :early_rows], grad_up).astype(BF16)
    grad_gate, early_up, grad_down = lax.optimization_barrier((grad_gate, early_up, grad_down))
    early_up, grad_down = lax.psum((early_up, grad_down), "dp")
    grad_attn, grad_hidden_local, grad_gain_two = mlp_exit(
        grad_gate, grad_up, w_gate_up, hidden, full_cot, hidden_local, cotangent, gains,
        mlp_gain.astype(F32)[None],
    )
    grad_gate_w = dot_tn(normed_two, grad_gate).astype(BF16)
    late_up = dot_tn(normed_two[:, early_rows:], grad_up).astype(BF16)
    grad_w_out = cut_heads(dot_tn(grouped, grad_attn).astype(BF16), 0)

    grad_grouped = dot_nt(grad_attn, w_out_pad)
    parts = []
    for n in range(seq_count):
        rows = slice(n * length, (n + 1) * length)
        parts.append(
            attend_backward(
                proj[rows], starts[n], counts[n], taps, mixes, gain_heads, kept[n][0], kept[n][1],
                grad_grouped[rows],
            )
        )
    grad_proj = jnp.concatenate([one[0] for one in parts], axis=0)
    inner_part = jnp.concatenate([one[1] for one in parts], axis=0)
    grad_group_gain = sum(cut_heads(one[2][0], 0) for one in parts)
    grad_kernel = sum(one[3][:, :, 0] for one in parts).reshape(heads_here, n_taps, key_taps)
    grad_mix = sum(one[4][:, :, 0] for one in parts).reshape(heads_here, 2)

    grad_qkv = [
        dot_tn(normed_one, grad_proj[:, c * local_width : (c + 1) * local_width]).astype(BF16)
        for c in range(3)
    ]
    tokens_grad, grad_gain_one, layer_out, small, sums = last_exit(
        grad_proj, w_qkv, tokens, grad_hidden_local, scale_one, inner_part, attn_gain.astype(F32)[None],
        act, w_down, hidden_local, (grad_kernel, grad_mix, grad_group_gain, grad_gain_two[0]),
        (grad_gate_w, late_up, grad_w_out, *grad_qkv),
    )
    grad_kernel, grad_mix, grad_group_gain, grad_gain_two = small
    grad_gate_w, late_up, grad_w_out, *grad_qkv = sums
    grad_gate_up, grad_down, grad_w_out, grad_qkv, tokens_grad, layer_out = widen(
        grad_gate_w, early_up, late_up, grad_down, grad_w_out, *grad_qkv, tokens_grad, layer_out
    )
    return (
        layer_out,
        tokens_grad,
        grad_gain_one,
        grad_qkv,
        grad_kernel,
        grad_mix,
        grad_group_gain,
        grad_w_out,
        grad_gain_two,
        grad_gate_up,
        grad_down,
    )


def solution(mesh):
    in_specs = (
        P("dp", "tensor"),
        P("dp", None),
        P("tensor"),
        P(None, None, "tensor"),
        P("tensor", None, None),
        P("tensor", None),
        P("tensor"),
        P("tensor", None),
        P("tensor"),
        P(None, None, "tensor"),
        P("tensor", None),
        P("dp", "tensor"),
    )
    out_specs = (
        P("dp", "tensor"),
        P("dp", "tensor"),
        P("tensor"),
        P(None, None, "tensor"),
        P("tensor", None, None),
        P("tensor", None),
        P("tensor"),
        P("tensor", None),
        P("tensor"),
        P(None, None, "tensor"),
        P("tensor", None),
    )
    return jax.shard_map(
        on_device, mesh=mesh, in_specs=in_specs, out_specs=out_specs, check_vma=False
    )
```

```python
import functools

import jax
import jax.numpy as jnp
from jax import lax
from jax.experimental import pallas as pl
from jax.experimental.pallas import tpu as pltpu
from jax.sharding import PartitionSpec as P

HEAD_DIM = 96
PAD_DIM = 128
DOC_MOST = 512
EPS = 1e-05
NEG = -1e30

COST = pl.CostEstimate(flops=1 << 20, bytes_accessed=1 << 10, transcendentals=0)
EARLY_SHARE = 0.75
ROWS = 128
HALO = 16
WIN = 256
OWN = 16
STEP = WIN - 2 * OWN
TOP = 256
EXT = ROWS + HALO

F32 = jnp.float32
BF16 = jnp.bfloat16


def windows_most(key_half):
    return -(-(DOC_MOST - 1 + ROWS + key_half) // STEP)


def dot_nt(a, b):
    return lax.dot_general(a, b, (((1,), (1,)), ((), ())), preferred_element_type=F32)


def dot_tn(a, b):
    return lax.dot_general(a, b, (((0,), (0,)), ((), ())), preferred_element_type=F32)


def dot_nn(a, b):
    return jnp.dot(a, b, preferred_element_type=F32)


def fill_padded(dst, src, top, length):
    total = dst.shape[0]
    dst[0:top, :] = jnp.zeros((top, dst.shape[1]), dst.dtype)
    dst[top : top + length, :] = src[...]
    if total > top + length:
        dst[top + length : total, :] = jnp.zeros((total - top - length, dst.shape[1]), dst.dtype)


def lanes_between(first, last, width):
    lane = lax.broadcasted_iota(jnp.int32, (first.shape[0], width), 1)
    return (lane >= first) & (lane <= last)


def row_numbers(base, count):
    return base + lax.broadcasted_iota(jnp.int32, (count, 1), 0)


def forward_kernel(
    n_taps, key_half, most, count_ref, mix_ref, q_ref, k_ref, v_ref, start_ref, base_ref, gain_ref,
    probs_ref, heads_ref, grouped_ref, qs, ks, vs, logit_ref, band_ref, inputs,
):
    pair = pl.program_id(0)
    block = pl.program_id(1)
    length = q_ref.shape[0]
    scale = HEAD_DIM ** (-0.5)

    @pl.when(block == 0)
    def _():
        fill_padded(qs, q_ref, HALO, length)
        fill_padded(ks, k_ref, TOP, length)
        fill_padded(vs, v_ref, TOP, length)
        for s in range(2):
            for a in range(n_taps):
                band = banded(band_line(base_ref[a, pl.ds(2 * pair + s, 1), :], key_half, 1))
                high = band.astype(BF16)
                band_ref[s, a, 0:WIN] = high
                band_ref[s, a, WIN : 2 * WIN] = high
                band_ref[s, a, 2 * WIN : 3 * WIN] = (band - high.astype(F32)).astype(BF16)

    row0 = pl.multiple_of(block * ROWS, ROWS)

    def body(n):
        start = start_ref[pl.ds(row0, EXT), :]
        place = row_numbers(row0 - HALO, EXT)
        firsts, lasts = [], []
        for k in range(n):
            base = row0 + ROWS - STEP * (k + 1) - OWN
            at = pl.multiple_of(TOP + base, 16)
            firsts.append(start - base)
            lasts.append(place - base)
            valid = lanes_between(firsts[k], lasts[k], WIN)
            rows = slice(k * EXT, (k + 1) * EXT)
            for s in range(2):
                cols = pl.ds(s * PAD_DIM, PAD_DIM)
                raw = dot_nt(qs[pl.ds(row0, EXT), cols], ks[pl.ds(at, WIN), cols])
                masked = jnp.where(valid, raw * scale, 0.0)
                high = masked.astype(BF16)
                inputs[s, rows, 0:WIN] = high
                inputs[s, rows, WIN : 2 * WIN] = (masked - high.astype(F32)).astype(BF16)
                inputs[s, rows, 2 * WIN : 3 * WIN] = high
        peaks = [None, None]
        for s in range(2):
            total = None
            for a in reversed(range(n_taps)):
                term = dot_nn(inputs[s, 0 : n * EXT, :], band_ref[s, a])
                total = term if total is None else pltpu.roll(total, 1, 0) + term
            for k in range(n):
                shown = lanes_between(
                    jnp.maximum(firsts[k][HALO:], key_half + 1),
                    jnp.minimum(lasts[k][HALO:], WIN - 2 - key_half),
                    WIN,
                )
                logits = jnp.where(shown, total[k * EXT + HALO : (k + 1) * EXT], NEG)
                logit_ref[s, k] = logits
                top = jnp.max(logits, axis=-1, keepdims=True)
                peaks[s] = top if peaks[s] is None else jnp.maximum(peaks[s], top)
        lane = lax.broadcasted_iota(jnp.int32, (ROWS, WIN), 1)
        own = (lane >= OWN) & (lane < WIN - OWN)
        sums = [None, None]
        for k in range(n):
            for s in range(2):
                expo = jnp.exp(logit_ref[s, k] - peaks[s])
                logit_ref[s, k] = expo
                part = jnp.sum(jnp.where(own, expo, 0.0), axis=-1, keepdims=True)
                sums[s] = part if sums[s] is None else sums[s] + part
        inverse = [1.0 / sums[s] for s in range(2)]
        outs = [None, None]
        for k in range(n):
            base = row0 + ROWS - STEP * (k + 1) - OWN
            at = pl.multiple_of(TOP + base, 16)
            probs = []
            for s in range(2):
                prob = logit_ref[s, k] * inverse[s]
                probs_ref[s, 0, k] = prob
                probs.append(jnp.where(own, prob, 0.0))
            for h in range(2):
                mixed = (
                    mix_ref[0, 2 * pair + h] * probs[0] + mix_ref[1, 2 * pair + h] * probs[1]
                ).astype(BF16)
                part = dot_nn(mixed, vs[pl.ds(at, WIN), pl.ds(h * PAD_DIM, PAD_DIM)])
                outs[h] = part if outs[h] is None else outs[h] + part
        for h in range(2):
            cols = slice(h * PAD_DIM, (h + 1) * PAD_DIM)
            out = outs[h]
            heads_ref[:, cols] = out
            factor = lax.rsqrt(jnp.sum(out * out, axis=-1, keepdims=True) * (1.0 / HEAD_DIM) + EPS)
            grouped_ref[:, cols] = (out * factor * gain_ref[:, cols]).astype(BF16)

    for n in range(1, most + 1):
        pl.when(count_ref[0, block] == n)(functools.partial(body, n))


def attend_forward(proj, start, counts, base, mix, gain):
    length = proj.shape[0]
    n_taps, heads = base.shape[:2]
    pairs = heads // 2
    blocks = length // ROWS
    key_half = 5
    most = windows_most(key_half)
    two = 2 * PAD_DIM
    grid_spec = pltpu.PrefetchScalarGridSpec(
        num_scalar_prefetch=2,
        grid=(pairs, blocks),
        in_specs=[
            pl.BlockSpec((length, two), lambda p, b, *_: (0, p)),
            pl.BlockSpec((length, two), lambda p, b, *_: (0, pairs + p)),
            pl.BlockSpec((length, two), lambda p, b, *_: (0, 2 * pairs + p)),
            pl.BlockSpec((HALO + length, 1), lambda p, b, *_: (0, 0)),
            pl.BlockSpec(base.shape, lambda p, b, *_: (0, 0, 0)),
            pl.BlockSpec((1, two), lambda p, b, *_: (0, p)),
        ],
        out_specs=[
            pl.BlockSpec((2, 1, most, ROWS, WIN), lambda p, b, *_: (p, b, 0, 0, 0)),
            pl.BlockSpec((ROWS, two), lambda p, b, *_: (b, p)),
            pl.BlockSpec((ROWS, two), lambda p, b, *_: (b, p)),
        ],
        scratch_shapes=[
            pltpu.VMEM((HALO + length, two), BF16),
            pltpu.VMEM((TOP + length + HALO, two), BF16),
            pltpu.VMEM((TOP + length + HALO, two), BF16),
            pltpu.VMEM((2, most, ROWS, WIN), F32),
            pltpu.VMEM((2, n_taps, 3 * WIN, WIN), BF16),
            pltpu.VMEM((2, most * EXT, 3 * WIN), BF16),
        ],
    )
    return pl.pallas_call(
        functools.partial(forward_kernel, n_taps, key_half, most),
        grid_spec=grid_spec,
        out_shape=[
            jax.ShapeDtypeStruct((heads, blocks, most, ROWS, WIN), F32),
            jax.ShapeDtypeStruct((length, heads * PAD_DIM), F32),
            jax.ShapeDtypeStruct((length, heads * PAD_DIM), BF16),
        ],
        compiler_params=pltpu.CompilerParams(vmem_limit_bytes=56 << 20),
        cost_estimate=COST,
        name="attend_forward",
    )(counts, mix, proj, proj, proj, start, base, gain)


def backward_kernel(
    n_taps, key_half, most, count_ref, mix_ref, q_ref, k_ref, v_ref, start_ref, base_ref, gain_ref,
    probs_ref, heads_ref, grad_ref, dqkv_ref, inner_ref, gain_grad_ref, tap_ref, mix_grad_ref,
    qs, ks, vs, dq_sum, dk_sum, dv_sum, taps, inputs, tap_sum, mixed_grad, t_back_ref, kept, inner_sum,
):
    pair = pl.program_id(0)
    block = pl.program_id(1)
    length = q_ref.shape[0]
    scale = HEAD_DIM ** (-0.5)

    @pl.when(block == 0)
    def _():
        fill_padded(qs, q_ref, HALO, length)
        fill_padded(ks, k_ref, TOP, length)
        fill_padded(vs, v_ref, TOP, length)
        dq_sum[...] = jnp.zeros_like(dq_sum)
        dk_sum[...] = jnp.zeros_like(dk_sum)
        dv_sum[...] = jnp.zeros_like(dv_sum)
        tap_sum[...] = jnp.zeros_like(tap_sum)
        gain_grad_ref[...] = jnp.zeros_like(gain_grad_ref)
        mix_grad_ref[...] = jnp.zeros_like(mix_grad_ref)
        for s in range(2):
            for a in range(n_taps):
                t_back_ref[s, a * WIN : (a + 1) * WIN, :] = banded(
                    band_line(base_ref[a, pl.ds(2 * pair + s, 1), :], key_half, -1)
                ).astype(BF16)

    row0 = pl.multiple_of(block * ROWS, ROWS)

    def body(n):
        grads = []
        for h in range(2):
            cols = slice(h * PAD_DIM, (h + 1) * PAD_DIM)
            out = heads_ref[:, cols]
            factor = lax.rsqrt(jnp.sum(out * out, axis=-1, keepdims=True) * (1.0 / HEAD_DIM) + EPS)
            unit = out * factor
            grad = grad_ref[:, cols]
            gain_grad_ref[:, cols] += jnp.sum(grad * unit, axis=0, keepdims=True)
            scaled = grad * gain_ref[:, cols]
            inner = jnp.sum(scaled * unit, axis=-1, keepdims=True) * (1.0 / HEAD_DIM)
            grads.append((factor * (scaled - unit * inner)).astype(BF16))
        lane = lax.broadcasted_iota(jnp.int32, (ROWS, WIN), 1)
        own = (lane >= OWN) & (lane < WIN - OWN)
        inner = [[None, None], [None, None]]
        for k in range(n):
            base = row0 + ROWS - STEP * (k + 1) - OWN
            at = pl.multiple_of(TOP + base, 16)
            probs = [jnp.where(own, probs_ref[s, 0, k], 0.0) for s in range(2)]
            for h in range(2):
                cols = pl.ds(h * PAD_DIM, PAD_DIM)
                grad_mixed = dot_nt(grads[h], vs[pl.ds(at, WIN), cols])
                mixed_grad[h, k] = grad_mixed
                for s in range(2):
                    part = jnp.sum(grad_mixed * probs[s], axis=-1, keepdims=True)
                    inner[h][s] = part if inner[h][s] is None else inner[h][s] + part
                mixed = (
                    mix_ref[0, 2 * pair + h] * probs[0] + mix_ref[1, 2 * pair + h] * probs[1]
                ).astype(BF16)
                dv_sum[pl.ds(at, WIN), cols] += dot_tn(mixed, grads[h])
        for h in range(2):
            for s in range(2):
                row = 2 * h + s
                mix_grad_ref[0, row : row + 1, :] += jnp.broadcast_to(
                    jnp.sum(inner[h][s], axis=0, keepdims=True), (1, PAD_DIM)
                )
        start = start_ref[pl.ds(row0, EXT), :]
        place = row_numbers(row0 - HALO, EXT)
        for s in range(2):
            cols = pl.ds(s * PAD_DIM, PAD_DIM)
            mix0 = mix_ref[s, 2 * pair]
            mix1 = mix_ref[s, 2 * pair + 1]
            delta = mix0 * inner[0][s] + mix1 * inner[1][s]
            query = qs[pl.ds(row0, EXT), cols]
            for k in range(n):
                grad_prob = mix0 * mixed_grad[0, k] + mix1 * mixed_grad[1, k]
                grad_logit = probs_ref[s, 0, k] * (grad_prob - delta)
                grown = jnp.concatenate([jnp.zeros((HALO, WIN), F32), grad_logit], axis=0)
                for a in range(n_taps):
                    moved = grown if a == 0 else pltpu.roll(grown, EXT - a, 0)
                    taps[k * EXT : (k + 1) * EXT, a * WIN : (a + 1) * WIN] = moved.astype(BF16)
            grad_inputs = dot_nn(taps[0 : n * EXT, :], t_back_ref[s])
            for k in range(n):
                base = row0 + ROWS - STEP * (k + 1) - OWN
                at = pl.multiple_of(TOP + base, 16)
                keys = ks[pl.ds(at, WIN), cols]
                mine = lanes_between(
                    jnp.maximum(start - base, OWN), jnp.minimum(place - base, WIN - OWN - 1), WIN
                )
                grad_masked = grad_inputs[k * EXT : (k + 1) * EXT]
                grad_score = jnp.where(mine, grad_masked * scale, 0.0).astype(BF16)
                dq_sum[pl.ds(row0, EXT), cols] += dot_nn(grad_score, keys)
                dk_sum[pl.ds(at, WIN), cols] += dot_tn(grad_score, query)
                raw = dot_nt(query, keys)
                inputs[k * EXT : (k + 1) * EXT, :] = jnp.where(mine, raw * scale, 0.0).astype(BF16)
            tap_sum[s] += dot_tn(inputs[0 : n * EXT, :], taps[0 : n * EXT, :])

    for n in range(1, most + 1):
        pl.when(count_ref[0, block] == n)(functools.partial(body, n))

    @pl.when(block == pl.num_programs(1) - 1)
    def _():
        inner = None
        sums = ((dq_sum, HALO, q_ref), (dk_sum, TOP, k_ref), (dv_sum, TOP, v_ref))
        for c, (total, top, given) in enumerate(sums):
            grad = total[top : top + length, :].astype(BF16)
            kept[pair, c] = grad
            part = jnp.sum(grad.astype(F32) * given[...].astype(F32), axis=-1, keepdims=True)
            inner = part if inner is None else inner + part

        @pl.when(pair == 0)
        def _():
            inner_sum[...] = inner

        @pl.when(pair > 0)
        def _():
            inner_sum[...] += inner

        row = lax.broadcasted_iota(jnp.int32, (WIN, WIN), 0)
        lane = lax.broadcasted_iota(jnp.int32, (WIN, WIN), 1)
        for s in range(2):
            for a in range(n_taps):
                whole = tap_sum[s, :, a * WIN : (a + 1) * WIN]
                for b in range(2 * key_half + 1):
                    part = jnp.where(lane - row == b - key_half, whole, 0.0)
                    part = jnp.sum(part, axis=0, keepdims=True)
                    part = jnp.sum(part, axis=1, keepdims=True)
                    at = a * (2 * key_half + 1) + b
                    tap_ref[s, at : at + 1, :] = jnp.broadcast_to(part, (1, PAD_DIM))

    pairs = kept.shape[0]

    @pl.when((block == pl.num_programs(1) - 1) & (pair == pairs - 1))
    def _():
        width = 2 * pairs * HEAD_DIM

        def rows_out(n, carry):
            at = pl.ds(pl.multiple_of(n * ROWS, ROWS), ROWS)
            for c in range(3):
                heads = [
                    kept[p, c, at, s * PAD_DIM : s * PAD_DIM + HEAD_DIM]
                    for p in range(pairs)
                    for s in range(2)
                ]
                dqkv_ref[at, c * width : (c + 1) * width] = jnp.concatenate(heads, axis=1)
            column = jnp.broadcast_to(inner_sum[at, :], (ROWS, PAD_DIM))
            inner_ref[pl.ds(n, 1), :] = column.T[0:1, :]
            return carry

        lax.fori_loop(0, length // ROWS, rows_out, 0)


def attend_backward(proj, start, counts, base, mix, gain, probs, heads_out, grad_grouped):
    length = proj.shape[0]
    n_taps, heads = base.shape[:2]
    pairs = heads // 2
    blocks = length // ROWS
    key_half = 5
    most = windows_most(key_half)
    two = 2 * PAD_DIM
    tap_rows = n_taps * (2 * key_half + 1)
    grid_spec = pltpu.PrefetchScalarGridSpec(
        num_scalar_prefetch=2,
        grid=(pairs, blocks),
        in_specs=[
            pl.BlockSpec((length, two), lambda p, b, *_: (0, p)),
            pl.BlockSpec((length, two), lambda p, b, *_: (0, pairs + p)),
            pl.BlockSpec((length, two), lambda p, b, *_: (0, 2 * pairs + p)),
            pl.BlockSpec((HALO + length, 1), lambda p, b, *_: (0, 0)),
            pl.BlockSpec(base.shape, lambda p, b, *_: (0, 0, 0)),
            pl.BlockSpec((1, two), lambda p, b, *_: (0, p)),
            pl.BlockSpec((2, 1, most, ROWS, WIN), lambda p, b, *_: (p, b, 0, 0, 0)),
            pl.BlockSpec((ROWS, two), lambda p, b, *_: (b, p)),
            pl.BlockSpec((ROWS, two), lambda p, b, *_: (b, p)),
        ],
        out_specs=[
            pl.BlockSpec((length, 3 * heads * HEAD_DIM), lambda p, b, *_: (0, 0)),
            pl.BlockSpec((length // ROWS, ROWS), lambda p, b, *_: (0, 0)),
            pl.BlockSpec((1, two), lambda p, b, *_: (0, p)),
            pl.BlockSpec((2, tap_rows, PAD_DIM), lambda p, b, *_: (p, 0, 0)),
            pl.BlockSpec((1, 4, PAD_DIM), lambda p, b, *_: (p, 0, 0)),
        ],
        scratch_shapes=[
            pltpu.VMEM((HALO + length, two), BF16),
            pltpu.VMEM((TOP + length + HALO, two), BF16),
            pltpu.VMEM((TOP + length + HALO, two), BF16),
            pltpu.VMEM((HALO + length, two), F32),
            pltpu.VMEM((TOP + length + HALO, two), F32),
            pltpu.VMEM((TOP + length + HALO, two), F32),
            pltpu.VMEM((most * EXT, n_taps * WIN), BF16),
            pltpu.VMEM((most * EXT, WIN), BF16),
            pltpu.VMEM((2, WIN, n_taps * WIN), F32),
            pltpu.VMEM((2, most, ROWS, WIN), F32),
            pltpu.VMEM((2, n_taps * WIN, WIN), BF16),
            pltpu.VMEM((pairs, 3, length, two), BF16),
            pltpu.VMEM((length, 1), F32),
        ],
    )
    return pl.pallas_call(
        functools.partial(backward_kernel, n_taps, key_half, most),
        grid_spec=grid_spec,
        out_shape=[
            jax.ShapeDtypeStruct((length, 3 * heads * HEAD_DIM), BF16),
            jax.ShapeDtypeStruct((length // ROWS, ROWS), F32),
            jax.ShapeDtypeStruct((1, heads * PAD_DIM), F32),
            jax.ShapeDtypeStruct((heads, tap_rows, PAD_DIM), F32),
            jax.ShapeDtypeStruct((pairs, 4, PAD_DIM), F32),
        ],
        compiler_params=pltpu.CompilerParams(vmem_limit_bytes=56 << 20),
        cost_estimate=COST,
        name="attend_backward",
    )(counts, mix, proj, proj, proj, start, base, gain, probs, heads_out, grad_grouped)


MESH_ID = pl.DeviceIdType.MESH


def ring_place(member, n):
    z, y = member // 2, member % 2
    return (1 - y) * z + y * (n - 1 - z)


def ring_member(place, n):
    upper = place // (n // 2)
    return (1 - upper) * 2 * place + upper * (2 * (n - 1 - place) + 1)


def ring_peers(n):
    place = ring_place(lax.axis_index("dp"), n)
    ahead = ring_member(lax.rem(place + 1, n), n)
    behind = ring_member(lax.rem(place + n - 1, n), n)
    return place, (ahead, behind)


def ring_scratch(arrays, n):
    return [pltpu.VMEM((2, n - 1) + a.shape[2:], a.dtype) for a in arrays] + [
        pltpu.SemaphoreType.DMA((2, len(arrays), n - 1))
    ] * 4


def ring_split(array, n):
    return array.reshape(n, 2, -1, array.shape[-1])


def make_ring(n, sources, ins, outs, finals, leave_sem, scratch):
    count = len(ins)
    slots = scratch[:count]
    rs_send, rs_recv, ag_send, ag_recv = scratch[count:]
    place, to = ring_peers(n)

    def chunk(way, back):
        return lax.rem(place - back + 2 * n if way == 0 else place + back, n)

    def sum_copy(way, k, s, src):
        return pltpu.make_async_remote_copy(
            src_ref=src,
            dst_ref=slots[k].at[way, s],
            send_sem=rs_send.at[way, k, s],
            recv_sem=rs_recv.at[way, k, s],
            device_id={"dp": to[way]},
            device_id_type=MESH_ID,
        )

    def share_copy(way, k, s, c):
        return pltpu.make_async_remote_copy(
            src_ref=outs[k].at[c, way],
            dst_ref=outs[k].at[c, way],
            send_sem=ag_send.at[way, k, s],
            recv_sem=ag_recv.at[way, k, s],
            device_id={"dp": to[way]},
            device_id_type=MESH_ID,
        )

    def add(way, k, s, c, dst):
        total = slots[k][way, s].astype(F32) + ins[k][c, way].astype(F32)
        dst[...] = total.astype(dst.dtype)

    both = [(k, way) for k in range(count) for way in range(2)]

    def leave(way, k, c):
        return pltpu.make_async_copy(outs[k].at[c, way], finals[k].at[c, way], leave_sem.at[way, k, c])

    def start():
        for k, way in both:
            sum_copy(way, k, 0, sources[k].at[chunk(way, 1), way]).start()

    def tick(now):
        @pl.when(now < n - 2)
        def _():
            for k, way in both:
                sum_copy(way, k, now, slots[k].at[way, now]).wait_recv()
                add(way, k, now, chunk(way, 2 + now), slots[k].at[way, now])
                sum_copy(way, k, now + 1, slots[k].at[way, now]).start()

        @pl.when(now == n - 2)
        def _():
            for k, way in both:
                sum_copy(way, k, n - 2, slots[k].at[way, n - 2]).wait_recv()
                add(way, k, n - 2, place, outs[k].at[place, way])
                share_copy(way, k, 0, place).start()
                leave(way, k, place).start()

        @pl.when((now > n - 2) & (now < 2 * n - 3))
        def _():
            step = now - (n - 1)
            for k, way in both:
                share_copy(way, k, step, chunk(way, step + 1)).wait_recv()
                share_copy(way, k, step + 1, chunk(way, step + 1)).start()
                leave(way, k, chunk(way, step + 1)).start()

        @pl.when(now == 2 * n - 3)
        def _():
            for k, way in both:
                share_copy(way, k, n - 2, chunk(way, n - 1)).wait_recv()
                leave(way, k, chunk(way, n - 1)).start()

    def drain():
        def one(s, carry):
            for k, way in both:
                sum_copy(way, k, s, slots[k].at[way, s]).wait_send()
                share_copy(way, k, s, place).wait_send()
            return carry

        lax.fori_loop(0, n - 1, one, 0)

        def left(c, carry):
            for k, way in both:
                leave(way, k, c).wait()
            return carry

        lax.fori_loop(0, n, left, 0)

    return start, tick, drain


def small_rows(size):
    return -(-size // PAD_DIM)


def pack_small(arrays, rows):
    packed = []
    for a in arrays:
        flat = a.reshape(-1)
        packed.append(jnp.pad(flat, (0, -flat.size % PAD_DIM)).reshape(-1, PAD_DIM))
    packed = jnp.concatenate(packed, axis=0)
    return jnp.pad(packed, ((0, rows - packed.shape[0]), (0, 0)))


def unpack_small(packed, arrays):
    found, at = [], 0
    for a in arrays:
        rows = small_rows(a.size)
        found.append(packed[at : at + rows].reshape(-1)[: a.size].reshape(a.shape))
        at += rows
    return found


CHUNK = 128
GROUP = 256


LIVE = 4


def exchange_scratch(steps, width, ranks, share=True, chunk=CHUNK):
    half = ranks // 2
    live = steps if share else LIVE
    shared = [pltpu.VMEM((steps, ranks, chunk, width), BF16)] if share else []
    return [
        pltpu.VMEM((steps, half, chunk, width), BF16),
        pltpu.VMEM((steps, half, chunk, width), BF16),
        pltpu.VMEM((live, half, chunk, width), F32),
        pltpu.VMEM((steps, chunk, width), BF16),
        pltpu.VMEM((steps, chunk, width), BF16),
        pltpu.SemaphoreType.DMA((5, steps)),
        pltpu.SemaphoreType.DMA((5, steps)),
    ] + shared


def tensor_peers():
    me = lax.axis_index("tensor")
    return me, me + 1 - 2 * lax.rem(me, 2), lax.rem(me + 2, 4)


def meet(signals):
    barrier = pltpu.get_barrier_semaphore()
    for device in signals:
        pl.semaphore_signal(barrier, inc=1, device_id=device, device_id_type=MESH_ID)
    pl.semaphore_wait(barrier, len(signals))


def exchange_copies(scratch):
    out_a, in_a, _, out_b, in_b, send, recv, *full = scratch
    me, near, far = tensor_peers()

    def copy(kind, step, src, dst, peer):
        return pltpu.make_async_remote_copy(
            src_ref=src,
            dst_ref=dst,
            send_sem=send.at[kind, step],
            recv_sem=recv.at[kind, step],
            device_id={"tensor": peer},
            device_id_type=MESH_ID,
        )

    def cores(step):
        return copy(0, step, out_a.at[step], in_a.at[step], near)

    def chips(step):
        return copy(1, step, out_b.at[step], in_b.at[step], far)

    def back_far(step):
        return copy(2, step, full[0].at[step, me], full[0].at[step, me], far)

    def back_near(step):
        return copy(3, step, full[0].at[step, me], full[0].at[step, me], near)

    def pass_near(step):
        return copy(4, step, full[0].at[step, far], full[0].at[step, far], near)

    return cores, chips, back_far, back_near, pass_near


def exchange_stages(scratch, partial, live, chunk):
    out_a, in_a, kept, out_b, in_b = scratch[:5]
    cores, chips = exchange_copies(scratch)[:2]
    many = GROUP // chunk
    me, near, far = tensor_peers()

    def begin(step):
        for n, owner in ((0, near), (1, lax.rem(near + 2, 4))):

            def put(term, n=n):
                term = term.astype(BF16)
                for m in range(many):
                    out_a[step + m, n] = term[m * chunk : (m + 1) * chunk]

            partial(step, owner, put)
        for m in range(many):
            cores(step + m).start()
        for n, owner in ((1, far), (0, me)):

            def put(term, n=n):
                for m in range(many):
                    kept[lax.rem(step + m, live), n] = term[m * chunk : (m + 1) * chunk]

            partial(step, owner, put)

    def over(step):
        cores(step).wait_recv()
        out_b[step] = (kept[lax.rem(step, live), 1] + in_a[step, 1].astype(F32)).astype(BF16)
        chips(step).start()

    def total(step):
        chips(step).wait_recv()
        return kept[lax.rem(step, live), 0] + in_a[step, 0].astype(F32) + in_b[step].astype(F32)

    return begin, over, total


def make_exchange(steps, scratch, partial, local, between, chunk):
    cores, chips = exchange_copies(scratch)[:2]
    begin, over, total = exchange_stages(scratch, partial, LIVE, chunk)
    many = GROUP // chunk

    def tick(now):
        @pl.when((lax.rem(now, many) == 0) & (now < steps))
        def _():
            begin(now)

        between(now)

        @pl.when((now >= 1) & (now < steps + 1))
        def _():
            over(now - 1)

        @pl.when((now >= 2) & (now < steps + 2))
        def _():
            local(now - 2, total(now - 2))

    def drain():
        def one(step, carry):
            cores(step).wait_send()
            chips(step).wait_send()
            return carry

        lax.fori_loop(0, steps, one, 0)

    return tick, steps + 2, drain


def run_exchange(steps, scratch, partial, local, whole, beside=None, ahead=None):
    cores, chips, back_far, back_near, pass_near = exchange_copies(scratch)
    begin, over, total = exchange_stages(scratch, partial, steps, CHUNK)
    full = scratch[7]
    many = GROUP // CHUNK
    me = tensor_peers()[0]

    def send_group(group, carry):
        @pl.when(group < steps // many)
        def _():
            begin(group * many)

        @pl.when(group >= 1)
        def _():
            for m in range(many):
                over((group - 1) * many + m)

        return carry

    lax.fori_loop(0, steps // many + 1, send_group, 0)

    def sum_group(group, carry):
        if beside is not None:
            beside(group)
        for m in range(many):
            step = group * many + m
            full[step, me] = local(step, total(step)).astype(BF16)
            back_far(step).start()
            back_near(step).start()
        return carry

    lax.fori_loop(0, steps // many, sum_group, 0)
    if ahead is not None:
        ahead()

    def share_step(now, carry):
        @pl.when(now < steps)
        def _():
            back_far(now).wait_recv()
            pass_near(now).start()

        @pl.when(now >= 1)
        def _():
            back_near(now - 1).wait_recv()
            pass_near(now - 1).wait_recv()
            whole(now - 1, full)

        return carry

    lax.fori_loop(0, steps + 1, share_step, 0)

    def drain(step, carry):
        for copy in (cores, chips, back_far, back_near, pass_near):
            copy(step).wait_send()
        return carry

    lax.fori_loop(0, steps, drain, 0)


def run_ticks(count, *ticks):
    def one(now, carry):
        for tick in ticks:
            tick(now)
        return carry

    lax.fori_loop(0, count, one, 0)


def group_rows(step, chunk=CHUNK):
    return pl.ds(pl.multiple_of(step * chunk, chunk), GROUP)


def owner_cols(owner, width):
    return pl.ds(pl.multiple_of(owner * width, PAD_DIM), width)


def step_rows(step, chunk=CHUNK):
    return pl.ds(pl.multiple_of(step * chunk, chunk), chunk)


def first_entry_kernel(
    key_half, tokens_ref, w_in, gains_line_ref, segments_ref, proj_out, normed_out, factor_ref, gains_all_ref, gain_heads_ref,
    start_ref, count_ref, w_ref, proj_ref, normed_ref, load, store, full, gains_ref, gains_in, send, recv, gains_send, gains_recv,
):
    weights = pltpu.make_async_copy(w_in, w_ref, load.at[0])
    weights.start()
    rows, width = tokens_ref.shape
    ranks = normed_ref.shape[1] // width
    heads = width // HEAD_DIM
    steps, many = rows // CHUNK, GROUP // CHUNK
    me, near, far = tensor_peers()
    across = lax.rem(near + 2, 4)
    meet([{"tensor": near}, {"tensor": far}, {"tensor": across}])

    def copy(kind, step, src, dst, peer):
        return pltpu.make_async_remote_copy(
            src_ref=src,
            dst_ref=dst,
            send_sem=send.at[kind, step],
            recv_sem=recv.at[kind, step],
            device_id={"tensor": peer},
            device_id_type=MESH_ID,
        )

    def to_far(step):
        return copy(0, step, tokens_ref.at[step_rows(step)], full.at[step, me], far)

    def to_near(step):
        return copy(1, step, tokens_ref.at[step_rows(step)], full.at[step, me], near)

    def pass_near(step):
        return copy(2, step, full.at[step, far], full.at[step, far], near)

    def gains_copy(kind, peer, sender):
        return pltpu.make_async_remote_copy(
            src_ref=gains_ref,
            dst_ref=gains_in.at[sender],
            send_sem=gains_send.at[kind],
            recv_sem=gains_recv.at[sender],
            device_id={"tensor": peer},
            device_id_type=MESH_ID,
        )

    gains_ref[...] = jnp.zeros_like(gains_ref)
    for n in range(3):
        gains_ref[n : n + 1, :] = gains_line_ref[:, n * width : (n + 1) * width].astype(F32)
    peers = (near, far, across)
    for kind, peer in enumerate(peers):
        gains_copy(kind, peer, me).start()

    def send_all(step, carry):
        to_far(step).start()
        to_near(step).start()
        full[step, me] = tokens_ref[step_rows(step), :]
        return carry

    lax.fori_loop(0, steps, send_all, 0)
    gains_in[me] = gains_ref[...]
    for kind, peer in enumerate(peers):
        gains_copy(kind, peer, peer).wait()
    for n in range(ranks):
        gains_all_ref[:, n * width : (n + 1) * width] = gains_in[n]

    def stores(group):
        at = group_rows(group * many)
        return [
            pltpu.make_async_copy(src.at[at], dst.at[at], store.at[n, group])
            for n, (src, dst) in enumerate(((proj_ref, proj_out), (normed_ref, normed_out)))
        ]

    weights.wait()
    for h in range(heads):
        own = gains_ref[2:3, h * HEAD_DIM : (h + 1) * HEAD_DIM]
        gain_heads_ref[:, h * PAD_DIM : (h + 1) * PAD_DIM] = jnp.concatenate(
            [own, jnp.zeros((1, PAD_DIM - HEAD_DIM), F32)], axis=1
        )
    seqs, length = segments_ref.shape
    for n in range(seqs):
        lead = n * (HALO + length)
        start_ref[lead : lead + HALO, :] = jnp.full((HALO, 1), 1 << 20, jnp.int32)
        line = segments_ref[n : n + 1, :].astype(F32)
        for b in range(length // ROWS):
            column = jnp.broadcast_to(line[:, b * ROWS : (b + 1) * ROWS], (ROWS, ROWS)).T[:, 0:1]
            before = jnp.sum(jnp.where(line < column, 1.0, 0.0), axis=1, keepdims=True)
            at = lead + HALO + b * ROWS
            before = before.astype(jnp.int32)
            start_ref[at : at + ROWS, :] = before
            count = jnp.ones((1, 1), jnp.int32)
            for k in range(1, windows_most(key_half)):
                reach = b * ROWS + ROWS - STEP * k + key_half
                count = count + jnp.where(before[0:1] < reach, 1, 0)
            count_ref[n : n + 1, b : b + 1] = count

    def tick(now):
        @pl.when(now < steps)
        def _():
            to_far(now).wait_recv()
            pass_near(now).start()

        @pl.when(now >= 1)
        def _():
            to_near(now - 1).wait_recv()
            pass_near(now - 1).wait_recv()

        @pl.when((now >= many) & (lax.rem(now, many) == 0))
        def _():
            first = now - many
            at = group_rows(first)
            blocks = [
                jnp.concatenate([full[first + m, n] for m in range(many)], axis=0).astype(F32)
                for n in range(ranks)
            ]
            squares = sum(jnp.sum(block * block, axis=-1, keepdims=True) for block in blocks)
            factor = lax.rsqrt(squares * (1.0 / (ranks * width)) + EPS)
            factor_ref[at, :] = factor
            for n, block in enumerate(blocks):
                cols = slice(n * width, (n + 1) * width)
                normed_ref[at, cols] = (block * factor * gains_all_ref[0:1, cols]).astype(BF16)
            for c in range(3):
                out = dot_nn(normed_ref[at, :], w_ref[c])
                empty = jnp.zeros((GROUP, PAD_DIM - HEAD_DIM), F32)
                for h in range(heads):
                    head = jnp.concatenate([out[:, h * HEAD_DIM : (h + 1) * HEAD_DIM], empty], axis=1)
                    lane = (c * heads + h) * PAD_DIM
                    proj_ref[at, lane : lane + PAD_DIM] = head.astype(BF16)
            for one in stores(first // many):
                one.start()

    run_ticks(steps + 1, tick)

    def stored(group, carry):
        for one in stores(group):
            one.wait()
        return carry

    lax.fori_loop(0, steps // many, stored, 0)

    def drain(step, carry):
        to_far(step).wait_send()
        to_near(step).wait_send()
        pass_near(step).wait_send()
        return carry

    lax.fori_loop(0, steps, drain, 0)


def first_entry(tokens, w_qkv, gains, segments, key_half):
    rows, width = tokens.shape
    full_width = w_qkv.shape[1]
    ranks = full_width // width
    steps = rows // CHUNK
    padded = 3 * width // HEAD_DIM * PAD_DIM
    vmem = pl.BlockSpec(memory_space=pltpu.VMEM)
    anywhere = pl.BlockSpec(memory_space=pl.ANY)
    return pl.pallas_call(
        functools.partial(first_entry_kernel, key_half),
        out_shape=[
            jax.ShapeDtypeStruct((rows, padded), BF16),
            jax.ShapeDtypeStruct((rows, full_width), BF16),
            jax.ShapeDtypeStruct((rows, 1), F32),
            jax.ShapeDtypeStruct((8, full_width), F32),
            jax.ShapeDtypeStruct((1, width // HEAD_DIM * PAD_DIM), F32),
            jax.ShapeDtypeStruct((segments.shape[0] * (HALO + segments.shape[1]), 1), jnp.int32),
            jax.ShapeDtypeStruct((segments.shape[0], segments.shape[1] // ROWS), jnp.int32),
        ],
        in_specs=[vmem, anywhere, vmem, vmem],
        out_specs=[anywhere, anywhere] + [vmem] * 5,
        scratch_shapes=[
            pltpu.VMEM(w_qkv.shape, BF16),
            pltpu.VMEM((rows, padded), BF16),
            pltpu.VMEM((rows, full_width), BF16),
            pltpu.SemaphoreType.DMA((1,)),
            pltpu.SemaphoreType.DMA((2, rows // GROUP)),
            pltpu.VMEM((steps, ranks, CHUNK, width), BF16),
            pltpu.VMEM((8, width), F32),
            pltpu.VMEM((ranks, 8, width), F32),
            pltpu.SemaphoreType.DMA((3, steps)),
            pltpu.SemaphoreType.DMA((3, steps)),
            pltpu.SemaphoreType.DMA((3,)),
            pltpu.SemaphoreType.DMA((ranks,)),
        ],
        compiler_params=pltpu.CompilerParams(
            collective_id=4, has_side_effects=True, vmem_limit_bytes=60 << 20
        ),
        cost_estimate=COST,
        name="first_entry",
    )(tokens, w_qkv, gains, segments)


def attn_exit_kernel(
    grouped_ref, w_out_ref, tokens_ref, gain_ref, cot_in, w_gate_up_in, w_down_in, hidden_local_ref,
    hidden_out, normed_out, w_ref, act_out, grad_gate_out, grad_up_out, hidden_ref, normed_ref, act_ref,
    grad_gate_ref, grad_up_ref, grad_act, cot_ref, w_gate_up_ref, w_down_ref, load, store, *scratch
):
    loads = [
        pltpu.make_async_copy(src, dst, load.at[n])
        for n, (src, dst) in enumerate(
            ((cot_in, cot_ref), (w_down_in, w_down_ref), (w_gate_up_in, w_gate_up_ref))
        )
    ]
    for one in loads:
        one.start()
    rows, width = tokens_ref.shape
    ranks = hidden_ref.shape[1] // width
    many = GROUP // CHUNK
    for h in range(width // HEAD_DIM):
        lead = h * PAD_DIM
        w_ref[lead : lead + HEAD_DIM, :] = w_out_ref[h * HEAD_DIM : (h + 1) * HEAD_DIM, :]
        w_ref[lead + HEAD_DIM : lead + PAD_DIM, :] = jnp.zeros((PAD_DIM - HEAD_DIM, w_ref.shape[1]), BF16)

    def partial(step, owner, put):
        put(dot_nn(grouped_ref[group_rows(step), :], w_ref[:, owner_cols(owner, width)]))

    def local(step, total):
        hidden = tokens_ref[step_rows(step), :].astype(F32) + total
        hidden_local_ref[step_rows(step), :] = hidden
        return hidden

    def whole(step, full):
        squares = None
        for n in range(ranks):
            block = full[step, n]
            hidden_ref[step_rows(step), n * width : (n + 1) * width] = block
            block = block.astype(F32)
            part = jnp.sum(block * block, axis=-1, keepdims=True)
            squares = part if squares is None else squares + part
        factor = lax.rsqrt(squares * (1.0 / (ranks * width)) + EPS)
        for n in range(ranks):
            cols = slice(n * width, (n + 1) * width)
            unit = full[step, n].astype(F32) * factor
            normed_ref[step_rows(step), cols] = (unit * gain_ref[1:2, cols]).astype(BF16)

        @pl.when(lax.rem(step, many) == many - 1)
        def _():
            at = group_rows(step - (many - 1))
            gate = dot_nn(normed_ref[at, :], w_gate_up_ref[0])
            up = dot_nn(normed_ref[at, :], w_gate_up_ref[1])
            sigmoid = jax.nn.sigmoid(gate)
            swish = gate * sigmoid
            grad = grad_act[at, :]
            act_ref[at, :] = (swish * up).astype(BF16)
            grad_gate_ref[at, :] = (grad * up * sigmoid * (1.0 + gate * (1.0 - sigmoid))).astype(BF16)
            grad_up_ref[at, :] = (grad * swish).astype(BF16)
            for one in stores(step // many):
                one.start()

    def stores(group):
        at = group_rows(group * many)
        pairs = (
            (hidden_ref, hidden_out),
            (normed_ref, normed_out),
            (act_ref, act_out),
            (grad_gate_ref, grad_gate_out),
            (grad_up_ref, grad_up_out),
        )
        return [
            pltpu.make_async_copy(src.at[at], dst.at[at], store.at[n, group])
            for n, (src, dst) in enumerate(pairs)
        ]

    def beside(group):
        @pl.when(group == 0)
        def _():
            loads[0].wait()
            loads[1].wait()

        at = group_rows(group * many)
        grad_act[at, :] = dot_nt(cot_ref[at, :], w_down_ref[...])

    me, near, far = tensor_peers()
    meet([{"tensor": near}, {"tensor": far}])
    run_exchange(rows // CHUNK, scratch, partial, local, whole, beside, loads[2].wait)

    def stored(group, carry):
        for one in stores(group):
            one.wait()
        return carry

    lax.fori_loop(0, rows // GROUP, stored, 0)


def attn_exit(grouped, w_out, tokens, gain, full_cot, w_gate_up, w_down):
    rows, width = tokens.shape
    full_width = w_out.shape[1]
    units = w_down.shape[0]
    vmem = pl.BlockSpec(memory_space=pltpu.VMEM)
    anywhere = pl.BlockSpec(memory_space=pl.ANY)
    return pl.pallas_call(
        attn_exit_kernel,
        out_shape=[
            jax.ShapeDtypeStruct((rows, width), F32),
            jax.ShapeDtypeStruct((rows, full_width), BF16),
            jax.ShapeDtypeStruct((rows, full_width), BF16),
            jax.ShapeDtypeStruct((grouped.shape[1], full_width), BF16),
        ]
        + [jax.ShapeDtypeStruct((rows, units), BF16)] * 3,
        in_specs=[vmem] * 4 + [anywhere] * 3,
        out_specs=[vmem, anywhere, anywhere, vmem] + [anywhere] * 3,
        scratch_shapes=[pltpu.VMEM((rows, full_width), BF16)] * 2
        + [pltpu.VMEM((rows, units), BF16)] * 3
        + [
            pltpu.VMEM((rows, units), F32),
            pltpu.VMEM(full_cot.shape, BF16),
            pltpu.VMEM(w_gate_up.shape, BF16),
            pltpu.VMEM(w_down.shape, BF16),
            pltpu.SemaphoreType.DMA((3,)),
            pltpu.SemaphoreType.DMA((5, rows // GROUP)),
        ]
        + exchange_scratch(rows // CHUNK, width, full_width // width),
        compiler_params=pltpu.CompilerParams(
            collective_id=1, has_side_effects=True, vmem_limit_bytes=56 << 20
        ),
        cost_estimate=COST,
        name="attn_exit",
    )(grouped, w_out, tokens, gain, full_cot, w_gate_up, w_down)


def mlp_exit_kernel(
    gate_ref, up_ref, w_ref, hidden_in, cot_in, hidden_local_ref, cot_local_ref, gain_ref, gain_local_ref,
    grad_attn_ref, grad_hidden_ref, gain_grad_ref, grad_local, hidden_ref, cot_ref, load, *scratch
):
    loads = [
        pltpu.make_async_copy(hidden_in, hidden_ref, load.at[0]),
        pltpu.make_async_copy(cot_in, cot_ref, load.at[1]),
    ]
    for one in loads:
        one.start()
    rows, width = cot_local_ref.shape
    full_width = hidden_ref.shape[1]
    ranks = full_width // width
    gain_grad_ref[...] = jnp.zeros_like(gain_grad_ref)

    def partial(step, owner, put):
        cols = owner_cols(owner, width)
        at = group_rows(step)
        put(dot_nt(gate_ref[at, :], w_ref[0, cols, :]) + dot_nt(up_ref[at, :], w_ref[1, cols, :]))

    def local(step, total):
        grad_local[step_rows(step), :] = total
        return total

    def whole(step, full):
        at = step_rows(step)
        squares, inner = None, None
        for n in range(ranks):
            cols = slice(n * width, (n + 1) * width)
            hidden = hidden_ref[at, cols].astype(F32)
            part = jnp.sum(hidden * hidden, axis=-1, keepdims=True)
            squares = part if squares is None else squares + part
            part = jnp.sum(full[step, n].astype(F32) * gain_ref[1:2, cols] * hidden, axis=-1, keepdims=True)
            inner = part if inner is None else inner + part
        factor = lax.rsqrt(squares * (1.0 / full_width) + EPS)
        inner = inner * factor * (1.0 / full_width)
        for n in range(ranks):
            cols = slice(n * width, (n + 1) * width)
            unit = hidden_ref[at, cols].astype(F32) * factor
            grad = full[step, n].astype(F32) * gain_ref[1:2, cols] - unit * inner
            grad_attn_ref[at, cols] = (cot_ref[at, cols].astype(F32) + factor * grad).astype(BF16)
        total = grad_local[at, :]
        unit = hidden_local_ref[at, :] * factor
        gain_grad_ref[...] += jnp.sum(total * unit, axis=0, keepdims=True)
        grad_hidden_ref[at, :] = cot_local_ref[at, :].astype(F32) + factor * (
            total * gain_local_ref[...] - unit * inner
        )

    me, near, far = tensor_peers()
    meet([{"tensor": near}, {"tensor": far}])

    def ahead():
        for one in loads:
            one.wait()

    run_exchange(rows // CHUNK, scratch, partial, local, whole, ahead=ahead)


def mlp_exit(grad_gate, grad_up, w_gate_up, hidden, full_cot, hidden_local, cotangent, gain, gain_local):
    rows, width = hidden_local.shape
    full_width = hidden.shape[1]
    vmem = pl.BlockSpec(memory_space=pltpu.VMEM)
    return pl.pallas_call(
        mlp_exit_kernel,
        out_shape=[
            jax.ShapeDtypeStruct((rows, full_width), BF16),
            jax.ShapeDtypeStruct((rows, width), F32),
            jax.ShapeDtypeStruct((1, width), F32),
        ],
        in_specs=[vmem] * 3 + [pl.BlockSpec(memory_space=pl.ANY)] * 2 + [vmem] * 4,
        out_specs=[vmem] * 3,
        scratch_shapes=[
            pltpu.VMEM((rows, width), F32),
            pltpu.VMEM(hidden.shape, BF16),
            pltpu.VMEM(full_cot.shape, BF16),
            pltpu.SemaphoreType.DMA((2,)),
        ]
        + exchange_scratch(rows // CHUNK, width, full_width // width),
        compiler_params=pltpu.CompilerParams(
            collective_id=2, has_side_effects=True, vmem_limit_bytes=56 << 20
        ),
        cost_estimate=COST,
        name="mlp_exit",
    )(grad_gate, grad_up, w_gate_up, hidden, full_cot, hidden_local, cotangent, gain, gain_local)


def last_exit_kernel(
    n_ring, count, factor_ref, inner_ref, gain_ref, small_ref, *refs,
):
    given, sources, refs = refs[:7], refs[7 : 7 + count], refs[7 + count :]
    tokens_grad_ref, out_ref, small_sum_ref = refs[:3]
    finals, refs = refs[3 : 3 + count], refs[3 + count :]
    here_too, ins, load, refs = refs[:7], refs[7 : 7 + count], refs[7 + count], refs[8 + count :]
    outs, leave_sem, refs = refs[:count], refs[count], refs[count + 1 :]
    grad_ref, w_ref, tokens_ref, grad_hidden_ref, act_ref, w_down_ref, hidden_ref = here_too
    loads = [
        pltpu.make_async_copy(src, dst, load.at[n])
        for n, (src, dst) in enumerate(zip((*sources, *given), (*ins, *here_too)))
    ]
    for one in loads:
        one.start()
    gain_grad, mine, all_small, small_send, small_recv = refs[:5]
    inner_in, inner_sum, inner_col, inner_send, inner_recv = refs[5:10]
    ring_refs, scratch = refs[10 : 14 + count], refs[14 + count :]
    rows, width = tokens_ref.shape
    full_width = w_ref.shape[1]
    half = rows // GROUP
    me, near, far = tensor_peers()
    here = lax.axis_index("dp")
    gain_grad[...] = jnp.zeros_like(gain_grad)

    def partial(step, owner, put):
        cols = owner_cols(owner, width)

        @pl.when(step < half)
        def _():
            total = None
            for c in range(3):
                term = dot_nt(grad_ref[group_rows(step, GROUP), c * width : (c + 1) * width], w_ref[c, cols, :])
                total = term if total is None else total + term
            put(total)

        @pl.when(step >= half)
        def _():
            put(dot_nn(act_ref[group_rows(step - half, GROUP), :], w_down_ref[:, cols]))

    def between(now):
        def copy(n, src, peer):
            return pltpu.make_async_remote_copy(
                src_ref=src,
                dst_ref=inner_in.at[n],
                send_sem=inner_send.at[n],
                recv_sem=inner_recv.at[n],
                device_id={"tensor": peer},
                device_id_type=MESH_ID,
            )

        @pl.when(now == 0)
        def _():
            copy(0, inner_ref, near).start()

        @pl.when(now == 1)
        def _():
            copy(0, inner_ref, near).wait()
            inner_sum[...] = inner_ref[...] + inner_in[0]
            copy(1, inner_sum, far).start()

        @pl.when(now == 2)
        def _():
            copy(1, inner_sum, far).wait()
            total = (inner_sum[...] + inner_in[1]) * (1.0 / full_width)
            for n in range(rows // ROWS):
                line = jnp.broadcast_to(total[n : n + 1, :], (ROWS, ROWS))
                inner_col[n * ROWS : (n + 1) * ROWS, :] = line.T[:, 0:1]

    def local(step, total):
        @pl.when(step < half)
        def _():
            at = step_rows(step, GROUP)
            factor = factor_ref[at, :]
            unit = tokens_ref[at, :].astype(F32) * factor
            gain_grad[...] += jnp.sum(total * unit, axis=0, keepdims=True)
            tokens_grad_ref[at, :] = grad_hidden_ref[at, :] + factor * (
                total * gain_ref[...] - unit * inner_col[at, :]
            )

        @pl.when(step >= half)
        def _():
            at = step_rows(step - half, GROUP)
            out_ref[at, :] = (hidden_ref[at, :] + total).astype(BF16)

    def small_copy(peer, sender):
        return pltpu.make_async_remote_copy(
            src_ref=mine,
            dst_ref=all_small.at[sender],
            send_sem=small_send.at[peer],
            recv_sem=small_recv.at[sender],
            device_id={"dp": peer},
            device_id_type=MESH_ID,
        )

    def small_start(now):
        @pl.when(now == half + 2)
        def _():
            mine[...] = small_ref[...]
            for n in range(width // PAD_DIM):
                mine[n : n + 1, :] = gain_grad[:, n * PAD_DIM : (n + 1) * PAD_DIM]
            all_small[here] = mine[...]

            def one(away, carry):
                small_copy(lax.rem(here + away, n_ring), here).start()
                return carry

            lax.fori_loop(1, n_ring, one, 0)

    barrier = pltpu.get_barrier_semaphore()
    for peer in (near, far):
        pl.semaphore_signal(barrier, inc=1, device_id={"tensor": peer}, device_id_type=MESH_ID)

    def greet(away, carry):
        peer = lax.rem(here + away, n_ring)
        pl.semaphore_signal(barrier, inc=1, device_id={"dp": peer}, device_id_type=MESH_ID)
        return carry

    lax.fori_loop(1, n_ring, greet, 0)
    pl.semaphore_wait(barrier, 2 + n_ring - 1)

    ring_start, ring_tick, ring_drain = make_ring(n_ring, sources, ins, outs, finals, leave_sem, ring_refs)
    tick, ticks, drain = make_exchange(2 * half, scratch, partial, local, between, GROUP)
    ring_start()
    for one in loads:
        one.wait()
    run_ticks(max(ticks, 2 * (n_ring - 1)), ring_tick, tick, small_start)

    def one(away, carry):
        peer = lax.rem(here + away, n_ring)
        small_copy(peer, peer).wait()
        return carry

    lax.fori_loop(1, n_ring, one, 0)

    def add(n, total):
        return total + all_small[n]

    small_sum_ref[...] = lax.fori_loop(1, n_ring, add, all_small[0])
    drain()
    ring_drain()


def last_exit(
    grad_proj, w_qkv, tokens, grad_hidden, factor, inner, gain, act, w_down, hidden_local, small, sums
):
    rows, width = tokens.shape
    n_ring = lax.axis_size("dp")
    count = len(sums)
    split = [ring_split(a, n_ring) for a in sums]
    gain_rows = width // PAD_DIM
    need = gain_rows + sum(small_rows(a.size) for a in small)
    packed = jnp.pad(pack_small(small, need - gain_rows), ((gain_rows, -need % 8), (0, 0)))
    vmem = pl.BlockSpec(memory_space=pltpu.VMEM)
    steps = 2 * rows // GROUP
    given = (grad_proj, w_qkv, tokens, grad_hidden, act, w_down, hidden_local)
    tokens_grad, out, packed, *totals = pl.pallas_call(
        functools.partial(last_exit_kernel, n_ring, count),
        out_shape=[
            jax.ShapeDtypeStruct((rows, width), F32),
            jax.ShapeDtypeStruct((rows, width), BF16),
            jax.ShapeDtypeStruct(packed.shape, F32),
        ]
        + [jax.ShapeDtypeStruct(a.shape, a.dtype) for a in split],
        in_specs=[vmem] * 4 + [pl.BlockSpec(memory_space=pl.ANY)] * (7 + count),
        out_specs=[vmem] * 3 + [pl.BlockSpec(memory_space=pl.ANY)] * count,
        scratch_shapes=[pltpu.VMEM(a.shape, a.dtype) for a in (*given, *split)]
        + [
            pltpu.SemaphoreType.DMA((7 + count,)),
        ]
        + [pltpu.VMEM(a.shape, a.dtype) for a in split]
        + [
            pltpu.SemaphoreType.DMA((2, count, n_ring)),
            pltpu.VMEM((1, width), F32),
            pltpu.VMEM(packed.shape, F32),
            pltpu.VMEM((n_ring,) + packed.shape, F32),
            pltpu.SemaphoreType.DMA((n_ring,)),
            pltpu.SemaphoreType.DMA((n_ring,)),
            pltpu.VMEM((2,) + inner.shape, F32),
            pltpu.VMEM(inner.shape, F32),
            pltpu.VMEM((rows, 1), F32),
            pltpu.SemaphoreType.DMA((2,)),
            pltpu.SemaphoreType.DMA((2,)),
        ]
        + ring_scratch(split, n_ring)
        + exchange_scratch(steps, width, w_qkv.shape[1] // width, False, GROUP),
        compiler_params=pltpu.CompilerParams(
            collective_id=3, has_side_effects=True, vmem_limit_bytes=62 << 20
        ),
        cost_estimate=COST,
        name="last_exit",
    )(factor, inner, gain, packed, *given, *split)
    gain_grad = packed[:gain_rows].reshape(width)
    totals = [t.reshape(a.shape) for t, a in zip(totals, sums)]
    return tokens_grad, gain_grad, out, unpack_small(packed[gain_rows:], small), totals


def widen_kernel(
    early_steps, gate_ref, early_ref, late_ref, down_ref, out_ref, query_ref, key_ref, value_ref,
    tokens_ref, layer_ref, gate_up_to, down_to, out_to, qkv_to, tokens_to, layer_to,
):
    step = pl.program_id(0)
    tokens_to[...] = tokens_ref[...]
    layer_to[...] = layer_ref[...]
    gate_up_to[0] = gate_ref[...].astype(F32)

    @pl.when(step < early_steps)
    def _():
        gate_up_to[1] = early_ref[...].astype(F32)

    @pl.when(step >= early_steps)
    def _():
        gate_up_to[1] = late_ref[...].astype(F32)

    down_to[...] = down_ref[...].astype(F32)
    out_to[...] = out_ref[...].astype(F32)
    for c, ref in enumerate((query_ref, key_ref, value_ref)):
        qkv_to[c] = ref[...].astype(F32)


def widen(gate, early_up, late_up, down, out, query, key, value, tokens_grad, layer_out):
    steps = 8
    full_width, units = gate.shape
    rows = full_width // steps
    early_steps = early_up.shape[0] // rows
    width = query.shape[1]

    def block(array):
        return pl.BlockSpec((array.shape[0] // steps, array.shape[1]), lambda i: (i, 0))

    return pl.pallas_call(
        functools.partial(widen_kernel, early_steps),
        grid=(steps,),
        out_shape=[
            jax.ShapeDtypeStruct((2, full_width, units), F32),
            jax.ShapeDtypeStruct(down.shape, F32),
            jax.ShapeDtypeStruct(out.shape, F32),
            jax.ShapeDtypeStruct((3, full_width, width), F32),
            jax.ShapeDtypeStruct(tokens_grad.shape, tokens_grad.dtype),
            jax.ShapeDtypeStruct(layer_out.shape, layer_out.dtype),
        ],
        in_specs=[
            block(gate),
            pl.BlockSpec((rows, units), lambda i: (jnp.minimum(i, early_steps - 1), 0)),
            pl.BlockSpec((rows, units), lambda i: (jnp.maximum(i - early_steps, 0), 0)),
            block(down),
            block(out),
            block(query),
            block(key),
            block(value),
            block(tokens_grad),
            block(layer_out),
        ],
        out_specs=[
            pl.BlockSpec((2, rows, units), lambda i: (0, i, 0)),
            block(down),
            block(out),
            pl.BlockSpec((3, rows, width), lambda i: (0, i, 0)),
            block(tokens_grad),
            block(layer_out),
        ],
        compiler_params=pltpu.CompilerParams(vmem_limit_bytes=60 << 20),
        name="widen",
    )(gate, early_up, late_up, down, out, query, key, value, tokens_grad, layer_out)


def banded(line):
    return pltpu.roll(jnp.broadcast_to(line, (WIN, WIN)), 0, 1, stride=1, stride_axis=0)


def band_line(taps, half, sign):
    lane = lax.broadcasted_iota(jnp.int32, (1, WIN), 1)
    line = jnp.zeros((1, WIN), F32)
    for b in range(taps.shape[1]):
        line = jnp.where(lane == (sign * (b - half)) % WIN, taps[:, b : b + 1], line)
    return line


def cut_heads(array, axis):
    shape = array.shape
    heads = shape[axis] // PAD_DIM
    split = array.reshape(shape[:axis] + (heads, PAD_DIM) + shape[axis + 1 :])
    cut = lax.slice_in_dim(split, 0, HEAD_DIM, axis=axis + 1)
    return cut.reshape(shape[:axis] + (heads * HEAD_DIM,) + shape[axis + 1 :])


def on_device(
    tokens, segments, attn_gain, w_qkv, kq_kernel, head_mix, group_gain, w_out, mlp_gain, w_gate_up,
    w_down, cotangent,
):
    rows_here, local_width = tokens.shape
    seq_count, length = segments.shape
    heads_here = local_width // HEAD_DIM
    n_taps, key_taps = kq_kernel.shape[1:]
    key_half = key_taps // 2

    full_width = w_qkv.shape[1]
    own_gains = jnp.concatenate([attn_gain, mlp_gain, group_gain])[None]
    taps, mixes = kq_kernel.transpose(1, 0, 2), head_mix.T
    proj, normed_one, scale_one, gains, gain_heads, start, counts = first_entry(
        tokens, w_qkv, own_gains, segments, key_half
    )
    starts = [start[n * (HALO + length) : (n + 1) * (HALO + length)] for n in range(seq_count)]
    counts = [counts[n : n + 1] for n in range(seq_count)]
    cot_here, proj = lax.optimization_barrier((cotangent, proj))
    full_cot = lax.all_gather(cot_here, "tensor", axis=1, tiled=True)

    kept = []
    for n in range(seq_count):
        rows = slice(n * length, (n + 1) * length)
        kept.append(
            attend_forward(proj[rows], starts[n], counts[n], taps, mixes, gain_heads)
        )
    grouped = jnp.concatenate([one[2] for one in kept], axis=0)
    grouped, full_cot = lax.optimization_barrier((grouped, full_cot))
    hidden_local, hidden, normed_two, w_out_pad, act, grad_gate, grad_up = attn_exit(
        grouped, w_out, tokens, gains, full_cot, w_gate_up, w_down
    )

    grad_down = dot_tn(act, full_cot).astype(BF16)
    early_rows = int(full_width * EARLY_SHARE)
    early_up = dot_tn(normed_two[:, :early_rows], grad_up).astype(BF16)
    grad_gate, early_up, grad_down = lax.optimization_barrier((grad_gate, early_up, grad_down))
    early_up, grad_down = lax.psum((early_up, grad_down), "dp")
    grad_attn, grad_hidden_local, grad_gain_two = mlp_exit(
        grad_gate, grad_up, w_gate_up, hidden, full_cot, hidden_local, cotangent, gains,
        mlp_gain.astype(F32)[None],
    )
    grad_gate_w = dot_tn(normed_two, grad_gate).astype(BF16)
    late_up = dot_tn(normed_two[:, early_rows:], grad_up).astype(BF16)
    grad_w_out = cut_heads(dot_tn(grouped, grad_attn).astype(BF16), 0)

    grad_grouped = dot_nt(grad_attn, w_out_pad)
    parts = []
    for n in range(seq_count):
        rows = slice(n * length, (n + 1) * length)
        parts.append(
            attend_backward(
                proj[rows], starts[n], counts[n], taps, mixes, gain_heads, kept[n][0], kept[n][1],
                grad_grouped[rows],
            )
        )
    grad_proj = jnp.concatenate([one[0] for one in parts], axis=0)
    inner_part = jnp.concatenate([one[1] for one in parts], axis=0)
    grad_group_gain = sum(cut_heads(one[2][0], 0) for one in parts)
    grad_kernel = sum(one[3][:, :, 0] for one in parts).reshape(heads_here, n_taps, key_taps)
    grad_mix = sum(one[4][:, :, 0] for one in parts).reshape(heads_here, 2)

    grad_qkv = [
        dot_tn(normed_one, grad_proj[:, c * local_width : (c + 1) * local_width]).astype(BF16)
        for c in range(3)
    ]
    tokens_grad, grad_gain_one, layer_out, small, sums = last_exit(
        grad_proj, w_qkv, tokens, grad_hidden_local, scale_one, inner_part, attn_gain.astype(F32)[None],
        act, w_down, hidden_local, (grad_kernel, grad_mix, grad_group_gain, grad_gain_two[0]),
        (grad_gate_w, late_up, grad_w_out, *grad_qkv),
    )
    grad_kernel, grad_mix, grad_group_gain, grad_gain_two = small
    grad_gate_w, late_up, grad_w_out, *grad_qkv = sums
    grad_gate_up, grad_down, grad_w_out, grad_qkv, tokens_grad, layer_out = widen(
        grad_gate_w, early_up, late_up, grad_down, grad_w_out, *grad_qkv, tokens_grad, layer_out
    )
    return (
        layer_out,
        tokens_grad,
        grad_gain_one,
        grad_qkv,
        grad_kernel,
        grad_mix,
        grad_group_gain,
        grad_w_out,
        grad_gain_two,
        grad_gate_up,
        grad_down,
    )


def solution(mesh):
    in_specs = (
        P("dp", "tensor"),
        P("dp", None),
        P("tensor"),
        P(None, None, "tensor"),
        P("tensor", None, None),
        P("tensor", None),
        P("tensor"),
        P("tensor", None),
        P("tensor"),
        P(None, None, "tensor"),
        P("tensor", None),
        P("dp", "tensor"),
    )
    out_specs = (
        P("dp", "tensor"),
        P("dp", "tensor"),
        P("tensor"),
        P(None, None, "tensor"),
        P("tensor", None, None),
        P("tensor", None),
        P("tensor"),
        P("tensor", None),
        P("tensor"),
        P(None, None, "tensor"),
        P("tensor", None),
    )
    return jax.shard_map(
        on_device, mesh=mesh, in_specs=in_specs, out_specs=out_specs, check_vma=False
    )
```
